32 devices in a mesh: wide: 8 (over z, y), narrow: 4 (over x, core).
Axes of the slice: x: 2, y: 2, z: 4, core: 2. Of those that a mesh axis runs over, the one named last changes fastest.
Arguments:
- inputs: bfloat16 [32768, 768], P(('wide', 'narrow')), may hold values from -6 to 6
- w_qkv: bfloat16 [768, 2304], P(('wide', 'narrow')), may hold values from -0.21875 to 0.21875
- qv_bias: bfloat16 [1536], P(('wide', 'narrow')), may hold values from -3 to 3
- w_out: bfloat16 [768, 768], P(('wide', 'narrow')), may hold values from -0.875 to 0.875
- out_bias: bfloat16 [768], P(('wide', 'narrow')), may hold values from -3 to 3
- ln1_gain: bfloat16 [768], P(('wide', 'narrow')), may hold values from 0.5 to 1.5
- ln1_shift: bfloat16 [768], P(('wide', 'narrow')), may hold values from -3 to 3
- ln2_gain: bfloat16 [768], P(('wide', 'narrow')), may hold values from 0.5 to 1.5
- ln2_shift: bfloat16 [768], P(('wide', 'narrow')), may hold values from -3 to 3
- w_up: bfloat16 [768, 3072], P(('wide', 'narrow')), may hold values from -0.21875 to 0.21875
- up_bias: bfloat16 [3072], P(('wide', 'narrow')), may hold values from -3 to 3
- w_down: bfloat16 [3072, 768], P(('wide', 'narrow')), may hold values from -0.109375 to 0.109375
- down_bias: bfloat16 [768], P(('wide', 'narrow')), may hold values from -3 to 3
- segment_ids: int32 [64, 512], P(('wide', 'narrow')), may hold values from 0 to 10, as said below
- valid: int32 [64, 512], P(('wide', 'narrow')), may hold values from 0 to 1, as said below
- cotangent: bfloat16 [32768, 768], P(('wide', 'narrow')), may hold values from -6 to 6
Outputs:
- block_out: bfloat16 [32768, 768], P(('wide', 'narrow'))
- grad_inputs: float32 [32768, 768], P(('wide', 'narrow'))
- grad_w_qkv: float32 [768, 2304], P(('wide', 'narrow'))
- grad_qv_bias: float32 [1536], P(('wide', 'narrow'))
- grad_w_out: float32 [768, 768], P(('wide', 'narrow'))
- grad_out_bias: float32 [768], P(('wide', 'narrow'))
- grad_ln1_gain: float32 [768], P(('wide', 'narrow'))
- grad_ln1_shift: float32 [768], P(('wide', 'narrow'))
- grad_ln2_gain: float32 [768], P(('wide', 'narrow'))
- grad_ln2_shift: float32 [768], P(('wide', 'narrow'))
- grad_w_up: float32 [768, 3072], P(('wide', 'narrow'))
- grad_up_bias: float32 [3072], P(('wide', 'narrow'))
- grad_w_down: float32 [3072, 768], P(('wide', 'narrow'))
- grad_down_bias: float32 [768], P(('wide', 'narrow'))
The draws below stay inside these ranges and needn't reach their ends.
Inputs may be any that keep to these rules, and one draw needn't show every extreme that they name: `segment_ids`: never falling along a sequence; images of exactly 49 rows numbered from 0, then the padding rows as one last segment; the first sequence holds 10 images. `valid`: 0 exactly on the padding rows at the end of each sequence.
All inputs are finite; a program needn't handle non-finite values.
Results may differ from the reference program's by a relative error of at most 0.0086.
Values may be sent and summed in bfloat16 or wider, within the bound.
A program may use at most 192 MiB of HBM per device.

```python
import jax
import jax.numpy as jnp
from jax import lax

D = 768
HEADS = 12
HD = 64
FF = 3072
SEQ = 512
IMG = 49
SEQ_DEV = 2
SEQS = 64
TOKENS = 32768


def pack_layout(key):
    full_count = SEQ // IMG
    image_counts = jax.random.randint(jax.random.fold_in(key, 7), (SEQS,), full_count - 2, full_count + 1)
    image_counts = image_counts.at[0].set(full_count).astype(jnp.int32)
    positions = jnp.arange(SEQ, dtype=jnp.int32)
    seg_ids = jnp.minimum(positions[None, :] // IMG, image_counts[:, None]).astype(jnp.int32)
    live_rows = (positions[None, :] < image_counts[:, None] * IMG).astype(jnp.int32)
    return (seg_ids, live_rows)


def draw_segment_ids(key, part):
    return pack_layout(key)[0]


def draw_valid(key, part):
    return pack_layout(key)[1]


def raised(array, own_key, source, target, blocks, factor):
    def block_of(axis_at):
        return (jnp.arange(array.shape[axis_at]) // (array.shape[axis_at] // blocks)).reshape((-1,) + (1,) * (array.ndim - 1 - axis_at))

    near = jax.random.permutation(own_key, blocks)[block_of(target)]
    second = (block_of(target) + blocks // 2) % blocks
    return jnp.where((block_of(source) == near) | (block_of(source) == second), factor * array, array)


def block_levels(stream_key, shape, cuts, least, top_value):
    loudness = 1.0
    for position, blocks in cuts:
        steps = jax.random.uniform(jax.random.fold_in(jax.random.fold_in(stream_key, 6), position), (blocks,), jnp.float32, least / len(cuts), top_value / len(cuts))
        loudness = loudness * jnp.repeat(jnp.exp(steps), shape[position] // blocks).reshape((-1,) + (1,) * (len(shape) - 1 - position))
    return loudness


def noise(own_key, extent, width, limit, cuts=(), kind=jnp.bfloat16):
    level = block_levels(own_key, extent, cuts, -0.22, 0.18) if cuts else 1.0
    result = jax.random.normal(own_key, extent, jnp.float32) * width * level
    return jnp.minimum(jnp.maximum(result, -limit), limit).astype(kind)


def noise_with(rng, dims, spread, reach, split, heavy, kind=jnp.bfloat16):
    array = spread * jax.random.normal(rng, dims, jnp.float32)
    if split:
        array = array * block_levels(rng, dims, split, -0.22, 0.18)
    return jnp.clip(raised(array, jax.random.fold_in(rng, 3), *heavy), -reach, reach).astype(kind)


def setup_inputs(seed: int = 0) -> dict:
    key_of = jax.random.split(jax.random.key(seed), 17)
    inputs = noise(key_of[0], (TOKENS, D), 1.0, 6.0, ((0, 32),))
    w_qkv = noise(key_of[1], (D, 3 * D), D ** -0.5, 0.21875, ((0, 32),))
    qv_bias = noise(key_of[2], (2 * D,), 0.5, 3.0, ((0, 32),))
    w_out = noise(key_of[3], (D, D), (D // 16) ** -0.5, 0.875, ((0, 32),))
    out_bias = noise(key_of[4], (D,), 0.5, 3.0, ((0, 32),))
    ln1_gain = jnp.clip(1.0 + 0.1 * jax.random.normal(key_of[5], (D,), jnp.float32), 0.5, 1.5).astype(jnp.bfloat16)
    ln1_shift = noise(key_of[6], (D,), 0.5, 3.0, ((0, 32),))
    ln2_gain = jnp.clip(1.0 + 0.1 * jax.random.normal(key_of[7], (D,), jnp.float32), 0.5, 1.5).astype(jnp.bfloat16)
    ln2_shift = noise(key_of[8], (D,), 0.5, 3.0, ((0, 32),))
    w_up = noise(key_of[9], (D, FF), D ** -0.5, 0.21875, ((0, 32),))
    up_bias = noise(key_of[10], (FF,), 0.5, 3.0, ((0, 32),))
    w_down = noise(key_of[11], (FF, D), FF ** -0.5, 0.109375, ((0, 32),))
    down_bias = noise(key_of[12], (D,), 0.5, 3.0, ((0, 32),))
    segment_ids = draw_segment_ids(jax.random.fold_in(key_of[16], 71), 0)
    valid = draw_valid(jax.random.fold_in(key_of[16], 71), 0)
    cotangent = noise_with(key_of[15], (TOKENS, D), 1.0, 6.0, ((0, 32),), (0, 1, 32, 2.75))
    return {"inputs": inputs, "w_qkv": w_qkv, "qv_bias": qv_bias, "w_out": w_out, "out_bias": out_bias, "ln1_gain": ln1_gain, "ln1_shift": ln1_shift, "ln2_gain": ln2_gain, "ln2_shift": ln2_shift, "w_up": w_up, "up_bias": up_bias, "w_down": w_down, "down_bias": down_bias, "segment_ids": segment_ids, "valid": valid, "cotangent": cotangent}


@jax.custom_vjp
def low(v):
    return lax.optimization_barrier(v.astype(jnp.bfloat16)).astype(jnp.float32)

@jax.custom_vjp
def low_back(v):
    return v

def low_keep(v):
    return (low(v), None)

def low_pass(kept, grad):
    return (grad,)

def back_keep(v):
    return (v, None)

def back_low(kept, grad):
    return (low(grad),)
low.defvjp(low_keep, low_pass)
low_back.defvjp(back_keep, back_low)
HIGH = lax.Precision.HIGHEST

def layer_norm(rows, gain, shift):
    center = rows - lax.optimization_barrier(jnp.mean(rows, axis=-1, keepdims=True))
    var_rows = lax.optimization_barrier(jnp.mean(center * center, axis=-1, keepdims=True))
    return center * lax.rsqrt(var_rows + 1e-06) * gain + shift

def forward(rows, w_qkv, qv_bias, w_out, out_bias, ln1_gain, ln1_shift, ln2_gain, ln2_shift, w_up, up_bias, w_down, down_bias, allowed):
    group = rows.shape[0]
    h_one = low(layer_norm(rows, ln1_gain, ln1_shift))
    qkv_all = jnp.einsum('gsd,de->gse', h_one, w_qkv, precision=HIGH)
    queries = low(low_back(qkv_all[..., :D] + qv_bias[:D]))
    key_rows = low(low_back(qkv_all[..., D:2 * D]))
    value_rows = low(low_back(qkv_all[..., 2 * D:] + qv_bias[D:]))
    queries = queries.reshape(group, SEQ, HEADS, HD)
    key_rows = key_rows.reshape(group, SEQ, HEADS, HD)
    value_rows = value_rows.reshape(group, SEQ, HEADS, HD)
    scores = jnp.einsum('gqhe,gkhe->ghqk', queries, key_rows, precision=HIGH) * (1.0 / HD ** 0.5)
    scores = low_back(scores)
    scores = jnp.where(allowed[:, None], scores, -1e+30)
    soft_w = jax.nn.softmax(scores, axis=-1)
    attended = jnp.einsum('ghqk,gkhe->gqhe', low(soft_w), value_rows, precision=HIGH).reshape(group, SEQ, D)
    attended = low(low_back(attended))
    branch_a = low_back(jnp.einsum('gsc,cd->gsd', attended, w_out, precision=HIGH) + out_bias)
    mid_rows = rows + branch_a
    h_two = low(layer_norm(mid_rows, ln2_gain, ln2_shift))
    upper = low_back(jnp.einsum('gsd,df->gsf', h_two, w_up, precision=HIGH) + up_bias)
    gelu_rows = low(jax.nn.gelu(upper, approximate=False))
    branch_m = low_back(jnp.einsum('gsf,fd->gsd', gelu_rows, w_down, precision=HIGH) + down_bias)
    return mid_rows + branch_m

def reference(inputs, w_qkv, qv_bias, w_out, out_bias, ln1_gain, ln1_shift, ln2_gain, ln2_shift, w_up, up_bias, w_down, down_bias, segment_ids, valid, cotangent):
    group = 4 * SEQ_DEV
    groups = SEQS // group
    params = tuple((p.astype(jnp.float32) for p in (w_qkv, qv_bias, w_out, out_bias, ln1_gain, ln1_shift, ln2_gain, ln2_shift, w_up, up_bias, w_down, down_bias)))
    rows_all = inputs.astype(jnp.float32).reshape(groups, group, SEQ, D)
    grads_all = cotangent.astype(jnp.float32).reshape(groups, group, SEQ, D)
    segs = segment_ids.reshape(groups, group, SEQ)
    valids = valid.reshape(groups, group, SEQ)
    eye_mask = jnp.eye(SEQ, dtype=bool)

    def step(acc, item):
        rows, segment, valid_keys, dy_rows = item
        allowed = (segment[:, :, None] == segment[:, None, :]) & ((valid_keys[:, None, :] == 1) | eye_mask[None])

        def run(rr, *pp):
            return forward(rr, *pp, allowed)
        out_rows, pull = jax.vjp(run, rows, *params)
        grads = pull(dy_rows)
        acc = tuple((a + g for a, g in zip(acc, grads[1:])))
        return (acc, (out_rows.astype(jnp.bfloat16), grads[0]))
    zero = tuple((jnp.zeros_like(p) for p in params))
    acc, (outs, dxs) = lax.scan(step, zero, (rows_all, segs, valids, grads_all))
    return (outs.reshape(TOKENS, D), dxs.reshape(TOKENS, D)) + acc
```

```python
import functools
import jax
import jax.numpy as jnp
from jax import lax
from jax.experimental import pallas as pl
from jax.experimental.pallas import tpu as pltpu
from jax.sharding import PartitionSpec as P

HD = 64
ALL = ("wide", "narrow")

EPSILON = 1e-06


def norm_parts(rows):
    center = rows - jnp.mean(rows, axis=-1, keepdims=True)
    recip = lax.rsqrt(jnp.mean(center * center, axis=-1, keepdims=True) + EPSILON)
    return (center * recip, recip)


def norm_back(grad_h, gain, normed, recip):
    scaled = grad_h * gain
    return recip * (
        scaled
        - jnp.mean(scaled, axis=-1, keepdims=True)
        - normed * jnp.mean(scaled * normed, axis=-1, keepdims=True)
    )


def key_mask(segment, valid_keys):
    length = segment.shape[0]
    same = segment[:, None] == segment[None, :]
    return same & ((valid_keys[None, :] == 1) | jnp.eye(length, dtype=bool))


def attend(item):
    queries, key_rows, value_rows, segment, valid_keys = item
    allowed = key_mask(segment, valid_keys)
    scores = jnp.einsum("qhe,khe->hqk", queries, key_rows, preferred_element_type=jnp.float32) * (
        1.0 / HD**0.5
    )
    scores = jnp.where(allowed[None], scores, -1e30)
    top_score = jnp.max(scores, axis=-1, keepdims=True)
    expo = jnp.exp(scores - top_score)
    total = jnp.sum(expo, axis=-1, keepdims=True)
    soft_w = (expo / total).astype(jnp.bfloat16)
    attended = jnp.einsum("hqk,khe->qhe", soft_w, value_rows, preferred_element_type=jnp.float32)
    return (attended, top_score + jnp.log(total))


def attend_back(item):
    queries, key_rows, value_rows, grad_out, log_total, segment, valid_keys = item
    allowed = key_mask(segment, valid_keys)
    scores = jnp.einsum("qhe,khe->hqk", queries, key_rows, preferred_element_type=jnp.float32) * (
        1.0 / HD**0.5
    )
    soft_w = jnp.where(allowed[None], jnp.exp(scores - log_total), 0.0)
    grad_v = jnp.einsum(
        "hqk,qhe->khe", soft_w.astype(jnp.bfloat16), grad_out, preferred_element_type=jnp.float32
    )
    grad_p = jnp.einsum("qhe,khe->hqk", grad_out, value_rows, preferred_element_type=jnp.float32)
    row_term = jnp.sum(soft_w * grad_p, axis=-1, keepdims=True)
    grad_s = jnp.where(allowed[None], soft_w * (grad_p - row_term), 0.0).astype(jnp.bfloat16)
    grad_q = jnp.einsum("hqk,khe->qhe", grad_s, key_rows, preferred_element_type=jnp.float32) * (
        1.0 / HD**0.5
    )
    grad_k = jnp.einsum("hqk,qhe->khe", grad_s, queries, preferred_element_type=jnp.float32) * (
        1.0 / HD**0.5
    )
    return (grad_q, grad_k, grad_v)


def col_sum(rows):
    return jnp.sum(rows.astype(jnp.float32), axis=0)


MESH_ID = pl.DeviceIdType.MESH


def ring_maps(n_wide, n_narrow):
    n_dev = n_wide * n_narrow
    if (n_wide, n_narrow) == (8, 4):
        def pos_of(w, n):
            z, y, x, c = w // 2, w % 2, n // 2, n % 2
            q = 2 * x + (x + y) % 2
            k = 4 * q + z + (q % 2) * (3 - 2 * z)
            return 2 * k + c

        def coords_of(p):
            k, c = p // 2, p % 2
            q, r = k // 4, k % 4
            z = r + (q % 2) * (3 - 2 * r)
            x = q // 2
            y = (q % 2 + x) % 2
            return z * 2 + y, x * 2 + c

    else:
        def pos_of(w, n):
            return w * n_narrow + n

        def coords_of(p):
            return p // n_narrow, p % n_narrow

    return n_dev, pos_of, coords_of


def ring_reduce_scatter(parts, mesh_shape, collective_id=0):
    n_wide, n_narrow = mesh_shape
    n_dev, pos_of, coords_of = ring_maps(n_wide, n_narrow)
    specs = []
    for i, (a, rb, split) in enumerate(parts):
        cols = a.shape[1]
        if split:
            specs.append((i, 0, 0, cols // 2))
            specs.append((i, 1, cols // 2, cols // 2))
        else:
            specs.append((i, 0, 0, cols))
    n_in = len(parts)
    n_sp = len(specs)

    def kernel(*refs):
        ins = refs[:n_in]
        outs = refs[n_in : 2 * n_in]
        bufs = refs[2 * n_in : 2 * n_in + n_sp]
        locs = refs[2 * n_in + n_sp : 2 * n_in + 2 * n_sp]
        send_sem, recv_sem, loc_sem, credit = refs[2 * n_in + 2 * n_sp :]
        p = pos_of(lax.axis_index("wide"), lax.axis_index("narrow"))
        right = coords_of((p + 1) % n_dev)
        left = coords_of((p + n_dev - 1) % n_dev)
        nbr_send = (right, left)
        nbr_recv = (left, right)

        def rows_of(q, rb):
            cw, cn = coords_of(q % n_dev)
            start = (cw * n_narrow + cn) * rb
            if rb % 8 == 0:
                start = pl.multiple_of(start, 8)
            return pl.ds(start, rb)

        barrier = pltpu.get_barrier_semaphore()
        for nb in (left, right):
            pl.semaphore_signal(barrier, 1, device_id=nb, device_id_type=MESH_ID)
        pl.semaphore_wait(barrier, 2)

        for j, (i, dirn, c0, cw) in enumerate(specs):
            q = p + n_dev - 1 if dirn == 0 else p + 1
            cp = pltpu.make_async_copy(
                ins[i].at[rows_of(q, parts[i][1]), pl.ds(c0, cw)], bufs[j].at[0], loc_sem.at[j]
            )
            cp.start()
            cp.wait()

        def step(s, carry):
            slot = s % 2
            nslot = 1 - slot
            for dirn in (0, 1):

                @pl.when(s >= 1)
                def _():
                    pl.semaphore_wait(credit.at[dirn], 1)

            rcopies = []
            lcopies = []
            for j, (i, dirn, c0, cw) in enumerate(specs):
                rc = pltpu.make_async_remote_copy(
                    src_ref=bufs[j].at[slot],
                    dst_ref=bufs[j].at[nslot],
                    send_sem=send_sem.at[j, slot],
                    recv_sem=recv_sem.at[j, nslot],
                    device_id=nbr_send[dirn],
                    device_id_type=MESH_ID,
                )
                rc.start()
                rcopies.append(rc)
                q = (p + 2 * n_dev - s - 2) if dirn == 0 else (p + s + 2)
                lc = pltpu.make_async_copy(
                    ins[i].at[rows_of(q, parts[i][1]), pl.ds(c0, cw)], locs[j].at[slot], loc_sem.at[j]
                )
                lc.start()
                lcopies.append(lc)
            for j in range(n_sp):
                lcopies[j].wait()
                rcopies[j].wait_recv()
                bufs[j][nslot] = bufs[j][nslot] + locs[j][slot]
            for j in range(n_sp):
                rcopies[j].wait_send()
            for dirn in (0, 1):

                @pl.when(s < n_dev - 2)
                def _():
                    pl.semaphore_signal(
                        credit.at[dirn], 1, device_id=nbr_recv[dirn], device_id_type=MESH_ID
                    )

            return carry

        lax.fori_loop(0, n_dev - 1, step, 0)
        last = (n_dev - 1) % 2
        for j, (i, dirn, c0, cw) in enumerate(specs):
            outs[i][:, pl.ds(c0, cw)] = bufs[j][last]

    out_shape = [jax.ShapeDtypeStruct((rb, a.shape[1]), a.dtype) for (a, rb, _) in parts]
    scratch = [pltpu.VMEM((2, parts[i][1], cw), jnp.float32) for (i, _, _, cw) in specs] * 2
    scratch += [
        pltpu.SemaphoreType.DMA((n_sp, 2)),
        pltpu.SemaphoreType.DMA((n_sp, 2)),
        pltpu.SemaphoreType.DMA((n_sp,)),
        pltpu.SemaphoreType.REGULAR((2,)),
    ]
    total = sum(a.size * 4 for (a, _, _) in parts)
    return pl.pallas_call(
        kernel,
        out_shape=out_shape,
        in_specs=[pl.BlockSpec(memory_space=pl.ANY)] * n_in,
        out_specs=[pl.BlockSpec(memory_space=pltpu.VMEM)] * n_in,
        scratch_shapes=scratch,
        compiler_params=pltpu.CompilerParams(
            collective_id=collective_id, has_side_effects=True, vmem_limit_bytes=48 * 1024 * 1024
        ),
        cost_estimate=pl.CostEstimate(flops=total // 4, transcendentals=0, bytes_accessed=2 * total),
    )(*[a for (a, _, _) in parts])


def pack_rows(pieces, width):
    flat = jnp.concatenate(pieces)
    return jnp.pad(flat, (0, width - flat.shape[0]))[None, :]


def split_owned(packed, sizes):
    out = []
    at = 0
    for size in sizes:
        out.append(packed[:, at : at + size].reshape(-1))
        at += size
    return out


def on_device(
    inputs,
    w_qkv,
    qv_bias,
    w_out,
    out_bias,
    ln1_gain,
    ln1_shift,
    ln2_gain,
    ln2_shift,
    w_up,
    up_bias,
    w_down,
    down_bias,
    segment_ids,
    valid,
    cotangent,
    mesh_shape=None,
):
    row_count = inputs.shape[0]
    model_width = inputs.shape[1]
    seq_count = segment_ids.shape[0]
    seq_len = segment_ids.shape[1]
    head_count = model_width // HD
    n_dev = mesh_shape[0] * mesh_shape[1]
    small = (qv_bias, out_bias, ln1_gain, ln1_shift, ln2_gain, ln2_shift, up_bias, down_bias)
    small_sizes = [a.shape[0] for a in small]
    n_small = sum(small_sizes)
    rows_q = w_qkv.size // model_width
    rows_o = w_out.shape[0]
    attn_buf = jnp.concatenate(
        [w_qkv.reshape(rows_q, model_width), w_out, pack_rows(small, model_width)], axis=0
    )
    attn_all = lax.all_gather(attn_buf, ALL, axis=0, tiled=False)
    qkv_full = attn_all[:, :rows_q].reshape(-1, w_qkv.shape[1])
    out_full = attn_all[:, rows_q : rows_q + rows_o].reshape(-1, model_width)
    small_full = split_owned(attn_all[:, rows_q + rows_o, :n_small], small_sizes)
    qv_full, outb_full, gain_one, shift_one, gain_two, shift_two, upb_full, downb_full = small_full
    rows_u = w_up.size // model_width
    mlp_buf = jnp.concatenate([w_up.reshape(rows_u, model_width), w_down], axis=0)
    mlp_all = lax.all_gather(mlp_buf, ALL, axis=0, tiled=False)
    up_full = mlp_all[:, :rows_u].reshape(-1, w_up.shape[1])
    down_full = mlp_all[:, rows_u:].reshape(-1, model_width)

    gain_one = gain_one.astype(jnp.float32)
    shift_one = shift_one.astype(jnp.float32)
    qv_full = qv_full.astype(jnp.float32)
    rows = inputs.astype(jnp.float32)
    normed_one, recip_one = norm_parts(rows)
    h_one = (normed_one * gain_one + shift_one).astype(jnp.bfloat16)
    qkv_rows = jnp.dot(h_one, qkv_full, preferred_element_type=jnp.float32)
    queries = (qkv_rows[:, :model_width] + qv_full[:model_width]).astype(jnp.bfloat16)
    key_rows = qkv_rows[:, model_width : 2 * model_width].astype(jnp.bfloat16)
    value_rows = (qkv_rows[:, 2 * model_width :] + qv_full[model_width:]).astype(jnp.bfloat16)
    shape_seq = (seq_count, seq_len, head_count, HD)
    q_seq = queries.reshape(shape_seq)
    k_seq = key_rows.reshape(shape_seq)
    v_seq = value_rows.reshape(shape_seq)
    attended, log_total = lax.map(attend, (q_seq, k_seq, v_seq, segment_ids, valid))
    attended = attended.reshape(row_count, model_width).astype(jnp.bfloat16)
    mid_rows = (
        rows
        + jnp.dot(attended, out_full, preferred_element_type=jnp.float32)
        + outb_full.astype(jnp.float32)
    )
    gain_two = gain_two.astype(jnp.float32)
    shift_two = shift_two.astype(jnp.float32)
    normed_two, recip_two = norm_parts(mid_rows)
    h_two = (normed_two * gain_two + shift_two).astype(jnp.bfloat16)
    upper = jnp.dot(h_two, up_full, preferred_element_type=jnp.float32) + upb_full.astype(
        jnp.float32
    )
    gelu_rows = jax.nn.gelu(upper, approximate=False).astype(jnp.bfloat16)
    out_rows = (
        mid_rows
        + jnp.dot(gelu_rows, down_full, preferred_element_type=jnp.float32)
        + downb_full.astype(jnp.float32)
    )
    block_out = out_rows.astype(jnp.bfloat16)
    dy_rows = cotangent.astype(jnp.float32)
    grad_wdown = jnp.einsum("tf,td->fd", gelu_rows, cotangent, preferred_element_type=jnp.float32)
    grad_bdown = col_sum(cotangent)
    grad_g = jnp.einsum("td,fd->tf", cotangent, down_full, preferred_element_type=jnp.float32)
    cdf_part = 0.5 * (1.0 + jax.scipy.special.erf(upper * 0.7071067811865476))
    pdf_part = jnp.exp(-0.5 * upper * upper) * 0.3989422804014327
    grad_u = (grad_g * (cdf_part + upper * pdf_part)).astype(jnp.bfloat16)
    grad_bup = col_sum(grad_u)
    grad_wup = jnp.einsum("td,tf->df", h_two, grad_u, preferred_element_type=jnp.float32)
    grad_h2 = jnp.einsum("tf,df->td", grad_u, up_full, preferred_element_type=jnp.float32)
    grad_g2 = jnp.sum(grad_h2 * normed_two, axis=0)
    grad_c2 = jnp.sum(grad_h2, axis=0)
    grad_mid = dy_rows + norm_back(grad_h2, gain_two, normed_two, recip_two)
    grad_a = grad_mid.astype(jnp.bfloat16)
    grad_wout = jnp.einsum("tc,td->cd", attended, grad_a, preferred_element_type=jnp.float32)
    grad_bout = col_sum(grad_a)
    grad_o = jnp.einsum("td,cd->tc", grad_a, out_full, preferred_element_type=jnp.float32).astype(
        jnp.bfloat16
    )
    grad_q, grad_k, grad_v = lax.map(
        attend_back, (q_seq, k_seq, v_seq, grad_o.reshape(shape_seq), log_total, segment_ids, valid)
    )
    grad_q = grad_q.reshape(row_count, model_width).astype(jnp.bfloat16)
    grad_k = grad_k.reshape(row_count, model_width).astype(jnp.bfloat16)
    grad_v = grad_v.reshape(row_count, model_width).astype(jnp.bfloat16)
    grad_qkv = jnp.concatenate([grad_q, grad_k, grad_v], axis=1)
    grad_bqv = jnp.concatenate([col_sum(grad_q), col_sum(grad_v)])
    grad_wqkv = jnp.einsum("td,te->de", h_one, grad_qkv, preferred_element_type=jnp.float32)
    grad_h1 = jnp.einsum("te,de->td", grad_qkv, qkv_full, preferred_element_type=jnp.float32)
    grad_g1 = jnp.sum(grad_h1 * normed_one, axis=0)
    grad_c1 = jnp.sum(grad_h1, axis=0)
    grad_inputs = grad_mid + norm_back(grad_h1, gain_one, normed_one, recip_one)

    small_grads = (grad_bqv, grad_bout, grad_g1, grad_c1, grad_g2, grad_c2, grad_bup, grad_bdown)
    owned = jnp.concatenate([g.reshape(n_dev, -1) for g in small_grads], axis=1)
    lanes = 128
    small_rows = 8 * pl.cdiv(pl.cdiv(n_small, lanes), 8)
    owned = jnp.pad(owned, ((0, 0), (0, small_rows * lanes - n_small))).reshape(-1, lanes)
    parts = [
        (grad_wqkv, w_qkv.shape[0], True),
        (grad_wout, w_out.shape[0], True),
        (grad_wup, w_up.shape[0], True),
        (grad_wdown, w_down.shape[0], True),
        (owned, small_rows, False),
    ]
    if all(rb % 8 == 0 and a.shape[1] % 256 == 0 for (a, rb, _) in parts[:4]):
        sums = ring_reduce_scatter(parts, mesh_shape)
    else:
        sums = [lax.psum_scatter(a, ALL, scatter_dimension=0, tiled=True) for (a, _, _) in parts]
    small_sums = split_owned(sums[4].reshape(1, -1), [s for s in small_sizes])
    bqv, bout, g1, c1, g2, c2, bup, bdown = small_sums
    return (
        block_out,
        grad_inputs,
        sums[0],
        bqv,
        sums[1],
        bout,
        g1,
        c1,
        g2,
        c2,
        sums[2],
        bup,
        sums[3],
        bdown,
    )


def solution(mesh):
    in_specs = (
        P(("wide", "narrow"), None),
        P(("wide", "narrow"), None),
        P(("wide", "narrow")),
        P(("wide", "narrow"), None),
        P(("wide", "narrow")),
        P(("wide", "narrow")),
        P(("wide", "narrow")),
        P(("wide", "narrow")),
        P(("wide", "narrow")),
        P(("wide", "narrow"), None),
        P(("wide", "narrow")),
        P(("wide", "narrow"), None),
        P(("wide", "narrow")),
        P(("wide", "narrow"), None),
        P(("wide", "narrow"), None),
        P(("wide", "narrow"), None),
    )
    out_specs = (
        P(("wide", "narrow"), None),
        P(("wide", "narrow"), None),
        P(("wide", "narrow"), None),
        P(("wide", "narrow")),
        P(("wide", "narrow"), None),
        P(("wide", "narrow")),
        P(("wide", "narrow")),
        P(("wide", "narrow")),
        P(("wide", "narrow")),
        P(("wide", "narrow")),
        P(("wide", "narrow"), None),
        P(("wide", "narrow")),
        P(("wide", "narrow"), None),
        P(("wide", "narrow")),
    )
    body = functools.partial(on_device, mesh_shape=(mesh.shape["wide"], mesh.shape["narrow"]))
    return jax.shard_map(
        body, mesh=mesh, in_specs=in_specs, out_specs=out_specs, check_vma=False
    )
```

```python
import functools
import jax
import jax.numpy as jnp
from jax import lax
from jax.experimental import pallas as pl
from jax.experimental.pallas import tpu as pltpu
from jax.sharding import PartitionSpec as P

HD = 64
ALL = ("wide", "narrow")

EPSILON = 1e-06


def norm_parts(rows):
    center = rows - jnp.mean(rows, axis=-1, keepdims=True)
    recip = lax.rsqrt(jnp.mean(center * center, axis=-1, keepdims=True) + EPSILON)
    return (center * recip, recip)


def norm_back(grad_h, gain, normed, recip):
    scaled = grad_h * gain
    return recip * (
        scaled
        - jnp.mean(scaled, axis=-1, keepdims=True)
        - normed * jnp.mean(scaled * normed, axis=-1, keepdims=True)
    )


def col_sum(rows):
    return jnp.sum(rows.astype(jnp.float32), axis=0)


def seg_mask(seg_col, seg_row, val_row, n):
    rows = lax.broadcasted_iota(jnp.int32, (n, n), 0)
    cols = lax.broadcasted_iota(jnp.int32, (n, n), 1)
    return (seg_col == seg_row) & ((val_row == 1) | (rows == cols))


def soft_rows(qh, kh, allowed):
    scores = lax.dot_general(qh, kh, (((1,), (1,)), ((), ())), preferred_element_type=jnp.float32)
    scores = jnp.where(allowed, scores * (1.0 / HD**0.5), -1e30)
    top = jnp.max(scores, axis=-1, keepdims=True)
    expo = jnp.exp(scores - top)
    return expo * (1.0 / jnp.sum(expo, axis=-1, keepdims=True))


def attn_fwd_kernel(q_ref, k_ref, v_ref, sc_ref, sr_ref, vr_ref, o_ref):
    n = q_ref.shape[0]
    allowed = seg_mask(sc_ref[...], sr_ref[...], vr_ref[...], n)
    outs = []
    for j in range(q_ref.shape[1] // HD):
        cols = slice(j * HD, (j + 1) * HD)
        probs = soft_rows(q_ref[:, cols], k_ref[:, cols], allowed).astype(jnp.bfloat16)
        outs.append(jnp.dot(probs, v_ref[:, cols], preferred_element_type=jnp.float32))
    o_ref[...] = jnp.concatenate(outs, axis=1).astype(o_ref.dtype)


def attn_bwd_kernel(q_ref, k_ref, v_ref, do_ref, sc_ref, sr_ref, vr_ref, dqkv_ref):
    n = q_ref.shape[0]
    width = q_ref.shape[1]
    hp = pl.program_id(1)
    model_width = dqkv_ref.shape[1] // 3
    allowed = seg_mask(sc_ref[...], sr_ref[...], vr_ref[...], n)
    dqs, dks, dvs = [], [], []
    for j in range(width // HD):
        cols = slice(j * HD, (j + 1) * HD)
        qh, kh, vh, doh = q_ref[:, cols], k_ref[:, cols], v_ref[:, cols], do_ref[:, cols]
        probs = soft_rows(qh, kh, allowed)
        dvs.append(
            lax.dot_general(probs.astype(jnp.bfloat16), doh, (((0,), (0,)), ((), ())),
                            preferred_element_type=jnp.float32)
        )
        dprobs = lax.dot_general(doh, vh, (((1,), (1,)), ((), ())), preferred_element_type=jnp.float32)
        row_term = jnp.sum(probs * dprobs, axis=-1, keepdims=True)
        dscore = jnp.where(allowed, probs * (dprobs - row_term), 0.0).astype(jnp.bfloat16)
        dqs.append(jnp.dot(dscore, kh, preferred_element_type=jnp.float32) * (1.0 / HD**0.5))
        dks.append(
            lax.dot_general(dscore, qh, (((0,), (0,)), ((), ())), preferred_element_type=jnp.float32)
            * (1.0 / HD**0.5)
        )
    at = pl.multiple_of(hp * width, width)
    dqkv_ref[:, pl.ds(at, width)] = jnp.concatenate(dqs, axis=1).astype(dqkv_ref.dtype)
    dqkv_ref[:, pl.ds(at + model_width, width)] = jnp.concatenate(dks, axis=1).astype(dqkv_ref.dtype)
    dqkv_ref[:, pl.ds(at + 2 * model_width, width)] = jnp.concatenate(dvs, axis=1).astype(dqkv_ref.dtype)


def mask_operands(segment_ids, valid):
    return (segment_ids[:, :, None], segment_ids[:, None, :], valid[:, None, :])


def attention_fwd(qkv, segment_ids, valid):
    rows, width3 = qkv.shape
    model_width = width3 // 3
    n_seq, seq_len = segment_ids.shape
    blk = 2 * HD
    n_hp = model_width // blk
    off = model_width // blk
    seg_spec = [
        pl.BlockSpec((None, seq_len, 1), lambda s, h: (s, 0, 0)),
        pl.BlockSpec((None, 1, seq_len), lambda s, h: (s, 0, 0)),
        pl.BlockSpec((None, 1, seq_len), lambda s, h: (s, 0, 0)),
    ]
    flops = 4 * n_seq * seq_len * seq_len * model_width
    return pl.pallas_call(
        attn_fwd_kernel,
        out_shape=jax.ShapeDtypeStruct((rows, model_width), jnp.bfloat16),
        grid=(n_seq, n_hp),
        in_specs=[
            pl.BlockSpec((seq_len, blk), lambda s, h: (s, h)),
            pl.BlockSpec((seq_len, blk), lambda s, h: (s, off + h)),
            pl.BlockSpec((seq_len, blk), lambda s, h: (s, 2 * off + h)),
        ]
        + seg_spec,
        out_specs=pl.BlockSpec((seq_len, blk), lambda s, h: (s, h)),
        cost_estimate=pl.CostEstimate(
            flops=flops,
            transcendentals=n_seq * seq_len * seq_len * (model_width // HD),
            bytes_accessed=qkv.size * 2 + rows * model_width * 2,
        ),
    )(qkv, qkv, qkv, *mask_operands(segment_ids, valid))


def attention_bwd(qkv, grad_o, segment_ids, valid):
    rows, width3 = qkv.shape
    model_width = width3 // 3
    n_seq, seq_len = segment_ids.shape
    blk = 2 * HD
    n_hp = model_width // blk
    off = model_width // blk
    seg_spec = [
        pl.BlockSpec((None, seq_len, 1), lambda s, h: (s, 0, 0)),
        pl.BlockSpec((None, 1, seq_len), lambda s, h: (s, 0, 0)),
        pl.BlockSpec((None, 1, seq_len), lambda s, h: (s, 0, 0)),
    ]
    flops = 10 * n_seq * seq_len * seq_len * model_width
    return pl.pallas_call(
        attn_bwd_kernel,
        out_shape=jax.ShapeDtypeStruct((rows, width3), jnp.bfloat16),
        grid=(n_seq, n_hp),
        in_specs=[
            pl.BlockSpec((seq_len, blk), lambda s, h: (s, h)),
            pl.BlockSpec((seq_len, blk), lambda s, h: (s, off + h)),
            pl.BlockSpec((seq_len, blk), lambda s, h: (s, 2 * off + h)),
            pl.BlockSpec((seq_len, blk), lambda s, h: (s, h)),
        ]
        + seg_spec,
        out_specs=pl.BlockSpec((seq_len, width3), lambda s, h: (s, 0)),
        cost_estimate=pl.CostEstimate(
            flops=flops,
            transcendentals=n_seq * seq_len * seq_len * (model_width // HD),
            bytes_accessed=qkv.size * 4 + rows * model_width * 2,
        ),
    )(qkv, qkv, qkv, grad_o, *mask_operands(segment_ids, valid))


MESH_ID = pl.DeviceIdType.MESH


def ring_maps(n_wide, n_narrow):
    n_dev = n_wide * n_narrow
    if (n_wide, n_narrow) == (8, 4):
        def pos_of(w, n):
            z, y, x, c = w // 2, w % 2, n // 2, n % 2
            q = 2 * x + (x + y) % 2
            k = 4 * q + z + (q % 2) * (3 - 2 * z)
            return 2 * k + c

        def coords_of(p):
            k, c = p // 2, p % 2
            q, r = k // 4, k % 4
            z = r + (q % 2) * (3 - 2 * r)
            x = q // 2
            y = (q % 2 + x) % 2
            return z * 2 + y, x * 2 + c

    else:
        def pos_of(w, n):
            return w * n_narrow + n

        def coords_of(p):
            return p // n_narrow, p % n_narrow

    return n_dev, pos_of, coords_of


def ring_reduce_scatter(parts, mesh_shape, collective_id=0):
    n_wide, n_narrow = mesh_shape
    n_dev, pos_of, coords_of = ring_maps(n_wide, n_narrow)
    specs = []
    for i, (a, rb, split) in enumerate(parts):
        cols = a.shape[1]
        if split:
            specs.append((i, 0, 0, cols // 2))
            specs.append((i, 1, cols // 2, cols // 2))
        else:
            specs.append((i, 0, 0, cols))
    n_in = len(parts)
    n_sp = len(specs)

    def kernel(*refs):
        ins = refs[:n_in]
        outs = refs[n_in : 2 * n_in]
        bufs = refs[2 * n_in : 2 * n_in + n_sp]
        locs = refs[2 * n_in + n_sp : 2 * n_in + 2 * n_sp]
        send_sem, recv_sem, loc_sem, credit = refs[2 * n_in + 2 * n_sp :]
        p = pos_of(lax.axis_index("wide"), lax.axis_index("narrow"))
        right = coords_of((p + 1) % n_dev)
        left = coords_of((p + n_dev - 1) % n_dev)
        nbr_send = (right, left)
        nbr_recv = (left, right)

        def rows_of(q, rb):
            cw, cn = coords_of(q % n_dev)
            start = (cw * n_narrow + cn) * rb
            if rb % 8 == 0:
                start = pl.multiple_of(start, 8)
            return pl.ds(start, rb)

        barrier = pltpu.get_barrier_semaphore()
        for nb in (left, right):
            pl.semaphore_signal(barrier, 1, device_id=nb, device_id_type=MESH_ID)
        pl.semaphore_wait(barrier, 2)

        for j, (i, dirn, c0, cw) in enumerate(specs):
            q = p + n_dev - 1 if dirn == 0 else p + 1
            cp = pltpu.make_async_copy(
                ins[i].at[rows_of(q, parts[i][1]), pl.ds(c0, cw)], bufs[j].at[0], loc_sem.at[j]
            )
            cp.start()
            cp.wait()

        def step(s, carry):
            slot = s % 2
            nslot = 1 - slot
            for dirn in (0, 1):

                @pl.when(s >= 1)
                def _():
                    pl.semaphore_wait(credit.at[dirn], 1)

            rcopies = []
            lcopies = []
            for j, (i, dirn, c0, cw) in enumerate(specs):
                rc = pltpu.make_async_remote_copy(
                    src_ref=bufs[j].at[slot],
                    dst_ref=bufs[j].at[nslot],
                    send_sem=send_sem.at[j, slot],
                    recv_sem=recv_sem.at[j, nslot],
                    device_id=nbr_send[dirn],
                    device_id_type=MESH_ID,
                )
                rc.start()
                rcopies.append(rc)
                q = (p + 2 * n_dev - s - 2) if dirn == 0 else (p + s + 2)
                lc = pltpu.make_async_copy(
                    ins[i].at[rows_of(q, parts[i][1]), pl.ds(c0, cw)], locs[j].at[slot], loc_sem.at[j]
                )
                lc.start()
                lcopies.append(lc)
            for j in range(n_sp):
                lcopies[j].wait()
                rcopies[j].wait_recv()
                bufs[j][nslot] = bufs[j][nslot] + locs[j][slot]
            for j in range(n_sp):
                rcopies[j].wait_send()
            for dirn in (0, 1):

                @pl.when(s < n_dev - 2)
                def _():
                    pl.semaphore_signal(
                        credit.at[dirn], 1, device_id=nbr_recv[dirn], device_id_type=MESH_ID
                    )

            return carry

        lax.fori_loop(0, n_dev - 1, step, 0)
        last = (n_dev - 1) % 2
        for j, (i, dirn, c0, cw) in enumerate(specs):
            outs[i][:, pl.ds(c0, cw)] = bufs[j][last]

    out_shape = [jax.ShapeDtypeStruct((rb, a.shape[1]), a.dtype) for (a, rb, _) in parts]
    scratch = [pltpu.VMEM((2, parts[i][1], cw), jnp.float32) for (i, _, _, cw) in specs] * 2
    scratch += [
        pltpu.SemaphoreType.DMA((n_sp, 2)),
        pltpu.SemaphoreType.DMA((n_sp, 2)),
        pltpu.SemaphoreType.DMA((n_sp,)),
        pltpu.SemaphoreType.REGULAR((2,)),
    ]
    total = sum(a.size * 4 for (a, _, _) in parts)
    return pl.pallas_call(
        kernel,
        out_shape=out_shape,
        in_specs=[pl.BlockSpec(memory_space=pl.ANY)] * n_in,
        out_specs=[pl.BlockSpec(memory_space=pltpu.VMEM)] * n_in,
        scratch_shapes=scratch,
        compiler_params=pltpu.CompilerParams(
            collective_id=collective_id, has_side_effects=True, vmem_limit_bytes=48 * 1024 * 1024
        ),
        cost_estimate=pl.CostEstimate(flops=total // 4, transcendentals=0, bytes_accessed=2 * total),
    )(*[a for (a, _, _) in parts])


def pack_rows(pieces, width):
    flat = jnp.concatenate(pieces)
    return jnp.pad(flat, (0, width - flat.shape[0]))[None, :]


def split_owned(packed, sizes):
    out = []
    at = 0
    for size in sizes:
        out.append(packed[:, at : at + size].reshape(-1))
        at += size
    return out


def on_device(
    inputs,
    w_qkv,
    qv_bias,
    w_out,
    out_bias,
    ln1_gain,
    ln1_shift,
    ln2_gain,
    ln2_shift,
    w_up,
    up_bias,
    w_down,
    down_bias,
    segment_ids,
    valid,
    cotangent,
    mesh_shape=None,
):
    row_count = inputs.shape[0]
    model_width = inputs.shape[1]
    seq_count = segment_ids.shape[0]
    seq_len = segment_ids.shape[1]
    head_count = model_width // HD
    n_dev = mesh_shape[0] * mesh_shape[1]
    small = (qv_bias, out_bias, ln1_gain, ln1_shift, ln2_gain, ln2_shift, up_bias, down_bias)
    small_sizes = [a.shape[0] for a in small]
    n_small = sum(small_sizes)
    rows_q = w_qkv.size // model_width
    rows_o = w_out.shape[0]
    attn_buf = jnp.concatenate(
        [w_qkv.reshape(rows_q, model_width), w_out, pack_rows(small, model_width)], axis=0
    )
    attn_all = lax.all_gather(attn_buf, ALL, axis=0, tiled=False)
    qkv_full = attn_all[:, :rows_q].reshape(-1, w_qkv.shape[1])
    out_full = attn_all[:, rows_q : rows_q + rows_o].reshape(-1, model_width)
    small_full = split_owned(attn_all[:, rows_q + rows_o, :n_small], small_sizes)
    qv_full, outb_full, gain_one, shift_one, gain_two, shift_two, upb_full, downb_full = small_full
    rows_u = w_up.size // model_width
    mlp_buf = jnp.concatenate([w_up.reshape(rows_u, model_width), w_down], axis=0)
    mlp_all = lax.all_gather(mlp_buf, ALL, axis=0, tiled=False)
    up_full = mlp_all[:, :rows_u].reshape(-1, w_up.shape[1])
    down_full = mlp_all[:, rows_u:].reshape(-1, model_width)

    gain_one = gain_one.astype(jnp.float32)
    shift_one = shift_one.astype(jnp.float32)
    qv_full = qv_full.astype(jnp.float32)
    rows = inputs.astype(jnp.float32)
    normed_one, recip_one = norm_parts(rows)
    h_one = (normed_one * gain_one + shift_one).astype(jnp.bfloat16)
    qkv_rows = jnp.dot(h_one, qkv_full, preferred_element_type=jnp.float32)
    zero_bias = jnp.zeros((model_width,), jnp.float32)
    qkv_bias = jnp.concatenate([qv_full[:model_width], zero_bias, qv_full[model_width:]])
    qkv_b = (qkv_rows + qkv_bias).astype(jnp.bfloat16)
    attended = attention_fwd(qkv_b, segment_ids, valid)
    mid_rows = (
        rows
        + jnp.dot(attended, out_full, preferred_element_type=jnp.float32)
        + outb_full.astype(jnp.float32)
    )
    gain_two = gain_two.astype(jnp.float32)
    shift_two = shift_two.astype(jnp.float32)
    normed_two, recip_two = norm_parts(mid_rows)
    h_two = (normed_two * gain_two + shift_two).astype(jnp.bfloat16)
    upper = jnp.dot(h_two, up_full, preferred_element_type=jnp.float32) + upb_full.astype(
        jnp.float32
    )
    gelu_rows = jax.nn.gelu(upper, approximate=False).astype(jnp.bfloat16)
    out_rows = (
        mid_rows
        + jnp.dot(gelu_rows, down_full, preferred_element_type=jnp.float32)
        + downb_full.astype(jnp.float32)
    )
    block_out = out_rows.astype(jnp.bfloat16)
    dy_rows = cotangent.astype(jnp.float32)
    grad_wdown = jnp.einsum("tf,td->fd", gelu_rows, cotangent, preferred_element_type=jnp.float32)
    grad_bdown = col_sum(cotangent)
    grad_g = jnp.einsum("td,fd->tf", cotangent, down_full, preferred_element_type=jnp.float32)
    cdf_part = 0.5 * (1.0 + jax.scipy.special.erf(upper * 0.7071067811865476))
    pdf_part = jnp.exp(-0.5 * upper * upper) * 0.3989422804014327
    grad_u = (grad_g * (cdf_part + upper * pdf_part)).astype(jnp.bfloat16)
    grad_bup = col_sum(grad_u)
    grad_wup = jnp.einsum("td,tf->df", h_two, grad_u, preferred_element_type=jnp.float32)
    grad_h2 = jnp.einsum("tf,df->td", grad_u, up_full, preferred_element_type=jnp.float32)
    grad_g2 = jnp.sum(grad_h2 * normed_two, axis=0)
    grad_c2 = jnp.sum(grad_h2, axis=0)
    grad_mid = dy_rows + norm_back(grad_h2, gain_two, normed_two, recip_two)
    grad_a = grad_mid.astype(jnp.bfloat16)
    grad_wout = jnp.einsum("tc,td->cd", attended, grad_a, preferred_element_type=jnp.float32)
    grad_bout = col_sum(grad_a)
    grad_o = jnp.einsum("td,cd->tc", grad_a, out_full, preferred_element_type=jnp.float32).astype(
        jnp.bfloat16
    )
    grad_qkv = attention_bwd(qkv_b, grad_o, segment_ids, valid)
    grad_cols = col_sum(grad_qkv)
    grad_bqv = jnp.concatenate([grad_cols[:model_width], grad_cols[2 * model_width :]])
    grad_wqkv = jnp.einsum("td,te->de", h_one, grad_qkv, preferred_element_type=jnp.float32)
    grad_h1 = jnp.einsum("te,de->td", grad_qkv, qkv_full, preferred_element_type=jnp.float32)
    grad_g1 = jnp.sum(grad_h1 * normed_one, axis=0)
    grad_c1 = jnp.sum(grad_h1, axis=0)
    grad_inputs = grad_mid + norm_back(grad_h1, gain_one, normed_one, recip_one)

    small_grads = (grad_bqv, grad_bout, grad_g1, grad_c1, grad_g2, grad_c2, grad_bup, grad_bdown)
    owned = jnp.concatenate([g.reshape(n_dev, -1) for g in small_grads], axis=1)
    lanes = 128
    small_rows = 8 * pl.cdiv(pl.cdiv(n_small, lanes), 8)
    owned = jnp.pad(owned, ((0, 0), (0, small_rows * lanes - n_small))).reshape(-1, lanes)
    parts = [
        (grad_wqkv, w_qkv.shape[0], True),
        (grad_wout, w_out.shape[0], True),
        (grad_wup, w_up.shape[0], True),
        (grad_wdown, w_down.shape[0], True),
        (owned, small_rows, False),
    ]
    if all(rb % 8 == 0 and a.shape[1] % 256 == 0 for (a, rb, _) in parts[:4]):
        sums = ring_reduce_scatter(parts, mesh_shape)
    else:
        sums = [lax.psum_scatter(a, ALL, scatter_dimension=0, tiled=True) for (a, _, _) in parts]
    small_sums = split_owned(sums[4].reshape(1, -1), [s for s in small_sizes])
    bqv, bout, g1, c1, g2, c2, bup, bdown = small_sums
    return (
        block_out,
        grad_inputs,
        sums[0],
        bqv,
        sums[1],
        bout,
        g1,
        c1,
        g2,
        c2,
        sums[2],
        bup,
        sums[3],
        bdown,
    )


def solution(mesh):
    in_specs = (
        P(("wide", "narrow"), None),
        P(("wide", "narrow"), None),
        P(("wide", "narrow")),
        P(("wide", "narrow"), None),
        P(("wide", "narrow")),
        P(("wide", "narrow")),
        P(("wide", "narrow")),
        P(("wide", "narrow")),
        P(("wide", "narrow")),
        P(("wide", "narrow"), None),
        P(("wide", "narrow")),
        P(("wide", "narrow"), None),
        P(("wide", "narrow")),
        P(("wide", "narrow"), None),
        P(("wide", "narrow"), None),
        P(("wide", "narrow"), None),
    )
    out_specs = (
        P(("wide", "narrow"), None),
        P(("wide", "narrow"), None),
        P(("wide", "narrow"), None),
        P(("wide", "narrow")),
        P(("wide", "narrow"), None),
        P(("wide", "narrow")),
        P(("wide", "narrow")),
        P(("wide", "narrow")),
        P(("wide", "narrow")),
        P(("wide", "narrow")),
        P(("wide", "narrow"), None),
        P(("wide", "narrow")),
        P(("wide", "narrow"), None),
        P(("wide", "narrow")),
    )
    body = functools.partial(on_device, mesh_shape=(mesh.shape["wide"], mesh.shape["narrow"]))
    return jax.shard_map(
        body, mesh=mesh, in_specs=in_specs, out_specs=out_specs, check_vma=False
    )
```

```python
import functools
import jax
import jax.numpy as jnp
from jax import lax
from jax.experimental import pallas as pl
from jax.experimental.pallas import tpu as pltpu
from jax.sharding import PartitionSpec as P

HD = 64
ALL = ("wide", "narrow")

EPSILON = 1e-06


def norm_parts(rows):
    center = rows - jnp.mean(rows, axis=-1, keepdims=True)
    recip = lax.rsqrt(jnp.mean(center * center, axis=-1, keepdims=True) + EPSILON)
    return (center * recip, recip)


def norm_back(grad_h, gain, normed, recip):
    scaled = grad_h * gain
    return recip * (
        scaled
        - jnp.mean(scaled, axis=-1, keepdims=True)
        - normed * jnp.mean(scaled * normed, axis=-1, keepdims=True)
    )


def col_sum(rows):
    return jnp.sum(rows.astype(jnp.float32), axis=0)


def seg_mask(seg_col, seg_row, val_row, n):
    rows = lax.broadcasted_iota(jnp.int32, (n, n), 0)
    cols = lax.broadcasted_iota(jnp.int32, (n, n), 1)
    return (seg_col == seg_row) & ((val_row == 1) | (rows == cols))


def soft_rows(qh, kh, allowed):
    scores = lax.dot_general(qh, kh, (((1,), (1,)), ((), ())), preferred_element_type=jnp.float32)
    scores = jnp.where(allowed, scores * (1.0 / HD**0.5), -1e30)
    top = jnp.max(scores, axis=-1, keepdims=True)
    expo = jnp.exp(scores - top)
    return expo * (1.0 / jnp.sum(expo, axis=-1, keepdims=True))


def attn_fwd_kernel(q_ref, k_ref, v_ref, sc_ref, sr_ref, vr_ref, o_ref):
    n = q_ref.shape[0]
    allowed = seg_mask(sc_ref[...], sr_ref[...], vr_ref[...], n)
    outs = []
    for j in range(q_ref.shape[1] // HD):
        cols = slice(j * HD, (j + 1) * HD)
        probs = soft_rows(q_ref[:, cols], k_ref[:, cols], allowed).astype(jnp.bfloat16)
        outs.append(jnp.dot(probs, v_ref[:, cols], preferred_element_type=jnp.float32))
    o_ref[...] = jnp.concatenate(outs, axis=1).astype(o_ref.dtype)


def attn_bwd_kernel(q_ref, k_ref, v_ref, do_ref, sc_ref, sr_ref, vr_ref, dqkv_ref):
    n = q_ref.shape[0]
    width = q_ref.shape[1]
    hp = pl.program_id(1)
    model_width = dqkv_ref.shape[1] // 3
    allowed = seg_mask(sc_ref[...], sr_ref[...], vr_ref[...], n)
    dqs, dks, dvs = [], [], []
    for j in range(width // HD):
        cols = slice(j * HD, (j + 1) * HD)
        qh, kh, vh, doh = q_ref[:, cols], k_ref[:, cols], v_ref[:, cols], do_ref[:, cols]
        probs = soft_rows(qh, kh, allowed)
        dvs.append(
            lax.dot_general(probs.astype(jnp.bfloat16), doh, (((0,), (0,)), ((), ())),
                            preferred_element_type=jnp.float32)
        )
        dprobs = lax.dot_general(doh, vh, (((1,), (1,)), ((), ())), preferred_element_type=jnp.float32)
        row_term = jnp.sum(probs * dprobs, axis=-1, keepdims=True)
        dscore = jnp.where(allowed, probs * (dprobs - row_term), 0.0).astype(jnp.bfloat16)
        dqs.append(jnp.dot(dscore, kh, preferred_element_type=jnp.float32) * (1.0 / HD**0.5))
        dks.append(
            lax.dot_general(dscore, qh, (((0,), (0,)), ((), ())), preferred_element_type=jnp.float32)
            * (1.0 / HD**0.5)
        )
    at = pl.multiple_of(hp * width, width)
    dqkv_ref[:, pl.ds(at, width)] = jnp.concatenate(dqs, axis=1).astype(dqkv_ref.dtype)
    dqkv_ref[:, pl.ds(at + model_width, width)] = jnp.concatenate(dks, axis=1).astype(dqkv_ref.dtype)
    dqkv_ref[:, pl.ds(at + 2 * model_width, width)] = jnp.concatenate(dvs, axis=1).astype(dqkv_ref.dtype)


def mask_operands(segment_ids, valid):
    return (segment_ids[:, :, None], segment_ids[:, None, :], valid[:, None, :])


def attention_fwd(qkv, segment_ids, valid):
    rows, width3 = qkv.shape
    model_width = width3 // 3
    n_seq, seq_len = segment_ids.shape
    blk = 2 * HD
    n_hp = model_width // blk
    off = model_width // blk
    seg_spec = [
        pl.BlockSpec((None, seq_len, 1), lambda s, h: (s, 0, 0)),
        pl.BlockSpec((None, 1, seq_len), lambda s, h: (s, 0, 0)),
        pl.BlockSpec((None, 1, seq_len), lambda s, h: (s, 0, 0)),
    ]
    flops = 4 * n_seq * seq_len * seq_len * model_width
    return pl.pallas_call(
        attn_fwd_kernel,
        out_shape=jax.ShapeDtypeStruct((rows, model_width), jnp.bfloat16),
        grid=(n_seq, n_hp),
        in_specs=[
            pl.BlockSpec((seq_len, blk), lambda s, h: (s, h)),
            pl.BlockSpec((seq_len, blk), lambda s, h: (s, off + h)),
            pl.BlockSpec((seq_len, blk), lambda s, h: (s, 2 * off + h)),
        ]
        + seg_spec,
        out_specs=pl.BlockSpec((seq_len, blk), lambda s, h: (s, h)),
        cost_estimate=pl.CostEstimate(
            flops=flops,
            transcendentals=n_seq * seq_len * seq_len * (model_width // HD),
            bytes_accessed=qkv.size * 2 + rows * model_width * 2,
        ),
    )(qkv, qkv, qkv, *mask_operands(segment_ids, valid))


def attention_bwd(qkv, grad_o, segment_ids, valid):
    rows, width3 = qkv.shape
    model_width = width3 // 3
    n_seq, seq_len = segment_ids.shape
    blk = 2 * HD
    n_hp = model_width // blk
    off = model_width // blk
    seg_spec = [
        pl.BlockSpec((None, seq_len, 1), lambda s, h: (s, 0, 0)),
        pl.BlockSpec((None, 1, seq_len), lambda s, h: (s, 0, 0)),
        pl.BlockSpec((None, 1, seq_len), lambda s, h: (s, 0, 0)),
    ]
    flops = 10 * n_seq * seq_len * seq_len * model_width
    return pl.pallas_call(
        attn_bwd_kernel,
        out_shape=jax.ShapeDtypeStruct((rows, width3), jnp.bfloat16),
        grid=(n_seq, n_hp),
        in_specs=[
            pl.BlockSpec((seq_len, blk), lambda s, h: (s, h)),
            pl.BlockSpec((seq_len, blk), lambda s, h: (s, off + h)),
            pl.BlockSpec((seq_len, blk), lambda s, h: (s, 2 * off + h)),
            pl.BlockSpec((seq_len, blk), lambda s, h: (s, h)),
        ]
        + seg_spec,
        out_specs=pl.BlockSpec((seq_len, width3), lambda s, h: (s, 0)),
        cost_estimate=pl.CostEstimate(
            flops=flops,
            transcendentals=n_seq * seq_len * seq_len * (model_width // HD),
            bytes_accessed=qkv.size * 4 + rows * model_width * 2,
        ),
    )(qkv, qkv, qkv, grad_o, *mask_operands(segment_ids, valid))


MESH_ID = pl.DeviceIdType.MESH


def ring_maps(n_wide, n_narrow):
    n_dev = n_wide * n_narrow
    if (n_wide, n_narrow) == (8, 4):
        def pos_of(w, n):
            z, y, x, c = w // 2, w % 2, n // 2, n % 2
            q = 2 * x + (x + y) % 2
            k = 4 * q + z + (q % 2) * (3 - 2 * z)
            return 2 * k + c

        def coords_of(p):
            k, c = p // 2, p % 2
            q, r = k // 4, k % 4
            z = r + (q % 2) * (3 - 2 * r)
            x = q // 2
            y = (q % 2 + x) % 2
            return z * 2 + y, x * 2 + c

    else:
        def pos_of(w, n):
            return w * n_narrow + n

        def coords_of(p):
            return p // n_narrow, p % n_narrow

    return n_dev, pos_of, coords_of


def ring_reduce_scatter(parts, mesh_shape, after=(), collective_id=0):
    n_wide, n_narrow = mesh_shape
    n_dev, pos_of, coords_of = ring_maps(n_wide, n_narrow)
    specs = []
    for i, (a, rb, split) in enumerate(parts):
        cols = a.shape[1]
        if split:
            specs.append((i, 0, 0, cols // 2))
        else:
            specs.append((i, 0, 0, cols))
    for i, (a, rb, split) in enumerate(parts):
        if split:
            specs.append((i, 1, a.shape[1] // 2, a.shape[1] // 2))
    n_in = len(parts)
    n_after = len(after)
    n_sp = len(specs)
    last_step = n_dev - 2

    def kernel(*refs):
        ins = refs[:n_in]
        outs = refs[n_in + n_after : 2 * n_in + n_after]
        at = 2 * n_in + n_after
        bufs = refs[at : at + n_sp]
        locs = refs[at + n_sp : at + 2 * n_sp]
        send_sem, recv_sem, loc_sem, credit = refs[at + 2 * n_sp :]
        p = pos_of(lax.axis_index("wide"), lax.axis_index("narrow"))
        right = coords_of((p + 1) % n_dev)
        left = coords_of((p + n_dev - 1) % n_dev)
        nbr_send = (right, left)
        nbr_recv = (left, right)

        def rows_of(q, rb):
            cw, cn = coords_of(q % n_dev)
            start = (cw * n_narrow + cn) * rb
            if rb % 8 == 0:
                start = pl.multiple_of(start, 8)
            return pl.ds(start, rb)

        def remote(j, s):
            return pltpu.make_async_remote_copy(
                src_ref=bufs[j].at[s % 3],
                dst_ref=bufs[j].at[(s + 1) % 3],
                send_sem=send_sem.at[j, s % 3],
                recv_sem=recv_sem.at[j, (s + 1) % 3],
                device_id=nbr_send[specs[j][1]],
                device_id_type=MESH_ID,
            )

        def local(j, s):
            i, dirn, c0, cw = specs[j]
            q = (p + 2 * n_dev - s - 2) if dirn == 0 else (p + s + 2)
            return pltpu.make_async_copy(
                ins[i].at[rows_of(q, parts[i][1]), pl.ds(c0, cw)], locs[j].at[s % 2], loc_sem.at[j, s % 2]
            )

        barrier = pltpu.get_barrier_semaphore()
        for nb in (left, right):
            pl.semaphore_signal(barrier, 1, device_id=nb, device_id_type=MESH_ID)
        pl.semaphore_wait(barrier, 2)

        for j, (i, dirn, c0, cw) in enumerate(specs):
            q = p + n_dev - 1 if dirn == 0 else p + 1
            cp = pltpu.make_async_copy(
                ins[i].at[rows_of(q, parts[i][1]), pl.ds(c0, cw)], bufs[j].at[0], loc_sem.at[j, 1]
            )
            cp.start()
            cp.wait()
        for j in range(n_sp):
            remote(j, 0).start()
            local(j, 0).start()

        def step(s, carry):
            for j in range(n_sp):
                dirn = specs[j][1]
                local(j, s).wait()
                remote(j, s).wait_recv()
                nxt = (s + 1) % 3
                bufs[j][nxt] = bufs[j][nxt] + locs[j][s % 2]
                if j == 0 or specs[j - 1][1] != dirn:

                    @pl.when((s >= 1) & (s + 1 <= last_step))
                    def _():
                        pl.semaphore_wait(credit.at[dirn], 1)

                @pl.when(s + 1 <= last_step)
                def _():
                    remote(j, s + 1).start()
                    local(j, s + 1).start()

            for j in range(n_sp):
                remote(j, s).wait_send()
            for dirn in (0, 1):

                @pl.when(s <= last_step - 2)
                def _():
                    pl.semaphore_signal(
                        credit.at[dirn], 1, device_id=nbr_recv[dirn], device_id_type=MESH_ID
                    )

            return carry

        lax.fori_loop(0, last_step + 1, step, 0)
        fin = (last_step + 1) % 3
        for j, (i, dirn, c0, cw) in enumerate(specs):
            outs[i][:, pl.ds(c0, cw)] = bufs[j][fin]

    out_shape = [jax.ShapeDtypeStruct((rb, a.shape[1]), a.dtype) for (a, rb, _) in parts]
    scratch = [pltpu.VMEM((3, parts[i][1], cw), jnp.float32) for (i, _, _, cw) in specs]
    scratch += [pltpu.VMEM((2, parts[i][1], cw), jnp.float32) for (i, _, _, cw) in specs]
    scratch += [
        pltpu.SemaphoreType.DMA((n_sp, 3)),
        pltpu.SemaphoreType.DMA((n_sp, 3)),
        pltpu.SemaphoreType.DMA((n_sp, 2)),
        pltpu.SemaphoreType.REGULAR((2,)),
    ]
    total = sum(a.size * 4 for (a, _, _) in parts)
    return pl.pallas_call(
        kernel,
        out_shape=out_shape,
        in_specs=[pl.BlockSpec(memory_space=pl.ANY)] * (n_in + n_after),
        out_specs=[pl.BlockSpec(memory_space=pltpu.VMEM)] * n_in,
        scratch_shapes=scratch,
        compiler_params=pltpu.CompilerParams(
            collective_id=collective_id, has_side_effects=True, vmem_limit_bytes=48 * 1024 * 1024
        ),
        cost_estimate=pl.CostEstimate(flops=total // 4, transcendentals=0, bytes_accessed=2 * total),
    )(*[a for (a, _, _) in parts], *after)


def pack_rows(pieces, width):
    flat = jnp.concatenate(pieces)
    return jnp.pad(flat, (0, width - flat.shape[0]))[None, :]


def split_owned(packed, sizes):
    out = []
    at = 0
    for size in sizes:
        out.append(packed[:, at : at + size].reshape(-1))
        at += size
    return out


def on_device(
    inputs,
    w_qkv,
    qv_bias,
    w_out,
    out_bias,
    ln1_gain,
    ln1_shift,
    ln2_gain,
    ln2_shift,
    w_up,
    up_bias,
    w_down,
    down_bias,
    segment_ids,
    valid,
    cotangent,
    mesh_shape=None,
):
    row_count = inputs.shape[0]
    model_width = inputs.shape[1]
    seq_count = segment_ids.shape[0]
    seq_len = segment_ids.shape[1]
    head_count = model_width // HD
    n_dev = mesh_shape[0] * mesh_shape[1]
    small = (qv_bias, out_bias, ln1_gain, ln1_shift, ln2_gain, ln2_shift, up_bias, down_bias)
    small_sizes = [a.shape[0] for a in small]
    n_small = sum(small_sizes)
    rows_q = w_qkv.size // model_width
    rows_o = w_out.shape[0]
    attn_buf = jnp.concatenate(
        [w_qkv.reshape(rows_q, model_width), w_out, pack_rows(small, model_width)], axis=0
    )
    attn_all = lax.all_gather(attn_buf, ALL, axis=0, tiled=False)
    qkv_full = attn_all[:, :rows_q].reshape(-1, w_qkv.shape[1])
    out_full = attn_all[:, rows_q : rows_q + rows_o].reshape(-1, model_width)
    small_full = split_owned(attn_all[:, rows_q + rows_o, :n_small], small_sizes)
    qv_full, outb_full, gain_one, shift_one, gain_two, shift_two, upb_full, downb_full = small_full
    rows_u = w_up.size // model_width
    mlp_buf = jnp.concatenate([w_up.reshape(rows_u, model_width), w_down], axis=0)
    mlp_all = lax.all_gather(mlp_buf, ALL, axis=0, tiled=False)
    up_full = mlp_all[:, :rows_u].reshape(-1, w_up.shape[1])
    down_full = mlp_all[:, rows_u:].reshape(-1, model_width)

    gain_one = gain_one.astype(jnp.float32)
    shift_one = shift_one.astype(jnp.float32)
    qv_full = qv_full.astype(jnp.float32)
    rows = inputs.astype(jnp.float32)
    normed_one, recip_one = norm_parts(rows)
    h_one = (normed_one * gain_one + shift_one).astype(jnp.bfloat16)
    qkv_rows = jnp.dot(h_one, qkv_full, preferred_element_type=jnp.float32)
    zero_bias = jnp.zeros((model_width,), jnp.float32)
    qkv_bias = jnp.concatenate([qv_full[:model_width], zero_bias, qv_full[model_width:]])
    qkv_b = (qkv_rows + qkv_bias).astype(jnp.bfloat16)
    attended = attention_fwd(qkv_b, segment_ids, valid)
    mid_rows = (
        rows
        + jnp.dot(attended, out_full, preferred_element_type=jnp.float32)
        + outb_full.astype(jnp.float32)
    )
    gain_two = gain_two.astype(jnp.float32)
    shift_two = shift_two.astype(jnp.float32)
    normed_two, recip_two = norm_parts(mid_rows)
    h_two = (normed_two * gain_two + shift_two).astype(jnp.bfloat16)
    upper = jnp.dot(h_two, up_full, preferred_element_type=jnp.float32) + upb_full.astype(
        jnp.float32
    )
    gelu_rows = jax.nn.gelu(upper, approximate=False).astype(jnp.bfloat16)
    out_rows = (
        mid_rows
        + jnp.dot(gelu_rows, down_full, preferred_element_type=jnp.float32)
        + downb_full.astype(jnp.float32)
    )
    block_out = out_rows.astype(jnp.bfloat16)
    dy_rows = cotangent.astype(jnp.float32)
    grad_wdown = jnp.einsum("tf,td->fd", gelu_rows, cotangent, preferred_element_type=jnp.float32)
    grad_bdown = col_sum(cotangent)
    grad_g = jnp.einsum("td,fd->tf", cotangent, down_full, preferred_element_type=jnp.float32)
    cdf_part = 0.5 * (1.0 + jax.scipy.special.erf(upper * 0.7071067811865476))
    pdf_part = jnp.exp(-0.5 * upper * upper) * 0.3989422804014327
    grad_u = (grad_g * (cdf_part + upper * pdf_part)).astype(jnp.bfloat16)
    grad_bup = col_sum(grad_u)
    grad_wup = jnp.einsum("td,tf->df", h_two, grad_u, preferred_element_type=jnp.float32)
    grad_h2 = jnp.einsum("tf,df->td", grad_u, up_full, preferred_element_type=jnp.float32)
    grad_g2 = jnp.sum(grad_h2 * normed_two, axis=0)
    grad_c2 = jnp.sum(grad_h2, axis=0)
    grad_mid = dy_rows + norm_back(grad_h2, gain_two, normed_two, recip_two)
    grad_a = grad_mid.astype(jnp.bfloat16)
    grad_wout = jnp.einsum("tc,td->cd", attended, grad_a, preferred_element_type=jnp.float32)
    grad_bout = col_sum(grad_a)
    grad_o = jnp.einsum("td,cd->tc", grad_a, out_full, preferred_element_type=jnp.float32).astype(
        jnp.bfloat16
    )
    grad_qkv = attention_bwd(qkv_b, grad_o, segment_ids, valid)
    grad_cols = col_sum(grad_qkv)
    grad_bqv = jnp.concatenate([grad_cols[:model_width], grad_cols[2 * model_width :]])
    grad_wqkv = jnp.einsum("td,te->de", h_one, grad_qkv, preferred_element_type=jnp.float32)
    grad_h1 = jnp.einsum("te,de->td", grad_qkv, qkv_full, preferred_element_type=jnp.float32)
    grad_g1 = jnp.sum(grad_h1 * normed_one, axis=0)
    grad_c1 = jnp.sum(grad_h1, axis=0)
    grad_inputs = grad_mid + norm_back(grad_h1, gain_one, normed_one, recip_one)

    small_grads = (grad_bqv, grad_bout, grad_g1, grad_c1, grad_g2, grad_c2, grad_bup, grad_bdown)
    owned = jnp.concatenate([g.reshape(n_dev, -1) for g in small_grads], axis=1)
    lanes = 128
    small_rows = 8 * pl.cdiv(pl.cdiv(n_small, lanes), 8)
    owned = jnp.pad(owned, ((0, 0), (0, small_rows * lanes - n_small))).reshape(-1, lanes)
    parts = [
        (grad_wqkv, w_qkv.shape[0], True),
        (grad_wout, w_out.shape[0], True),
        (grad_wup, w_up.shape[0], True),
        (grad_wdown, w_down.shape[0], True),
        (owned, small_rows, False),
    ]
    if all(rb % 8 == 0 and a.shape[1] % 256 == 0 for (a, rb, _) in parts[:4]):
        sums = ring_reduce_scatter(parts, mesh_shape, after=(grad_inputs,))
    else:
        sums = [lax.psum_scatter(a, ALL, scatter_dimension=0, tiled=True) for (a, _, _) in parts]
    small_sums = split_owned(sums[4].reshape(1, -1), [s for s in small_sizes])
    bqv, bout, g1, c1, g2, c2, bup, bdown = small_sums
    return (
        block_out,
        grad_inputs,
        sums[0],
        bqv,
        sums[1],
        bout,
        g1,
        c1,
        g2,
        c2,
        sums[2],
        bup,
        sums[3],
        bdown,
    )


def solution(mesh):
    in_specs = (
        P(("wide", "narrow"), None),
        P(("wide", "narrow"), None),
        P(("wide", "narrow")),
        P(("wide", "narrow"), None),
        P(("wide", "narrow")),
        P(("wide", "narrow")),
        P(("wide", "narrow")),
        P(("wide", "narrow")),
        P(("wide", "narrow")),
        P(("wide", "narrow"), None),
        P(("wide", "narrow")),
        P(("wide", "narrow"), None),
        P(("wide", "narrow")),
        P(("wide", "narrow"), None),
        P(("wide", "narrow"), None),
        P(("wide", "narrow"), None),
    )
    out_specs = (
        P(("wide", "narrow"), None),
        P(("wide", "narrow"), None),
        P(("wide", "narrow"), None),
        P(("wide", "narrow")),
        P(("wide", "narrow"), None),
        P(("wide", "narrow")),
        P(("wide", "narrow")),
        P(("wide", "narrow")),
        P(("wide", "narrow")),
        P(("wide", "narrow")),
        P(("wide", "narrow"), None),
        P(("wide", "narrow")),
        P(("wide", "narrow"), None),
        P(("wide", "narrow")),
    )
    body = functools.partial(on_device, mesh_shape=(mesh.shape["wide"], mesh.shape["narrow"]))
    return jax.shard_map(
        body, mesh=mesh, in_specs=in_specs, out_specs=out_specs, check_vma=False
    )
```

```python
import functools
import jax
import jax.numpy as jnp
from jax import lax
from jax.experimental import pallas as pl
from jax.experimental.pallas import tpu as pltpu
from jax.sharding import PartitionSpec as P

HD = 64
ALL = ("wide", "narrow")

EPSILON = 1e-06


def norm_parts(rows):
    center = rows - jnp.mean(rows, axis=-1, keepdims=True)
    recip = lax.rsqrt(jnp.mean(center * center, axis=-1, keepdims=True) + EPSILON)
    return (center * recip, recip)


def norm_back(grad_h, gain, normed, recip):
    scaled = grad_h * gain
    return recip * (
        scaled
        - jnp.mean(scaled, axis=-1, keepdims=True)
        - normed * jnp.mean(scaled * normed, axis=-1, keepdims=True)
    )


def col_sum(rows):
    return jnp.sum(rows.astype(jnp.float32), axis=0)


def seg_mask(seg_col, seg_row, val_row, n):
    rows = lax.broadcasted_iota(jnp.int32, (n, n), 0)
    cols = lax.broadcasted_iota(jnp.int32, (n, n), 1)
    return (seg_col == seg_row) & ((val_row == 1) | (rows == cols))


def soft_rows(qh, kh, allowed):
    scores = lax.dot_general(qh, kh, (((1,), (1,)), ((), ())), preferred_element_type=jnp.float32)
    scores = jnp.where(allowed, scores * (1.0 / HD**0.5), -1e30)
    top = jnp.max(scores, axis=-1, keepdims=True)
    expo = jnp.exp(scores - top)
    return expo * (1.0 / jnp.sum(expo, axis=-1, keepdims=True))


def attn_fwd_kernel(q_ref, k_ref, v_ref, sc_ref, sr_ref, vr_ref, o_ref):
    n = q_ref.shape[0]
    allowed = seg_mask(sc_ref[...], sr_ref[...], vr_ref[...], n)
    outs = []
    for j in range(q_ref.shape[1] // HD):
        cols = slice(j * HD, (j + 1) * HD)
        probs = soft_rows(q_ref[:, cols], k_ref[:, cols], allowed).astype(jnp.bfloat16)
        outs.append(jnp.dot(probs, v_ref[:, cols], preferred_element_type=jnp.float32))
    o_ref[...] = jnp.concatenate(outs, axis=1).astype(o_ref.dtype)


def attn_bwd_kernel(q_ref, k_ref, v_ref, do_ref, sc_ref, sr_ref, vr_ref, dqkv_ref):
    n = q_ref.shape[0]
    width = q_ref.shape[1]
    hp = pl.program_id(1)
    model_width = dqkv_ref.shape[1] // 3
    allowed = seg_mask(sc_ref[...], sr_ref[...], vr_ref[...], n)
    dqs, dks, dvs = [], [], []
    for j in range(width // HD):
        cols = slice(j * HD, (j + 1) * HD)
        qh, kh, vh, doh = q_ref[:, cols], k_ref[:, cols], v_ref[:, cols], do_ref[:, cols]
        probs = soft_rows(qh, kh, allowed)
        dvs.append(
            lax.dot_general(probs.astype(jnp.bfloat16), doh, (((0,), (0,)), ((), ())),
                            preferred_element_type=jnp.float32)
        )
        dprobs = lax.dot_general(doh, vh, (((1,), (1,)), ((), ())), preferred_element_type=jnp.float32)
        row_term = jnp.sum(probs * dprobs, axis=-1, keepdims=True)
        dscore = jnp.where(allowed, probs * (dprobs - row_term), 0.0).astype(jnp.bfloat16)
        dqs.append(jnp.dot(dscore, kh, preferred_element_type=jnp.float32) * (1.0 / HD**0.5))
        dks.append(
            lax.dot_general(dscore, qh, (((0,), (0,)), ((), ())), preferred_element_type=jnp.float32)
            * (1.0 / HD**0.5)
        )
    at = pl.multiple_of(hp * width, width)
    dqkv_ref[:, pl.ds(at, width)] = jnp.concatenate(dqs, axis=1).astype(dqkv_ref.dtype)
    dqkv_ref[:, pl.ds(at + model_width, width)] = jnp.concatenate(dks, axis=1).astype(dqkv_ref.dtype)
    dqkv_ref[:, pl.ds(at + 2 * model_width, width)] = jnp.concatenate(dvs, axis=1).astype(dqkv_ref.dtype)


def mask_operands(segment_ids, valid):
    return (segment_ids[:, :, None], segment_ids[:, None, :], valid[:, None, :])


def attention_fwd(qkv, segment_ids, valid):
    rows, width3 = qkv.shape
    model_width = width3 // 3
    n_seq, seq_len = segment_ids.shape
    blk = 2 * HD
    n_hp = model_width // blk
    off = model_width // blk
    seg_spec = [
        pl.BlockSpec((None, seq_len, 1), lambda s, h: (s, 0, 0)),
        pl.BlockSpec((None, 1, seq_len), lambda s, h: (s, 0, 0)),
        pl.BlockSpec((None, 1, seq_len), lambda s, h: (s, 0, 0)),
    ]
    flops = 4 * n_seq * seq_len * seq_len * model_width
    return pl.pallas_call(
        attn_fwd_kernel,
        out_shape=jax.ShapeDtypeStruct((rows, model_width), jnp.bfloat16),
        grid=(n_seq, n_hp),
        in_specs=[
            pl.BlockSpec((seq_len, blk), lambda s, h: (s, h)),
            pl.BlockSpec((seq_len, blk), lambda s, h: (s, off + h)),
            pl.BlockSpec((seq_len, blk), lambda s, h: (s, 2 * off + h)),
        ]
        + seg_spec,
        out_specs=pl.BlockSpec((seq_len, blk), lambda s, h: (s, h)),
        cost_estimate=pl.CostEstimate(
            flops=flops,
            transcendentals=n_seq * seq_len * seq_len * (model_width // HD),
            bytes_accessed=qkv.size * 2 + rows * model_width * 2,
        ),
    )(qkv, qkv, qkv, *mask_operands(segment_ids, valid))


def attention_bwd(qkv, grad_o, segment_ids, valid):
    rows, width3 = qkv.shape
    model_width = width3 // 3
    n_seq, seq_len = segment_ids.shape
    blk = 2 * HD
    n_hp = model_width // blk
    off = model_width // blk
    seg_spec = [
        pl.BlockSpec((None, seq_len, 1), lambda s, h: (s, 0, 0)),
        pl.BlockSpec((None, 1, seq_len), lambda s, h: (s, 0, 0)),
        pl.BlockSpec((None, 1, seq_len), lambda s, h: (s, 0, 0)),
    ]
    flops = 10 * n_seq * seq_len * seq_len * model_width
    return pl.pallas_call(
        attn_bwd_kernel,
        out_shape=jax.ShapeDtypeStruct((rows, width3), jnp.bfloat16),
        grid=(n_seq, n_hp),
        in_specs=[
            pl.BlockSpec((seq_len, blk), lambda s, h: (s, h)),
            pl.BlockSpec((seq_len, blk), lambda s, h: (s, off + h)),
            pl.BlockSpec((seq_len, blk), lambda s, h: (s, 2 * off + h)),
            pl.BlockSpec((seq_len, blk), lambda s, h: (s, h)),
        ]
        + seg_spec,
        out_specs=pl.BlockSpec((seq_len, width3), lambda s, h: (s, 0)),
        cost_estimate=pl.CostEstimate(
            flops=flops,
            transcendentals=n_seq * seq_len * seq_len * (model_width // HD),
            bytes_accessed=qkv.size * 4 + rows * model_width * 2,
        ),
    )(qkv, qkv, qkv, grad_o, *mask_operands(segment_ids, valid))


MESH_ID = pl.DeviceIdType.MESH


def ring_maps(n_wide, n_narrow):
    n_dev = n_wide * n_narrow
    if (n_wide, n_narrow) == (8, 4):
        def pos_of(w, n):
            z, y, x, c = w // 2, w % 2, n // 2, n % 2
            q = 2 * x + (x + y) % 2
            k = 4 * q + z + (q % 2) * (3 - 2 * z)
            return 2 * k + c

        def coords_of(p):
            k, c = p // 2, p % 2
            q, r = k // 4, k % 4
            z = r + (q % 2) * (3 - 2 * r)
            x = q // 2
            y = (q % 2 + x) % 2
            return z * 2 + y, x * 2 + c

    else:
        def pos_of(w, n):
            return w * n_narrow + n

        def coords_of(p):
            return p // n_narrow, p % n_narrow

    return n_dev, pos_of, coords_of


def ring_reduce_scatter(parts, mesh_shape, after=(), collective_id=0):
    n_wide, n_narrow = mesh_shape
    n_dev, pos_of, coords_of = ring_maps(n_wide, n_narrow)
    specs = []
    for i, (a, rb, split) in enumerate(parts):
        cols = a.shape[1]
        if split:
            specs.append((i, 0, 0, cols // 2))
        else:
            specs.append((i, 0, 0, cols))
    for i, (a, rb, split) in enumerate(parts):
        if split:
            specs.append((i, 1, a.shape[1] // 2, a.shape[1] // 2))
    n_in = len(parts)
    n_after = len(after)
    n_sp = len(specs)
    last_step = n_dev - 2

    def kernel(*refs):
        ins = refs[:n_in]
        outs = refs[n_in + n_after : 2 * n_in + n_after]
        at = 2 * n_in + n_after
        bufs = refs[at : at + n_sp]
        locs = refs[at + n_sp : at + 2 * n_sp]
        send_sem, recv_sem, loc_sem, credit = refs[at + 2 * n_sp :]
        p = pos_of(lax.axis_index("wide"), lax.axis_index("narrow"))
        right = coords_of((p + 1) % n_dev)
        left = coords_of((p + n_dev - 1) % n_dev)
        nbr_send = (right, left)
        nbr_recv = (left, right)

        def rows_of(q, rb):
            cw, cn = coords_of(q % n_dev)
            start = (cw * n_narrow + cn) * rb
            if rb % 8 == 0:
                start = pl.multiple_of(start, 8)
            return pl.ds(start, rb)

        def remote(j, s):
            return pltpu.make_async_remote_copy(
                src_ref=bufs[j].at[s % 3],
                dst_ref=bufs[j].at[(s + 1) % 3],
                send_sem=send_sem.at[j, s % 3],
                recv_sem=recv_sem.at[j, (s + 1) % 3],
                device_id=nbr_send[specs[j][1]],
                device_id_type=MESH_ID,
            )

        def local(j, s):
            i, dirn, c0, cw = specs[j]
            q = (p + 2 * n_dev - s - 2) if dirn == 0 else (p + s + 2)
            return pltpu.make_async_copy(
                ins[i].at[rows_of(q, parts[i][1]), pl.ds(c0, cw)], locs[j].at[s % 2], loc_sem.at[j, s % 2]
            )

        barrier = pltpu.get_barrier_semaphore()
        for nb in (left, right):
            pl.semaphore_signal(barrier, 1, device_id=nb, device_id_type=MESH_ID)
        pl.semaphore_wait(barrier, 2)

        for j, (i, dirn, c0, cw) in enumerate(specs):
            q = p + n_dev - 1 if dirn == 0 else p + 1
            cp = pltpu.make_async_copy(
                ins[i].at[rows_of(q, parts[i][1]), pl.ds(c0, cw)], bufs[j].at[0], loc_sem.at[j, 1]
            )
            cp.start()
            cp.wait()
        for j in range(n_sp):
            remote(j, 0).start()
            local(j, 0).start()

        def step(s, carry):
            for j in range(n_sp):
                dirn = specs[j][1]
                local(j, s).wait()
                remote(j, s).wait_recv()
                nxt = (s + 1) % 3
                bufs[j][nxt] = bufs[j][nxt] + locs[j][s % 2]
                if j == 0 or specs[j - 1][1] != dirn:

                    @pl.when((s >= 1) & (s + 1 <= last_step))
                    def _():
                        pl.semaphore_wait(credit.at[dirn], 1)

                @pl.when(s + 1 <= last_step)
                def _():
                    remote(j, s + 1).start()
                    local(j, s + 1).start()

            for j in range(n_sp):
                remote(j, s).wait_send()
            for dirn in (0, 1):

                @pl.when(s <= last_step - 2)
                def _():
                    pl.semaphore_signal(
                        credit.at[dirn], 1, device_id=nbr_recv[dirn], device_id_type=MESH_ID
                    )

            return carry

        lax.fori_loop(0, last_step + 1, step, 0)
        fin = (last_step + 1) % 3
        for j, (i, dirn, c0, cw) in enumerate(specs):
            outs[i][:, pl.ds(c0, cw)] = bufs[j][fin]

    out_shape = [jax.ShapeDtypeStruct((rb, a.shape[1]), a.dtype) for (a, rb, _) in parts]
    scratch = [pltpu.VMEM((3, parts[i][1], cw), jnp.float32) for (i, _, _, cw) in specs]
    scratch += [pltpu.VMEM((2, parts[i][1], cw), jnp.float32) for (i, _, _, cw) in specs]
    scratch += [
        pltpu.SemaphoreType.DMA((n_sp, 3)),
        pltpu.SemaphoreType.DMA((n_sp, 3)),
        pltpu.SemaphoreType.DMA((n_sp, 2)),
        pltpu.SemaphoreType.REGULAR((2,)),
    ]
    total = sum(a.size * 4 for (a, _, _) in parts)
    return pl.pallas_call(
        kernel,
        out_shape=out_shape,
        in_specs=[pl.BlockSpec(memory_space=pl.ANY)] * (n_in + n_after),
        out_specs=[pl.BlockSpec(memory_space=pltpu.VMEM)] * n_in,
        scratch_shapes=scratch,
        compiler_params=pltpu.CompilerParams(
            collective_id=collective_id, has_side_effects=True, vmem_limit_bytes=48 * 1024 * 1024
        ),
        cost_estimate=pl.CostEstimate(flops=total // 4, transcendentals=0, bytes_accessed=2 * total),
    )(*[a for (a, _, _) in parts], *after)


def pack_rows(pieces, width):
    flat = jnp.concatenate(pieces)
    return jnp.pad(flat, (0, width - flat.shape[0]))[None, :]


def split_owned(packed, sizes):
    out = []
    at = 0
    for size in sizes:
        out.append(packed[:, at : at + size].reshape(-1))
        at += size
    return out


def on_device(
    inputs,
    w_qkv,
    qv_bias,
    w_out,
    out_bias,
    ln1_gain,
    ln1_shift,
    ln2_gain,
    ln2_shift,
    w_up,
    up_bias,
    w_down,
    down_bias,
    segment_ids,
    valid,
    cotangent,
    mesh_shape=None,
):
    row_count = inputs.shape[0]
    model_width = inputs.shape[1]
    seq_count = segment_ids.shape[0]
    seq_len = segment_ids.shape[1]
    head_count = model_width // HD
    n_dev = mesh_shape[0] * mesh_shape[1]
    small = (qv_bias, out_bias, ln1_gain, ln1_shift, ln2_gain, ln2_shift, up_bias, down_bias)
    small_sizes = [a.shape[0] for a in small]
    n_small = sum(small_sizes)
    rows_q = w_qkv.size // model_width
    rows_o = w_out.shape[0]
    attn_buf = jnp.concatenate(
        [w_qkv.reshape(rows_q, model_width), w_out, pack_rows(small, model_width)], axis=0
    )
    attn_all = lax.all_gather(attn_buf, ALL, axis=0, tiled=False)
    qkv_full = attn_all[:, :rows_q].reshape(-1, w_qkv.shape[1])
    out_full = attn_all[:, rows_q : rows_q + rows_o].reshape(-1, model_width)
    small_full = split_owned(attn_all[:, rows_q + rows_o, :n_small], small_sizes)
    qv_full, outb_full, gain_one, shift_one, gain_two, shift_two, upb_full, downb_full = small_full
    rows_u = w_up.size // model_width
    mlp_buf = jnp.concatenate([w_up.reshape(rows_u, model_width), w_down], axis=0)
    mlp_all = lax.all_gather(mlp_buf, ALL, axis=0, tiled=False)
    up_full = mlp_all[:, :rows_u].reshape(-1, w_up.shape[1])
    down_full = mlp_all[:, rows_u:].reshape(-1, model_width)

    gain_one = gain_one.astype(jnp.float32)
    shift_one = shift_one.astype(jnp.float32)
    qv_full = qv_full.astype(jnp.float32)
    rows = inputs.astype(jnp.float32)
    normed_one, recip_one = norm_parts(rows)
    h_one = (normed_one * gain_one + shift_one).astype(jnp.bfloat16)
    qkv_rows = jnp.dot(h_one, qkv_full, preferred_element_type=jnp.float32)
    zero_bias = jnp.zeros((model_width,), jnp.float32)
    qkv_bias = jnp.concatenate([qv_full[:model_width], zero_bias, qv_full[model_width:]])
    qkv_b = (qkv_rows + qkv_bias).astype(jnp.bfloat16)
    attended = attention_fwd(qkv_b, segment_ids, valid)
    mid_rows = (
        rows
        + jnp.dot(attended, out_full, preferred_element_type=jnp.float32)
        + outb_full.astype(jnp.float32)
    )
    gain_two = gain_two.astype(jnp.float32)
    shift_two = shift_two.astype(jnp.float32)
    normed_two, recip_two = norm_parts(mid_rows)
    h_two = (normed_two * gain_two + shift_two).astype(jnp.bfloat16)
    upper = jnp.dot(h_two, up_full, preferred_element_type=jnp.float32) + upb_full.astype(
        jnp.float32
    )
    gelu_rows = jax.nn.gelu(upper, approximate=False).astype(jnp.bfloat16)
    out_rows = (
        mid_rows
        + jnp.dot(gelu_rows, down_full, preferred_element_type=jnp.float32)
        + downb_full.astype(jnp.float32)
    )
    block_out = out_rows.astype(jnp.bfloat16)
    dy_rows = cotangent.astype(jnp.float32)
    grad_wdown = jnp.einsum("tf,td->fd", gelu_rows, cotangent, preferred_element_type=jnp.float32)
    grad_bdown = col_sum(cotangent)
    grad_g = jnp.einsum("td,fd->tf", cotangent, down_full, preferred_element_type=jnp.float32)
    cdf_part = 0.5 * (1.0 + jax.scipy.special.erf(upper * 0.7071067811865476))
    pdf_part = jnp.exp(-0.5 * upper * upper) * 0.3989422804014327
    grad_u = (grad_g * (cdf_part + upper * pdf_part)).astype(jnp.bfloat16)
    grad_bup = col_sum(grad_u)
    grad_wup = jnp.einsum("td,tf->df", h_two, grad_u, preferred_element_type=jnp.float32)
    grad_h2 = jnp.einsum("tf,df->td", grad_u, up_full, preferred_element_type=jnp.float32)
    grad_g2 = jnp.sum(grad_h2 * normed_two, axis=0)
    grad_c2 = jnp.sum(grad_h2, axis=0)
    grad_mid = dy_rows + norm_back(grad_h2, gain_two, normed_two, recip_two)
    grad_a = grad_mid.astype(jnp.bfloat16)
    grad_wout = jnp.einsum("tc,td->cd", attended, grad_a, preferred_element_type=jnp.float32)
    grad_bout = col_sum(grad_a)
    grad_o = jnp.einsum("td,cd->tc", grad_a, out_full, preferred_element_type=jnp.float32).astype(
        jnp.bfloat16
    )
    grad_qkv = attention_bwd(qkv_b, grad_o, segment_ids, valid)
    grad_cols = col_sum(grad_qkv)
    grad_bqv = jnp.concatenate([grad_cols[:model_width], grad_cols[2 * model_width :]])
    grad_wqkv = jnp.einsum("td,te->de", h_one, grad_qkv, preferred_element_type=jnp.float32)
    grad_h1 = jnp.einsum("te,de->td", grad_qkv, qkv_full, preferred_element_type=jnp.float32)
    grad_g1 = jnp.sum(grad_h1 * normed_one, axis=0)
    grad_c1 = jnp.sum(grad_h1, axis=0)
    grad_inputs = grad_mid + norm_back(grad_h1, gain_one, normed_one, recip_one)

    small_grads = (grad_bqv, grad_bout, grad_g1, grad_c1, grad_g2, grad_c2, grad_bup, grad_bdown)
    owned = jnp.concatenate([g.reshape(n_dev, -1) for g in small_grads], axis=1)
    lanes = 128
    small_rows = 8 * pl.cdiv(pl.cdiv(n_small, lanes), 8)
    owned = jnp.pad(owned, ((0, 0), (0, small_rows * lanes - n_small))).reshape(-1, lanes)
    parts = [
        (grad_wqkv, w_qkv.shape[0], True),
        (grad_wout, w_out.shape[0], True),
        (grad_wup, w_up.shape[0], True),
        (owned, small_rows, False),
    ]
    down_sum = lax.psum_scatter(grad_wdown, ALL, scatter_dimension=0, tiled=True)
    if all(rb % 8 == 0 and a.shape[1] % 256 == 0 for (a, rb, _) in parts[:3]):
        sums = ring_reduce_scatter(parts, mesh_shape, after=(grad_inputs,))
    else:
        sums = [lax.psum_scatter(a, ALL, scatter_dimension=0, tiled=True) for (a, _, _) in parts]
    sums = list(sums[:3]) + [down_sum] + list(sums[3:])
    small_sums = split_owned(sums[4].reshape(1, -1), small_sizes)
    bqv, bout, g1, c1, g2, c2, bup, bdown = small_sums
    return (
        block_out,
        grad_inputs,
        sums[0],
        bqv,
        sums[1],
        bout,
        g1,
        c1,
        g2,
        c2,
        sums[2],
        bup,
        sums[3],
        bdown,
    )


def solution(mesh):
    in_specs = (
        P(("wide", "narrow"), None),
        P(("wide", "narrow"), None),
        P(("wide", "narrow")),
        P(("wide", "narrow"), None),
        P(("wide", "narrow")),
        P(("wide", "narrow")),
        P(("wide", "narrow")),
        P(("wide", "narrow")),
        P(("wide", "narrow")),
        P(("wide", "narrow"), None),
        P(("wide", "narrow")),
        P(("wide", "narrow"), None),
        P(("wide", "narrow")),
        P(("wide", "narrow"), None),
        P(("wide", "narrow"), None),
        P(("wide", "narrow"), None),
    )
    out_specs = (
        P(("wide", "narrow"), None),
        P(("wide", "narrow"), None),
        P(("wide", "narrow"), None),
        P(("wide", "narrow")),
        P(("wide", "narrow"), None),
        P(("wide", "narrow")),
        P(("wide", "narrow")),
        P(("wide", "narrow")),
        P(("wide", "narrow")),
        P(("wide", "narrow")),
        P(("wide", "narrow"), None),
        P(("wide", "narrow")),
        P(("wide", "narrow"), None),
        P(("wide", "narrow")),
    )
    body = functools.partial(on_device, mesh_shape=(mesh.shape["wide"], mesh.shape["narrow"]))
    return jax.shard_map(
        body, mesh=mesh, in_specs=in_specs, out_specs=out_specs, check_vma=False
    )
```

```python
import functools
import jax
import jax.numpy as jnp
from jax import lax
from jax.experimental import pallas as pl
from jax.experimental.pallas import tpu as pltpu
from jax.sharding import PartitionSpec as P

HD = 64
ALL = ("wide", "narrow")

EPSILON = 1e-06


def norm_parts(rows):
    center = rows - jnp.mean(rows, axis=-1, keepdims=True)
    recip = lax.rsqrt(jnp.mean(center * center, axis=-1, keepdims=True) + EPSILON)
    return (center * recip, recip)


def norm_back(grad_h, gain, normed, recip):
    scaled = grad_h * gain
    return recip * (
        scaled
        - jnp.mean(scaled, axis=-1, keepdims=True)
        - normed * jnp.mean(scaled * normed, axis=-1, keepdims=True)
    )


def col_sum(rows):
    return jnp.sum(rows.astype(jnp.float32), axis=0)


def seg_mask(seg_col, seg_row, val_row, n):
    rows = lax.broadcasted_iota(jnp.int32, (n, n), 0)
    cols = lax.broadcasted_iota(jnp.int32, (n, n), 1)
    return (seg_col == seg_row) & ((val_row == 1) | (rows == cols))


def soft_rows(qh, kh, allowed):
    scores = lax.dot_general(qh, kh, (((1,), (1,)), ((), ())), preferred_element_type=jnp.float32)
    scores = jnp.where(allowed, scores * (1.0 / HD**0.5), -1e30)
    top = jnp.max(scores, axis=-1, keepdims=True)
    expo = jnp.exp(scores - top)
    return expo * (1.0 / jnp.sum(expo, axis=-1, keepdims=True))


def attn_fwd_kernel(q_ref, k_ref, v_ref, sc_ref, sr_ref, vr_ref, o_ref):
    n = q_ref.shape[0]
    allowed = seg_mask(sc_ref[...], sr_ref[...], vr_ref[...], n)
    outs = []
    for j in range(q_ref.shape[1] // HD):
        cols = slice(j * HD, (j + 1) * HD)
        probs = soft_rows(q_ref[:, cols], k_ref[:, cols], allowed).astype(jnp.bfloat16)
        outs.append(jnp.dot(probs, v_ref[:, cols], preferred_element_type=jnp.float32))
    o_ref[...] = jnp.concatenate(outs, axis=1).astype(o_ref.dtype)


def attn_bwd_kernel(q_ref, k_ref, v_ref, do_ref, sc_ref, sr_ref, vr_ref, dqkv_ref):
    n = q_ref.shape[0]
    width = q_ref.shape[1]
    hp = pl.program_id(1)
    model_width = dqkv_ref.shape[1] // 3
    allowed = seg_mask(sc_ref[...], sr_ref[...], vr_ref[...], n)
    dqs, dks, dvs = [], [], []
    for j in range(width // HD):
        cols = slice(j * HD, (j + 1) * HD)
        qh, kh, vh, doh = q_ref[:, cols], k_ref[:, cols], v_ref[:, cols], do_ref[:, cols]
        probs = soft_rows(qh, kh, allowed)
        dvs.append(
            lax.dot_general(probs.astype(jnp.bfloat16), doh, (((0,), (0,)), ((), ())),
                            preferred_element_type=jnp.float32)
        )
        dprobs = lax.dot_general(doh, vh, (((1,), (1,)), ((), ())), preferred_element_type=jnp.float32)
        row_term = jnp.sum(probs * dprobs, axis=-1, keepdims=True)
        dscore = jnp.where(allowed, probs * (dprobs - row_term), 0.0).astype(jnp.bfloat16)
        dqs.append(jnp.dot(dscore, kh, preferred_element_type=jnp.float32) * (1.0 / HD**0.5))
        dks.append(
            lax.dot_general(dscore, qh, (((0,), (0,)), ((), ())), preferred_element_type=jnp.float32)
            * (1.0 / HD**0.5)
        )
    at = pl.multiple_of(hp * width, width)
    dqkv_ref[:, pl.ds(at, width)] = jnp.concatenate(dqs, axis=1).astype(dqkv_ref.dtype)
    dqkv_ref[:, pl.ds(at + model_width, width)] = jnp.concatenate(dks, axis=1).astype(dqkv_ref.dtype)
    dqkv_ref[:, pl.ds(at + 2 * model_width, width)] = jnp.concatenate(dvs, axis=1).astype(dqkv_ref.dtype)


def mask_operands(segment_ids, valid):
    return (segment_ids[:, :, None], segment_ids[:, None, :], valid[:, None, :])


def attention_fwd(qkv, segment_ids, valid):
    rows, width3 = qkv.shape
    model_width = width3 // 3
    n_seq, seq_len = segment_ids.shape
    blk = 2 * HD
    n_hp = model_width // blk
    off = model_width // blk
    seg_spec = [
        pl.BlockSpec((None, seq_len, 1), lambda s, h: (s, 0, 0)),
        pl.BlockSpec((None, 1, seq_len), lambda s, h: (s, 0, 0)),
        pl.BlockSpec((None, 1, seq_len), lambda s, h: (s, 0, 0)),
    ]
    flops = 4 * n_seq * seq_len * seq_len * model_width
    return pl.pallas_call(
        attn_fwd_kernel,
        out_shape=jax.ShapeDtypeStruct((rows, model_width), jnp.bfloat16),
        grid=(n_seq, n_hp),
        in_specs=[
            pl.BlockSpec((seq_len, blk), lambda s, h: (s, h)),
            pl.BlockSpec((seq_len, blk), lambda s, h: (s, off + h)),
            pl.BlockSpec((seq_len, blk), lambda s, h: (s, 2 * off + h)),
        ]
        + seg_spec,
        out_specs=pl.BlockSpec((seq_len, blk), lambda s, h: (s, h)),
        cost_estimate=pl.CostEstimate(
            flops=flops,
            transcendentals=n_seq * seq_len * seq_len * (model_width // HD),
            bytes_accessed=qkv.size * 2 + rows * model_width * 2,
        ),
    )(qkv, qkv, qkv, *mask_operands(segment_ids, valid))


def attention_bwd(qkv, grad_o, segment_ids, valid):
    rows, width3 = qkv.shape
    model_width = width3 // 3
    n_seq, seq_len = segment_ids.shape
    blk = 2 * HD
    n_hp = model_width // blk
    off = model_width // blk
    seg_spec = [
        pl.BlockSpec((None, seq_len, 1), lambda s, h: (s, 0, 0)),
        pl.BlockSpec((None, 1, seq_len), lambda s, h: (s, 0, 0)),
        pl.BlockSpec((None, 1, seq_len), lambda s, h: (s, 0, 0)),
    ]
    flops = 10 * n_seq * seq_len * seq_len * model_width
    return pl.pallas_call(
        attn_bwd_kernel,
        out_shape=jax.ShapeDtypeStruct((rows, width3), jnp.bfloat16),
        grid=(n_seq, n_hp),
        in_specs=[
            pl.BlockSpec((seq_len, blk), lambda s, h: (s, h)),
            pl.BlockSpec((seq_len, blk), lambda s, h: (s, off + h)),
            pl.BlockSpec((seq_len, blk), lambda s, h: (s, 2 * off + h)),
            pl.BlockSpec((seq_len, blk), lambda s, h: (s, h)),
        ]
        + seg_spec,
        out_specs=pl.BlockSpec((seq_len, width3), lambda s, h: (s, 0)),
        cost_estimate=pl.CostEstimate(
            flops=flops,
            transcendentals=n_seq * seq_len * seq_len * (model_width // HD),
            bytes_accessed=qkv.size * 4 + rows * model_width * 2,
        ),
    )(qkv, qkv, qkv, grad_o, *mask_operands(segment_ids, valid))


MESH_ID = pl.DeviceIdType.MESH


def ring_maps(n_wide, n_narrow):
    n_dev = n_wide * n_narrow
    if (n_wide, n_narrow) == (8, 4):
        def pos_of(w, n):
            z, y, x, c = w // 2, w % 2, n // 2, n % 2
            q = 2 * x + (x + y) % 2
            k = 4 * q + z + (q % 2) * (3 - 2 * z)
            return 2 * k + c

        def coords_of(p):
            k, c = p // 2, p % 2
            q, r = k // 4, k % 4
            z = r + (q % 2) * (3 - 2 * r)
            x = q // 2
            y = (q % 2 + x) % 2
            return z * 2 + y, x * 2 + c

    else:
        def pos_of(w, n):
            return w * n_narrow + n

        def coords_of(p):
            return p // n_narrow, p % n_narrow

    return n_dev, pos_of, coords_of


def ring_reduce_scatter(parts, mesh_shape, after=(), collective_id=0):
    n_wide, n_narrow = mesh_shape
    n_dev, pos_of, coords_of = ring_maps(n_wide, n_narrow)
    specs = []
    for i, (a, rb, split) in enumerate(parts):
        cols = a.shape[1]
        if split:
            specs.append((i, 0, 0, cols // 2))
        else:
            specs.append((i, 0, 0, cols))
    for i, (a, rb, split) in enumerate(parts):
        if split:
            specs.append((i, 1, a.shape[1] // 2, a.shape[1] // 2))
    n_in = len(parts)
    n_after = len(after)
    n_sp = len(specs)
    last_step = n_dev - 2

    def kernel(*refs):
        ins = refs[:n_in]
        outs = refs[n_in + n_after : 2 * n_in + n_after]
        at = 2 * n_in + n_after
        bufs = refs[at : at + n_sp]
        locs = refs[at + n_sp : at + 2 * n_sp]
        send_sem, recv_sem, loc_sem, credit = refs[at + 2 * n_sp :]
        p = pos_of(lax.axis_index("wide"), lax.axis_index("narrow"))
        right = coords_of((p + 1) % n_dev)
        left = coords_of((p + n_dev - 1) % n_dev)
        nbr_send = (right, left)
        nbr_recv = (left, right)

        def rows_of(q, rb):
            cw, cn = coords_of(q % n_dev)
            start = (cw * n_narrow + cn) * rb
            if rb % 8 == 0:
                start = pl.multiple_of(start, 8)
            return pl.ds(start, rb)

        def remote(j, s):
            return pltpu.make_async_remote_copy(
                src_ref=bufs[j].at[s % 3],
                dst_ref=bufs[j].at[(s + 1) % 3],
                send_sem=send_sem.at[j, s % 3],
                recv_sem=recv_sem.at[j, (s + 1) % 3],
                device_id=nbr_send[specs[j][1]],
                device_id_type=MESH_ID,
            )

        def local(j, s):
            i, dirn, c0, cw = specs[j]
            q = (p + 2 * n_dev - s - 2) if dirn == 0 else (p + s + 2)
            return pltpu.make_async_copy(
                ins[i].at[rows_of(q, parts[i][1]), pl.ds(c0, cw)], locs[j].at[s % 2], loc_sem.at[j, s % 2]
            )

        barrier = pltpu.get_barrier_semaphore()
        for nb in (left, right):
            pl.semaphore_signal(barrier, 1, device_id=nb, device_id_type=MESH_ID)
        pl.semaphore_wait(barrier, 2)

        for j, (i, dirn, c0, cw) in enumerate(specs):
            q = p + n_dev - 1 if dirn == 0 else p + 1
            cp = pltpu.make_async_copy(
                ins[i].at[rows_of(q, parts[i][1]), pl.ds(c0, cw)], bufs[j].at[0], loc_sem.at[j, 1]
            )
            cp.start()
            cp.wait()
        for j in range(n_sp):
            remote(j, 0).start()
            local(j, 0).start()

        def step(s, carry):
            for j in range(n_sp):
                dirn = specs[j][1]
                local(j, s).wait()
                remote(j, s).wait_recv()
                nxt = (s + 1) % 3
                bufs[j][nxt] = bufs[j][nxt] + locs[j][s % 2]
                if j == 0 or specs[j - 1][1] != dirn:

                    @pl.when((s >= 1) & (s + 1 <= last_step))
                    def _():
                        pl.semaphore_wait(credit.at[dirn], 1)

                @pl.when(s + 1 <= last_step)
                def _():
                    remote(j, s + 1).start()
                    local(j, s + 1).start()

            for j in range(n_sp):
                remote(j, s).wait_send()
            for dirn in (0, 1):

                @pl.when(s <= last_step - 2)
                def _():
                    pl.semaphore_signal(
                        credit.at[dirn], 1, device_id=nbr_recv[dirn], device_id_type=MESH_ID
                    )

            return carry

        lax.fori_loop(0, last_step + 1, step, 0)
        fin = (last_step + 1) % 3
        for j, (i, dirn, c0, cw) in enumerate(specs):
            outs[i][:, pl.ds(c0, cw)] = bufs[j][fin]

    out_shape = [jax.ShapeDtypeStruct((rb, a.shape[1]), a.dtype) for (a, rb, _) in parts]
    scratch = [pltpu.VMEM((3, parts[i][1], cw), jnp.float32) for (i, _, _, cw) in specs]
    scratch += [pltpu.VMEM((2, parts[i][1], cw), jnp.float32) for (i, _, _, cw) in specs]
    scratch += [
        pltpu.SemaphoreType.DMA((n_sp, 3)),
        pltpu.SemaphoreType.DMA((n_sp, 3)),
        pltpu.SemaphoreType.DMA((n_sp, 2)),
        pltpu.SemaphoreType.REGULAR((2,)),
    ]
    total = sum(a.size * 4 for (a, _, _) in parts)
    return pl.pallas_call(
        kernel,
        out_shape=out_shape,
        in_specs=[pl.BlockSpec(memory_space=pl.ANY)] * (n_in + n_after),
        out_specs=[pl.BlockSpec(memory_space=pltpu.VMEM)] * n_in,
        scratch_shapes=scratch,
        compiler_params=pltpu.CompilerParams(
            collective_id=collective_id, has_side_effects=True, vmem_limit_bytes=48 * 1024 * 1024
        ),
        cost_estimate=pl.CostEstimate(flops=total // 4, transcendentals=0, bytes_accessed=2 * total),
    )(*[a for (a, _, _) in parts], *after)


def pack_rows(pieces, width):
    flat = jnp.concatenate(pieces)
    return jnp.pad(flat, (0, width - flat.shape[0]))[None, :]


def split_owned(packed, sizes):
    out = []
    at = 0
    for size in sizes:
        out.append(packed[:, at : at + size].reshape(-1))
        at += size
    return out


def on_device(
    inputs,
    w_qkv,
    qv_bias,
    w_out,
    out_bias,
    ln1_gain,
    ln1_shift,
    ln2_gain,
    ln2_shift,
    w_up,
    up_bias,
    w_down,
    down_bias,
    segment_ids,
    valid,
    cotangent,
    mesh_shape=None,
):
    row_count = inputs.shape[0]
    model_width = inputs.shape[1]
    seq_count = segment_ids.shape[0]
    seq_len = segment_ids.shape[1]
    head_count = model_width // HD
    n_dev = mesh_shape[0] * mesh_shape[1]
    small = (qv_bias, out_bias, ln1_gain, ln1_shift, ln2_gain, ln2_shift, up_bias, down_bias)
    small_sizes = [a.shape[0] for a in small]
    n_small = sum(small_sizes)
    rows_q = w_qkv.size // model_width
    rows_o = w_out.shape[0]
    attn_buf = jnp.concatenate(
        [w_qkv.reshape(rows_q, model_width), w_out, pack_rows(small, model_width)], axis=0
    )
    attn_all = lax.all_gather(attn_buf, ALL, axis=0, tiled=False)
    qkv_full = attn_all[:, :rows_q].reshape(-1, w_qkv.shape[1])
    out_full = attn_all[:, rows_q : rows_q + rows_o].reshape(-1, model_width)
    small_full = split_owned(attn_all[:, rows_q + rows_o, :n_small], small_sizes)
    qv_full, outb_full, gain_one, shift_one, gain_two, shift_two, upb_full, downb_full = small_full
    rows_u = w_up.size // model_width
    mlp_buf = jnp.concatenate([w_up.reshape(rows_u, model_width), w_down], axis=0)
    mlp_all = lax.all_gather(mlp_buf, ALL, axis=0, tiled=False)
    up_full = mlp_all[:, :rows_u].reshape(-1, w_up.shape[1])
    down_full = mlp_all[:, rows_u:].reshape(-1, model_width)

    gain_one = gain_one.astype(jnp.float32)
    shift_one = shift_one.astype(jnp.float32)
    qv_full = qv_full.astype(jnp.float32)
    rows = inputs.astype(jnp.float32)
    normed_one, recip_one = norm_parts(rows)
    h_one = (normed_one * gain_one + shift_one).astype(jnp.bfloat16)
    qkv_rows = jnp.dot(h_one, qkv_full, preferred_element_type=jnp.float32)
    zero_bias = jnp.zeros((model_width,), jnp.float32)
    qkv_bias = jnp.concatenate([qv_full[:model_width], zero_bias, qv_full[model_width:]])
    qkv_b = (qkv_rows + qkv_bias).astype(jnp.bfloat16)
    attended = attention_fwd(qkv_b, segment_ids, valid)
    mid_rows = (
        rows
        + jnp.dot(attended, out_full, preferred_element_type=jnp.float32)
        + outb_full.astype(jnp.float32)
    )
    gain_two = gain_two.astype(jnp.float32)
    shift_two = shift_two.astype(jnp.float32)
    normed_two, recip_two = norm_parts(mid_rows)
    h_two = (normed_two * gain_two + shift_two).astype(jnp.bfloat16)
    upper = jnp.dot(h_two, up_full, preferred_element_type=jnp.float32) + upb_full.astype(
        jnp.float32
    )
    gelu_rows = jax.nn.gelu(upper, approximate=False).astype(jnp.bfloat16)
    out_rows = (
        mid_rows
        + jnp.dot(gelu_rows, down_full, preferred_element_type=jnp.float32)
        + downb_full.astype(jnp.float32)
    )
    block_out = out_rows.astype(jnp.bfloat16)
    dy_rows = cotangent.astype(jnp.float32)
    grad_wdown = jnp.einsum("tf,td->fd", gelu_rows, cotangent, preferred_element_type=jnp.float32)
    grad_bdown = col_sum(cotangent)
    grad_g = jnp.einsum("td,fd->tf", cotangent, down_full, preferred_element_type=jnp.float32)
    cdf_part = 0.5 * (1.0 + jax.scipy.special.erf(upper * 0.7071067811865476))
    pdf_part = jnp.exp(-0.5 * upper * upper) * 0.3989422804014327
    grad_u = (grad_g * (cdf_part + upper * pdf_part)).astype(jnp.bfloat16)
    grad_bup = col_sum(grad_u)
    grad_wup = jnp.einsum("td,tf->df", h_two, grad_u, preferred_element_type=jnp.float32)
    grad_h2 = jnp.einsum("tf,df->td", grad_u, up_full, preferred_element_type=jnp.float32)
    grad_g2 = jnp.sum(grad_h2 * normed_two, axis=0)
    grad_c2 = jnp.sum(grad_h2, axis=0)
    grad_mid = dy_rows + norm_back(grad_h2, gain_two, normed_two, recip_two)
    grad_a = grad_mid.astype(jnp.bfloat16)
    grad_wout = jnp.einsum("tc,td->cd", attended, grad_a, preferred_element_type=jnp.float32)
    grad_bout = col_sum(grad_a)
    grad_o = jnp.einsum("td,cd->tc", grad_a, out_full, preferred_element_type=jnp.float32).astype(
        jnp.bfloat16
    )
    grad_qkv = attention_bwd(qkv_b, grad_o, segment_ids, valid)
    grad_cols = col_sum(grad_qkv)
    grad_bqv = jnp.concatenate([grad_cols[:model_width], grad_cols[2 * model_width :]])
    grad_wqkv = jnp.einsum("td,te->de", h_one, grad_qkv, preferred_element_type=jnp.float32)
    grad_h1 = jnp.einsum("te,de->td", grad_qkv, qkv_full, preferred_element_type=jnp.float32)
    grad_g1 = jnp.sum(grad_h1 * normed_one, axis=0)
    grad_c1 = jnp.sum(grad_h1, axis=0)
    grad_inputs = grad_mid + norm_back(grad_h1, gain_one, normed_one, recip_one)

    small_grads = (grad_bqv, grad_bout, grad_g1, grad_c1, grad_g2, grad_c2, grad_bup, grad_bdown)
    owned = jnp.concatenate([g.reshape(n_dev, -1) for g in small_grads], axis=1)
    lanes = 128
    small_rows = 8 * pl.cdiv(pl.cdiv(n_small, lanes), 8)
    owned = jnp.pad(owned, ((0, 0), (0, small_rows * lanes - n_small))).reshape(-1, lanes)
    half_up = grad_wup.shape[1] // 2
    parts = [
        (grad_wqkv, w_qkv.shape[0], True),
        (grad_wout, w_out.shape[0], True),
        (grad_wup[:, half_up:], w_up.shape[0], True),
        (owned, small_rows, False),
    ]
    down_sum = lax.psum_scatter(grad_wdown, ALL, scatter_dimension=0, tiled=True)
    up_sum = lax.psum_scatter(grad_wup[:, :half_up], ALL, scatter_dimension=0, tiled=True)
    if all(rb % 8 == 0 and a.shape[1] % 256 == 0 for (a, rb, _) in parts[:3]):
        sums = ring_reduce_scatter(parts, mesh_shape, after=(grad_inputs,))
    else:
        sums = [lax.psum_scatter(a, ALL, scatter_dimension=0, tiled=True) for (a, _, _) in parts]
    sums = list(sums[:2]) + [jnp.concatenate([up_sum, sums[2]], axis=1), down_sum] + list(sums[3:])
    small_sums = split_owned(sums[4].reshape(1, -1), small_sizes)
    bqv, bout, g1, c1, g2, c2, bup, bdown = small_sums
    return (
        block_out,
        grad_inputs,
        sums[0],
        bqv,
        sums[1],
        bout,
        g1,
        c1,
        g2,
        c2,
        sums[2],
        bup,
        sums[3],
        bdown,
    )


def solution(mesh):
    in_specs = (
        P(("wide", "narrow"), None),
        P(("wide", "narrow"), None),
        P(("wide", "narrow")),
        P(("wide", "narrow"), None),
        P(("wide", "narrow")),
        P(("wide", "narrow")),
        P(("wide", "narrow")),
        P(("wide", "narrow")),
        P(("wide", "narrow")),
        P(("wide", "narrow"), None),
        P(("wide", "narrow")),
        P(("wide", "narrow"), None),
        P(("wide", "narrow")),
        P(("wide", "narrow"), None),
        P(("wide", "narrow"), None),
        P(("wide", "narrow"), None),
    )
    out_specs = (
        P(("wide", "narrow"), None),
        P(("wide", "narrow"), None),
        P(("wide", "narrow"), None),
        P(("wide", "narrow")),
        P(("wide", "narrow"), None),
        P(("wide", "narrow")),
        P(("wide", "narrow")),
        P(("wide", "narrow")),
        P(("wide", "narrow")),
        P(("wide", "narrow")),
        P(("wide", "narrow"), None),
        P(("wide", "narrow")),
        P(("wide", "narrow"), None),
        P(("wide", "narrow")),
    )
    body = functools.partial(on_device, mesh_shape=(mesh.shape["wide"], mesh.shape["narrow"]))
    return jax.shard_map(
        body, mesh=mesh, in_specs=in_specs, out_specs=out_specs, check_vma=False
    )
```

```python
import functools
import jax
import jax.numpy as jnp
from jax import lax
from jax.experimental import pallas as pl
from jax.experimental.pallas import tpu as pltpu
from jax.sharding import PartitionSpec as P

HD = 64
ALL = ("wide", "narrow")

EPSILON = 1e-06


def norm_parts(rows):
    center = rows - jnp.mean(rows, axis=-1, keepdims=True)
    recip = lax.rsqrt(jnp.mean(center * center, axis=-1, keepdims=True) + EPSILON)
    return (center * recip, recip)


def norm_back(grad_h, gain, normed, recip):
    scaled = grad_h * gain
    return recip * (
        scaled
        - jnp.mean(scaled, axis=-1, keepdims=True)
        - normed * jnp.mean(scaled * normed, axis=-1, keepdims=True)
    )


def col_sum(rows):
    return jnp.sum(rows.astype(jnp.float32), axis=0)


def seg_mask(seg_col, seg_row, val_row, n):
    rows = lax.broadcasted_iota(jnp.int32, (n, n), 0)
    cols = lax.broadcasted_iota(jnp.int32, (n, n), 1)
    return (seg_col == seg_row) & ((val_row == 1) | (rows == cols))


def soft_rows(qh, kh, allowed):
    scores = lax.dot_general(qh, kh, (((1,), (1,)), ((), ())), preferred_element_type=jnp.float32)
    scores = jnp.where(allowed, scores * (1.0 / HD**0.5), -1e30)
    top = jnp.max(scores, axis=-1, keepdims=True)
    expo = jnp.exp(scores - top)
    return expo * (1.0 / jnp.sum(expo, axis=-1, keepdims=True))


def attn_fwd_kernel(q_ref, k_ref, v_ref, sc_ref, sr_ref, vr_ref, o_ref):
    n = q_ref.shape[0]
    allowed = seg_mask(sc_ref[...], sr_ref[...], vr_ref[...], n)
    outs = []
    for j in range(q_ref.shape[1] // HD):
        cols = slice(j * HD, (j + 1) * HD)
        probs = soft_rows(q_ref[:, cols], k_ref[:, cols], allowed).astype(jnp.bfloat16)
        outs.append(jnp.dot(probs, v_ref[:, cols], preferred_element_type=jnp.float32))
    o_ref[...] = jnp.concatenate(outs, axis=1).astype(o_ref.dtype)


def attn_bwd_kernel(q_ref, k_ref, v_ref, do_ref, sc_ref, sr_ref, vr_ref, dqkv_ref):
    n = q_ref.shape[0]
    width = q_ref.shape[1]
    hp = pl.program_id(1)
    model_width = dqkv_ref.shape[1] // 3
    allowed = seg_mask(sc_ref[...], sr_ref[...], vr_ref[...], n)
    dqs, dks, dvs = [], [], []
    for j in range(width // HD):
        cols = slice(j * HD, (j + 1) * HD)
        qh, kh, vh, doh = q_ref[:, cols], k_ref[:, cols], v_ref[:, cols], do_ref[:, cols]
        probs = soft_rows(qh, kh, allowed)
        dvs.append(
            lax.dot_general(probs.astype(jnp.bfloat16), doh, (((0,), (0,)), ((), ())),
                            preferred_element_type=jnp.float32)
        )
        dprobs = lax.dot_general(doh, vh, (((1,), (1,)), ((), ())), preferred_element_type=jnp.float32)
        row_term = jnp.sum(probs * dprobs, axis=-1, keepdims=True)
        dscore = jnp.where(allowed, probs * (dprobs - row_term), 0.0).astype(jnp.bfloat16)
        dqs.append(jnp.dot(dscore, kh, preferred_element_type=jnp.float32) * (1.0 / HD**0.5))
        dks.append(
            lax.dot_general(dscore, qh, (((0,), (0,)), ((), ())), preferred_element_type=jnp.float32)
            * (1.0 / HD**0.5)
        )
    at = pl.multiple_of(hp * width, width)
    dqkv_ref[:, pl.ds(at, width)] = jnp.concatenate(dqs, axis=1).astype(dqkv_ref.dtype)
    dqkv_ref[:, pl.ds(at + model_width, width)] = jnp.concatenate(dks, axis=1).astype(dqkv_ref.dtype)
    dqkv_ref[:, pl.ds(at + 2 * model_width, width)] = jnp.concatenate(dvs, axis=1).astype(dqkv_ref.dtype)


def mask_operands(segment_ids, valid):
    return (segment_ids[:, :, None], segment_ids[:, None, :], valid[:, None, :])


def attention_fwd(qkv, segment_ids, valid):
    rows, width3 = qkv.shape
    model_width = width3 // 3
    n_seq, seq_len = segment_ids.shape
    blk = 2 * HD
    n_hp = model_width // blk
    off = model_width // blk
    seg_spec = [
        pl.BlockSpec((None, seq_len, 1), lambda s, h: (s, 0, 0)),
        pl.BlockSpec((None, 1, seq_len), lambda s, h: (s, 0, 0)),
        pl.BlockSpec((None, 1, seq_len), lambda s, h: (s, 0, 0)),
    ]
    flops = 4 * n_seq * seq_len * seq_len * model_width
    return pl.pallas_call(
        attn_fwd_kernel,
        out_shape=jax.ShapeDtypeStruct((rows, model_width), jnp.bfloat16),
        grid=(n_seq, n_hp),
        in_specs=[
            pl.BlockSpec((seq_len, blk), lambda s, h: (s, h)),
            pl.BlockSpec((seq_len, blk), lambda s, h: (s, off + h)),
            pl.BlockSpec((seq_len, blk), lambda s, h: (s, 2 * off + h)),
        ]
        + seg_spec,
        out_specs=pl.BlockSpec((seq_len, blk), lambda s, h: (s, h)),
        cost_estimate=pl.CostEstimate(
            flops=flops,
            transcendentals=n_seq * seq_len * seq_len * (model_width // HD),
            bytes_accessed=qkv.size * 2 + rows * model_width * 2,
        ),
    )(qkv, qkv, qkv, *mask_operands(segment_ids, valid))


def attention_bwd(qkv, grad_o, segment_ids, valid):
    rows, width3 = qkv.shape
    model_width = width3 // 3
    n_seq, seq_len = segment_ids.shape
    blk = 2 * HD
    n_hp = model_width // blk
    off = model_width // blk
    seg_spec = [
        pl.BlockSpec((None, seq_len, 1), lambda s, h: (s, 0, 0)),
        pl.BlockSpec((None, 1, seq_len), lambda s, h: (s, 0, 0)),
        pl.BlockSpec((None, 1, seq_len), lambda s, h: (s, 0, 0)),
    ]
    flops = 10 * n_seq * seq_len * seq_len * model_width
    return pl.pallas_call(
        attn_bwd_kernel,
        out_shape=jax.ShapeDtypeStruct((rows, width3), jnp.bfloat16),
        grid=(n_seq, n_hp),
        in_specs=[
            pl.BlockSpec((seq_len, blk), lambda s, h: (s, h)),
            pl.BlockSpec((seq_len, blk), lambda s, h: (s, off + h)),
            pl.BlockSpec((seq_len, blk), lambda s, h: (s, 2 * off + h)),
            pl.BlockSpec((seq_len, blk), lambda s, h: (s, h)),
        ]
        + seg_spec,
        out_specs=pl.BlockSpec((seq_len, width3), lambda s, h: (s, 0)),
        cost_estimate=pl.CostEstimate(
            flops=flops,
            transcendentals=n_seq * seq_len * seq_len * (model_width // HD),
            bytes_accessed=qkv.size * 4 + rows * model_width * 2,
        ),
    )(qkv, qkv, qkv, grad_o, *mask_operands(segment_ids, valid))


MESH_ID = pl.DeviceIdType.MESH


def ring_maps(n_wide, n_narrow):
    n_dev = n_wide * n_narrow
    if (n_wide, n_narrow) == (8, 4):
        def pos_of(w, n):
            z, y, x, c = w // 2, w % 2, n // 2, n % 2
            q = 2 * x + (x + y) % 2
            k = 4 * q + z + (q % 2) * (3 - 2 * z)
            return 2 * k + c

        def coords_of(p):
            k, c = p // 2, p % 2
            q, r = k // 4, k % 4
            z = r + (q % 2) * (3 - 2 * r)
            x = q // 2
            y = (q % 2 + x) % 2
            return z * 2 + y, x * 2 + c

    else:
        def pos_of(w, n):
            return w * n_narrow + n

        def coords_of(p):
            return p // n_narrow, p % n_narrow

    return n_dev, pos_of, coords_of


def ring_reduce_scatter(parts, mesh_shape, after=(), collective_id=0):
    n_wide, n_narrow = mesh_shape
    n_dev, pos_of, coords_of = ring_maps(n_wide, n_narrow)
    specs = []
    for i, (a, rb, split) in enumerate(parts):
        cols = a.shape[1]
        if split:
            specs.append((i, 0, 0, cols // 2))
        else:
            specs.append((i, 0, 0, cols))
    for i, (a, rb, split) in enumerate(parts):
        if split:
            specs.append((i, 1, a.shape[1] // 2, a.shape[1] // 2))
    n_in = len(parts)
    n_after = len(after)
    n_sp = len(specs)
    last_step = n_dev - 2

    def kernel(*refs):
        ins = refs[:n_in]
        outs = refs[n_in + n_after : 2 * n_in + n_after]
        at = 2 * n_in + n_after
        bufs = refs[at : at + n_sp]
        locs = refs[at + n_sp : at + 2 * n_sp]
        send_sem, recv_sem, loc_sem, credit = refs[at + 2 * n_sp :]
        p = pos_of(lax.axis_index("wide"), lax.axis_index("narrow"))
        right = coords_of((p + 1) % n_dev)
        left = coords_of((p + n_dev - 1) % n_dev)
        nbr_send = (right, left)
        nbr_recv = (left, right)

        def rows_of(q, rb):
            cw, cn = coords_of(q % n_dev)
            start = (cw * n_narrow + cn) * rb
            if rb % 8 == 0:
                start = pl.multiple_of(start, 8)
            return pl.ds(start, rb)

        def remote(j, s):
            return pltpu.make_async_remote_copy(
                src_ref=bufs[j].at[s % 3],
                dst_ref=bufs[j].at[(s + 1) % 3],
                send_sem=send_sem.at[j, s % 3],
                recv_sem=recv_sem.at[j, (s + 1) % 3],
                device_id=nbr_send[specs[j][1]],
                device_id_type=MESH_ID,
            )

        def local(j, s):
            i, dirn, c0, cw = specs[j]
            q = (p + 2 * n_dev - s - 2) if dirn == 0 else (p + s + 2)
            return pltpu.make_async_copy(
                ins[i].at[rows_of(q, parts[i][1]), pl.ds(c0, cw)], locs[j].at[s % 2], loc_sem.at[j, s % 2]
            )

        barrier = pltpu.get_barrier_semaphore()
        for nb in (left, right):
            pl.semaphore_signal(barrier, 1, device_id=nb, device_id_type=MESH_ID)
        pl.semaphore_wait(barrier, 2)

        for j, (i, dirn, c0, cw) in enumerate(specs):
            q = p + n_dev - 1 if dirn == 0 else p + 1
            cp = pltpu.make_async_copy(
                ins[i].at[rows_of(q, parts[i][1]), pl.ds(c0, cw)], bufs[j].at[0], loc_sem.at[j, 1]
            )
            cp.start()
            cp.wait()
        for j in range(n_sp):
            remote(j, 0).start()
            local(j, 0).start()

        def step(s, carry):
            for j in range(n_sp):
                dirn = specs[j][1]
                local(j, s).wait()
                remote(j, s).wait_recv()
                nxt = (s + 1) % 3
                bufs[j][nxt] = bufs[j][nxt] + locs[j][s % 2]
                if j == 0 or specs[j - 1][1] != dirn:

                    @pl.when((s >= 1) & (s + 1 <= last_step))
                    def _():
                        pl.semaphore_wait(credit.at[dirn], 1)

                @pl.when(s + 1 <= last_step)
                def _():
                    remote(j, s + 1).start()
                    local(j, s + 1).start()

            for j in range(n_sp):
                remote(j, s).wait_send()
            for dirn in (0, 1):

                @pl.when(s <= last_step - 2)
                def _():
                    pl.semaphore_signal(
                        credit.at[dirn], 1, device_id=nbr_recv[dirn], device_id_type=MESH_ID
                    )

            return carry

        lax.fori_loop(0, last_step + 1, step, 0)
        fin = (last_step + 1) % 3
        for j, (i, dirn, c0, cw) in enumerate(specs):
            outs[i][:, pl.ds(c0, cw)] = bufs[j][fin]

    out_shape = [jax.ShapeDtypeStruct((rb, a.shape[1]), a.dtype) for (a, rb, _) in parts]
    scratch = [pltpu.VMEM((3, parts[i][1], cw), jnp.float32) for (i, _, _, cw) in specs]
    scratch += [pltpu.VMEM((2, parts[i][1], cw), jnp.float32) for (i, _, _, cw) in specs]
    scratch += [
        pltpu.SemaphoreType.DMA((n_sp, 3)),
        pltpu.SemaphoreType.DMA((n_sp, 3)),
        pltpu.SemaphoreType.DMA((n_sp, 2)),
        pltpu.SemaphoreType.REGULAR((2,)),
    ]
    total = sum(a.size * 4 for (a, _, _) in parts)
    return pl.pallas_call(
        kernel,
        out_shape=out_shape,
        in_specs=[pl.BlockSpec(memory_space=pl.ANY)] * (n_in + n_after),
        out_specs=[pl.BlockSpec(memory_space=pltpu.VMEM)] * n_in,
        scratch_shapes=scratch,
        compiler_params=pltpu.CompilerParams(
            collective_id=collective_id, has_side_effects=True, vmem_limit_bytes=48 * 1024 * 1024
        ),
        cost_estimate=pl.CostEstimate(flops=total // 4, transcendentals=0, bytes_accessed=2 * total),
    )(*[a for (a, _, _) in parts], *after)


def pack_rows(pieces, width):
    flat = jnp.concatenate(pieces)
    return jnp.pad(flat, (0, width - flat.shape[0]))[None, :]


def split_owned(packed, sizes):
    out = []
    at = 0
    for size in sizes:
        out.append(packed[:, at : at + size].reshape(-1))
        at += size
    return out


def on_device(
    inputs,
    w_qkv,
    qv_bias,
    w_out,
    out_bias,
    ln1_gain,
    ln1_shift,
    ln2_gain,
    ln2_shift,
    w_up,
    up_bias,
    w_down,
    down_bias,
    segment_ids,
    valid,
    cotangent,
    mesh_shape=None,
):
    row_count = inputs.shape[0]
    model_width = inputs.shape[1]
    seq_count = segment_ids.shape[0]
    seq_len = segment_ids.shape[1]
    head_count = model_width // HD
    n_dev = mesh_shape[0] * mesh_shape[1]
    small = (qv_bias, out_bias, ln1_gain, ln1_shift, ln2_gain, ln2_shift, up_bias, down_bias)
    small_sizes = [a.shape[0] for a in small]
    n_small = sum(small_sizes)
    width_q = w_qkv.shape[1]
    rows_q = w_qkv.shape[0]
    rows_o = w_out.size // width_q
    attn_buf = jnp.concatenate(
        [w_qkv, w_out.reshape(rows_o, width_q), pack_rows(small, width_q)], axis=0
    )
    attn_all = lax.all_gather(attn_buf, ALL, axis=0, tiled=False)
    qkv_full = attn_all[:, :rows_q].reshape(-1, width_q)
    out_full = attn_all[:, rows_q : rows_q + rows_o].reshape(-1, model_width)
    small_full = split_owned(attn_all[:, rows_q + rows_o, :n_small], small_sizes)
    qv_full, outb_full, gain_one, shift_one, gain_two, shift_two, upb_full, downb_full = small_full
    width_u = w_up.shape[1]
    rows_u = w_up.shape[0]
    rows_d = w_down.size // width_u
    mlp_buf = jnp.concatenate([w_up, w_down.reshape(rows_d, width_u)], axis=0)
    mlp_all = lax.all_gather(mlp_buf, ALL, axis=0, tiled=False)
    up_full = mlp_all[:, :rows_u].reshape(-1, width_u)
    down_full = mlp_all[:, rows_u:].reshape(-1, model_width)

    gain_one = gain_one.astype(jnp.float32)
    shift_one = shift_one.astype(jnp.float32)
    qv_full = qv_full.astype(jnp.float32)
    rows = inputs.astype(jnp.float32)
    normed_one, recip_one = norm_parts(rows)
    h_one = (normed_one * gain_one + shift_one).astype(jnp.bfloat16)
    qkv_rows = jnp.dot(h_one, qkv_full, preferred_element_type=jnp.float32)
    zero_bias = jnp.zeros((model_width,), jnp.float32)
    qkv_bias = jnp.concatenate([qv_full[:model_width], zero_bias, qv_full[model_width:]])
    qkv_b = (qkv_rows + qkv_bias).astype(jnp.bfloat16)
    attended = attention_fwd(qkv_b, segment_ids, valid)
    mid_rows = (
        rows
        + jnp.dot(attended, out_full, preferred_element_type=jnp.float32)
        + outb_full.astype(jnp.float32)
    )
    gain_two = gain_two.astype(jnp.float32)
    shift_two = shift_two.astype(jnp.float32)
    normed_two, recip_two = norm_parts(mid_rows)
    h_two = (normed_two * gain_two + shift_two).astype(jnp.bfloat16)
    upper = jnp.dot(h_two, up_full, preferred_element_type=jnp.float32) + upb_full.astype(
        jnp.float32
    )
    gelu_rows = jax.nn.gelu(upper, approximate=False).astype(jnp.bfloat16)
    out_rows = (
        mid_rows
        + jnp.dot(gelu_rows, down_full, preferred_element_type=jnp.float32)
        + downb_full.astype(jnp.float32)
    )
    block_out = out_rows.astype(jnp.bfloat16)
    dy_rows = cotangent.astype(jnp.float32)
    grad_wdown = jnp.einsum("tf,td->fd", gelu_rows, cotangent, preferred_element_type=jnp.float32)
    grad_bdown = col_sum(cotangent)
    grad_g = jnp.einsum("td,fd->tf", cotangent, down_full, preferred_element_type=jnp.float32)
    cdf_part = 0.5 * (1.0 + jax.scipy.special.erf(upper * 0.7071067811865476))
    pdf_part = jnp.exp(-0.5 * upper * upper) * 0.3989422804014327
    grad_u = (grad_g * (cdf_part + upper * pdf_part)).astype(jnp.bfloat16)
    grad_bup = col_sum(grad_u)
    grad_wup = jnp.einsum("td,tf->df", h_two, grad_u, preferred_element_type=jnp.float32)
    grad_h2 = jnp.einsum("tf,df->td", grad_u, up_full, preferred_element_type=jnp.float32)
    grad_g2 = jnp.sum(grad_h2 * normed_two, axis=0)
    grad_c2 = jnp.sum(grad_h2, axis=0)
    grad_mid = dy_rows + norm_back(grad_h2, gain_two, normed_two, recip_two)
    grad_a = grad_mid.astype(jnp.bfloat16)
    grad_wout = jnp.einsum("tc,td->cd", attended, grad_a, preferred_element_type=jnp.float32)
    grad_bout = col_sum(grad_a)
    grad_o = jnp.einsum("td,cd->tc", grad_a, out_full, preferred_element_type=jnp.float32).astype(
        jnp.bfloat16
    )
    grad_qkv = attention_bwd(qkv_b, grad_o, segment_ids, valid)
    grad_cols = col_sum(grad_qkv)
    grad_bqv = jnp.concatenate([grad_cols[:model_width], grad_cols[2 * model_width :]])
    grad_wqkv = jnp.einsum("td,te->de", h_one, grad_qkv, preferred_element_type=jnp.float32)
    grad_h1 = jnp.einsum("te,de->td", grad_qkv, qkv_full, preferred_element_type=jnp.float32)
    grad_g1 = jnp.sum(grad_h1 * normed_one, axis=0)
    grad_c1 = jnp.sum(grad_h1, axis=0)
    grad_inputs = grad_mid + norm_back(grad_h1, gain_one, normed_one, recip_one)

    small_grads = (grad_bqv, grad_bout, grad_g1, grad_c1, grad_g2, grad_c2, grad_bup, grad_bdown)
    owned = jnp.concatenate([g.reshape(n_dev, -1) for g in small_grads], axis=1)
    lanes = 128
    small_rows = 8 * pl.cdiv(pl.cdiv(n_small, lanes), 8)
    owned = jnp.pad(owned, ((0, 0), (0, small_rows * lanes - n_small))).reshape(-1, lanes)
    parts = [
        (grad_wqkv, w_qkv.shape[0], True),
        (grad_wout, w_out.shape[0], True),
        (grad_wup, w_up.shape[0], True),
        (owned, small_rows, False),
    ]
    down_sum = lax.psum_scatter(grad_wdown, ALL, scatter_dimension=0, tiled=True)
    if all(rb % 8 == 0 and a.shape[1] % 256 == 0 for (a, rb, _) in parts[:3]):
        sums = ring_reduce_scatter(parts, mesh_shape, after=(grad_inputs,))
    else:
        sums = [lax.psum_scatter(a, ALL, scatter_dimension=0, tiled=True) for (a, _, _) in parts]
    sums = list(sums[:3]) + [down_sum] + list(sums[3:])
    small_sums = split_owned(sums[4].reshape(1, -1), small_sizes)
    bqv, bout, g1, c1, g2, c2, bup, bdown = small_sums
    return (
        block_out,
        grad_inputs,
        sums[0],
        bqv,
        sums[1],
        bout,
        g1,
        c1,
        g2,
        c2,
        sums[2],
        bup,
        sums[3],
        bdown,
    )


def solution(mesh):
    in_specs = (
        P(("wide", "narrow"), None),
        P(("wide", "narrow"), None),
        P(("wide", "narrow")),
        P(("wide", "narrow"), None),
        P(("wide", "narrow")),
        P(("wide", "narrow")),
        P(("wide", "narrow")),
        P(("wide", "narrow")),
        P(("wide", "narrow")),
        P(("wide", "narrow"), None),
        P(("wide", "narrow")),
        P(("wide", "narrow"), None),
        P(("wide", "narrow")),
        P(("wide", "narrow"), None),
        P(("wide", "narrow"), None),
        P(("wide", "narrow"), None),
    )
    out_specs = (
        P(("wide", "narrow"), None),
        P(("wide", "narrow"), None),
        P(("wide", "narrow"), None),
        P(("wide", "narrow")),
        P(("wide", "narrow"), None),
        P(("wide", "narrow")),
        P(("wide", "narrow")),
        P(("wide", "narrow")),
        P(("wide", "narrow")),
        P(("wide", "narrow")),
        P(("wide", "narrow"), None),
        P(("wide", "narrow")),
        P(("wide", "narrow"), None),
        P(("wide", "narrow")),
    )
    body = functools.partial(on_device, mesh_shape=(mesh.shape["wide"], mesh.shape["narrow"]))
    return jax.shard_map(
        body, mesh=mesh, in_specs=in_specs, out_specs=out_specs, check_vma=False
    )
```

```python
import functools
import jax
import jax.numpy as jnp
from jax import lax
from jax.experimental import pallas as pl
from jax.experimental.pallas import tpu as pltpu
from jax.sharding import PartitionSpec as P

HD = 64
ALL = ("wide", "narrow")

EPSILON = 1e-06


def norm_parts(rows):
    center = rows - jnp.mean(rows, axis=-1, keepdims=True)
    recip = lax.rsqrt(jnp.mean(center * center, axis=-1, keepdims=True) + EPSILON)
    return (center * recip, recip)


def norm_back(grad_h, gain, normed, recip):
    scaled = grad_h * gain
    return recip * (
        scaled
        - jnp.mean(scaled, axis=-1, keepdims=True)
        - normed * jnp.mean(scaled * normed, axis=-1, keepdims=True)
    )


def col_sum(rows):
    return jnp.sum(rows.astype(jnp.float32), axis=0)


Q_TILE = 64
K_WIN = 256


def seg_mask(seg_col, seg_row, val_row, q0, k0):
    rows = q0 + lax.broadcasted_iota(jnp.int32, (seg_col.shape[0], seg_row.shape[1]), 0)
    cols = k0 + lax.broadcasted_iota(jnp.int32, (seg_col.shape[0], seg_row.shape[1]), 1)
    return (seg_col == seg_row) & ((val_row == 1) | (rows == cols))


def soft_rows(qh, kh, allowed):
    scores = lax.dot_general(qh, kh, (((1,), (1,)), ((), ())), preferred_element_type=jnp.float32)
    scores = jnp.where(allowed, scores * (1.0 / HD**0.5), -1e30)
    top = jnp.max(scores, axis=-1, keepdims=True)
    expo = jnp.exp(scores - top)
    return expo * (1.0 / jnp.sum(expo, axis=-1, keepdims=True))


def windows(n):
    win = min(K_WIN, n)
    out = []
    for q0 in range(0, n, Q_TILE):
        k0 = min(max(q0 - (win - Q_TILE) // 2, 0), n - win)
        out.append((q0, k0, win))
    return out


def attn_fwd_kernel(q_ref, k_ref, v_ref, sc_ref, sr_ref, vr_ref, o_ref):
    n = q_ref.shape[0]
    for q0, k0, win in windows(n):
        qs, ks = slice(q0, q0 + Q_TILE), slice(k0, k0 + win)
        allowed = seg_mask(sc_ref[qs, :], sr_ref[:, ks], vr_ref[:, ks], q0, k0)
        outs = []
        for j in range(q_ref.shape[1] // HD):
            cols = slice(j * HD, (j + 1) * HD)
            probs = soft_rows(q_ref[qs, cols], k_ref[ks, cols], allowed).astype(jnp.bfloat16)
            outs.append(jnp.dot(probs, v_ref[ks, cols], preferred_element_type=jnp.float32))
        o_ref[qs, :] = jnp.concatenate(outs, axis=1).astype(o_ref.dtype)


def attn_bwd_kernel(q_ref, k_ref, v_ref, do_ref, sc_ref, sr_ref, vr_ref, dqkv_ref, dk_acc, dv_acc):
    n = q_ref.shape[0]
    width = q_ref.shape[1]
    hp = pl.program_id(1)
    model_width = dqkv_ref.shape[1] // 3
    dk_acc[...] = jnp.zeros_like(dk_acc)
    dv_acc[...] = jnp.zeros_like(dv_acc)
    at = pl.multiple_of(hp * width, width)
    for q0, k0, win in windows(n):
        qs, ks = slice(q0, q0 + Q_TILE), slice(k0, k0 + win)
        allowed = seg_mask(sc_ref[qs, :], sr_ref[:, ks], vr_ref[:, ks], q0, k0)
        dqs, dks, dvs = [], [], []
        for j in range(width // HD):
            cols = slice(j * HD, (j + 1) * HD)
            qh, kh, vh, doh = q_ref[qs, cols], k_ref[ks, cols], v_ref[ks, cols], do_ref[qs, cols]
            probs = soft_rows(qh, kh, allowed)
            dvs.append(
                lax.dot_general(probs.astype(jnp.bfloat16), doh, (((0,), (0,)), ((), ())),
                                preferred_element_type=jnp.float32)
            )
            dprobs = lax.dot_general(doh, vh, (((1,), (1,)), ((), ())), preferred_element_type=jnp.float32)
            row_term = jnp.sum(probs * dprobs, axis=-1, keepdims=True)
            dscore = jnp.where(allowed, probs * (dprobs - row_term), 0.0).astype(jnp.bfloat16)
            dqs.append(jnp.dot(dscore, kh, preferred_element_type=jnp.float32) * (1.0 / HD**0.5))
            dks.append(
                lax.dot_general(dscore, qh, (((0,), (0,)), ((), ())), preferred_element_type=jnp.float32)
                * (1.0 / HD**0.5)
            )
        dqkv_ref[qs, pl.ds(at, width)] = jnp.concatenate(dqs, axis=1).astype(dqkv_ref.dtype)
        dk_acc[ks, :] += jnp.concatenate(dks, axis=1)
        dv_acc[ks, :] += jnp.concatenate(dvs, axis=1)
    dqkv_ref[:, pl.ds(at + model_width, width)] = dk_acc[...].astype(dqkv_ref.dtype)
    dqkv_ref[:, pl.ds(at + 2 * model_width, width)] = dv_acc[...].astype(dqkv_ref.dtype)


def mask_operands(segment_ids, valid):
    return (segment_ids[:, :, None], segment_ids[:, None, :], valid[:, None, :])


def attention_fwd(qkv, segment_ids, valid):
    rows, width3 = qkv.shape
    model_width = width3 // 3
    n_seq, seq_len = segment_ids.shape
    blk = 2 * HD
    n_hp = model_width // blk
    off = model_width // blk
    seg_spec = [
        pl.BlockSpec((None, seq_len, 1), lambda s, h: (s, 0, 0)),
        pl.BlockSpec((None, 1, seq_len), lambda s, h: (s, 0, 0)),
        pl.BlockSpec((None, 1, seq_len), lambda s, h: (s, 0, 0)),
    ]
    flops = 4 * n_seq * seq_len * seq_len * model_width
    return pl.pallas_call(
        attn_fwd_kernel,
        out_shape=jax.ShapeDtypeStruct((rows, model_width), jnp.bfloat16),
        grid=(n_seq, n_hp),
        in_specs=[
            pl.BlockSpec((seq_len, blk), lambda s, h: (s, h)),
            pl.BlockSpec((seq_len, blk), lambda s, h: (s, off + h)),
            pl.BlockSpec((seq_len, blk), lambda s, h: (s, 2 * off + h)),
        ]
        + seg_spec,
        out_specs=pl.BlockSpec((seq_len, blk), lambda s, h: (s, h)),
        cost_estimate=pl.CostEstimate(
            flops=flops,
            transcendentals=n_seq * seq_len * seq_len * (model_width // HD),
            bytes_accessed=qkv.size * 2 + rows * model_width * 2,
        ),
    )(qkv, qkv, qkv, *mask_operands(segment_ids, valid))


def attention_bwd(qkv, grad_o, segment_ids, valid):
    rows, width3 = qkv.shape
    model_width = width3 // 3
    n_seq, seq_len = segment_ids.shape
    blk = 2 * HD
    n_hp = model_width // blk
    off = model_width // blk
    seg_spec = [
        pl.BlockSpec((None, seq_len, 1), lambda s, h: (s, 0, 0)),
        pl.BlockSpec((None, 1, seq_len), lambda s, h: (s, 0, 0)),
        pl.BlockSpec((None, 1, seq_len), lambda s, h: (s, 0, 0)),
    ]
    flops = 10 * n_seq * seq_len * seq_len * model_width
    return pl.pallas_call(
        attn_bwd_kernel,
        out_shape=jax.ShapeDtypeStruct((rows, width3), jnp.bfloat16),
        grid=(n_seq, n_hp),
        in_specs=[
            pl.BlockSpec((seq_len, blk), lambda s, h: (s, h)),
            pl.BlockSpec((seq_len, blk), lambda s, h: (s, off + h)),
            pl.BlockSpec((seq_len, blk), lambda s, h: (s, 2 * off + h)),
            pl.BlockSpec((seq_len, blk), lambda s, h: (s, h)),
        ]
        + seg_spec,
        out_specs=pl.BlockSpec((seq_len, width3), lambda s, h: (s, 0)),
        scratch_shapes=[pltpu.VMEM((seq_len, blk), jnp.float32), pltpu.VMEM((seq_len, blk), jnp.float32)],
        cost_estimate=pl.CostEstimate(
            flops=flops,
            transcendentals=n_seq * seq_len * seq_len * (model_width // HD),
            bytes_accessed=qkv.size * 4 + rows * model_width * 2,
        ),
    )(qkv, qkv, qkv, grad_o, *mask_operands(segment_ids, valid))


MESH_ID = pl.DeviceIdType.MESH


def ring_maps(n_wide, n_narrow):
    n_dev = n_wide * n_narrow
    if (n_wide, n_narrow) == (8, 4):
        def pos_of(w, n):
            z, y, x, c = w // 2, w % 2, n // 2, n % 2
            q = 2 * x + (x + y) % 2
            k = 4 * q + z + (q % 2) * (3 - 2 * z)
            return 2 * k + c

        def coords_of(p):
            k, c = p // 2, p % 2
            q, r = k // 4, k % 4
            z = r + (q % 2) * (3 - 2 * r)
            x = q // 2
            y = (q % 2 + x) % 2
            return z * 2 + y, x * 2 + c

    else:
        def pos_of(w, n):
            return w * n_narrow + n

        def coords_of(p):
            return p // n_narrow, p % n_narrow

    return n_dev, pos_of, coords_of


def ring_reduce_scatter(parts, mesh_shape, after=(), collective_id=0):
    n_wide, n_narrow = mesh_shape
    n_dev, pos_of, coords_of = ring_maps(n_wide, n_narrow)
    specs = []
    for i, (a, rb, split) in enumerate(parts):
        cols = a.shape[1]
        if split:
            specs.append((i, 0, 0, cols // 2))
        else:
            specs.append((i, 0, 0, cols))
    for i, (a, rb, split) in enumerate(parts):
        if split:
            specs.append((i, 1, a.shape[1] // 2, a.shape[1] // 2))
    n_in = len(parts)
    n_after = len(after)
    n_sp = len(specs)
    last_step = n_dev - 2

    def kernel(*refs):
        ins = refs[:n_in]
        outs = refs[n_in + n_after : 2 * n_in + n_after]
        at = 2 * n_in + n_after
        bufs = refs[at : at + n_sp]
        locs = refs[at + n_sp : at + 2 * n_sp]
        send_sem, recv_sem, loc_sem, credit = refs[at + 2 * n_sp :]
        p = pos_of(lax.axis_index("wide"), lax.axis_index("narrow"))
        right = coords_of((p + 1) % n_dev)
        left = coords_of((p + n_dev - 1) % n_dev)
        nbr_send = (right, left)
        nbr_recv = (left, right)

        def rows_of(q, rb):
            cw, cn = coords_of(q % n_dev)
            start = (cw * n_narrow + cn) * rb
            if rb % 8 == 0:
                start = pl.multiple_of(start, 8)
            return pl.ds(start, rb)

        def remote(j, s):
            return pltpu.make_async_remote_copy(
                src_ref=bufs[j].at[s % 3],
                dst_ref=bufs[j].at[(s + 1) % 3],
                send_sem=send_sem.at[j, s % 3],
                recv_sem=recv_sem.at[j, (s + 1) % 3],
                device_id=nbr_send[specs[j][1]],
                device_id_type=MESH_ID,
            )

        def local(j, s):
            i, dirn, c0, cw = specs[j]
            q = (p + 2 * n_dev - s - 2) if dirn == 0 else (p + s + 2)
            return pltpu.make_async_copy(
                ins[i].at[rows_of(q, parts[i][1]), pl.ds(c0, cw)], locs[j].at[s % 2], loc_sem.at[j, s % 2]
            )

        barrier = pltpu.get_barrier_semaphore()
        for nb in (left, right):
            pl.semaphore_signal(barrier, 1, device_id=nb, device_id_type=MESH_ID)
        pl.semaphore_wait(barrier, 2)

        for j, (i, dirn, c0, cw) in enumerate(specs):
            q = p + n_dev - 1 if dirn == 0 else p + 1
            cp = pltpu.make_async_copy(
                ins[i].at[rows_of(q, parts[i][1]), pl.ds(c0, cw)], bufs[j].at[0], loc_sem.at[j, 1]
            )
            cp.start()
            cp.wait()
        for j in range(n_sp):
            remote(j, 0).start()
            local(j, 0).start()

        def step(s, carry):
            for j in range(n_sp):
                dirn = specs[j][1]
                local(j, s).wait()
                remote(j, s).wait_recv()
                nxt = (s + 1) % 3
                bufs[j][nxt] = bufs[j][nxt] + locs[j][s % 2]
                if j == 0 or specs[j - 1][1] != dirn:

                    @pl.when((s >= 1) & (s + 1 <= last_step))
                    def _():
                        pl.semaphore_wait(credit.at[dirn], 1)

                @pl.when(s + 1 <= last_step)
                def _():
                    remote(j, s + 1).start()
                    local(j, s + 1).start()

            for j in range(n_sp):
                remote(j, s).wait_send()
            for dirn in (0, 1):

                @pl.when(s <= last_step - 2)
                def _():
                    pl.semaphore_signal(
                        credit.at[dirn], 1, device_id=nbr_recv[dirn], device_id_type=MESH_ID
                    )

            return carry

        lax.fori_loop(0, last_step + 1, step, 0)
        fin = (last_step + 1) % 3
        for j, (i, dirn, c0, cw) in enumerate(specs):
            outs[i][:, pl.ds(c0, cw)] = bufs[j][fin]

    out_shape = [jax.ShapeDtypeStruct((rb, a.shape[1]), a.dtype) for (a, rb, _) in parts]
    scratch = [pltpu.VMEM((3, parts[i][1], cw), jnp.float32) for (i, _, _, cw) in specs]
    scratch += [pltpu.VMEM((2, parts[i][1], cw), jnp.float32) for (i, _, _, cw) in specs]
    scratch += [
        pltpu.SemaphoreType.DMA((n_sp, 3)),
        pltpu.SemaphoreType.DMA((n_sp, 3)),
        pltpu.SemaphoreType.DMA((n_sp, 2)),
        pltpu.SemaphoreType.REGULAR((2,)),
    ]
    total = sum(a.size * 4 for (a, _, _) in parts)
    return pl.pallas_call(
        kernel,
        out_shape=out_shape,
        in_specs=[pl.BlockSpec(memory_space=pl.ANY)] * (n_in + n_after),
        out_specs=[pl.BlockSpec(memory_space=pltpu.VMEM)] * n_in,
        scratch_shapes=scratch,
        compiler_params=pltpu.CompilerParams(
            collective_id=collective_id, has_side_effects=True, vmem_limit_bytes=48 * 1024 * 1024
        ),
        cost_estimate=pl.CostEstimate(flops=total // 4, transcendentals=0, bytes_accessed=2 * total),
    )(*[a for (a, _, _) in parts], *after)


def pack_rows(pieces, width):
    flat = jnp.concatenate(pieces)
    return jnp.pad(flat, (0, width - flat.shape[0]))[None, :]


def split_owned(packed, sizes):
    out = []
    at = 0
    for size in sizes:
        out.append(packed[:, at : at + size].reshape(-1))
        at += size
    return out


def on_device(
    inputs,
    w_qkv,
    qv_bias,
    w_out,
    out_bias,
    ln1_gain,
    ln1_shift,
    ln2_gain,
    ln2_shift,
    w_up,
    up_bias,
    w_down,
    down_bias,
    segment_ids,
    valid,
    cotangent,
    mesh_shape=None,
):
    row_count = inputs.shape[0]
    model_width = inputs.shape[1]
    seq_count = segment_ids.shape[0]
    seq_len = segment_ids.shape[1]
    head_count = model_width // HD
    n_dev = mesh_shape[0] * mesh_shape[1]
    small = (qv_bias, out_bias, ln1_gain, ln1_shift, ln2_gain, ln2_shift, up_bias, down_bias)
    small_sizes = [a.shape[0] for a in small]
    n_small = sum(small_sizes)
    rows_q = w_qkv.size // model_width
    rows_o = w_out.shape[0]
    attn_buf = jnp.concatenate(
        [w_qkv.reshape(rows_q, model_width), w_out, pack_rows(small, model_width)], axis=0
    )
    attn_all = lax.all_gather(attn_buf, ALL, axis=0, tiled=False)
    qkv_full = attn_all[:, :rows_q].reshape(-1, w_qkv.shape[1])
    out_full = attn_all[:, rows_q : rows_q + rows_o].reshape(-1, model_width)
    small_full = split_owned(attn_all[:, rows_q + rows_o, :n_small], small_sizes)
    qv_full, outb_full, gain_one, shift_one, gain_two, shift_two, upb_full, downb_full = small_full
    rows_u = w_up.size // model_width
    mlp_buf = jnp.concatenate([w_up.reshape(rows_u, model_width), w_down], axis=0)
    mlp_all = lax.all_gather(mlp_buf, ALL, axis=0, tiled=False)
    up_full = mlp_all[:, :rows_u].reshape(-1, w_up.shape[1])
    down_full = mlp_all[:, rows_u:].reshape(-1, model_width)

    gain_one = gain_one.astype(jnp.float32)
    shift_one = shift_one.astype(jnp.float32)
    qv_full = qv_full.astype(jnp.float32)
    rows = inputs.astype(jnp.float32)
    normed_one, recip_one = norm_parts(rows)
    h_one = (normed_one * gain_one + shift_one).astype(jnp.bfloat16)
    qkv_rows = jnp.dot(h_one, qkv_full, preferred_element_type=jnp.float32)
    zero_bias = jnp.zeros((model_width,), jnp.float32)
    qkv_bias = jnp.concatenate([qv_full[:model_width], zero_bias, qv_full[model_width:]])
    qkv_b = (qkv_rows + qkv_bias).astype(jnp.bfloat16)
    attended = attention_fwd(qkv_b, segment_ids, valid)
    mid_rows = (
        rows
        + jnp.dot(attended, out_full, preferred_element_type=jnp.float32)
        + outb_full.astype(jnp.float32)
    )
    gain_two = gain_two.astype(jnp.float32)
    shift_two = shift_two.astype(jnp.float32)
    normed_two, recip_two = norm_parts(mid_rows)
    h_two = (normed_two * gain_two + shift_two).astype(jnp.bfloat16)
    upper = jnp.dot(h_two, up_full, preferred_element_type=jnp.float32) + upb_full.astype(
        jnp.float32
    )
    gelu_rows = jax.nn.gelu(upper, approximate=False).astype(jnp.bfloat16)
    out_rows = (
        mid_rows
        + jnp.dot(gelu_rows, down_full, preferred_element_type=jnp.float32)
        + downb_full.astype(jnp.float32)
    )
    block_out = out_rows.astype(jnp.bfloat16)
    dy_rows = cotangent.astype(jnp.float32)
    grad_wdown = jnp.einsum("tf,td->fd", gelu_rows, cotangent, preferred_element_type=jnp.float32)
    grad_bdown = col_sum(cotangent)
    grad_g = jnp.einsum("td,fd->tf", cotangent, down_full, preferred_element_type=jnp.float32)
    cdf_part = 0.5 * (1.0 + jax.scipy.special.erf(upper * 0.7071067811865476))
    pdf_part = jnp.exp(-0.5 * upper * upper) * 0.3989422804014327
    grad_u = (grad_g * (cdf_part + upper * pdf_part)).astype(jnp.bfloat16)
    grad_bup = col_sum(grad_u)
    grad_wup = jnp.einsum("td,tf->df", h_two, grad_u, preferred_element_type=jnp.float32)
    grad_h2 = jnp.einsum("tf,df->td", grad_u, up_full, preferred_element_type=jnp.float32)
    grad_g2 = jnp.sum(grad_h2 * normed_two, axis=0)
    grad_c2 = jnp.sum(grad_h2, axis=0)
    grad_mid = dy_rows + norm_back(grad_h2, gain_two, normed_two, recip_two)
    grad_a = grad_mid.astype(jnp.bfloat16)
    grad_wout = jnp.einsum("tc,td->cd", attended, grad_a, preferred_element_type=jnp.float32)
    grad_bout = col_sum(grad_a)
    grad_o = jnp.einsum("td,cd->tc", grad_a, out_full, preferred_element_type=jnp.float32).astype(
        jnp.bfloat16
    )
    grad_qkv = attention_bwd(qkv_b, grad_o, segment_ids, valid)
    grad_cols = col_sum(grad_qkv)
    grad_bqv = jnp.concatenate([grad_cols[:model_width], grad_cols[2 * model_width :]])
    grad_wqkv = jnp.einsum("td,te->de", h_one, grad_qkv, preferred_element_type=jnp.float32)
    grad_h1 = jnp.einsum("te,de->td", grad_qkv, qkv_full, preferred_element_type=jnp.float32)
    grad_g1 = jnp.sum(grad_h1 * normed_one, axis=0)
    grad_c1 = jnp.sum(grad_h1, axis=0)
    grad_inputs = grad_mid + norm_back(grad_h1, gain_one, normed_one, recip_one)

    small_grads = (grad_bqv, grad_bout, grad_g1, grad_c1, grad_g2, grad_c2, grad_bup, grad_bdown)
    owned = jnp.concatenate([g.reshape(n_dev, -1) for g in small_grads], axis=1)
    lanes = 128
    small_rows = 8 * pl.cdiv(pl.cdiv(n_small, lanes), 8)
    owned = jnp.pad(owned, ((0, 0), (0, small_rows * lanes - n_small))).reshape(-1, lanes)
    parts = [
        (grad_wqkv, w_qkv.shape[0], True),
        (grad_wout, w_out.shape[0], True),
        (grad_wup, w_up.shape[0], True),
        (owned, small_rows, False),
    ]
    down_sum = lax.psum_scatter(grad_wdown, ALL, scatter_dimension=0, tiled=True)
    if all(rb % 8 == 0 and a.shape[1] % 256 == 0 for (a, rb, _) in parts[:3]):
        sums = ring_reduce_scatter(parts, mesh_shape, after=(grad_inputs,))
    else:
        sums = [lax.psum_scatter(a, ALL, scatter_dimension=0, tiled=True) for (a, _, _) in parts]
    sums = list(sums[:3]) + [down_sum] + list(sums[3:])
    small_sums = split_owned(sums[4].reshape(1, -1), small_sizes)
    bqv, bout, g1, c1, g2, c2, bup, bdown = small_sums
    return (
        block_out,
        grad_inputs,
        sums[0],
        bqv,
        sums[1],
        bout,
        g1,
        c1,
        g2,
        c2,
        sums[2],
        bup,
        sums[3],
        bdown,
    )


def solution(mesh):
    in_specs = (
        P(("wide", "narrow"), None),
        P(("wide", "narrow"), None),
        P(("wide", "narrow")),
        P(("wide", "narrow"), None),
        P(("wide", "narrow")),
        P(("wide", "narrow")),
        P(("wide", "narrow")),
        P(("wide", "narrow")),
        P(("wide", "narrow")),
        P(("wide", "narrow"), None),
        P(("wide", "narrow")),
        P(("wide", "narrow"), None),
        P(("wide", "narrow")),
        P(("wide", "narrow"), None),
        P(("wide", "narrow"), None),
        P(("wide", "narrow"), None),
    )
    out_specs = (
        P(("wide", "narrow"), None),
        P(("wide", "narrow"), None),
        P(("wide", "narrow"), None),
        P(("wide", "narrow")),
        P(("wide", "narrow"), None),
        P(("wide", "narrow")),
        P(("wide", "narrow")),
        P(("wide", "narrow")),
        P(("wide", "narrow")),
        P(("wide", "narrow")),
        P(("wide", "narrow"), None),
        P(("wide", "narrow")),
        P(("wide", "narrow"), None),
        P(("wide", "narrow")),
    )
    body = functools.partial(on_device, mesh_shape=(mesh.shape["wide"], mesh.shape["narrow"]))
    return jax.shard_map(
        body, mesh=mesh, in_specs=in_specs, out_specs=out_specs, check_vma=False
    )
```

```python
import functools
import jax
import jax.numpy as jnp
from jax import lax
from jax.experimental import pallas as pl
from jax.experimental.pallas import tpu as pltpu
from jax.sharding import PartitionSpec as P

HD = 64
ALL = ("wide", "narrow")

EPSILON = 1e-06


def norm_parts(rows):
    center = rows - jnp.mean(rows, axis=-1, keepdims=True)
    recip = lax.rsqrt(jnp.mean(center * center, axis=-1, keepdims=True) + EPSILON)
    return (center * recip, recip)


def norm_back(grad_h, gain, normed, recip):
    scaled = grad_h * gain
    return recip * (
        scaled
        - jnp.mean(scaled, axis=-1, keepdims=True)
        - normed * jnp.mean(scaled * normed, axis=-1, keepdims=True)
    )


def col_sum(rows):
    return jnp.sum(rows.astype(jnp.float32), axis=0)


def seg_mask(seg_col, seg_row, val_row, n):
    rows = lax.broadcasted_iota(jnp.int32, (n, n), 0)
    cols = lax.broadcasted_iota(jnp.int32, (n, n), 1)
    return (seg_col == seg_row) & ((val_row == 1) | (rows == cols))


def soft_rows(qh, kh, allowed):
    scores = lax.dot_general(qh, kh, (((1,), (1,)), ((), ())), preferred_element_type=jnp.float32)
    scores = jnp.where(allowed, scores * (1.0 / HD**0.5), -1e30)
    top = jnp.max(scores, axis=-1, keepdims=True)
    expo = jnp.exp(scores - top)
    return expo * (1.0 / jnp.sum(expo, axis=-1, keepdims=True))


def attn_fwd_kernel(q_ref, k_ref, v_ref, sc_ref, sr_ref, vr_ref, o_ref):
    n = q_ref.shape[0]
    allowed = seg_mask(sc_ref[...], sr_ref[...], vr_ref[...], n)
    outs = []
    for j in range(q_ref.shape[1] // HD):
        cols = slice(j * HD, (j + 1) * HD)
        probs = soft_rows(q_ref[:, cols], k_ref[:, cols], allowed).astype(jnp.bfloat16)
        outs.append(jnp.dot(probs, v_ref[:, cols], preferred_element_type=jnp.float32))
    o_ref[...] = jnp.concatenate(outs, axis=1).astype(o_ref.dtype)


def attn_bwd_kernel(q_ref, k_ref, v_ref, do_ref, sc_ref, sr_ref, vr_ref, dqkv_ref):
    n = q_ref.shape[0]
    width = q_ref.shape[1]
    hp = pl.program_id(1)
    model_width = dqkv_ref.shape[1] // 3
    allowed = seg_mask(sc_ref[...], sr_ref[...], vr_ref[...], n)
    dqs, dks, dvs = [], [], []
    for j in range(width // HD):
        cols = slice(j * HD, (j + 1) * HD)
        qh, kh, vh, doh = q_ref[:, cols], k_ref[:, cols], v_ref[:, cols], do_ref[:, cols]
        probs = soft_rows(qh, kh, allowed)
        dvs.append(
            lax.dot_general(probs.astype(jnp.bfloat16), doh, (((0,), (0,)), ((), ())),
                            preferred_element_type=jnp.float32)
        )
        dprobs = lax.dot_general(doh, vh, (((1,), (1,)), ((), ())), preferred_element_type=jnp.float32)
        row_term = jnp.sum(probs * dprobs, axis=-1, keepdims=True)
        dscore = jnp.where(allowed, probs * (dprobs - row_term), 0.0).astype(jnp.bfloat16)
        dqs.append(jnp.dot(dscore, kh, preferred_element_type=jnp.float32) * (1.0 / HD**0.5))
        dks.append(
            lax.dot_general(dscore, qh, (((0,), (0,)), ((), ())), preferred_element_type=jnp.float32)
            * (1.0 / HD**0.5)
        )
    at = pl.multiple_of(hp * width, width)
    dqkv_ref[:, pl.ds(at, width)] = jnp.concatenate(dqs, axis=1).astype(dqkv_ref.dtype)
    dqkv_ref[:, pl.ds(at + model_width, width)] = jnp.concatenate(dks, axis=1).astype(dqkv_ref.dtype)
    dqkv_ref[:, pl.ds(at + 2 * model_width, width)] = jnp.concatenate(dvs, axis=1).astype(dqkv_ref.dtype)


def mask_operands(segment_ids, valid):
    return (segment_ids[:, :, None], segment_ids[:, None, :], valid[:, None, :])


def attention_fwd(qkv, segment_ids, valid):
    rows, width3 = qkv.shape
    model_width = width3 // 3
    n_seq, seq_len = segment_ids.shape
    blk = 2 * HD
    n_hp = model_width // blk
    off = model_width // blk
    seg_spec = [
        pl.BlockSpec((None, seq_len, 1), lambda s, h: (s, 0, 0)),
        pl.BlockSpec((None, 1, seq_len), lambda s, h: (s, 0, 0)),
        pl.BlockSpec((None, 1, seq_len), lambda s, h: (s, 0, 0)),
    ]
    flops = 4 * n_seq * seq_len * seq_len * model_width
    return pl.pallas_call(
        attn_fwd_kernel,
        out_shape=jax.ShapeDtypeStruct((rows, model_width), jnp.bfloat16),
        grid=(n_seq, n_hp),
        in_specs=[
            pl.BlockSpec((seq_len, blk), lambda s, h: (s, h)),
            pl.BlockSpec((seq_len, blk), lambda s, h: (s, off + h)),
            pl.BlockSpec((seq_len, blk), lambda s, h: (s, 2 * off + h)),
        ]
        + seg_spec,
        out_specs=pl.BlockSpec((seq_len, blk), lambda s, h: (s, h)),
        cost_estimate=pl.CostEstimate(
            flops=flops,
            transcendentals=n_seq * seq_len * seq_len * (model_width // HD),
            bytes_accessed=qkv.size * 2 + rows * model_width * 2,
        ),
    )(qkv, qkv, qkv, *mask_operands(segment_ids, valid))


def attention_bwd(qkv, grad_o, segment_ids, valid):
    rows, width3 = qkv.shape
    model_width = width3 // 3
    n_seq, seq_len = segment_ids.shape
    blk = 2 * HD
    n_hp = model_width // blk
    off = model_width // blk
    seg_spec = [
        pl.BlockSpec((None, seq_len, 1), lambda s, h: (s, 0, 0)),
        pl.BlockSpec((None, 1, seq_len), lambda s, h: (s, 0, 0)),
        pl.BlockSpec((None, 1, seq_len), lambda s, h: (s, 0, 0)),
    ]
    flops = 10 * n_seq * seq_len * seq_len * model_width
    return pl.pallas_call(
        attn_bwd_kernel,
        out_shape=jax.ShapeDtypeStruct((rows, width3), jnp.bfloat16),
        grid=(n_seq, n_hp),
        in_specs=[
            pl.BlockSpec((seq_len, blk), lambda s, h: (s, h)),
            pl.BlockSpec((seq_len, blk), lambda s, h: (s, off + h)),
            pl.BlockSpec((seq_len, blk), lambda s, h: (s, 2 * off + h)),
            pl.BlockSpec((seq_len, blk), lambda s, h: (s, h)),
        ]
        + seg_spec,
        out_specs=pl.BlockSpec((seq_len, width3), lambda s, h: (s, 0)),
        cost_estimate=pl.CostEstimate(
            flops=flops,
            transcendentals=n_seq * seq_len * seq_len * (model_width // HD),
            bytes_accessed=qkv.size * 4 + rows * model_width * 2,
        ),
    )(qkv, qkv, qkv, grad_o, *mask_operands(segment_ids, valid))


MESH_ID = pl.DeviceIdType.MESH


def ring_maps(n_wide, n_narrow):
    n_dev = n_wide * n_narrow
    if (n_wide, n_narrow) == (8, 4):
        def pos_of(w, n):
            z, y, x, c = w // 2, w % 2, n // 2, n % 2
            q = 2 * x + (x + y) % 2
            k = 4 * q + z + (q % 2) * (3 - 2 * z)
            return 2 * k + c

        def coords_of(p):
            k, c = p // 2, p % 2
            q, r = k // 4, k % 4
            z = r + (q % 2) * (3 - 2 * r)
            x = q // 2
            y = (q % 2 + x) % 2
            return z * 2 + y, x * 2 + c

    else:
        def pos_of(w, n):
            return w * n_narrow + n

        def coords_of(p):
            return p // n_narrow, p % n_narrow

    return n_dev, pos_of, coords_of


def ring_reduce_scatter(parts, mesh_shape, after=(), collective_id=0):
    n_wide, n_narrow = mesh_shape
    n_dev, pos_of, coords_of = ring_maps(n_wide, n_narrow)
    specs = []
    for i, (a, rb, split) in enumerate(parts):
        cols = a.shape[1]
        if split:
            specs.append((i, 0, 0, cols // 2))
        else:
            specs.append((i, 0, 0, cols))
    for i, (a, rb, split) in enumerate(parts):
        if split:
            specs.append((i, 1, a.shape[1] // 2, a.shape[1] // 2))
    n_in = len(parts)
    n_after = len(after)
    n_sp = len(specs)
    last_step = n_dev - 2

    def kernel(*refs):
        ins = refs[:n_in]
        outs = refs[n_in + n_after : 2 * n_in + n_after]
        at = 2 * n_in + n_after
        bufs = refs[at : at + n_sp]
        locs = refs[at + n_sp : at + 2 * n_sp]
        send_sem, recv_sem, loc_sem, credit = refs[at + 2 * n_sp :]
        p = pos_of(lax.axis_index("wide"), lax.axis_index("narrow"))
        right = coords_of((p + 1) % n_dev)
        left = coords_of((p + n_dev - 1) % n_dev)
        nbr_send = (right, left)
        nbr_recv = (left, right)

        def rows_of(q, rb):
            cw, cn = coords_of(q % n_dev)
            start = (cw * n_narrow + cn) * rb
            if rb % 8 == 0:
                start = pl.multiple_of(start, 8)
            return pl.ds(start, rb)

        def remote(j, s):
            return pltpu.make_async_remote_copy(
                src_ref=bufs[j].at[s % 3],
                dst_ref=bufs[j].at[(s + 1) % 3],
                send_sem=send_sem.at[j, s % 3],
                recv_sem=recv_sem.at[j, (s + 1) % 3],
                device_id=nbr_send[specs[j][1]],
                device_id_type=MESH_ID,
            )

        def local(j, s):
            i, dirn, c0, cw = specs[j]
            q = (p + 2 * n_dev - s - 2) if dirn == 0 else (p + s + 2)
            return pltpu.make_async_copy(
                ins[i].at[rows_of(q, parts[i][1]), pl.ds(c0, cw)], locs[j].at[s % 2], loc_sem.at[j, s % 2]
            )

        barrier = pltpu.get_barrier_semaphore()
        for nb in (left, right):
            pl.semaphore_signal(barrier, 1, device_id=nb, device_id_type=MESH_ID)
        pl.semaphore_wait(barrier, 2)

        for j, (i, dirn, c0, cw) in enumerate(specs):
            q = p + n_dev - 1 if dirn == 0 else p + 1
            cp = pltpu.make_async_copy(
                ins[i].at[rows_of(q, parts[i][1]), pl.ds(c0, cw)], bufs[j].at[0], loc_sem.at[j, 1]
            )
            cp.start()
            cp.wait()
        for j in range(n_sp):
            remote(j, 0).start()
            local(j, 0).start()

        def step(s, carry):
            for j in range(n_sp):
                dirn = specs[j][1]
                local(j, s).wait()
                remote(j, s).wait_recv()
                nxt = (s + 1) % 3
                bufs[j][nxt] = bufs[j][nxt] + locs[j][s % 2]
                if j == 0 or specs[j - 1][1] != dirn:

                    @pl.when((s >= 1) & (s + 1 <= last_step))
                    def _():
                        pl.semaphore_wait(credit.at[dirn], 1)

                @pl.when(s + 1 <= last_step)
                def _():
                    remote(j, s + 1).start()
                    local(j, s + 1).start()

            for j in range(n_sp):
                remote(j, s).wait_send()
            for dirn in (0, 1):

                @pl.when(s <= last_step - 2)
                def _():
                    pl.semaphore_signal(
                        credit.at[dirn], 1, device_id=nbr_recv[dirn], device_id_type=MESH_ID
                    )

            return carry

        lax.fori_loop(0, last_step + 1, step, 0)
        fin = (last_step + 1) % 3
        for j, (i, dirn, c0, cw) in enumerate(specs):
            outs[i][:, pl.ds(c0, cw)] = bufs[j][fin]

    out_shape = [jax.ShapeDtypeStruct((rb, a.shape[1]), a.dtype) for (a, rb, _) in parts]
    scratch = [pltpu.VMEM((3, parts[i][1], cw), jnp.float32) for (i, _, _, cw) in specs]
    scratch += [pltpu.VMEM((2, parts[i][1], cw), jnp.float32) for (i, _, _, cw) in specs]
    scratch += [
        pltpu.SemaphoreType.DMA((n_sp, 3)),
        pltpu.SemaphoreType.DMA((n_sp, 3)),
        pltpu.SemaphoreType.DMA((n_sp, 2)),
        pltpu.SemaphoreType.REGULAR((2,)),
    ]
    total = sum(a.size * 4 for (a, _, _) in parts)
    return pl.pallas_call(
        kernel,
        out_shape=out_shape,
        in_specs=[pl.BlockSpec(memory_space=pl.ANY)] * (n_in + n_after),
        out_specs=[pl.BlockSpec(memory_space=pltpu.VMEM)] * n_in,
        scratch_shapes=scratch,
        compiler_params=pltpu.CompilerParams(
            collective_id=collective_id, has_side_effects=True, vmem_limit_bytes=48 * 1024 * 1024
        ),
        cost_estimate=pl.CostEstimate(flops=total // 4, transcendentals=0, bytes_accessed=2 * total),
    )(*[a for (a, _, _) in parts], *after)


def pack_rows(pieces, width):
    flat = jnp.concatenate(pieces)
    return jnp.pad(flat, (0, width - flat.shape[0]))[None, :]


def split_owned(packed, sizes):
    out = []
    at = 0
    for size in sizes:
        out.append(packed[:, at : at + size].reshape(-1))
        at += size
    return out


def on_device(
    inputs,
    w_qkv,
    qv_bias,
    w_out,
    out_bias,
    ln1_gain,
    ln1_shift,
    ln2_gain,
    ln2_shift,
    w_up,
    up_bias,
    w_down,
    down_bias,
    segment_ids,
    valid,
    cotangent,
    mesh_shape=None,
):
    row_count = inputs.shape[0]
    model_width = inputs.shape[1]
    seq_count = segment_ids.shape[0]
    seq_len = segment_ids.shape[1]
    head_count = model_width // HD
    n_dev = mesh_shape[0] * mesh_shape[1]
    small = (qv_bias, out_bias, ln1_gain, ln1_shift, ln2_gain, ln2_shift, up_bias, down_bias)
    small_sizes = [a.shape[0] for a in small]
    n_small = sum(small_sizes)
    rows_q = w_qkv.size // model_width
    rows_o = w_out.shape[0]
    attn_buf = jnp.concatenate(
        [w_qkv.reshape(rows_q, model_width), w_out, pack_rows(small, model_width)], axis=0
    )
    attn_all = lax.all_gather(attn_buf, ALL, axis=0, tiled=False)
    qkv_full = attn_all[:, :rows_q].reshape(-1, w_qkv.shape[1])
    out_full = attn_all[:, rows_q : rows_q + rows_o].reshape(-1, model_width)
    small_full = split_owned(attn_all[:, rows_q + rows_o, :n_small], small_sizes)
    qv_full, outb_full, gain_one, shift_one, gain_two, shift_two, upb_full, downb_full = small_full
    rows_u = w_up.size // model_width
    mlp_buf = jnp.concatenate([w_up.reshape(rows_u, model_width), w_down], axis=0)
    mlp_all = lax.all_gather(mlp_buf, ALL, axis=0, tiled=False)
    up_full = mlp_all[:, :rows_u].reshape(-1, w_up.shape[1])
    down_full = mlp_all[:, rows_u:].reshape(-1, model_width)

    gain_one = gain_one.astype(jnp.float32)
    shift_one = shift_one.astype(jnp.float32)
    qv_full = qv_full.astype(jnp.float32)
    rows = inputs.astype(jnp.float32)
    normed_one, recip_one = norm_parts(rows)
    h_one = (normed_one * gain_one + shift_one).astype(jnp.bfloat16)
    qkv_rows = jnp.dot(h_one, qkv_full, preferred_element_type=jnp.float32)
    zero_bias = jnp.zeros((model_width,), jnp.float32)
    qkv_bias = jnp.concatenate([qv_full[:model_width], zero_bias, qv_full[model_width:]])
    qkv_b = (qkv_rows + qkv_bias).astype(jnp.bfloat16)
    attended = attention_fwd(qkv_b, segment_ids, valid)
    mid_rows = (
        rows
        + jnp.dot(attended, out_full, preferred_element_type=jnp.float32)
        + outb_full.astype(jnp.float32)
    )
    gain_two = gain_two.astype(jnp.float32)
    shift_two = shift_two.astype(jnp.float32)
    normed_two, recip_two = norm_parts(mid_rows)
    h_two = (normed_two * gain_two + shift_two).astype(jnp.bfloat16)
    upper = jnp.dot(h_two, up_full, preferred_element_type=jnp.float32) + upb_full.astype(
        jnp.float32
    )
    gelu_rows = jax.nn.gelu(upper, approximate=False).astype(jnp.bfloat16)
    out_rows = (
        mid_rows
        + jnp.dot(gelu_rows, down_full, preferred_element_type=jnp.float32)
        + downb_full.astype(jnp.float32)
    )
    block_out = out_rows.astype(jnp.bfloat16)
    dy_rows = cotangent.astype(jnp.float32)
    grad_wdown = jnp.einsum("tf,td->fd", gelu_rows, cotangent, preferred_element_type=jnp.float32)
    grad_bdown = col_sum(cotangent)
    grad_g = jnp.einsum("td,fd->tf", cotangent, down_full, preferred_element_type=jnp.float32)
    cdf_part = 0.5 * (1.0 + jax.scipy.special.erf(upper * 0.7071067811865476))
    pdf_part = jnp.exp(-0.5 * upper * upper) * 0.3989422804014327
    grad_u = (grad_g * (cdf_part + upper * pdf_part)).astype(jnp.bfloat16)
    grad_bup = col_sum(grad_u)
    grad_wup = jnp.einsum("td,tf->df", h_two, grad_u, preferred_element_type=jnp.float32)
    grad_h2 = jnp.einsum("tf,df->td", grad_u, up_full, preferred_element_type=jnp.float32)
    grad_g2 = jnp.sum(grad_h2 * normed_two, axis=0)
    grad_c2 = jnp.sum(grad_h2, axis=0)
    grad_mid = dy_rows + norm_back(grad_h2, gain_two, normed_two, recip_two)
    grad_a = grad_mid.astype(jnp.bfloat16)
    grad_wout = jnp.einsum("tc,td->cd", attended, grad_a, preferred_element_type=jnp.float32)
    grad_bout = col_sum(grad_a)
    grad_o = jnp.einsum("td,cd->tc", grad_a, out_full, preferred_element_type=jnp.float32).astype(
        jnp.bfloat16
    )
    grad_qkv = attention_bwd(qkv_b, grad_o, segment_ids, valid)
    grad_cols = col_sum(grad_qkv)
    grad_bqv = jnp.concatenate([grad_cols[:model_width], grad_cols[2 * model_width :]])
    grad_wqkv = jnp.einsum("td,te->de", h_one, grad_qkv, preferred_element_type=jnp.float32)
    grad_h1 = jnp.einsum("te,de->td", grad_qkv, qkv_full, preferred_element_type=jnp.float32)
    grad_g1 = jnp.sum(grad_h1 * normed_one, axis=0)
    grad_c1 = jnp.sum(grad_h1, axis=0)
    grad_inputs = grad_mid + norm_back(grad_h1, gain_one, normed_one, recip_one)

    small_grads = (grad_bqv, grad_bout, grad_g1, grad_c1, grad_g2, grad_c2, grad_bup, grad_bdown)
    owned = jnp.concatenate([g.reshape(n_dev, -1) for g in small_grads], axis=1)
    lanes = 128
    small_rows = 8 * pl.cdiv(pl.cdiv(n_small, lanes), 8)
    owned = jnp.pad(owned, ((0, 0), (0, small_rows * lanes - n_small))).reshape(-1, lanes)
    parts = [
        (grad_wqkv, w_qkv.shape[0], True),
        (grad_wout, w_out.shape[0], True),
        (grad_wup, w_up.shape[0], True),
        (owned, small_rows, False),
    ]
    down_sum = lax.psum_scatter(grad_wdown, ALL, scatter_dimension=0, tiled=True)
    if all(rb % 8 == 0 and a.shape[1] % 256 == 0 for (a, rb, _) in parts[:3]):
        sums = ring_reduce_scatter(parts, mesh_shape, after=(grad_inputs, block_out))
    else:
        sums = [lax.psum_scatter(a, ALL, scatter_dimension=0, tiled=True) for (a, _, _) in parts]
    sums = list(sums[:3]) + [down_sum] + list(sums[3:])
    small_sums = split_owned(sums[4].reshape(1, -1), small_sizes)
    bqv, bout, g1, c1, g2, c2, bup, bdown = small_sums
    return (
        block_out,
        grad_inputs,
        sums[0],
        bqv,
        sums[1],
        bout,
        g1,
        c1,
        g2,
        c2,
        sums[2],
        bup,
        sums[3],
        bdown,
    )


def solution(mesh):
    in_specs = (
        P(("wide", "narrow"), None),
        P(("wide", "narrow"), None),
        P(("wide", "narrow")),
        P(("wide", "narrow"), None),
        P(("wide", "narrow")),
        P(("wide", "narrow")),
        P(("wide", "narrow")),
        P(("wide", "narrow")),
        P(("wide", "narrow")),
        P(("wide", "narrow"), None),
        P(("wide", "narrow")),
        P(("wide", "narrow"), None),
        P(("wide", "narrow")),
        P(("wide", "narrow"), None),
        P(("wide", "narrow"), None),
        P(("wide", "narrow"), None),
    )
    out_specs = (
        P(("wide", "narrow"), None),
        P(("wide", "narrow"), None),
        P(("wide", "narrow"), None),
        P(("wide", "narrow")),
        P(("wide", "narrow"), None),
        P(("wide", "narrow")),
        P(("wide", "narrow")),
        P(("wide", "narrow")),
        P(("wide", "narrow")),
        P(("wide", "narrow")),
        P(("wide", "narrow"), None),
        P(("wide", "narrow")),
        P(("wide", "narrow"), None),
        P(("wide", "narrow")),
    )
    body = functools.partial(on_device, mesh_shape=(mesh.shape["wide"], mesh.shape["narrow"]))
    return jax.shard_map(
        body, mesh=mesh, in_specs=in_specs, out_specs=out_specs, check_vma=False
    )
```

```python
import functools
import jax
import jax.numpy as jnp
from jax import lax
from jax.experimental import pallas as pl
from jax.experimental.pallas import tpu as pltpu
from jax.sharding import PartitionSpec as P

HD = 64
ALL = ("wide", "narrow")

EPSILON = 1e-06


def norm_parts(rows):
    center = rows - jnp.mean(rows, axis=-1, keepdims=True)
    recip = lax.rsqrt(jnp.mean(center * center, axis=-1, keepdims=True) + EPSILON)
    return (center * recip, recip)


def norm_back(grad_h, gain, normed, recip):
    scaled = grad_h * gain
    return recip * (
        scaled
        - jnp.mean(scaled, axis=-1, keepdims=True)
        - normed * jnp.mean(scaled * normed, axis=-1, keepdims=True)
    )


def col_sum(rows):
    return jnp.sum(rows.astype(jnp.float32), axis=0)


Q_CHUNK = 128


def seg_mask(seg_col, seg_row, val_row, q0):
    shape = (seg_col.shape[0], seg_row.shape[1])
    rows = q0 + lax.broadcasted_iota(jnp.int32, shape, 0)
    cols = lax.broadcasted_iota(jnp.int32, shape, 1)
    return (seg_col == seg_row) & ((val_row == 1) | (rows == cols))


def soft_rows(qh, kh, allowed):
    scores = lax.dot_general(qh, kh, (((1,), (1,)), ((), ())), preferred_element_type=jnp.float32)
    scores = jnp.where(allowed, scores * (1.0 / HD**0.5), -1e30)
    top = jnp.max(scores, axis=-1, keepdims=True)
    expo = jnp.exp(scores - top)
    return expo * (1.0 / jnp.sum(expo, axis=-1, keepdims=True))


def attn_fwd_kernel(q_ref, k_ref, v_ref, sc_ref, sr_ref, vr_ref, o_ref):
    n = q_ref.shape[0]

    def chunk(c, carry):
        q0 = pl.multiple_of(c * Q_CHUNK, Q_CHUNK)
        qs = pl.ds(q0, Q_CHUNK)
        allowed = seg_mask(sc_ref[qs, :], sr_ref[...], vr_ref[...], q0)
        outs = []
        for j in range(q_ref.shape[1] // HD):
            cols = slice(j * HD, (j + 1) * HD)
            probs = soft_rows(q_ref[qs, cols], k_ref[:, cols], allowed).astype(jnp.bfloat16)
            outs.append(jnp.dot(probs, v_ref[:, cols], preferred_element_type=jnp.float32))
        o_ref[qs, :] = jnp.concatenate(outs, axis=1).astype(o_ref.dtype)
        return carry

    lax.fori_loop(0, n // Q_CHUNK, chunk, 0)


def attn_bwd_kernel(q_ref, k_ref, v_ref, do_ref, sc_ref, sr_ref, vr_ref, dqkv_ref, dk_acc, dv_acc):
    n = q_ref.shape[0]
    width = q_ref.shape[1]
    hp = pl.program_id(1)
    model_width = dqkv_ref.shape[1] // 3
    at = pl.multiple_of(hp * width, width)
    dk_acc[...] = jnp.zeros_like(dk_acc)
    dv_acc[...] = jnp.zeros_like(dv_acc)

    def chunk(c, carry):
        q0 = pl.multiple_of(c * Q_CHUNK, Q_CHUNK)
        qs = pl.ds(q0, Q_CHUNK)
        allowed = seg_mask(sc_ref[qs, :], sr_ref[...], vr_ref[...], q0)
        dqs, dks, dvs = [], [], []
        for j in range(width // HD):
            cols = slice(j * HD, (j + 1) * HD)
            qh, kh, vh, doh = q_ref[qs, cols], k_ref[:, cols], v_ref[:, cols], do_ref[qs, cols]
            probs = soft_rows(qh, kh, allowed)
            dvs.append(
                lax.dot_general(probs.astype(jnp.bfloat16), doh, (((0,), (0,)), ((), ())),
                                preferred_element_type=jnp.float32)
            )
            dprobs = lax.dot_general(doh, vh, (((1,), (1,)), ((), ())), preferred_element_type=jnp.float32)
            row_term = jnp.sum(probs * dprobs, axis=-1, keepdims=True)
            dscore = jnp.where(allowed, probs * (dprobs - row_term), 0.0).astype(jnp.bfloat16)
            dqs.append(jnp.dot(dscore, kh, preferred_element_type=jnp.float32) * (1.0 / HD**0.5))
            dks.append(
                lax.dot_general(dscore, qh, (((0,), (0,)), ((), ())), preferred_element_type=jnp.float32)
                * (1.0 / HD**0.5)
            )
        dqkv_ref[qs, pl.ds(at, width)] = jnp.concatenate(dqs, axis=1).astype(dqkv_ref.dtype)
        dk_acc[...] += jnp.concatenate(dks, axis=1)
        dv_acc[...] += jnp.concatenate(dvs, axis=1)
        return carry

    lax.fori_loop(0, n // Q_CHUNK, chunk, 0)
    dqkv_ref[:, pl.ds(at + model_width, width)] = dk_acc[...].astype(dqkv_ref.dtype)
    dqkv_ref[:, pl.ds(at + 2 * model_width, width)] = dv_acc[...].astype(dqkv_ref.dtype)


def mask_operands(segment_ids, valid):
    return (segment_ids[:, :, None], segment_ids[:, None, :], valid[:, None, :])


def attention_fwd(qkv, segment_ids, valid):
    rows, width3 = qkv.shape
    model_width = width3 // 3
    n_seq, seq_len = segment_ids.shape
    blk = 2 * HD
    n_hp = model_width // blk
    off = model_width // blk
    seg_spec = [
        pl.BlockSpec((None, seq_len, 1), lambda s, h: (s, 0, 0)),
        pl.BlockSpec((None, 1, seq_len), lambda s, h: (s, 0, 0)),
        pl.BlockSpec((None, 1, seq_len), lambda s, h: (s, 0, 0)),
    ]
    flops = 4 * n_seq * seq_len * seq_len * model_width
    return pl.pallas_call(
        attn_fwd_kernel,
        out_shape=jax.ShapeDtypeStruct((rows, model_width), jnp.bfloat16),
        grid=(n_seq, n_hp),
        in_specs=[
            pl.BlockSpec((seq_len, blk), lambda s, h: (s, h)),
            pl.BlockSpec((seq_len, blk), lambda s, h: (s, off + h)),
            pl.BlockSpec((seq_len, blk), lambda s, h: (s, 2 * off + h)),
        ]
        + seg_spec,
        out_specs=pl.BlockSpec((seq_len, blk), lambda s, h: (s, h)),
        cost_estimate=pl.CostEstimate(
            flops=flops,
            transcendentals=n_seq * seq_len * seq_len * (model_width // HD),
            bytes_accessed=qkv.size * 2 + rows * model_width * 2,
        ),
    )(qkv, qkv, qkv, *mask_operands(segment_ids, valid))


def attention_bwd(qkv, grad_o, segment_ids, valid):
    rows, width3 = qkv.shape
    model_width = width3 // 3
    n_seq, seq_len = segment_ids.shape
    blk = 2 * HD
    n_hp = model_width // blk
    off = model_width // blk
    seg_spec = [
        pl.BlockSpec((None, seq_len, 1), lambda s, h: (s, 0, 0)),
        pl.BlockSpec((None, 1, seq_len), lambda s, h: (s, 0, 0)),
        pl.BlockSpec((None, 1, seq_len), lambda s, h: (s, 0, 0)),
    ]
    flops = 10 * n_seq * seq_len * seq_len * model_width
    return pl.pallas_call(
        attn_bwd_kernel,
        out_shape=jax.ShapeDtypeStruct((rows, width3), jnp.bfloat16),
        grid=(n_seq, n_hp),
        in_specs=[
            pl.BlockSpec((seq_len, blk), lambda s, h: (s, h)),
            pl.BlockSpec((seq_len, blk), lambda s, h: (s, off + h)),
            pl.BlockSpec((seq_len, blk), lambda s, h: (s, 2 * off + h)),
            pl.BlockSpec((seq_len, blk), lambda s, h: (s, h)),
        ]
        + seg_spec,
        out_specs=pl.BlockSpec((seq_len, width3), lambda s, h: (s, 0)),
        scratch_shapes=[pltpu.VMEM((seq_len, blk), jnp.float32), pltpu.VMEM((seq_len, blk), jnp.float32)],
        cost_estimate=pl.CostEstimate(
            flops=flops,
            transcendentals=n_seq * seq_len * seq_len * (model_width // HD),
            bytes_accessed=qkv.size * 4 + rows * model_width * 2,
        ),
    )(qkv, qkv, qkv, grad_o, *mask_operands(segment_ids, valid))


MESH_ID = pl.DeviceIdType.MESH


def ring_maps(n_wide, n_narrow):
    n_dev = n_wide * n_narrow
    if (n_wide, n_narrow) == (8, 4):
        def pos_of(w, n):
            z, y, x, c = w // 2, w % 2, n // 2, n % 2
            q = 2 * x + (x + y) % 2
            k = 4 * q + z + (q % 2) * (3 - 2 * z)
            return 2 * k + c

        def coords_of(p):
            k, c = p // 2, p % 2
            q, r = k // 4, k % 4
            z = r + (q % 2) * (3 - 2 * r)
            x = q // 2
            y = (q % 2 + x) % 2
            return z * 2 + y, x * 2 + c

    else:
        def pos_of(w, n):
            return w * n_narrow + n

        def coords_of(p):
            return p // n_narrow, p % n_narrow

    return n_dev, pos_of, coords_of


def ring_reduce_scatter(parts, mesh_shape, after=(), collective_id=0):
    n_wide, n_narrow = mesh_shape
    n_dev, pos_of, coords_of = ring_maps(n_wide, n_narrow)
    specs = []
    for i, (a, rb, split) in enumerate(parts):
        cols = a.shape[1]
        if split:
            specs.append((i, 0, 0, cols // 2))
        else:
            specs.append((i, 0, 0, cols))
    for i, (a, rb, split) in enumerate(parts):
        if split:
            specs.append((i, 1, a.shape[1] // 2, a.shape[1] // 2))
    n_in = len(parts)
    n_after = len(after)
    n_sp = len(specs)
    last_step = n_dev - 2

    def kernel(*refs):
        ins = refs[:n_in]
        outs = refs[n_in + n_after : 2 * n_in + n_after]
        at = 2 * n_in + n_after
        bufs = refs[at : at + n_sp]
        locs = refs[at + n_sp : at + 2 * n_sp]
        send_sem, recv_sem, loc_sem, credit = refs[at + 2 * n_sp :]
        p = pos_of(lax.axis_index("wide"), lax.axis_index("narrow"))
        right = coords_of((p + 1) % n_dev)
        left = coords_of((p + n_dev - 1) % n_dev)
        nbr_send = (right, left)
        nbr_recv = (left, right)

        def rows_of(q, rb):
            cw, cn = coords_of(q % n_dev)
            start = (cw * n_narrow + cn) * rb
            if rb % 8 == 0:
                start = pl.multiple_of(start, 8)
            return pl.ds(start, rb)

        def remote(j, s):
            return pltpu.make_async_remote_copy(
                src_ref=bufs[j].at[s % 3],
                dst_ref=bufs[j].at[(s + 1) % 3],
                send_sem=send_sem.at[j, s % 3],
                recv_sem=recv_sem.at[j, (s + 1) % 3],
                device_id=nbr_send[specs[j][1]],
                device_id_type=MESH_ID,
            )

        def local(j, s):
            i, dirn, c0, cw = specs[j]
            q = (p + 2 * n_dev - s - 2) if dirn == 0 else (p + s + 2)
            return pltpu.make_async_copy(
                ins[i].at[rows_of(q, parts[i][1]), pl.ds(c0, cw)], locs[j].at[s % 2], loc_sem.at[j, s % 2]
            )

        barrier = pltpu.get_barrier_semaphore()
        for nb in (left, right):
            pl.semaphore_signal(barrier, 1, device_id=nb, device_id_type=MESH_ID)
        pl.semaphore_wait(barrier, 2)

        for j, (i, dirn, c0, cw) in enumerate(specs):
            q = p + n_dev - 1 if dirn == 0 else p + 1
            cp = pltpu.make_async_copy(
                ins[i].at[rows_of(q, parts[i][1]), pl.ds(c0, cw)], bufs[j].at[0], loc_sem.at[j, 1]
            )
            cp.start()
            cp.wait()
        for j in range(n_sp):
            remote(j, 0).start()
            local(j, 0).start()

        def step(s, carry):
            for j in range(n_sp):
                dirn = specs[j][1]
                local(j, s).wait()
                remote(j, s).wait_recv()
                nxt = (s + 1) % 3
                bufs[j][nxt] = bufs[j][nxt] + locs[j][s % 2]
                if j == 0 or specs[j - 1][1] != dirn:

                    @pl.when((s >= 1) & (s + 1 <= last_step))
                    def _():
                        pl.semaphore_wait(credit.at[dirn], 1)

                @pl.when(s + 1 <= last_step)
                def _():
                    remote(j, s + 1).start()
                    local(j, s + 1).start()

            for j in range(n_sp):
                remote(j, s).wait_send()
            for dirn in (0, 1):

                @pl.when(s <= last_step - 2)
                def _():
                    pl.semaphore_signal(
                        credit.at[dirn], 1, device_id=nbr_recv[dirn], device_id_type=MESH_ID
                    )

            return carry

        lax.fori_loop(0, last_step + 1, step, 0)
        fin = (last_step + 1) % 3
        for j, (i, dirn, c0, cw) in enumerate(specs):
            outs[i][:, pl.ds(c0, cw)] = bufs[j][fin]

    out_shape = [jax.ShapeDtypeStruct((rb, a.shape[1]), a.dtype) for (a, rb, _) in parts]
    scratch = [pltpu.VMEM((3, parts[i][1], cw), jnp.float32) for (i, _, _, cw) in specs]
    scratch += [pltpu.VMEM((2, parts[i][1], cw), jnp.float32) for (i, _, _, cw) in specs]
    scratch += [
        pltpu.SemaphoreType.DMA((n_sp, 3)),
        pltpu.SemaphoreType.DMA((n_sp, 3)),
        pltpu.SemaphoreType.DMA((n_sp, 2)),
        pltpu.SemaphoreType.REGULAR((2,)),
    ]
    total = sum(a.size * 4 for (a, _, _) in parts)
    return pl.pallas_call(
        kernel,
        out_shape=out_shape,
        in_specs=[pl.BlockSpec(memory_space=pl.ANY)] * (n_in + n_after),
        out_specs=[pl.BlockSpec(memory_space=pltpu.VMEM)] * n_in,
        scratch_shapes=scratch,
        compiler_params=pltpu.CompilerParams(
            collective_id=collective_id, has_side_effects=True, vmem_limit_bytes=48 * 1024 * 1024
        ),
        cost_estimate=pl.CostEstimate(flops=total // 4, transcendentals=0, bytes_accessed=2 * total),
    )(*[a for (a, _, _) in parts], *after)


def pack_rows(pieces, width):
    flat = jnp.concatenate(pieces)
    return jnp.pad(flat, (0, width - flat.shape[0]))[None, :]


def split_owned(packed, sizes):
    out = []
    at = 0
    for size in sizes:
        out.append(packed[:, at : at + size].reshape(-1))
        at += size
    return out


def on_device(
    inputs,
    w_qkv,
    qv_bias,
    w_out,
    out_bias,
    ln1_gain,
    ln1_shift,
    ln2_gain,
    ln2_shift,
    w_up,
    up_bias,
    w_down,
    down_bias,
    segment_ids,
    valid,
    cotangent,
    mesh_shape=None,
):
    row_count = inputs.shape[0]
    model_width = inputs.shape[1]
    seq_count = segment_ids.shape[0]
    seq_len = segment_ids.shape[1]
    head_count = model_width // HD
    n_dev = mesh_shape[0] * mesh_shape[1]
    small = (qv_bias, out_bias, ln1_gain, ln1_shift, ln2_gain, ln2_shift, up_bias, down_bias)
    small_sizes = [a.shape[0] for a in small]
    n_small = sum(small_sizes)
    rows_q = w_qkv.size // model_width
    rows_o = w_out.shape[0]
    attn_buf = jnp.concatenate(
        [w_qkv.reshape(rows_q, model_width), w_out, pack_rows(small, model_width)], axis=0
    )
    attn_all = lax.all_gather(attn_buf, ALL, axis=0, tiled=False)
    qkv_full = attn_all[:, :rows_q].reshape(-1, w_qkv.shape[1])
    out_full = attn_all[:, rows_q : rows_q + rows_o].reshape(-1, model_width)
    small_full = split_owned(attn_all[:, rows_q + rows_o, :n_small], small_sizes)
    qv_full, outb_full, gain_one, shift_one, gain_two, shift_two, upb_full, downb_full = small_full
    rows_u = w_up.size // model_width
    mlp_buf = jnp.concatenate([w_up.reshape(rows_u, model_width), w_down], axis=0)
    mlp_all = lax.all_gather(mlp_buf, ALL, axis=0, tiled=False)
    up_full = mlp_all[:, :rows_u].reshape(-1, w_up.shape[1])
    down_full = mlp_all[:, rows_u:].reshape(-1, model_width)

    gain_one = gain_one.astype(jnp.float32)
    shift_one = shift_one.astype(jnp.float32)
    qv_full = qv_full.astype(jnp.float32)
    rows = inputs.astype(jnp.float32)
    normed_one, recip_one = norm_parts(rows)
    h_one = (normed_one * gain_one + shift_one).astype(jnp.bfloat16)
    qkv_rows = jnp.dot(h_one, qkv_full, preferred_element_type=jnp.float32)
    zero_bias = jnp.zeros((model_width,), jnp.float32)
    qkv_bias = jnp.concatenate([qv_full[:model_width], zero_bias, qv_full[model_width:]])
    qkv_b = (qkv_rows + qkv_bias).astype(jnp.bfloat16)
    attended = attention_fwd(qkv_b, segment_ids, valid)
    mid_rows = (
        rows
        + jnp.dot(attended, out_full, preferred_element_type=jnp.float32)
        + outb_full.astype(jnp.float32)
    )
    gain_two = gain_two.astype(jnp.float32)
    shift_two = shift_two.astype(jnp.float32)
    normed_two, recip_two = norm_parts(mid_rows)
    h_two = (normed_two * gain_two + shift_two).astype(jnp.bfloat16)
    upper = jnp.dot(h_two, up_full, preferred_element_type=jnp.float32) + upb_full.astype(
        jnp.float32
    )
    gelu_rows = jax.nn.gelu(upper, approximate=False).astype(jnp.bfloat16)
    out_rows = (
        mid_rows
        + jnp.dot(gelu_rows, down_full, preferred_element_type=jnp.float32)
        + downb_full.astype(jnp.float32)
    )
    block_out = out_rows.astype(jnp.bfloat16)
    dy_rows = cotangent.astype(jnp.float32)
    grad_wdown = jnp.einsum("tf,td->fd", gelu_rows, cotangent, preferred_element_type=jnp.float32)
    grad_bdown = col_sum(cotangent)
    grad_g = jnp.einsum("td,fd->tf", cotangent, down_full, preferred_element_type=jnp.float32)
    cdf_part = 0.5 * (1.0 + jax.scipy.special.erf(upper * 0.7071067811865476))
    pdf_part = jnp.exp(-0.5 * upper * upper) * 0.3989422804014327
    grad_u = (grad_g * (cdf_part + upper * pdf_part)).astype(jnp.bfloat16)
    grad_bup = col_sum(grad_u)
    grad_wup = jnp.einsum("td,tf->df", h_two, grad_u, preferred_element_type=jnp.float32)
    grad_h2 = jnp.einsum("tf,df->td", grad_u, up_full, preferred_element_type=jnp.float32)
    grad_g2 = jnp.sum(grad_h2 * normed_two, axis=0)
    grad_c2 = jnp.sum(grad_h2, axis=0)
    grad_mid = dy_rows + norm_back(grad_h2, gain_two, normed_two, recip_two)
    grad_a = grad_mid.astype(jnp.bfloat16)
    grad_wout = jnp.einsum("tc,td->cd", attended, grad_a, preferred_element_type=jnp.float32)
    grad_bout = col_sum(grad_a)
    grad_o = jnp.einsum("td,cd->tc", grad_a, out_full, preferred_element_type=jnp.float32).astype(
        jnp.bfloat16
    )
    grad_qkv = attention_bwd(qkv_b, grad_o, segment_ids, valid)
    grad_cols = col_sum(grad_qkv)
    grad_bqv = jnp.concatenate([grad_cols[:model_width], grad_cols[2 * model_width :]])
    grad_wqkv = jnp.einsum("td,te->de", h_one, grad_qkv, preferred_element_type=jnp.float32)
    grad_h1 = jnp.einsum("te,de->td", grad_qkv, qkv_full, preferred_element_type=jnp.float32)
    grad_g1 = jnp.sum(grad_h1 * normed_one, axis=0)
    grad_c1 = jnp.sum(grad_h1, axis=0)
    grad_inputs = grad_mid + norm_back(grad_h1, gain_one, normed_one, recip_one)

    small_grads = (grad_bqv, grad_bout, grad_g1, grad_c1, grad_g2, grad_c2, grad_bup, grad_bdown)
    owned = jnp.concatenate([g.reshape(n_dev, -1) for g in small_grads], axis=1)
    lanes = 128
    small_rows = 8 * pl.cdiv(pl.cdiv(n_small, lanes), 8)
    owned = jnp.pad(owned, ((0, 0), (0, small_rows * lanes - n_small))).reshape(-1, lanes)
    parts = [
        (grad_wqkv, w_qkv.shape[0], True),
        (grad_wout, w_out.shape[0], True),
        (grad_wup, w_up.shape[0], True),
        (owned, small_rows, False),
    ]
    down_sum = lax.psum_scatter(grad_wdown, ALL, scatter_dimension=0, tiled=True)
    if all(rb % 8 == 0 and a.shape[1] % 256 == 0 for (a, rb, _) in parts[:3]):
        sums = ring_reduce_scatter(parts, mesh_shape, after=(grad_inputs, block_out))
    else:
        sums = [lax.psum_scatter(a, ALL, scatter_dimension=0, tiled=True) for (a, _, _) in parts]
    sums = list(sums[:3]) + [down_sum] + list(sums[3:])
    small_sums = split_owned(sums[4].reshape(1, -1), small_sizes)
    bqv, bout, g1, c1, g2, c2, bup, bdown = small_sums
    return (
        block_out,
        grad_inputs,
        sums[0],
        bqv,
        sums[1],
        bout,
        g1,
        c1,
        g2,
        c2,
        sums[2],
        bup,
        sums[3],
        bdown,
    )


def solution(mesh):
    in_specs = (
        P(("wide", "narrow"), None),
        P(("wide", "narrow"), None),
        P(("wide", "narrow")),
        P(("wide", "narrow"), None),
        P(("wide", "narrow")),
        P(("wide", "narrow")),
        P(("wide", "narrow")),
        P(("wide", "narrow")),
        P(("wide", "narrow")),
        P(("wide", "narrow"), None),
        P(("wide", "narrow")),
        P(("wide", "narrow"), None),
        P(("wide", "narrow")),
        P(("wide", "narrow"), None),
        P(("wide", "narrow"), None),
        P(("wide", "narrow"), None),
    )
    out_specs = (
        P(("wide", "narrow"), None),
        P(("wide", "narrow"), None),
        P(("wide", "narrow"), None),
        P(("wide", "narrow")),
        P(("wide", "narrow"), None),
        P(("wide", "narrow")),
        P(("wide", "narrow")),
        P(("wide", "narrow")),
        P(("wide", "narrow")),
        P(("wide", "narrow")),
        P(("wide", "narrow"), None),
        P(("wide", "narrow")),
        P(("wide", "narrow"), None),
        P(("wide", "narrow")),
    )
    body = functools.partial(on_device, mesh_shape=(mesh.shape["wide"], mesh.shape["narrow"]))
    return jax.shard_map(
        body, mesh=mesh, in_specs=in_specs, out_specs=out_specs, check_vma=False
    )
```

```python
import functools
import jax
import jax.numpy as jnp
from jax import lax
from jax.experimental import pallas as pl
from jax.experimental.pallas import tpu as pltpu
from jax.sharding import PartitionSpec as P

HD = 64
ALL = ("wide", "narrow")

EPSILON = 1e-06


def norm_parts(rows):
    center = rows - jnp.mean(rows, axis=-1, keepdims=True)
    recip = lax.rsqrt(jnp.mean(center * center, axis=-1, keepdims=True) + EPSILON)
    return (center * recip, recip)


def norm_back(grad_h, gain, normed, recip):
    scaled = grad_h * gain
    return recip * (
        scaled
        - jnp.mean(scaled, axis=-1, keepdims=True)
        - normed * jnp.mean(scaled * normed, axis=-1, keepdims=True)
    )


def col_sum(rows):
    return jnp.sum(rows.astype(jnp.float32), axis=0)


def seg_mask(seg_col, seg_row, val_row, n):
    rows = lax.broadcasted_iota(jnp.int32, (n, n), 0)
    cols = lax.broadcasted_iota(jnp.int32, (n, n), 1)
    return (seg_col == seg_row) & ((val_row == 1) | (rows == cols))


def soft_rows(qh, kh, allowed):
    scores = lax.dot_general(qh, kh, (((1,), (1,)), ((), ())), preferred_element_type=jnp.float32)
    scores = jnp.where(allowed, scores * (1.0 / HD**0.5), -1e30)
    top = jnp.max(scores, axis=-1, keepdims=True)
    expo = jnp.exp(scores - top)
    return expo * (1.0 / jnp.sum(expo, axis=-1, keepdims=True))


def attn_fwd_kernel(q_ref, k_ref, v_ref, sc_ref, sr_ref, vr_ref, o_ref):
    n = q_ref.shape[0]
    allowed = seg_mask(sc_ref[...], sr_ref[...], vr_ref[...], n)
    outs = []
    for j in range(q_ref.shape[1] // HD):
        cols = slice(j * HD, (j + 1) * HD)
        probs = soft_rows(q_ref[:, cols], k_ref[:, cols], allowed).astype(jnp.bfloat16)
        outs.append(jnp.dot(probs, v_ref[:, cols], preferred_element_type=jnp.float32))
    o_ref[...] = jnp.concatenate(outs, axis=1).astype(o_ref.dtype)


def attn_bwd_kernel(q_ref, k_ref, v_ref, do_ref, sc_ref, sr_ref, vr_ref, dqkv_ref):
    n = q_ref.shape[0]
    width = q_ref.shape[1]
    hp = pl.program_id(1)
    model_width = dqkv_ref.shape[1] // 3
    allowed = seg_mask(sc_ref[...], sr_ref[...], vr_ref[...], n)
    dqs, dks, dvs = [], [], []
    for j in range(width // HD):
        cols = slice(j * HD, (j + 1) * HD)
        qh, kh, vh, doh = q_ref[:, cols], k_ref[:, cols], v_ref[:, cols], do_ref[:, cols]
        probs = soft_rows(qh, kh, allowed)
        dvs.append(
            lax.dot_general(probs.astype(jnp.bfloat16), doh, (((0,), (0,)), ((), ())),
                            preferred_element_type=jnp.float32)
        )
        dprobs = lax.dot_general(doh, vh, (((1,), (1,)), ((), ())), preferred_element_type=jnp.float32)
        row_term = jnp.sum(probs * dprobs, axis=-1, keepdims=True)
        dscore = jnp.where(allowed, probs * (dprobs - row_term), 0.0).astype(jnp.bfloat16)
        dqs.append(jnp.dot(dscore, kh, preferred_element_type=jnp.float32) * (1.0 / HD**0.5))
        dks.append(
            lax.dot_general(dscore, qh, (((0,), (0,)), ((), ())), preferred_element_type=jnp.float32)
            * (1.0 / HD**0.5)
        )
    at = pl.multiple_of(hp * width, width)
    dqkv_ref[:, pl.ds(at, width)] = jnp.concatenate(dqs, axis=1).astype(dqkv_ref.dtype)
    dqkv_ref[:, pl.ds(at + model_width, width)] = jnp.concatenate(dks, axis=1).astype(dqkv_ref.dtype)
    dqkv_ref[:, pl.ds(at + 2 * model_width, width)] = jnp.concatenate(dvs, axis=1).astype(dqkv_ref.dtype)


def mask_operands(segment_ids, valid):
    return (segment_ids[:, :, None], segment_ids[:, None, :], valid[:, None, :])


def attention_fwd(qkv, segment_ids, valid):
    rows, width3 = qkv.shape
    model_width = width3 // 3
    n_seq, seq_len = segment_ids.shape
    blk = 2 * HD
    n_hp = model_width // blk
    off = model_width // blk
    seg_spec = [
        pl.BlockSpec((None, seq_len, 1), lambda s, h: (s, 0, 0)),
        pl.BlockSpec((None, 1, seq_len), lambda s, h: (s, 0, 0)),
        pl.BlockSpec((None, 1, seq_len), lambda s, h: (s, 0, 0)),
    ]
    flops = 4 * n_seq * seq_len * seq_len * model_width
    return pl.pallas_call(
        attn_fwd_kernel,
        out_shape=jax.ShapeDtypeStruct((rows, model_width), jnp.bfloat16),
        grid=(n_seq, n_hp),
        in_specs=[
            pl.BlockSpec((seq_len, blk), lambda s, h: (s, h)),
            pl.BlockSpec((seq_len, blk), lambda s, h: (s, off + h)),
            pl.BlockSpec((seq_len, blk), lambda s, h: (s, 2 * off + h)),
        ]
        + seg_spec,
        out_specs=pl.BlockSpec((seq_len, blk), lambda s, h: (s, h)),
        cost_estimate=pl.CostEstimate(
            flops=flops,
            transcendentals=n_seq * seq_len * seq_len * (model_width // HD),
            bytes_accessed=qkv.size * 2 + rows * model_width * 2,
        ),
    )(qkv, qkv, qkv, *mask_operands(segment_ids, valid))


def attention_bwd(qkv, grad_o, segment_ids, valid):
    rows, width3 = qkv.shape
    model_width = width3 // 3
    n_seq, seq_len = segment_ids.shape
    blk = 2 * HD
    n_hp = model_width // blk
    off = model_width // blk
    seg_spec = [
        pl.BlockSpec((None, seq_len, 1), lambda s, h: (s, 0, 0)),
        pl.BlockSpec((None, 1, seq_len), lambda s, h: (s, 0, 0)),
        pl.BlockSpec((None, 1, seq_len), lambda s, h: (s, 0, 0)),
    ]
    flops = 10 * n_seq * seq_len * seq_len * model_width
    return pl.pallas_call(
        attn_bwd_kernel,
        out_shape=jax.ShapeDtypeStruct((rows, width3), jnp.bfloat16),
        grid=(n_seq, n_hp),
        in_specs=[
            pl.BlockSpec((seq_len, blk), lambda s, h: (s, h)),
            pl.BlockSpec((seq_len, blk), lambda s, h: (s, off + h)),
            pl.BlockSpec((seq_len, blk), lambda s, h: (s, 2 * off + h)),
            pl.BlockSpec((seq_len, blk), lambda s, h: (s, h)),
        ]
        + seg_spec,
        out_specs=pl.BlockSpec((seq_len, width3), lambda s, h: (s, 0)),
        cost_estimate=pl.CostEstimate(
            flops=flops,
            transcendentals=n_seq * seq_len * seq_len * (model_width // HD),
            bytes_accessed=qkv.size * 4 + rows * model_width * 2,
        ),
    )(qkv, qkv, qkv, grad_o, *mask_operands(segment_ids, valid))


MESH_ID = pl.DeviceIdType.MESH


def ring_maps(n_wide, n_narrow):
    n_dev = n_wide * n_narrow
    if (n_wide, n_narrow) == (8, 4):
        def pos_of(w, n):
            z, y, x, c = w // 2, w % 2, n // 2, n % 2
            q = 2 * x + (x + y) % 2
            k = 4 * q + z + (q % 2) * (3 - 2 * z)
            return 2 * k + c

        def coords_of(p):
            k, c = p // 2, p % 2
            q, r = k // 4, k % 4
            z = r + (q % 2) * (3 - 2 * r)
            x = q // 2
            y = (q % 2 + x) % 2
            return z * 2 + y, x * 2 + c

    else:
        def pos_of(w, n):
            return w * n_narrow + n

        def coords_of(p):
            return p // n_narrow, p % n_narrow

    return n_dev, pos_of, coords_of


def ring_reduce_scatter(parts, mesh_shape, after=(), collective_id=0):
    n_wide, n_narrow = mesh_shape
    n_dev, pos_of, coords_of = ring_maps(n_wide, n_narrow)
    specs = []
    for i, (a, rb, split) in enumerate(parts):
        cols = a.shape[1]
        if split:
            specs.append((i, 0, 0, cols // 2))
        else:
            specs.append((i, 0, 0, cols))
    for i, (a, rb, split) in enumerate(parts):
        if split:
            specs.append((i, 1, a.shape[1] // 2, a.shape[1] // 2))
    n_in = len(parts)
    n_after = len(after)
    n_sp = len(specs)
    last_step = n_dev - 2

    def kernel(*refs):
        ins = refs[:n_in]
        outs = refs[n_in + n_after : 2 * n_in + n_after]
        at = 2 * n_in + n_after
        bufs = refs[at : at + n_sp]
        locs = refs[at + n_sp : at + 2 * n_sp]
        send_sem, recv_sem, loc_sem, credit = refs[at + 2 * n_sp :]
        p = pos_of(lax.axis_index("wide"), lax.axis_index("narrow"))
        right = coords_of((p + 1) % n_dev)
        left = coords_of((p + n_dev - 1) % n_dev)
        nbr_send = (right, left)
        nbr_recv = (left, right)

        def rows_of(q, rb):
            cw, cn = coords_of(q % n_dev)
            start = (cw * n_narrow + cn) * rb
            if rb % 8 == 0:
                start = pl.multiple_of(start, 8)
            return pl.ds(start, rb)

        def remote(j, s):
            return pltpu.make_async_remote_copy(
                src_ref=bufs[j].at[s % 3],
                dst_ref=bufs[j].at[(s + 1) % 3],
                send_sem=send_sem.at[j, s % 3],
                recv_sem=recv_sem.at[j, (s + 1) % 3],
                device_id=nbr_send[specs[j][1]],
                device_id_type=MESH_ID,
            )

        def local(j, s):
            i, dirn, c0, cw = specs[j]
            q = (p + 2 * n_dev - s - 2) if dirn == 0 else (p + s + 2)
            return pltpu.make_async_copy(
                ins[i].at[rows_of(q, parts[i][1]), pl.ds(c0, cw)], locs[j].at[s % 2], loc_sem.at[j, s % 2]
            )

        barrier = pltpu.get_barrier_semaphore()
        for nb in (left, right):
            pl.semaphore_signal(barrier, 1, device_id=nb, device_id_type=MESH_ID)
        pl.semaphore_wait(barrier, 2)

        for j, (i, dirn, c0, cw) in enumerate(specs):
            q = p + n_dev - 1 if dirn == 0 else p + 1
            cp = pltpu.make_async_copy(
                ins[i].at[rows_of(q, parts[i][1]), pl.ds(c0, cw)], bufs[j].at[0], loc_sem.at[j, 1]
            )
            cp.start()
            cp.wait()
        for j in range(n_sp):
            remote(j, 0).start()
            local(j, 0).start()

        def step(s, carry):
            for j in range(n_sp):
                dirn = specs[j][1]
                local(j, s).wait()
                remote(j, s).wait_recv()
                nxt = (s + 1) % 3
                bufs[j][nxt] = bufs[j][nxt] + locs[j][s % 2]
                if j == 0 or specs[j - 1][1] != dirn:

                    @pl.when((s >= 1) & (s + 1 <= last_step))
                    def _():
                        pl.semaphore_wait(credit.at[dirn], 1)

                @pl.when(s + 1 <= last_step)
                def _():
                    remote(j, s + 1).start()
                    local(j, s + 1).start()

            for j in range(n_sp):
                remote(j, s).wait_send()
            for dirn in (0, 1):

                @pl.when(s <= last_step - 2)
                def _():
                    pl.semaphore_signal(
                        credit.at[dirn], 1, device_id=nbr_recv[dirn], device_id_type=MESH_ID
                    )

            return carry

        lax.fori_loop(0, last_step + 1, step, 0)
        fin = (last_step + 1) % 3
        for j, (i, dirn, c0, cw) in enumerate(specs):
            outs[i][:, pl.ds(c0, cw)] = bufs[j][fin]

    out_shape = [jax.ShapeDtypeStruct((rb, a.shape[1]), a.dtype) for (a, rb, _) in parts]
    scratch = [pltpu.VMEM((3, parts[i][1], cw), jnp.float32) for (i, _, _, cw) in specs]
    scratch += [pltpu.VMEM((2, parts[i][1], cw), jnp.float32) for (i, _, _, cw) in specs]
    scratch += [
        pltpu.SemaphoreType.DMA((n_sp, 3)),
        pltpu.SemaphoreType.DMA((n_sp, 3)),
        pltpu.SemaphoreType.DMA((n_sp, 2)),
        pltpu.SemaphoreType.REGULAR((2,)),
    ]
    total = sum(a.size * 4 for (a, _, _) in parts)
    return pl.pallas_call(
        kernel,
        out_shape=out_shape,
        in_specs=[pl.BlockSpec(memory_space=pl.ANY)] * (n_in + n_after),
        out_specs=[pl.BlockSpec(memory_space=pltpu.VMEM)] * n_in,
        scratch_shapes=scratch,
        compiler_params=pltpu.CompilerParams(
            collective_id=collective_id, has_side_effects=True, vmem_limit_bytes=48 * 1024 * 1024
        ),
        cost_estimate=pl.CostEstimate(flops=total // 4, transcendentals=0, bytes_accessed=2 * total),
    )(*[a for (a, _, _) in parts], *after)


def pack_rows(pieces, width):
    flat = jnp.concatenate(pieces)
    return jnp.pad(flat, (0, width - flat.shape[0]))[None, :]


def split_owned(packed, sizes):
    out = []
    at = 0
    for size in sizes:
        out.append(packed[:, at : at + size].reshape(-1))
        at += size
    return out


def on_device(
    inputs,
    w_qkv,
    qv_bias,
    w_out,
    out_bias,
    ln1_gain,
    ln1_shift,
    ln2_gain,
    ln2_shift,
    w_up,
    up_bias,
    w_down,
    down_bias,
    segment_ids,
    valid,
    cotangent,
    mesh_shape=None,
):
    row_count = inputs.shape[0]
    model_width = inputs.shape[1]
    seq_count = segment_ids.shape[0]
    seq_len = segment_ids.shape[1]
    head_count = model_width // HD
    n_dev = mesh_shape[0] * mesh_shape[1]
    small = (qv_bias, out_bias, ln1_gain, ln1_shift, ln2_gain, ln2_shift, up_bias, down_bias)
    small_sizes = [a.shape[0] for a in small]
    n_small = sum(small_sizes)
    rows_q = w_qkv.size // model_width
    rows_o = w_out.shape[0]
    rows_u = w_up.size // model_width
    attn_buf = jnp.concatenate(
        [
            w_qkv.reshape(rows_q, model_width),
            w_out,
            w_up.reshape(rows_u, model_width),
            pack_rows(small, model_width),
        ],
        axis=0,
    )
    attn_all = lax.all_gather(attn_buf, ALL, axis=0, tiled=False)
    qkv_full = attn_all[:, :rows_q].reshape(-1, w_qkv.shape[1])
    out_full = attn_all[:, rows_q : rows_q + rows_o].reshape(-1, model_width)
    up_full = attn_all[:, rows_q + rows_o : rows_q + rows_o + rows_u].reshape(-1, w_up.shape[1])
    small_full = split_owned(attn_all[:, rows_q + rows_o + rows_u, :n_small], small_sizes)
    qv_full, outb_full, gain_one, shift_one, gain_two, shift_two, upb_full, downb_full = small_full
    down_full = lax.all_gather(w_down, ALL, axis=0, tiled=True)

    gain_one = gain_one.astype(jnp.float32)
    shift_one = shift_one.astype(jnp.float32)
    qv_full = qv_full.astype(jnp.float32)
    rows = inputs.astype(jnp.float32)
    normed_one, recip_one = norm_parts(rows)
    h_one = (normed_one * gain_one + shift_one).astype(jnp.bfloat16)
    qkv_rows = jnp.dot(h_one, qkv_full, preferred_element_type=jnp.float32)
    zero_bias = jnp.zeros((model_width,), jnp.float32)
    qkv_bias = jnp.concatenate([qv_full[:model_width], zero_bias, qv_full[model_width:]])
    qkv_b = (qkv_rows + qkv_bias).astype(jnp.bfloat16)
    attended = attention_fwd(qkv_b, segment_ids, valid)
    mid_rows = (
        rows
        + jnp.dot(attended, out_full, preferred_element_type=jnp.float32)
        + outb_full.astype(jnp.float32)
    )
    gain_two = gain_two.astype(jnp.float32)
    shift_two = shift_two.astype(jnp.float32)
    normed_two, recip_two = norm_parts(mid_rows)
    h_two = (normed_two * gain_two + shift_two).astype(jnp.bfloat16)
    upper = jnp.dot(h_two, up_full, preferred_element_type=jnp.float32) + upb_full.astype(
        jnp.float32
    )
    gelu_rows = jax.nn.gelu(upper, approximate=False).astype(jnp.bfloat16)
    out_rows = (
        mid_rows
        + jnp.dot(gelu_rows, down_full, preferred_element_type=jnp.float32)
        + downb_full.astype(jnp.float32)
    )
    block_out = out_rows.astype(jnp.bfloat16)
    dy_rows = cotangent.astype(jnp.float32)
    grad_wdown = jnp.einsum("tf,td->fd", gelu_rows, cotangent, preferred_element_type=jnp.float32)
    grad_bdown = col_sum(cotangent)
    grad_g = jnp.einsum("td,fd->tf", cotangent, down_full, preferred_element_type=jnp.float32)
    cdf_part = 0.5 * (1.0 + jax.scipy.special.erf(upper * 0.7071067811865476))
    pdf_part = jnp.exp(-0.5 * upper * upper) * 0.3989422804014327
    grad_u = (grad_g * (cdf_part + upper * pdf_part)).astype(jnp.bfloat16)
    grad_bup = col_sum(grad_u)
    grad_wup = jnp.einsum("td,tf->df", h_two, grad_u, preferred_element_type=jnp.float32)
    grad_h2 = jnp.einsum("tf,df->td", grad_u, up_full, preferred_element_type=jnp.float32)
    grad_g2 = jnp.sum(grad_h2 * normed_two, axis=0)
    grad_c2 = jnp.sum(grad_h2, axis=0)
    grad_mid = dy_rows + norm_back(grad_h2, gain_two, normed_two, recip_two)
    grad_a = grad_mid.astype(jnp.bfloat16)
    grad_wout = jnp.einsum("tc,td->cd", attended, grad_a, preferred_element_type=jnp.float32)
    grad_bout = col_sum(grad_a)
    grad_o = jnp.einsum("td,cd->tc", grad_a, out_full, preferred_element_type=jnp.float32).astype(
        jnp.bfloat16
    )
    grad_qkv = attention_bwd(qkv_b, grad_o, segment_ids, valid)
    grad_cols = col_sum(grad_qkv)
    grad_bqv = jnp.concatenate([grad_cols[:model_width], grad_cols[2 * model_width :]])
    grad_wqkv = jnp.einsum("td,te->de", h_one, grad_qkv, preferred_element_type=jnp.float32)
    grad_h1 = jnp.einsum("te,de->td", grad_qkv, qkv_full, preferred_element_type=jnp.float32)
    grad_g1 = jnp.sum(grad_h1 * normed_one, axis=0)
    grad_c1 = jnp.sum(grad_h1, axis=0)
    grad_inputs = grad_mid + norm_back(grad_h1, gain_one, normed_one, recip_one)

    small_grads = (grad_bqv, grad_bout, grad_g1, grad_c1, grad_g2, grad_c2, grad_bup, grad_bdown)
    owned = jnp.concatenate([g.reshape(n_dev, -1) for g in small_grads], axis=1)
    lanes = 128
    small_rows = 8 * pl.cdiv(pl.cdiv(n_small, lanes), 8)
    owned = jnp.pad(owned, ((0, 0), (0, small_rows * lanes - n_small))).reshape(-1, lanes)
    parts = [
        (grad_wqkv, w_qkv.shape[0], True),
        (grad_wout, w_out.shape[0], True),
        (grad_wup, w_up.shape[0], True),
        (owned, small_rows, False),
    ]
    down_sum = lax.psum_scatter(grad_wdown, ALL, scatter_dimension=0, tiled=True)
    if all(rb % 8 == 0 and a.shape[1] % 256 == 0 for (a, rb, _) in parts[:3]):
        sums = ring_reduce_scatter(parts, mesh_shape, after=(grad_inputs, block_out))
    else:
        sums = [lax.psum_scatter(a, ALL, scatter_dimension=0, tiled=True) for (a, _, _) in parts]
    sums = list(sums[:3]) + [down_sum] + list(sums[3:])
    small_sums = split_owned(sums[4].reshape(1, -1), small_sizes)
    bqv, bout, g1, c1, g2, c2, bup, bdown = small_sums
    return (
        block_out,
        grad_inputs,
        sums[0],
        bqv,
        sums[1],
        bout,
        g1,
        c1,
        g2,
        c2,
        sums[2],
        bup,
        sums[3],
        bdown,
    )


def solution(mesh):
    in_specs = (
        P(("wide", "narrow"), None),
        P(("wide", "narrow"), None),
        P(("wide", "narrow")),
        P(("wide", "narrow"), None),
        P(("wide", "narrow")),
        P(("wide", "narrow")),
        P(("wide", "narrow")),
        P(("wide", "narrow")),
        P(("wide", "narrow")),
        P(("wide", "narrow"), None),
        P(("wide", "narrow")),
        P(("wide", "narrow"), None),
        P(("wide", "narrow")),
        P(("wide", "narrow"), None),
        P(("wide", "narrow"), None),
        P(("wide", "narrow"), None),
    )
    out_specs = (
        P(("wide", "narrow"), None),
        P(("wide", "narrow"), None),
        P(("wide", "narrow"), None),
        P(("wide", "narrow")),
        P(("wide", "narrow"), None),
        P(("wide", "narrow")),
        P(("wide", "narrow")),
        P(("wide", "narrow")),
        P(("wide", "narrow")),
        P(("wide", "narrow")),
        P(("wide", "narrow"), None),
        P(("wide", "narrow")),
        P(("wide", "narrow"), None),
        P(("wide", "narrow")),
    )
    body = functools.partial(on_device, mesh_shape=(mesh.shape["wide"], mesh.shape["narrow"]))
    return jax.shard_map(
        body, mesh=mesh, in_specs=in_specs, out_specs=out_specs, check_vma=False
    )
```

```python
import functools
import jax
import jax.numpy as jnp
from jax import lax
from jax.experimental import pallas as pl
from jax.experimental.pallas import tpu as pltpu
from jax.sharding import PartitionSpec as P

HD = 64
ALL = ("wide", "narrow")

EPSILON = 1e-06


def norm_parts(rows):
    center = rows - jnp.mean(rows, axis=-1, keepdims=True)
    recip = lax.rsqrt(jnp.mean(center * center, axis=-1, keepdims=True) + EPSILON)
    return (center * recip, recip)


def norm_back(grad_h, gain, normed, recip):
    scaled = grad_h * gain
    return recip * (
        scaled
        - jnp.mean(scaled, axis=-1, keepdims=True)
        - normed * jnp.mean(scaled * normed, axis=-1, keepdims=True)
    )


def col_sum(rows):
    return jnp.sum(rows.astype(jnp.float32), axis=0)


def seg_mask(seg_col, seg_row, val_row, n):
    rows = lax.broadcasted_iota(jnp.int32, (n, n), 0)
    cols = lax.broadcasted_iota(jnp.int32, (n, n), 1)
    return (seg_col == seg_row) & ((val_row == 1) | (rows == cols))


def soft_rows(qh, kh, allowed):
    scores = lax.dot_general(qh, kh, (((1,), (1,)), ((), ())), preferred_element_type=jnp.float32)
    scores = jnp.where(allowed, scores * (1.0 / HD**0.5), -1e30)
    top = jnp.max(scores, axis=-1, keepdims=True)
    expo = jnp.exp(scores - top)
    return expo * (1.0 / jnp.sum(expo, axis=-1, keepdims=True))


def attn_fwd_kernel(q_ref, k_ref, v_ref, sc_ref, sr_ref, vr_ref, o_ref):
    n = q_ref.shape[0]
    allowed = seg_mask(sc_ref[...], sr_ref[...], vr_ref[...], n)
    outs = []
    for j in range(q_ref.shape[1] // HD):
        cols = slice(j * HD, (j + 1) * HD)
        probs = soft_rows(q_ref[:, cols], k_ref[:, cols], allowed).astype(jnp.bfloat16)
        outs.append(jnp.dot(probs, v_ref[:, cols], preferred_element_type=jnp.float32))
    o_ref[...] = jnp.concatenate(outs, axis=1).astype(o_ref.dtype)


def attn_bwd_kernel(q_ref, k_ref, v_ref, do_ref, sc_ref, sr_ref, vr_ref, dqkv_ref):
    n = q_ref.shape[0]
    width = q_ref.shape[1]
    hp = pl.program_id(1)
    model_width = dqkv_ref.shape[1] // 3
    allowed = seg_mask(sc_ref[...], sr_ref[...], vr_ref[...], n)
    dqs, dks, dvs = [], [], []
    for j in range(width // HD):
        cols = slice(j * HD, (j + 1) * HD)
        qh, kh, vh, doh = q_ref[:, cols], k_ref[:, cols], v_ref[:, cols], do_ref[:, cols]
        probs = soft_rows(qh, kh, allowed)
        dvs.append(
            lax.dot_general(probs.astype(jnp.bfloat16), doh, (((0,), (0,)), ((), ())),
                            preferred_element_type=jnp.float32)
        )
        dprobs = lax.dot_general(doh, vh, (((1,), (1,)), ((), ())), preferred_element_type=jnp.float32)
        row_term = jnp.sum(probs * dprobs, axis=-1, keepdims=True)
        dscore = jnp.where(allowed, probs * (dprobs - row_term), 0.0).astype(jnp.bfloat16)
        dqs.append(jnp.dot(dscore, kh, preferred_element_type=jnp.float32) * (1.0 / HD**0.5))
        dks.append(
            lax.dot_general(dscore, qh, (((0,), (0,)), ((), ())), preferred_element_type=jnp.float32)
            * (1.0 / HD**0.5)
        )
    at = pl.multiple_of(hp * width, width)
    dqkv_ref[:, pl.ds(at, width)] = jnp.concatenate(dqs, axis=1).astype(dqkv_ref.dtype)
    dqkv_ref[:, pl.ds(at + model_width, width)] = jnp.concatenate(dks, axis=1).astype(dqkv_ref.dtype)
    dqkv_ref[:, pl.ds(at + 2 * model_width, width)] = jnp.concatenate(dvs, axis=1).astype(dqkv_ref.dtype)


def mask_operands(segment_ids, valid):
    return (segment_ids[:, :, None], segment_ids[:, None, :], valid[:, None, :])


def attention_fwd(qkv, segment_ids, valid):
    rows, width3 = qkv.shape
    model_width = width3 // 3
    n_seq, seq_len = segment_ids.shape
    blk = 2 * HD
    n_hp = model_width // blk
    off = model_width // blk
    seg_spec = [
        pl.BlockSpec((None, seq_len, 1), lambda s, h: (s, 0, 0)),
        pl.BlockSpec((None, 1, seq_len), lambda s, h: (s, 0, 0)),
        pl.BlockSpec((None, 1, seq_len), lambda s, h: (s, 0, 0)),
    ]
    flops = 4 * n_seq * seq_len * seq_len * model_width
    return pl.pallas_call(
        attn_fwd_kernel,
        out_shape=jax.ShapeDtypeStruct((rows, model_width), jnp.bfloat16),
        grid=(n_seq, n_hp),
        in_specs=[
            pl.BlockSpec((seq_len, blk), lambda s, h: (s, h)),
            pl.BlockSpec((seq_len, blk), lambda s, h: (s, off + h)),
            pl.BlockSpec((seq_len, blk), lambda s, h: (s, 2 * off + h)),
        ]
        + seg_spec,
        out_specs=pl.BlockSpec((seq_len, blk), lambda s, h: (s, h)),
        cost_estimate=pl.CostEstimate(
            flops=flops,
            transcendentals=n_seq * seq_len * seq_len * (model_width // HD),
            bytes_accessed=qkv.size * 2 + rows * model_width * 2,
        ),
    )(qkv, qkv, qkv, *mask_operands(segment_ids, valid))


def attention_bwd(qkv, grad_o, segment_ids, valid):
    rows, width3 = qkv.shape
    model_width = width3 // 3
    n_seq, seq_len = segment_ids.shape
    blk = 2 * HD
    n_hp = model_width // blk
    off = model_width // blk
    seg_spec = [
        pl.BlockSpec((None, seq_len, 1), lambda s, h: (s, 0, 0)),
        pl.BlockSpec((None, 1, seq_len), lambda s, h: (s, 0, 0)),
        pl.BlockSpec((None, 1, seq_len), lambda s, h: (s, 0, 0)),
    ]
    flops = 10 * n_seq * seq_len * seq_len * model_width
    return pl.pallas_call(
        attn_bwd_kernel,
        out_shape=jax.ShapeDtypeStruct((rows, width3), jnp.bfloat16),
        grid=(n_seq, n_hp),
        in_specs=[
            pl.BlockSpec((seq_len, blk), lambda s, h: (s, h)),
            pl.BlockSpec((seq_len, blk), lambda s, h: (s, off + h)),
            pl.BlockSpec((seq_len, blk), lambda s, h: (s, 2 * off + h)),
            pl.BlockSpec((seq_len, blk), lambda s, h: (s, h)),
        ]
        + seg_spec,
        out_specs=pl.BlockSpec((seq_len, width3), lambda s, h: (s, 0)),
        cost_estimate=pl.CostEstimate(
            flops=flops,
            transcendentals=n_seq * seq_len * seq_len * (model_width // HD),
            bytes_accessed=qkv.size * 4 + rows * model_width * 2,
        ),
    )(qkv, qkv, qkv, grad_o, *mask_operands(segment_ids, valid))


MESH_ID = pl.DeviceIdType.MESH


def ring_maps(n_wide, n_narrow):
    n_dev = n_wide * n_narrow
    if (n_wide, n_narrow) == (8, 4):
        def pos_of(w, n):
            z, y, x, c = w // 2, w % 2, n // 2, n % 2
            q = 2 * x + (x + y) % 2
            k = 4 * q + z + (q % 2) * (3 - 2 * z)
            return 2 * k + c

        def coords_of(p):
            k, c = p // 2, p % 2
            q, r = k // 4, k % 4
            z = r + (q % 2) * (3 - 2 * r)
            x = q // 2
            y = (q % 2 + x) % 2
            return z * 2 + y, x * 2 + c

    else:
        def pos_of(w, n):
            return w * n_narrow + n

        def coords_of(p):
            return p // n_narrow, p % n_narrow

    return n_dev, pos_of, coords_of


def ring_reduce_scatter(parts, mesh_shape, after=(), collective_id=0):
    n_wide, n_narrow = mesh_shape
    n_dev, pos_of, coords_of = ring_maps(n_wide, n_narrow)
    specs = []
    for i, (a, rb, split) in enumerate(parts):
        cols = a.shape[1]
        if split:
            specs.append((i, 0, 0, cols // 2))
        else:
            specs.append((i, 0, 0, cols))
    for i, (a, rb, split) in enumerate(parts):
        if split:
            specs.append((i, 1, a.shape[1] // 2, a.shape[1] // 2))
    n_in = len(parts)
    n_after = len(after)
    n_sp = len(specs)
    last_step = n_dev - 2

    def kernel(*refs):
        ins = refs[:n_in]
        outs = refs[n_in + n_after : 2 * n_in + n_after]
        at = 2 * n_in + n_after
        bufs = refs[at : at + n_sp]
        locs = refs[at + n_sp : at + 2 * n_sp]
        send_sem, recv_sem, loc_sem, credit = refs[at + 2 * n_sp :]
        p = pos_of(lax.axis_index("wide"), lax.axis_index("narrow"))
        right = coords_of((p + 1) % n_dev)
        left = coords_of((p + n_dev - 1) % n_dev)
        nbr_send = (right, left)
        nbr_recv = (left, right)

        def rows_of(q, rb):
            cw, cn = coords_of(q % n_dev)
            start = (cw * n_narrow + cn) * rb
            if rb % 8 == 0:
                start = pl.multiple_of(start, 8)
            return pl.ds(start, rb)

        def remote(j, s):
            return pltpu.make_async_remote_copy(
                src_ref=bufs[j].at[s % 3],
                dst_ref=bufs[j].at[(s + 1) % 3],
                send_sem=send_sem.at[j, s % 3],
                recv_sem=recv_sem.at[j, (s + 1) % 3],
                device_id=nbr_send[specs[j][1]],
                device_id_type=MESH_ID,
            )

        def local(j, s):
            i, dirn, c0, cw = specs[j]
            q = (p + 2 * n_dev - s - 2) if dirn == 0 else (p + s + 2)
            return pltpu.make_async_copy(
                ins[i].at[rows_of(q, parts[i][1]), pl.ds(c0, cw)], locs[j].at[s % 2], loc_sem.at[j, s % 2]
            )

        barrier = pltpu.get_barrier_semaphore()
        for nb in (left, right):
            pl.semaphore_signal(barrier, 1, device_id=nb, device_id_type=MESH_ID)
        pl.semaphore_wait(barrier, 2)

        for j, (i, dirn, c0, cw) in enumerate(specs):
            q = p + n_dev - 1 if dirn == 0 else p + 1
            cp = pltpu.make_async_copy(
                ins[i].at[rows_of(q, parts[i][1]), pl.ds(c0, cw)], bufs[j].at[0], loc_sem.at[j, 1]
            )
            cp.start()
            cp.wait()
        for j in range(n_sp):
            remote(j, 0).start()
            local(j, 0).start()

        def step(s, carry):
            for j in range(n_sp):
                dirn = specs[j][1]
                local(j, s).wait()
                remote(j, s).wait_recv()
                nxt = (s + 1) % 3
                bufs[j][nxt] = bufs[j][nxt] + locs[j][s % 2]
                if j == 0 or specs[j - 1][1] != dirn:

                    @pl.when((s >= 1) & (s + 1 <= last_step))
                    def _():
                        pl.semaphore_wait(credit.at[dirn], 1)

                @pl.when(s + 1 <= last_step)
                def _():
                    remote(j, s + 1).start()
                    local(j, s + 1).start()

            for j in range(n_sp):
                remote(j, s).wait_send()
            for dirn in (0, 1):

                @pl.when(s <= last_step - 2)
                def _():
                    pl.semaphore_signal(
                        credit.at[dirn], 1, device_id=nbr_recv[dirn], device_id_type=MESH_ID
                    )

            return carry

        lax.fori_loop(0, last_step + 1, step, 0)
        fin = (last_step + 1) % 3
        for j, (i, dirn, c0, cw) in enumerate(specs):
            outs[i][:, pl.ds(c0, cw)] = bufs[j][fin]

    out_shape = [jax.ShapeDtypeStruct((rb, a.shape[1]), a.dtype) for (a, rb, _) in parts]
    scratch = [pltpu.VMEM((3, parts[i][1], cw), jnp.float32) for (i, _, _, cw) in specs]
    scratch += [pltpu.VMEM((2, parts[i][1], cw), jnp.float32) for (i, _, _, cw) in specs]
    scratch += [
        pltpu.SemaphoreType.DMA((n_sp, 3)),
        pltpu.SemaphoreType.DMA((n_sp, 3)),
        pltpu.SemaphoreType.DMA((n_sp, 2)),
        pltpu.SemaphoreType.REGULAR((2,)),
    ]
    total = sum(a.size * 4 for (a, _, _) in parts)
    return pl.pallas_call(
        kernel,
        out_shape=out_shape,
        in_specs=[pl.BlockSpec(memory_space=pl.ANY)] * (n_in + n_after),
        out_specs=[pl.BlockSpec(memory_space=pltpu.VMEM)] * n_in,
        scratch_shapes=scratch,
        compiler_params=pltpu.CompilerParams(
            collective_id=collective_id, has_side_effects=True, vmem_limit_bytes=48 * 1024 * 1024
        ),
        cost_estimate=pl.CostEstimate(flops=total // 4, transcendentals=0, bytes_accessed=2 * total),
    )(*[a for (a, _, _) in parts], *after)


def pack_rows(pieces, width):
    flat = jnp.concatenate(pieces)
    return jnp.pad(flat, (0, width - flat.shape[0]))[None, :]


def split_owned(packed, sizes):
    out = []
    at = 0
    for size in sizes:
        out.append(packed[:, at : at + size].reshape(-1))
        at += size
    return out


def on_device(
    inputs,
    w_qkv,
    qv_bias,
    w_out,
    out_bias,
    ln1_gain,
    ln1_shift,
    ln2_gain,
    ln2_shift,
    w_up,
    up_bias,
    w_down,
    down_bias,
    segment_ids,
    valid,
    cotangent,
    mesh_shape=None,
):
    row_count = inputs.shape[0]
    model_width = inputs.shape[1]
    seq_count = segment_ids.shape[0]
    seq_len = segment_ids.shape[1]
    head_count = model_width // HD
    n_dev = mesh_shape[0] * mesh_shape[1]
    small = (qv_bias, out_bias, ln1_gain, ln1_shift, ln2_gain, ln2_shift, up_bias, down_bias)
    small_sizes = [a.shape[0] for a in small]
    n_small = sum(small_sizes)
    width_q = w_qkv.shape[1]
    rows_q = w_qkv.shape[0]
    rows_o = w_out.size // width_q
    rows_u = w_up.size // width_q
    attn_buf = jnp.concatenate(
        [
            w_qkv,
            w_out.reshape(rows_o, width_q),
            w_up.reshape(rows_u, width_q),
            pack_rows(small, width_q),
        ],
        axis=0,
    )
    attn_all = lax.all_gather(attn_buf, ALL, axis=0, tiled=False)
    qkv_full = attn_all[:, :rows_q].reshape(-1, width_q)
    out_full = attn_all[:, rows_q : rows_q + rows_o].reshape(-1, model_width)
    up_full = attn_all[:, rows_q + rows_o : rows_q + rows_o + rows_u].reshape(-1, w_up.shape[1])
    small_full = split_owned(attn_all[:, rows_q + rows_o + rows_u, :n_small], small_sizes)
    qv_full, outb_full, gain_one, shift_one, gain_two, shift_two, upb_full, downb_full = small_full
    down_full = lax.all_gather(w_down, ALL, axis=0, tiled=True)

    gain_one = gain_one.astype(jnp.float32)
    shift_one = shift_one.astype(jnp.float32)
    qv_full = qv_full.astype(jnp.float32)
    rows = inputs.astype(jnp.float32)
    normed_one, recip_one = norm_parts(rows)
    h_one = (normed_one * gain_one + shift_one).astype(jnp.bfloat16)
    qkv_rows = jnp.dot(h_one, qkv_full, preferred_element_type=jnp.float32)
    zero_bias = jnp.zeros((model_width,), jnp.float32)
    qkv_bias = jnp.concatenate([qv_full[:model_width], zero_bias, qv_full[model_width:]])
    qkv_b = (qkv_rows + qkv_bias).astype(jnp.bfloat16)
    attended = attention_fwd(qkv_b, segment_ids, valid)
    mid_rows = (
        rows
        + jnp.dot(attended, out_full, preferred_element_type=jnp.float32)
        + outb_full.astype(jnp.float32)
    )
    gain_two = gain_two.astype(jnp.float32)
    shift_two = shift_two.astype(jnp.float32)
    normed_two, recip_two = norm_parts(mid_rows)
    h_two = (normed_two * gain_two + shift_two).astype(jnp.bfloat16)
    upper = jnp.dot(h_two, up_full, preferred_element_type=jnp.float32) + upb_full.astype(
        jnp.float32
    )
    gelu_rows = jax.nn.gelu(upper, approximate=False).astype(jnp.bfloat16)
    out_rows = (
        mid_rows
        + jnp.dot(gelu_rows, down_full, preferred_element_type=jnp.float32)
        + downb_full.astype(jnp.float32)
    )
    block_out = out_rows.astype(jnp.bfloat16)
    dy_rows = cotangent.astype(jnp.float32)
    grad_wdown = jnp.einsum("tf,td->fd", gelu_rows, cotangent, preferred_element_type=jnp.float32)
    grad_bdown = col_sum(cotangent)
    grad_g = jnp.einsum("td,fd->tf", cotangent, down_full, preferred_element_type=jnp.float32)
    cdf_part = 0.5 * (1.0 + jax.scipy.special.erf(upper * 0.7071067811865476))
    pdf_part = jnp.exp(-0.5 * upper * upper) * 0.3989422804014327
    grad_u = (grad_g * (cdf_part + upper * pdf_part)).astype(jnp.bfloat16)
    grad_bup = col_sum(grad_u)
    grad_wup = jnp.einsum("td,tf->df", h_two, grad_u, preferred_element_type=jnp.float32)
    grad_h2 = jnp.einsum("tf,df->td", grad_u, up_full, preferred_element_type=jnp.float32)
    grad_g2 = jnp.sum(grad_h2 * normed_two, axis=0)
    grad_c2 = jnp.sum(grad_h2, axis=0)
    grad_mid = dy_rows + norm_back(grad_h2, gain_two, normed_two, recip_two)
    grad_a = grad_mid.astype(jnp.bfloat16)
    grad_wout = jnp.einsum("tc,td->cd", attended, grad_a, preferred_element_type=jnp.float32)
    grad_bout = col_sum(grad_a)
    grad_o = jnp.einsum("td,cd->tc", grad_a, out_full, preferred_element_type=jnp.float32).astype(
        jnp.bfloat16
    )
    grad_qkv = attention_bwd(qkv_b, grad_o, segment_ids, valid)
    grad_cols = col_sum(grad_qkv)
    grad_bqv = jnp.concatenate([grad_cols[:model_width], grad_cols[2 * model_width :]])
    grad_wqkv = jnp.einsum("td,te->de", h_one, grad_qkv, preferred_element_type=jnp.float32)
    grad_h1 = jnp.einsum("te,de->td", grad_qkv, qkv_full, preferred_element_type=jnp.float32)
    grad_g1 = jnp.sum(grad_h1 * normed_one, axis=0)
    grad_c1 = jnp.sum(grad_h1, axis=0)
    grad_inputs = grad_mid + norm_back(grad_h1, gain_one, normed_one, recip_one)

    small_grads = (grad_bqv, grad_bout, grad_g1, grad_c1, grad_g2, grad_c2, grad_bup, grad_bdown)
    owned = jnp.concatenate([g.reshape(n_dev, -1) for g in small_grads], axis=1)
    lanes = 128
    small_rows = 8 * pl.cdiv(pl.cdiv(n_small, lanes), 8)
    owned = jnp.pad(owned, ((0, 0), (0, small_rows * lanes - n_small))).reshape(-1, lanes)
    parts = [
        (grad_wqkv, w_qkv.shape[0], True),
        (grad_wout, w_out.shape[0], True),
        (grad_wup, w_up.shape[0], True),
        (owned, small_rows, False),
    ]
    down_sum = lax.psum_scatter(grad_wdown, ALL, scatter_dimension=0, tiled=True)
    if all(rb % 8 == 0 and a.shape[1] % 256 == 0 for (a, rb, _) in parts[:3]):
        sums = ring_reduce_scatter(parts, mesh_shape, after=(grad_inputs, block_out))
    else:
        sums = [lax.psum_scatter(a, ALL, scatter_dimension=0, tiled=True) for (a, _, _) in parts]
    sums = list(sums[:3]) + [down_sum] + list(sums[3:])
    small_sums = split_owned(sums[4].reshape(1, -1), small_sizes)
    bqv, bout, g1, c1, g2, c2, bup, bdown = small_sums
    return (
        block_out,
        grad_inputs,
        sums[0],
        bqv,
        sums[1],
        bout,
        g1,
        c1,
        g2,
        c2,
        sums[2],
        bup,
        sums[3],
        bdown,
    )


def solution(mesh):
    in_specs = (
        P(("wide", "narrow"), None),
        P(("wide", "narrow"), None),
        P(("wide", "narrow")),
        P(("wide", "narrow"), None),
        P(("wide", "narrow")),
        P(("wide", "narrow")),
        P(("wide", "narrow")),
        P(("wide", "narrow")),
        P(("wide", "narrow")),
        P(("wide", "narrow"), None),
        P(("wide", "narrow")),
        P(("wide", "narrow"), None),
        P(("wide", "narrow")),
        P(("wide", "narrow"), None),
        P(("wide", "narrow"), None),
        P(("wide", "narrow"), None),
    )
    out_specs = (
        P(("wide", "narrow"), None),
        P(("wide", "narrow"), None),
        P(("wide", "narrow"), None),
        P(("wide", "narrow")),
        P(("wide", "narrow"), None),
        P(("wide", "narrow")),
        P(("wide", "narrow")),
        P(("wide", "narrow")),
        P(("wide", "narrow")),
        P(("wide", "narrow")),
        P(("wide", "narrow"), None),
        P(("wide", "narrow")),
        P(("wide", "narrow"), None),
        P(("wide", "narrow")),
    )
    body = functools.partial(on_device, mesh_shape=(mesh.shape["wide"], mesh.shape["narrow"]))
    return jax.shard_map(
        body, mesh=mesh, in_specs=in_specs, out_specs=out_specs, check_vma=False
    )
```

```python
import functools
import jax
import jax.numpy as jnp
from jax import lax
from jax.experimental import pallas as pl
from jax.experimental.pallas import tpu as pltpu
from jax.sharding import PartitionSpec as P

HD = 64
ALL = ("wide", "narrow")

EPSILON = 1e-06


def norm_parts(rows):
    center = rows - jnp.mean(rows, axis=-1, keepdims=True)
    recip = lax.rsqrt(jnp.mean(center * center, axis=-1, keepdims=True) + EPSILON)
    return (center * recip, recip)


def norm_back(grad_h, gain, normed, recip):
    scaled = grad_h * gain
    return recip * (
        scaled
        - jnp.mean(scaled, axis=-1, keepdims=True)
        - normed * jnp.mean(scaled * normed, axis=-1, keepdims=True)
    )


def col_sum(rows):
    return jnp.sum(rows.astype(jnp.float32), axis=0)


def seg_mask(seg_col, seg_row, val_row, n):
    rows = lax.broadcasted_iota(jnp.int32, (n, n), 0)
    cols = lax.broadcasted_iota(jnp.int32, (n, n), 1)
    return (seg_col == seg_row) & ((val_row == 1) | (rows == cols))


def soft_rows(qh, kh, allowed):
    scores = lax.dot_general(qh, kh, (((1,), (1,)), ((), ())), preferred_element_type=jnp.float32)
    scores = jnp.where(allowed, scores * (1.0 / HD**0.5), -1e30)
    top = jnp.max(scores, axis=-1, keepdims=True)
    expo = jnp.exp(scores - top)
    return expo * (1.0 / jnp.sum(expo, axis=-1, keepdims=True))


def attn_fwd_kernel(q_ref, k_ref, v_ref, sc_ref, sr_ref, vr_ref, o_ref):
    n = q_ref.shape[0]
    allowed = seg_mask(sc_ref[...], sr_ref[...], vr_ref[...], n)
    outs = []
    for j in range(q_ref.shape[1] // HD):
        cols = slice(j * HD, (j + 1) * HD)
        probs = soft_rows(q_ref[:, cols], k_ref[:, cols], allowed).astype(jnp.bfloat16)
        outs.append(jnp.dot(probs, v_ref[:, cols], preferred_element_type=jnp.float32))
    o_ref[...] = jnp.concatenate(outs, axis=1).astype(o_ref.dtype)


def attn_bwd_kernel(q_ref, k_ref, v_ref, do_ref, sc_ref, sr_ref, vr_ref, dqkv_ref):
    n = q_ref.shape[0]
    width = q_ref.shape[1]
    hp = pl.program_id(1)
    model_width = dqkv_ref.shape[1] // 3
    allowed = seg_mask(sc_ref[...], sr_ref[...], vr_ref[...], n)
    dqs, dks, dvs = [], [], []
    for j in range(width // HD):
        cols = slice(j * HD, (j + 1) * HD)
        qh, kh, vh, doh = q_ref[:, cols], k_ref[:, cols], v_ref[:, cols], do_ref[:, cols]
        probs = soft_rows(qh, kh, allowed)
        dvs.append(
            lax.dot_general(probs.astype(jnp.bfloat16), doh, (((0,), (0,)), ((), ())),
                            preferred_element_type=jnp.float32)
        )
        dprobs = lax.dot_general(doh, vh, (((1,), (1,)), ((), ())), preferred_element_type=jnp.float32)
        row_term = jnp.sum(probs * dprobs, axis=-1, keepdims=True)
        dscore = jnp.where(allowed, probs * (dprobs - row_term), 0.0).astype(jnp.bfloat16)
        dqs.append(jnp.dot(dscore, kh, preferred_element_type=jnp.float32) * (1.0 / HD**0.5))
        dks.append(
            lax.dot_general(dscore, qh, (((0,), (0,)), ((), ())), preferred_element_type=jnp.float32)
            * (1.0 / HD**0.5)
        )
    at = pl.multiple_of(hp * width, width)
    dqkv_ref[:, pl.ds(at, width)] = jnp.concatenate(dqs, axis=1).astype(dqkv_ref.dtype)
    dqkv_ref[:, pl.ds(at + model_width, width)] = jnp.concatenate(dks, axis=1).astype(dqkv_ref.dtype)
    dqkv_ref[:, pl.ds(at + 2 * model_width, width)] = jnp.concatenate(dvs, axis=1).astype(dqkv_ref.dtype)


def mask_operands(segment_ids, valid):
    return (segment_ids[:, :, None], segment_ids[:, None, :], valid[:, None, :])


def attention_fwd(qkv, segment_ids, valid):
    rows, width3 = qkv.shape
    model_width = width3 // 3
    n_seq, seq_len = segment_ids.shape
    blk = 2 * HD
    n_hp = model_width // blk
    off = model_width // blk
    seg_spec = [
        pl.BlockSpec((None, seq_len, 1), lambda s, h: (s, 0, 0)),
        pl.BlockSpec((None, 1, seq_len), lambda s, h: (s, 0, 0)),
        pl.BlockSpec((None, 1, seq_len), lambda s, h: (s, 0, 0)),
    ]
    flops = 4 * n_seq * seq_len * seq_len * model_width
    return pl.pallas_call(
        attn_fwd_kernel,
        out_shape=jax.ShapeDtypeStruct((rows, model_width), jnp.bfloat16),
        grid=(n_seq, n_hp),
        in_specs=[
            pl.BlockSpec((seq_len, blk), lambda s, h: (s, h)),
            pl.BlockSpec((seq_len, blk), lambda s, h: (s, off + h)),
            pl.BlockSpec((seq_len, blk), lambda s, h: (s, 2 * off + h)),
        ]
        + seg_spec,
        out_specs=pl.BlockSpec((seq_len, blk), lambda s, h: (s, h)),
        cost_estimate=pl.CostEstimate(
            flops=flops,
            transcendentals=n_seq * seq_len * seq_len * (model_width // HD),
            bytes_accessed=qkv.size * 2 + rows * model_width * 2,
        ),
    )(qkv, qkv, qkv, *mask_operands(segment_ids, valid))


def attention_bwd(qkv, grad_o, segment_ids, valid):
    rows, width3 = qkv.shape
    model_width = width3 // 3
    n_seq, seq_len = segment_ids.shape
    blk = 2 * HD
    n_hp = model_width // blk
    off = model_width // blk
    seg_spec = [
        pl.BlockSpec((None, seq_len, 1), lambda s, h: (s, 0, 0)),
        pl.BlockSpec((None, 1, seq_len), lambda s, h: (s, 0, 0)),
        pl.BlockSpec((None, 1, seq_len), lambda s, h: (s, 0, 0)),
    ]
    flops = 10 * n_seq * seq_len * seq_len * model_width
    return pl.pallas_call(
        attn_bwd_kernel,
        out_shape=jax.ShapeDtypeStruct((rows, width3), jnp.bfloat16),
        grid=(n_seq, n_hp),
        in_specs=[
            pl.BlockSpec((seq_len, blk), lambda s, h: (s, h)),
            pl.BlockSpec((seq_len, blk), lambda s, h: (s, off + h)),
            pl.BlockSpec((seq_len, blk), lambda s, h: (s, 2 * off + h)),
            pl.BlockSpec((seq_len, blk), lambda s, h: (s, h)),
        ]
        + seg_spec,
        out_specs=pl.BlockSpec((seq_len, width3), lambda s, h: (s, 0)),
        cost_estimate=pl.CostEstimate(
            flops=flops,
            transcendentals=n_seq * seq_len * seq_len * (model_width // HD),
            bytes_accessed=qkv.size * 4 + rows * model_width * 2,
        ),
    )(qkv, qkv, qkv, grad_o, *mask_operands(segment_ids, valid))


MESH_ID = pl.DeviceIdType.MESH


def ring_maps(n_wide, n_narrow):
    n_dev = n_wide * n_narrow
    if (n_wide, n_narrow) == (8, 4):
        def pos_of(w, n):
            z, y, x, c = w // 2, w % 2, n // 2, n % 2
            q = 2 * x + (x + y) % 2
            k = 4 * q + z + (q % 2) * (3 - 2 * z)
            return 2 * k + c

        def coords_of(p):
            k, c = p // 2, p % 2
            q, r = k // 4, k % 4
            z = r + (q % 2) * (3 - 2 * r)
            x = q // 2
            y = (q % 2 + x) % 2
            return z * 2 + y, x * 2 + c

    else:
        def pos_of(w, n):
            return w * n_narrow + n

        def coords_of(p):
            return p // n_narrow, p % n_narrow

    return n_dev, pos_of, coords_of


def ring_reduce_scatter(parts, mesh_shape, after=(), collective_id=0):
    n_wide, n_narrow = mesh_shape
    n_dev, pos_of, coords_of = ring_maps(n_wide, n_narrow)
    specs = []
    for i, (a, rb, split) in enumerate(parts):
        cols = a.shape[1]
        if split:
            specs.append((i, 0, 0, cols // 2))
        else:
            specs.append((i, 0, 0, cols))
    for i, (a, rb, split) in enumerate(parts):
        if split:
            specs.append((i, 1, a.shape[1] // 2, a.shape[1] // 2))
    n_in = len(parts)
    n_after = len(after)
    n_sp = len(specs)
    last_step = n_dev - 2

    def kernel(*refs):
        ins = refs[:n_in]
        outs = refs[n_in + n_after : 2 * n_in + n_after]
        at = 2 * n_in + n_after
        bufs = refs[at : at + n_sp]
        locs = refs[at + n_sp : at + 2 * n_sp]
        send_sem, recv_sem, loc_sem, credit = refs[at + 2 * n_sp :]
        p = pos_of(lax.axis_index("wide"), lax.axis_index("narrow"))
        right = coords_of((p + 1) % n_dev)
        left = coords_of((p + n_dev - 1) % n_dev)
        nbr_send = (right, left)
        nbr_recv = (left, right)

        def rows_of(q, rb):
            cw, cn = coords_of(q % n_dev)
            start = (cw * n_narrow + cn) * rb
            if rb % 8 == 0:
                start = pl.multiple_of(start, 8)
            return pl.ds(start, rb)

        def remote(j, s):
            return pltpu.make_async_remote_copy(
                src_ref=bufs[j].at[s % 3],
                dst_ref=bufs[j].at[(s + 1) % 3],
                send_sem=send_sem.at[j, s % 3],
                recv_sem=recv_sem.at[j, (s + 1) % 3],
                device_id=nbr_send[specs[j][1]],
                device_id_type=MESH_ID,
            )

        def local(j, s):
            i, dirn, c0, cw = specs[j]
            q = (p + 2 * n_dev - s - 2) if dirn == 0 else (p + s + 2)
            return pltpu.make_async_copy(
                ins[i].at[rows_of(q, parts[i][1]), pl.ds(c0, cw)], locs[j].at[s % 2], loc_sem.at[j, s % 2]
            )

        barrier = pltpu.get_barrier_semaphore()
        for nb in (left, right):
            pl.semaphore_signal(barrier, 1, device_id=nb, device_id_type=MESH_ID)
        pl.semaphore_wait(barrier, 2)

        for j, (i, dirn, c0, cw) in enumerate(specs):
            q = p + n_dev - 1 if dirn == 0 else p + 1
            cp = pltpu.make_async_copy(
                ins[i].at[rows_of(q, parts[i][1]), pl.ds(c0, cw)], bufs[j].at[0], loc_sem.at[j, 1]
            )
            cp.start()
            cp.wait()
        for j in range(n_sp):
            remote(j, 0).start()
            local(j, 0).start()

        def step(s, carry):
            for j in range(n_sp):
                dirn = specs[j][1]
                local(j, s).wait()
                remote(j, s).wait_recv()
                nxt = (s + 1) % 3
                bufs[j][nxt] = bufs[j][nxt] + locs[j][s % 2]
                if j == 0 or specs[j - 1][1] != dirn:

                    @pl.when((s >= 1) & (s + 1 <= last_step))
                    def _():
                        pl.semaphore_wait(credit.at[dirn], 1)

                @pl.when(s + 1 <= last_step)
                def _():
                    remote(j, s + 1).start()
                    local(j, s + 1).start()

            for j in range(n_sp):
                remote(j, s).wait_send()
            for dirn in (0, 1):

                @pl.when(s <= last_step - 2)
                def _():
                    pl.semaphore_signal(
                        credit.at[dirn], 1, device_id=nbr_recv[dirn], device_id_type=MESH_ID
                    )

            return carry

        lax.fori_loop(0, last_step + 1, step, 0)
        fin = (last_step + 1) % 3
        for j, (i, dirn, c0, cw) in enumerate(specs):
            outs[i][:, pl.ds(c0, cw)] = bufs[j][fin]

    out_shape = [jax.ShapeDtypeStruct((rb, a.shape[1]), a.dtype) for (a, rb, _) in parts]
    scratch = [pltpu.VMEM((3, parts[i][1], cw), jnp.float32) for (i, _, _, cw) in specs]
    scratch += [pltpu.VMEM((2, parts[i][1], cw), jnp.float32) for (i, _, _, cw) in specs]
    scratch += [
        pltpu.SemaphoreType.DMA((n_sp, 3)),
        pltpu.SemaphoreType.DMA((n_sp, 3)),
        pltpu.SemaphoreType.DMA((n_sp, 2)),
        pltpu.SemaphoreType.REGULAR((2,)),
    ]
    total = sum(a.size * 4 for (a, _, _) in parts)
    return pl.pallas_call(
        kernel,
        out_shape=out_shape,
        in_specs=[pl.BlockSpec(memory_space=pl.ANY)] * (n_in + n_after),
        out_specs=[pl.BlockSpec(memory_space=pltpu.VMEM)] * n_in,
        scratch_shapes=scratch,
        compiler_params=pltpu.CompilerParams(
            collective_id=collective_id, has_side_effects=True, vmem_limit_bytes=48 * 1024 * 1024
        ),
        cost_estimate=pl.CostEstimate(flops=total // 4, transcendentals=0, bytes_accessed=2 * total),
    )(*[a for (a, _, _) in parts], *after)


def ring_all_gather(parts, mesh_shape, collective_id=1):
    n_wide, n_narrow = mesh_shape
    n_dev, pos_of, coords_of = ring_maps(n_wide, n_narrow)
    n_in = len(parts)
    steps = (n_dev // 2, n_dev - 1 - n_dev // 2)

    def kernel(*refs):
        ins = refs[:n_in]
        outs = refs[n_in : 2 * n_in]
        send_sem, recv_sem, loc_sem = refs[2 * n_in :]
        p = pos_of(lax.axis_index("wide"), lax.axis_index("narrow"))
        right = coords_of((p + 1) % n_dev)
        left = coords_of((p + n_dev - 1) % n_dev)
        nbr_send = (right, left)

        def rows_of(q, rb):
            cw, cn = coords_of(q % n_dev)
            return pl.ds(pl.multiple_of((cw * n_narrow + cn) * rb, rb), rb)

        def copy(i, dirn, s, q):
            view = outs[i].at[rows_of(q, parts[i].shape[0])]
            return pltpu.make_async_remote_copy(
                src_ref=view,
                dst_ref=view,
                send_sem=send_sem.at[dirn, i, s],
                recv_sem=recv_sem.at[dirn, i, s],
                device_id=nbr_send[dirn],
                device_id_type=MESH_ID,
            )

        def sent(i, dirn, s):
            return copy(i, dirn, s, (p + n_dev - s) if dirn == 0 else (p + s))

        def arriving(i, dirn, s):
            return copy(i, dirn, s, (p + n_dev - 1 - s) if dirn == 0 else (p + 1 + s))

        barrier = pltpu.get_barrier_semaphore()
        for nb in (left, right):
            pl.semaphore_signal(barrier, 1, device_id=nb, device_id_type=MESH_ID)
        pl.semaphore_wait(barrier, 2)

        for i in range(n_in):
            cp = pltpu.make_async_copy(ins[i], outs[i].at[rows_of(p, parts[i].shape[0])], loc_sem.at[i])
            cp.start()
            cp.wait()

        def step(s, carry):
            for dirn in (0, 1):

                @pl.when(s < steps[dirn])
                def _():
                    for i in range(n_in):
                        sent(i, dirn, s).start()

            for dirn in (0, 1):

                @pl.when(s < steps[dirn])
                def _():
                    for i in range(n_in):
                        arriving(i, dirn, s).wait_recv()

            return carry

        lax.fori_loop(0, steps[0], step, 0)

        def drain(s, carry):
            for dirn in (0, 1):

                @pl.when(s < steps[dirn])
                def _():
                    for i in range(n_in):
                        sent(i, dirn, s).wait_send()

            return carry

        lax.fori_loop(0, steps[0], drain, 0)

    out_shape = [jax.ShapeDtypeStruct((n_dev * a.shape[0], a.shape[1]), a.dtype) for a in parts]
    total = sum(n_dev * a.size * a.dtype.itemsize for a in parts)
    return pl.pallas_call(
        kernel,
        out_shape=out_shape,
        in_specs=[pl.BlockSpec(memory_space=pl.ANY)] * n_in,
        out_specs=[pl.BlockSpec(memory_space=pltpu.VMEM)] * n_in,
        scratch_shapes=[
            pltpu.SemaphoreType.DMA((2, n_in, steps[0])),
            pltpu.SemaphoreType.DMA((2, n_in, steps[0])),
            pltpu.SemaphoreType.DMA((n_in,)),
        ],
        compiler_params=pltpu.CompilerParams(collective_id=collective_id, has_side_effects=True),
        cost_estimate=pl.CostEstimate(flops=0, transcendentals=0, bytes_accessed=2 * total),
    )(*parts)


def pack_rows(pieces, width):
    flat = jnp.concatenate(pieces)
    return jnp.pad(flat, (0, width - flat.shape[0]))[None, :]


def split_owned(packed, sizes):
    out = []
    at = 0
    for size in sizes:
        out.append(packed[:, at : at + size].reshape(-1))
        at += size
    return out


def on_device(
    inputs,
    w_qkv,
    qv_bias,
    w_out,
    out_bias,
    ln1_gain,
    ln1_shift,
    ln2_gain,
    ln2_shift,
    w_up,
    up_bias,
    w_down,
    down_bias,
    segment_ids,
    valid,
    cotangent,
    mesh_shape=None,
):
    row_count = inputs.shape[0]
    model_width = inputs.shape[1]
    seq_count = segment_ids.shape[0]
    seq_len = segment_ids.shape[1]
    head_count = model_width // HD
    n_dev = mesh_shape[0] * mesh_shape[1]
    small = (qv_bias, out_bias, ln1_gain, ln1_shift, ln2_gain, ln2_shift, up_bias, down_bias)
    small_sizes = [a.shape[0] for a in small]
    n_small = sum(small_sizes)
    width_q = w_qkv.shape[1]
    rows_q = w_qkv.shape[0]
    rows_o = w_out.size // width_q
    rows_u = w_up.size // width_q
    up_view = 16
    ring_up = mesh_shape == (8, 4) and w_up.size % (up_view * 128) == 0
    pieces = [w_qkv, w_out.reshape(rows_o, width_q)]
    if not ring_up:
        pieces.append(w_up.reshape(rows_u, width_q))
    attn_buf = jnp.concatenate(pieces + [pack_rows(small, width_q)], axis=0)
    attn_all = lax.all_gather(attn_buf, ALL, axis=0, tiled=False)
    qkv_full = attn_all[:, :rows_q].reshape(-1, width_q)
    out_full = attn_all[:, rows_q : rows_q + rows_o].reshape(-1, model_width)
    at = rows_q + rows_o
    if ring_up:
        (up_all,) = ring_all_gather([w_up.reshape(up_view, -1)], mesh_shape)
        up_full = up_all.reshape(-1, w_up.shape[1])
    else:
        up_full = attn_all[:, at : at + rows_u].reshape(-1, w_up.shape[1])
        at = at + rows_u
    small_full = split_owned(attn_all[:, at, :n_small], small_sizes)
    qv_full, outb_full, gain_one, shift_one, gain_two, shift_two, upb_full, downb_full = small_full
    down_full = lax.all_gather(w_down, ALL, axis=0, tiled=True)

    gain_one = gain_one.astype(jnp.float32)
    shift_one = shift_one.astype(jnp.float32)
    qv_full = qv_full.astype(jnp.float32)
    rows = inputs.astype(jnp.float32)
    normed_one, recip_one = norm_parts(rows)
    h_one = (normed_one * gain_one + shift_one).astype(jnp.bfloat16)
    qkv_rows = jnp.dot(h_one, qkv_full, preferred_element_type=jnp.float32)
    zero_bias = jnp.zeros((model_width,), jnp.float32)
    qkv_bias = jnp.concatenate([qv_full[:model_width], zero_bias, qv_full[model_width:]])
    qkv_b = (qkv_rows + qkv_bias).astype(jnp.bfloat16)
    attended = attention_fwd(qkv_b, segment_ids, valid)
    mid_rows = (
        rows
        + jnp.dot(attended, out_full, preferred_element_type=jnp.float32)
        + outb_full.astype(jnp.float32)
    )
    gain_two = gain_two.astype(jnp.float32)
    shift_two = shift_two.astype(jnp.float32)
    normed_two, recip_two = norm_parts(mid_rows)
    h_two = (normed_two * gain_two + shift_two).astype(jnp.bfloat16)
    upper = jnp.dot(h_two, up_full, preferred_element_type=jnp.float32) + upb_full.astype(
        jnp.float32
    )
    gelu_rows = jax.nn.gelu(upper, approximate=False).astype(jnp.bfloat16)
    out_rows = (
        mid_rows
        + jnp.dot(gelu_rows, down_full, preferred_element_type=jnp.float32)
        + downb_full.astype(jnp.float32)
    )
    block_out = out_rows.astype(jnp.bfloat16)
    dy_rows = cotangent.astype(jnp.float32)
    grad_wdown = jnp.einsum("tf,td->fd", gelu_rows, cotangent, preferred_element_type=jnp.float32)
    grad_bdown = col_sum(cotangent)
    grad_g = jnp.einsum("td,fd->tf", cotangent, down_full, preferred_element_type=jnp.float32)
    cdf_part = 0.5 * (1.0 + jax.scipy.special.erf(upper * 0.7071067811865476))
    pdf_part = jnp.exp(-0.5 * upper * upper) * 0.3989422804014327
    grad_u = (grad_g * (cdf_part + upper * pdf_part)).astype(jnp.bfloat16)
    grad_bup = col_sum(grad_u)
    grad_wup = jnp.einsum("td,tf->df", h_two, grad_u, preferred_element_type=jnp.float32)
    grad_h2 = jnp.einsum("tf,df->td", grad_u, up_full, preferred_element_type=jnp.float32)
    grad_g2 = jnp.sum(grad_h2 * normed_two, axis=0)
    grad_c2 = jnp.sum(grad_h2, axis=0)
    grad_mid = dy_rows + norm_back(grad_h2, gain_two, normed_two, recip_two)
    grad_a = grad_mid.astype(jnp.bfloat16)
    grad_wout = jnp.einsum("tc,td->cd", attended, grad_a, preferred_element_type=jnp.float32)
    grad_bout = col_sum(grad_a)
    grad_o = jnp.einsum("td,cd->tc", grad_a, out_full, preferred_element_type=jnp.float32).astype(
        jnp.bfloat16
    )
    grad_qkv = attention_bwd(qkv_b, grad_o, segment_ids, valid)
    grad_cols = col_sum(grad_qkv)
    grad_bqv = jnp.concatenate([grad_cols[:model_width], grad_cols[2 * model_width :]])
    grad_wqkv = jnp.einsum("td,te->de", h_one, grad_qkv, preferred_element_type=jnp.float32)
    grad_h1 = jnp.einsum("te,de->td", grad_qkv, qkv_full, preferred_element_type=jnp.float32)
    grad_g1 = jnp.sum(grad_h1 * normed_one, axis=0)
    grad_c1 = jnp.sum(grad_h1, axis=0)
    grad_inputs = grad_mid + norm_back(grad_h1, gain_one, normed_one, recip_one)

    small_grads = (grad_bqv, grad_bout, grad_g1, grad_c1, grad_g2, grad_c2, grad_bup, grad_bdown)
    owned = jnp.concatenate([g.reshape(n_dev, -1) for g in small_grads], axis=1)
    lanes = 128
    small_rows = 8 * pl.cdiv(pl.cdiv(n_small, lanes), 8)
    owned = jnp.pad(owned, ((0, 0), (0, small_rows * lanes - n_small))).reshape(-1, lanes)
    parts = [
        (grad_wqkv, w_qkv.shape[0], True),
        (grad_wout, w_out.shape[0], True),
        (grad_wup, w_up.shape[0], True),
        (owned, small_rows, False),
    ]
    down_sum = lax.psum_scatter(grad_wdown, ALL, scatter_dimension=0, tiled=True)
    if all(rb % 8 == 0 and a.shape[1] % 256 == 0 for (a, rb, _) in parts[:3]):
        sums = ring_reduce_scatter(parts, mesh_shape, after=(grad_inputs, block_out))
    else:
        sums = [lax.psum_scatter(a, ALL, scatter_dimension=0, tiled=True) for (a, _, _) in parts]
    sums = list(sums[:3]) + [down_sum] + list(sums[3:])
    small_sums = split_owned(sums[4].reshape(1, -1), small_sizes)
    bqv, bout, g1, c1, g2, c2, bup, bdown = small_sums
    return (
        block_out,
        grad_inputs,
        sums[0],
        bqv,
        sums[1],
        bout,
        g1,
        c1,
        g2,
        c2,
        sums[2],
        bup,
        sums[3],
        bdown,
    )


def solution(mesh):
    in_specs = (
        P(("wide", "narrow"), None),
        P(("wide", "narrow"), None),
        P(("wide", "narrow")),
        P(("wide", "narrow"), None),
        P(("wide", "narrow")),
        P(("wide", "narrow")),
        P(("wide", "narrow")),
        P(("wide", "narrow")),
        P(("wide", "narrow")),
        P(("wide", "narrow"), None),
        P(("wide", "narrow")),
        P(("wide", "narrow"), None),
        P(("wide", "narrow")),
        P(("wide", "narrow"), None),
        P(("wide", "narrow"), None),
        P(("wide", "narrow"), None),
    )
    out_specs = (
        P(("wide", "narrow"), None),
        P(("wide", "narrow"), None),
        P(("wide", "narrow"), None),
        P(("wide", "narrow")),
        P(("wide", "narrow"), None),
        P(("wide", "narrow")),
        P(("wide", "narrow")),
        P(("wide", "narrow")),
        P(("wide", "narrow")),
        P(("wide", "narrow")),
        P(("wide", "narrow"), None),
        P(("wide", "narrow")),
        P(("wide", "narrow"), None),
        P(("wide", "narrow")),
    )
    body = functools.partial(on_device, mesh_shape=(mesh.shape["wide"], mesh.shape["narrow"]))
    return jax.shard_map(
        body, mesh=mesh, in_specs=in_specs, out_specs=out_specs, check_vma=False
    )
```

```python
import functools
import jax
import jax.numpy as jnp
from jax import lax
from jax.experimental import pallas as pl
from jax.experimental.pallas import tpu as pltpu
from jax.sharding import PartitionSpec as P

HD = 64
ALL = ("wide", "narrow")

EPSILON = 1e-06


def norm_parts(rows):
    center = rows - jnp.mean(rows, axis=-1, keepdims=True)
    recip = lax.rsqrt(jnp.mean(center * center, axis=-1, keepdims=True) + EPSILON)
    return (center * recip, recip)


def norm_back(grad_h, gain, normed, recip):
    scaled = grad_h * gain
    return recip * (
        scaled
        - jnp.mean(scaled, axis=-1, keepdims=True)
        - normed * jnp.mean(scaled * normed, axis=-1, keepdims=True)
    )


def col_sum(rows):
    return jnp.sum(rows.astype(jnp.float32), axis=0)


def seg_mask(seg_col, seg_row, val_row, n):
    rows = lax.broadcasted_iota(jnp.int32, (n, n), 0)
    cols = lax.broadcasted_iota(jnp.int32, (n, n), 1)
    return (seg_col == seg_row) & ((val_row == 1) | (rows == cols))


def soft_rows(qh, kh, allowed):
    scores = lax.dot_general(qh, kh, (((1,), (1,)), ((), ())), preferred_element_type=jnp.float32)
    scores = jnp.where(allowed, scores * (1.0 / HD**0.5), -1e30)
    top = jnp.max(scores, axis=-1, keepdims=True)
    expo = jnp.exp(scores - top)
    return expo * (1.0 / jnp.sum(expo, axis=-1, keepdims=True))


def attn_fwd_kernel(q_ref, k_ref, v_ref, sc_ref, sr_ref, vr_ref, o_ref):
    n = q_ref.shape[0]
    allowed = seg_mask(sc_ref[...], sr_ref[...], vr_ref[...], n)
    outs = []
    for j in range(q_ref.shape[1] // HD):
        cols = slice(j * HD, (j + 1) * HD)
        probs = soft_rows(q_ref[:, cols], k_ref[:, cols], allowed).astype(jnp.bfloat16)
        outs.append(jnp.dot(probs, v_ref[:, cols], preferred_element_type=jnp.float32))
    o_ref[...] = jnp.concatenate(outs, axis=1).astype(o_ref.dtype)


def attn_bwd_kernel(q_ref, k_ref, v_ref, do_ref, sc_ref, sr_ref, vr_ref, dqkv_ref):
    n = q_ref.shape[0]
    width = q_ref.shape[1]
    hp = pl.program_id(1)
    model_width = dqkv_ref.shape[1] // 3
    allowed = seg_mask(sc_ref[...], sr_ref[...], vr_ref[...], n)
    dqs, dks, dvs = [], [], []
    for j in range(width // HD):
        cols = slice(j * HD, (j + 1) * HD)
        qh, kh, vh, doh = q_ref[:, cols], k_ref[:, cols], v_ref[:, cols], do_ref[:, cols]
        probs = soft_rows(qh, kh, allowed)
        dvs.append(
            lax.dot_general(probs.astype(jnp.bfloat16), doh, (((0,), (0,)), ((), ())),
                            preferred_element_type=jnp.float32)
        )
        dprobs = lax.dot_general(doh, vh, (((1,), (1,)), ((), ())), preferred_element_type=jnp.float32)
        row_term = jnp.sum(probs * dprobs, axis=-1, keepdims=True)
        dscore = jnp.where(allowed, probs * (dprobs - row_term), 0.0).astype(jnp.bfloat16)
        dqs.append(jnp.dot(dscore, kh, preferred_element_type=jnp.float32) * (1.0 / HD**0.5))
        dks.append(
            lax.dot_general(dscore, qh, (((0,), (0,)), ((), ())), preferred_element_type=jnp.float32)
            * (1.0 / HD**0.5)
        )
    at = pl.multiple_of(hp * width, width)
    dqkv_ref[:, pl.ds(at, width)] = jnp.concatenate(dqs, axis=1).astype(dqkv_ref.dtype)
    dqkv_ref[:, pl.ds(at + model_width, width)] = jnp.concatenate(dks, axis=1).astype(dqkv_ref.dtype)
    dqkv_ref[:, pl.ds(at + 2 * model_width, width)] = jnp.concatenate(dvs, axis=1).astype(dqkv_ref.dtype)


def mask_operands(segment_ids, valid):
    return (segment_ids[:, :, None], segment_ids[:, None, :], valid[:, None, :])


def attention_fwd(qkv, segment_ids, valid):
    rows, width3 = qkv.shape
    model_width = width3 // 3
    n_seq, seq_len = segment_ids.shape
    blk = 2 * HD
    n_hp = model_width // blk
    off = model_width // blk
    seg_spec = [
        pl.BlockSpec((None, seq_len, 1), lambda s, h: (s, 0, 0)),
        pl.BlockSpec((None, 1, seq_len), lambda s, h: (s, 0, 0)),
        pl.BlockSpec((None, 1, seq_len), lambda s, h: (s, 0, 0)),
    ]
    flops = 4 * n_seq * seq_len * seq_len * model_width
    return pl.pallas_call(
        attn_fwd_kernel,
        out_shape=jax.ShapeDtypeStruct((rows, model_width), jnp.bfloat16),
        grid=(n_seq, n_hp),
        in_specs=[
            pl.BlockSpec((seq_len, blk), lambda s, h: (s, h)),
            pl.BlockSpec((seq_len, blk), lambda s, h: (s, off + h)),
            pl.BlockSpec((seq_len, blk), lambda s, h: (s, 2 * off + h)),
        ]
        + seg_spec,
        out_specs=pl.BlockSpec((seq_len, blk), lambda s, h: (s, h)),
        cost_estimate=pl.CostEstimate(
            flops=flops,
            transcendentals=n_seq * seq_len * seq_len * (model_width // HD),
            bytes_accessed=qkv.size * 2 + rows * model_width * 2,
        ),
    )(qkv, qkv, qkv, *mask_operands(segment_ids, valid))


def attention_bwd(qkv, grad_o, segment_ids, valid):
    rows, width3 = qkv.shape
    model_width = width3 // 3
    n_seq, seq_len = segment_ids.shape
    blk = 2 * HD
    n_hp = model_width // blk
    off = model_width // blk
    seg_spec = [
        pl.BlockSpec((None, seq_len, 1), lambda s, h: (s, 0, 0)),
        pl.BlockSpec((None, 1, seq_len), lambda s, h: (s, 0, 0)),
        pl.BlockSpec((None, 1, seq_len), lambda s, h: (s, 0, 0)),
    ]
    flops = 10 * n_seq * seq_len * seq_len * model_width
    return pl.pallas_call(
        attn_bwd_kernel,
        out_shape=jax.ShapeDtypeStruct((rows, width3), jnp.bfloat16),
        grid=(n_seq, n_hp),
        in_specs=[
            pl.BlockSpec((seq_len, blk), lambda s, h: (s, h)),
            pl.BlockSpec((seq_len, blk), lambda s, h: (s, off + h)),
            pl.BlockSpec((seq_len, blk), lambda s, h: (s, 2 * off + h)),
            pl.BlockSpec((seq_len, blk), lambda s, h: (s, h)),
        ]
        + seg_spec,
        out_specs=pl.BlockSpec((seq_len, width3), lambda s, h: (s, 0)),
        cost_estimate=pl.CostEstimate(
            flops=flops,
            transcendentals=n_seq * seq_len * seq_len * (model_width // HD),
            bytes_accessed=qkv.size * 4 + rows * model_width * 2,
        ),
    )(qkv, qkv, qkv, grad_o, *mask_operands(segment_ids, valid))


MESH_ID = pl.DeviceIdType.MESH


def ring_maps(n_wide, n_narrow):
    n_dev = n_wide * n_narrow
    if (n_wide, n_narrow) == (8, 4):
        def pos_of(w, n):
            z, y, x, c = w // 2, w % 2, n // 2, n % 2
            q = 2 * x + (x + y) % 2
            k = 4 * q + z + (q % 2) * (3 - 2 * z)
            return 2 * k + c

        def coords_of(p):
            k, c = p // 2, p % 2
            q, r = k // 4, k % 4
            z = r + (q % 2) * (3 - 2 * r)
            x = q // 2
            y = (q % 2 + x) % 2
            return z * 2 + y, x * 2 + c

    else:
        def pos_of(w, n):
            return w * n_narrow + n

        def coords_of(p):
            return p // n_narrow, p % n_narrow

    return n_dev, pos_of, coords_of


def ring_reduce_scatter(parts, mesh_shape, after=(), collective_id=0):
    n_wide, n_narrow = mesh_shape
    n_dev, pos_of, coords_of = ring_maps(n_wide, n_narrow)
    specs = []
    for i, (a, rb, split) in enumerate(parts):
        cols = a.shape[1]
        if split:
            specs.append((i, 0, 0, cols // 2))
        else:
            specs.append((i, 0, 0, cols))
    for i, (a, rb, split) in enumerate(parts):
        if split:
            specs.append((i, 1, a.shape[1] // 2, a.shape[1] // 2))
    n_in = len(parts)
    n_after = len(after)
    n_sp = len(specs)
    last_step = n_dev - 2

    def kernel(*refs):
        ins = refs[:n_in]
        outs = refs[n_in + n_after : 2 * n_in + n_after]
        at = 2 * n_in + n_after
        bufs = refs[at : at + n_sp]
        locs = refs[at + n_sp : at + 2 * n_sp]
        send_sem, recv_sem, loc_sem, credit = refs[at + 2 * n_sp :]
        p = pos_of(lax.axis_index("wide"), lax.axis_index("narrow"))
        right = coords_of((p + 1) % n_dev)
        left = coords_of((p + n_dev - 1) % n_dev)
        nbr_send = (right, left)
        nbr_recv = (left, right)

        def rows_of(q, rb):
            cw, cn = coords_of(q % n_dev)
            start = (cw * n_narrow + cn) * rb
            if rb % 8 == 0:
                start = pl.multiple_of(start, 8)
            return pl.ds(start, rb)

        def remote(j, s):
            return pltpu.make_async_remote_copy(
                src_ref=bufs[j].at[s % 3],
                dst_ref=bufs[j].at[(s + 1) % 3],
                send_sem=send_sem.at[j, s % 3],
                recv_sem=recv_sem.at[j, (s + 1) % 3],
                device_id=nbr_send[specs[j][1]],
                device_id_type=MESH_ID,
            )

        def local(j, s):
            i, dirn, c0, cw = specs[j]
            q = (p + 2 * n_dev - s - 2) if dirn == 0 else (p + s + 2)
            return pltpu.make_async_copy(
                ins[i].at[rows_of(q, parts[i][1]), pl.ds(c0, cw)], locs[j].at[s % 2], loc_sem.at[j, s % 2]
            )

        barrier = pltpu.get_barrier_semaphore()
        for nb in (left, right):
            pl.semaphore_signal(barrier, 1, device_id=nb, device_id_type=MESH_ID)
        pl.semaphore_wait(barrier, 2)

        for j, (i, dirn, c0, cw) in enumerate(specs):
            q = p + n_dev - 1 if dirn == 0 else p + 1
            cp = pltpu.make_async_copy(
                ins[i].at[rows_of(q, parts[i][1]), pl.ds(c0, cw)], bufs[j].at[0], loc_sem.at[j, 1]
            )
            cp.start()
            cp.wait()
        for j in range(n_sp):
            remote(j, 0).start()
            local(j, 0).start()

        def step(s, carry):
            for j in range(n_sp):
                dirn = specs[j][1]
                local(j, s).wait()
                remote(j, s).wait_recv()
                nxt = (s + 1) % 3
                bufs[j][nxt] = bufs[j][nxt] + locs[j][s % 2]
                if j == 0 or specs[j - 1][1] != dirn:

                    @pl.when((s >= 1) & (s + 1 <= last_step))
                    def _():
                        pl.semaphore_wait(credit.at[dirn], 1)

                @pl.when(s + 1 <= last_step)
                def _():
                    remote(j, s + 1).start()
                    local(j, s + 1).start()

            for j in range(n_sp):
                remote(j, s).wait_send()
            for dirn in (0, 1):

                @pl.when(s <= last_step - 2)
                def _():
                    pl.semaphore_signal(
                        credit.at[dirn], 1, device_id=nbr_recv[dirn], device_id_type=MESH_ID
                    )

            return carry

        lax.fori_loop(0, last_step + 1, step, 0)
        fin = (last_step + 1) % 3
        for j, (i, dirn, c0, cw) in enumerate(specs):
            outs[i][:, pl.ds(c0, cw)] = bufs[j][fin]

    out_shape = [jax.ShapeDtypeStruct((rb, a.shape[1]), a.dtype) for (a, rb, _) in parts]
    scratch = [pltpu.VMEM((3, parts[i][1], cw), jnp.float32) for (i, _, _, cw) in specs]
    scratch += [pltpu.VMEM((2, parts[i][1], cw), jnp.float32) for (i, _, _, cw) in specs]
    scratch += [
        pltpu.SemaphoreType.DMA((n_sp, 3)),
        pltpu.SemaphoreType.DMA((n_sp, 3)),
        pltpu.SemaphoreType.DMA((n_sp, 2)),
        pltpu.SemaphoreType.REGULAR((2,)),
    ]
    total = sum(a.size * 4 for (a, _, _) in parts)
    return pl.pallas_call(
        kernel,
        out_shape=out_shape,
        in_specs=[pl.BlockSpec(memory_space=pl.ANY)] * (n_in + n_after),
        out_specs=[pl.BlockSpec(memory_space=pltpu.VMEM)] * n_in,
        scratch_shapes=scratch,
        compiler_params=pltpu.CompilerParams(
            collective_id=collective_id, has_side_effects=True, vmem_limit_bytes=48 * 1024 * 1024
        ),
        cost_estimate=pl.CostEstimate(flops=total // 4, transcendentals=0, bytes_accessed=2 * total),
    )(*[a for (a, _, _) in parts], *after)


def ring_all_gather(parts, mesh_shape, collective_id=1):
    n_wide, n_narrow = mesh_shape
    n_dev, pos_of, coords_of = ring_maps(n_wide, n_narrow)
    n_in = len(parts)
    steps = (n_dev // 2, n_dev - 1 - n_dev // 2)

    def kernel(*refs):
        ins = refs[:n_in]
        outs = refs[n_in : 2 * n_in]
        send_sem, recv_sem, loc_sem = refs[2 * n_in :]
        p = pos_of(lax.axis_index("wide"), lax.axis_index("narrow"))
        right = coords_of((p + 1) % n_dev)
        left = coords_of((p + n_dev - 1) % n_dev)
        nbr_send = (right, left)

        def rows_of(q, rb):
            cw, cn = coords_of(q % n_dev)
            return pl.ds(pl.multiple_of((cw * n_narrow + cn) * rb, rb), rb)

        def copy(i, dirn, s, q):
            view = outs[i].at[rows_of(q, parts[i].shape[0])]
            return pltpu.make_async_remote_copy(
                src_ref=view,
                dst_ref=view,
                send_sem=send_sem.at[dirn, i, s],
                recv_sem=recv_sem.at[dirn, i, s],
                device_id=nbr_send[dirn],
                device_id_type=MESH_ID,
            )

        def sent(i, dirn, s):
            return copy(i, dirn, s, (p + n_dev - s) if dirn == 0 else (p + s))

        def arriving(i, dirn, s):
            return copy(i, dirn, s, (p + n_dev - 1 - s) if dirn == 0 else (p + 1 + s))

        barrier = pltpu.get_barrier_semaphore()
        for nb in (left, right):
            pl.semaphore_signal(barrier, 1, device_id=nb, device_id_type=MESH_ID)
        pl.semaphore_wait(barrier, 2)

        for i in range(n_in):
            cp = pltpu.make_async_copy(ins[i], outs[i].at[rows_of(p, parts[i].shape[0])], loc_sem.at[i])
            cp.start()
            cp.wait()

        def step(s, carry):
            for dirn in (0, 1):

                @pl.when(s < steps[dirn])
                def _():
                    for i in range(n_in):
                        sent(i, dirn, s).start()

            for dirn in (0, 1):

                @pl.when(s < steps[dirn])
                def _():
                    for i in range(n_in):
                        arriving(i, dirn, s).wait_recv()

            return carry

        lax.fori_loop(0, steps[0], step, 0)

        def drain(s, carry):
            for dirn in (0, 1):

                @pl.when(s < steps[dirn])
                def _():
                    for i in range(n_in):
                        sent(i, dirn, s).wait_send()

            return carry

        lax.fori_loop(0, steps[0], drain, 0)

    out_shape = [jax.ShapeDtypeStruct((n_dev * a.shape[0], a.shape[1]), a.dtype) for a in parts]
    total = sum(n_dev * a.size * a.dtype.itemsize for a in parts)
    return pl.pallas_call(
        kernel,
        out_shape=out_shape,
        in_specs=[pl.BlockSpec(memory_space=pl.ANY)] * n_in,
        out_specs=[pl.BlockSpec(memory_space=pltpu.VMEM)] * n_in,
        scratch_shapes=[
            pltpu.SemaphoreType.DMA((2, n_in, steps[0])),
            pltpu.SemaphoreType.DMA((2, n_in, steps[0])),
            pltpu.SemaphoreType.DMA((n_in,)),
        ],
        compiler_params=pltpu.CompilerParams(collective_id=collective_id, has_side_effects=True),
        cost_estimate=pl.CostEstimate(flops=0, transcendentals=0, bytes_accessed=2 * total),
    )(*parts)


def pack_rows(pieces, width):
    flat = jnp.concatenate(pieces)
    return jnp.pad(flat, (0, width - flat.shape[0]))[None, :]


def split_owned(packed, sizes):
    out = []
    at = 0
    for size in sizes:
        out.append(packed[:, at : at + size].reshape(-1))
        at += size
    return out


def on_device(
    inputs,
    w_qkv,
    qv_bias,
    w_out,
    out_bias,
    ln1_gain,
    ln1_shift,
    ln2_gain,
    ln2_shift,
    w_up,
    up_bias,
    w_down,
    down_bias,
    segment_ids,
    valid,
    cotangent,
    mesh_shape=None,
):
    row_count = inputs.shape[0]
    model_width = inputs.shape[1]
    seq_count = segment_ids.shape[0]
    seq_len = segment_ids.shape[1]
    head_count = model_width // HD
    n_dev = mesh_shape[0] * mesh_shape[1]
    small = (qv_bias, out_bias, ln1_gain, ln1_shift, ln2_gain, ln2_shift, up_bias, down_bias)
    small_sizes = [a.shape[0] for a in small]
    n_small = sum(small_sizes)
    width_q = w_qkv.shape[1]
    rows_q = w_qkv.shape[0]
    rows_o = w_out.size // width_q
    rows_u = w_up.size // width_q
    up_view = 16
    half_u = w_up.shape[1] // 2
    ring_up = (
        mesh_shape == (8, 4)
        and w_up.size % (2 * up_view * width_q) == 0
        and w_out.size % (up_view * 128) == 0
    )
    if ring_up:
        up_sc = w_up[:, :half_u].reshape(-1, width_q)
        pieces = [w_qkv, up_sc]
    else:
        pieces = [w_qkv, w_out.reshape(rows_o, width_q), w_up.reshape(rows_u, width_q)]
    attn_buf = jnp.concatenate(pieces + [pack_rows(small, width_q)], axis=0)
    attn_all = lax.all_gather(attn_buf, ALL, axis=0, tiled=False)
    qkv_full = attn_all[:, :rows_q].reshape(-1, width_q)
    at = rows_q
    if ring_up:
        rows_h = up_sc.shape[0]
        up_a = attn_all[:, at : at + rows_h].reshape(-1, half_u)
        at = at + rows_h
        out_all, up_b = ring_all_gather(
            [w_out.reshape(up_view, -1), w_up[:, half_u:].reshape(up_view, -1)], mesh_shape
        )
        out_full = out_all.reshape(-1, model_width)
        up_full = jnp.concatenate([up_a, up_b.reshape(-1, half_u)], axis=1)
    else:
        out_full = attn_all[:, at : at + rows_o].reshape(-1, model_width)
        up_full = attn_all[:, at + rows_o : at + rows_o + rows_u].reshape(-1, w_up.shape[1])
        at = at + rows_o + rows_u
    small_full = split_owned(attn_all[:, at, :n_small], small_sizes)
    qv_full, outb_full, gain_one, shift_one, gain_two, shift_two, upb_full, downb_full = small_full
    down_full = lax.all_gather(w_down, ALL, axis=0, tiled=True)

    gain_one = gain_one.astype(jnp.float32)
    shift_one = shift_one.astype(jnp.float32)
    qv_full = qv_full.astype(jnp.float32)
    rows = inputs.astype(jnp.float32)
    normed_one, recip_one = norm_parts(rows)
    h_one = (normed_one * gain_one + shift_one).astype(jnp.bfloat16)
    qkv_rows = jnp.dot(h_one, qkv_full, preferred_element_type=jnp.float32)
    zero_bias = jnp.zeros((model_width,), jnp.float32)
    qkv_bias = jnp.concatenate([qv_full[:model_width], zero_bias, qv_full[model_width:]])
    qkv_b = (qkv_rows + qkv_bias).astype(jnp.bfloat16)
    attended = attention_fwd(qkv_b, segment_ids, valid)
    mid_rows = (
        rows
        + jnp.dot(attended, out_full, preferred_element_type=jnp.float32)
        + outb_full.astype(jnp.float32)
    )
    gain_two = gain_two.astype(jnp.float32)
    shift_two = shift_two.astype(jnp.float32)
    normed_two, recip_two = norm_parts(mid_rows)
    h_two = (normed_two * gain_two + shift_two).astype(jnp.bfloat16)
    upper = jnp.dot(h_two, up_full, preferred_element_type=jnp.float32) + upb_full.astype(
        jnp.float32
    )
    gelu_rows = jax.nn.gelu(upper, approximate=False).astype(jnp.bfloat16)
    out_rows = (
        mid_rows
        + jnp.dot(gelu_rows, down_full, preferred_element_type=jnp.float32)
        + downb_full.astype(jnp.float32)
    )
    block_out = out_rows.astype(jnp.bfloat16)
    dy_rows = cotangent.astype(jnp.float32)
    grad_wdown = jnp.einsum("tf,td->fd", gelu_rows, cotangent, preferred_element_type=jnp.float32)
    grad_bdown = col_sum(cotangent)
    grad_g = jnp.einsum("td,fd->tf", cotangent, down_full, preferred_element_type=jnp.float32)
    cdf_part = 0.5 * (1.0 + jax.scipy.special.erf(upper * 0.7071067811865476))
    pdf_part = jnp.exp(-0.5 * upper * upper) * 0.3989422804014327
    grad_u = (grad_g * (cdf_part + upper * pdf_part)).astype(jnp.bfloat16)
    grad_bup = col_sum(grad_u)
    grad_wup = jnp.einsum("td,tf->df", h_two, grad_u, preferred_element_type=jnp.float32)
    grad_h2 = jnp.einsum("tf,df->td", grad_u, up_full, preferred_element_type=jnp.float32)
    grad_g2 = jnp.sum(grad_h2 * normed_two, axis=0)
    grad_c2 = jnp.sum(grad_h2, axis=0)
    grad_mid = dy_rows + norm_back(grad_h2, gain_two, normed_two, recip_two)
    grad_a = grad_mid.astype(jnp.bfloat16)
    grad_wout = jnp.einsum("tc,td->cd", attended, grad_a, preferred_element_type=jnp.float32)
    grad_bout = col_sum(grad_a)
    grad_o = jnp.einsum("td,cd->tc", grad_a, out_full, preferred_element_type=jnp.float32).astype(
        jnp.bfloat16
    )
    grad_qkv = attention_bwd(qkv_b, grad_o, segment_ids, valid)
    grad_cols = col_sum(grad_qkv)
    grad_bqv = jnp.concatenate([grad_cols[:model_width], grad_cols[2 * model_width :]])
    grad_wqkv = jnp.einsum("td,te->de", h_one, grad_qkv, preferred_element_type=jnp.float32)
    grad_h1 = jnp.einsum("te,de->td", grad_qkv, qkv_full, preferred_element_type=jnp.float32)
    grad_g1 = jnp.sum(grad_h1 * normed_one, axis=0)
    grad_c1 = jnp.sum(grad_h1, axis=0)
    grad_inputs = grad_mid + norm_back(grad_h1, gain_one, normed_one, recip_one)

    small_grads = (grad_bqv, grad_bout, grad_g1, grad_c1, grad_g2, grad_c2, grad_bup, grad_bdown)
    owned = jnp.concatenate([g.reshape(n_dev, -1) for g in small_grads], axis=1)
    lanes = 128
    small_rows = 8 * pl.cdiv(pl.cdiv(n_small, lanes), 8)
    owned = jnp.pad(owned, ((0, 0), (0, small_rows * lanes - n_small))).reshape(-1, lanes)
    parts = [
        (grad_wqkv, w_qkv.shape[0], True),
        (grad_wout, w_out.shape[0], True),
        (grad_wup, w_up.shape[0], True),
        (owned, small_rows, False),
    ]
    down_sum = lax.psum_scatter(grad_wdown, ALL, scatter_dimension=0, tiled=True)
    if all(rb % 8 == 0 and a.shape[1] % 256 == 0 for (a, rb, _) in parts[:3]):
        sums = ring_reduce_scatter(parts, mesh_shape, after=(grad_inputs, block_out))
    else:
        sums = [lax.psum_scatter(a, ALL, scatter_dimension=0, tiled=True) for (a, _, _) in parts]
    sums = list(sums[:3]) + [down_sum] + list(sums[3:])
    small_sums = split_owned(sums[4].reshape(1, -1), small_sizes)
    bqv, bout, g1, c1, g2, c2, bup, bdown = small_sums
    return (
        block_out,
        grad_inputs,
        sums[0],
        bqv,
        sums[1],
        bout,
        g1,
        c1,
        g2,
        c2,
        sums[2],
        bup,
        sums[3],
        bdown,
    )


def solution(mesh):
    in_specs = (
        P(("wide", "narrow"), None),
        P(("wide", "narrow"), None),
        P(("wide", "narrow")),
        P(("wide", "narrow"), None),
        P(("wide", "narrow")),
        P(("wide", "narrow")),
        P(("wide", "narrow")),
        P(("wide", "narrow")),
        P(("wide", "narrow")),
        P(("wide", "narrow"), None),
        P(("wide", "narrow")),
        P(("wide", "narrow"), None),
        P(("wide", "narrow")),
        P(("wide", "narrow"), None),
        P(("wide", "narrow"), None),
        P(("wide", "narrow"), None),
    )
    out_specs = (
        P(("wide", "narrow"), None),
        P(("wide", "narrow"), None),
        P(("wide", "narrow"), None),
        P(("wide", "narrow")),
        P(("wide", "narrow"), None),
        P(("wide", "narrow")),
        P(("wide", "narrow")),
        P(("wide", "narrow")),
        P(("wide", "narrow")),
        P(("wide", "narrow")),
        P(("wide", "narrow"), None),
        P(("wide", "narrow")),
        P(("wide", "narrow"), None),
        P(("wide", "narrow")),
    )
    body = functools.partial(on_device, mesh_shape=(mesh.shape["wide"], mesh.shape["narrow"]))
    return jax.shard_map(
        body, mesh=mesh, in_specs=in_specs, out_specs=out_specs, check_vma=False
    )
```

```python
import functools
import jax
import jax.numpy as jnp
from jax import lax
from jax.experimental import pallas as pl
from jax.experimental.pallas import tpu as pltpu
from jax.sharding import PartitionSpec as P

HD = 64
ALL = ("wide", "narrow")

EPSILON = 1e-06


def norm_parts(rows):
    center = rows - jnp.mean(rows, axis=-1, keepdims=True)
    recip = lax.rsqrt(jnp.mean(center * center, axis=-1, keepdims=True) + EPSILON)
    return (center * recip, recip)


def norm_back(grad_h, gain, normed, recip):
    scaled = grad_h * gain
    return recip * (
        scaled
        - jnp.mean(scaled, axis=-1, keepdims=True)
        - normed * jnp.mean(scaled * normed, axis=-1, keepdims=True)
    )


def col_sum(rows):
    return jnp.sum(rows.astype(jnp.float32), axis=0)


def seg_mask(seg_col, seg_row, val_row, n):
    rows = lax.broadcasted_iota(jnp.int32, (n, n), 0)
    cols = lax.broadcasted_iota(jnp.int32, (n, n), 1)
    return (seg_col == seg_row) & ((val_row == 1) | (rows == cols))


def soft_rows(qh, kh, allowed):
    scores = lax.dot_general(qh, kh, (((1,), (1,)), ((), ())), preferred_element_type=jnp.float32)
    scores = jnp.where(allowed, scores * (1.0 / HD**0.5), -1e30)
    top = jnp.max(scores, axis=-1, keepdims=True)
    expo = jnp.exp(scores - top)
    return expo * (1.0 / jnp.sum(expo, axis=-1, keepdims=True))


def attn_fwd_kernel(q_ref, k_ref, v_ref, sc_ref, sr_ref, vr_ref, o_ref):
    n = q_ref.shape[0]
    allowed = seg_mask(sc_ref[...], sr_ref[...], vr_ref[...], n)
    outs = []
    for j in range(q_ref.shape[1] // HD):
        cols = slice(j * HD, (j + 1) * HD)
        probs = soft_rows(q_ref[:, cols], k_ref[:, cols], allowed).astype(jnp.bfloat16)
        outs.append(jnp.dot(probs, v_ref[:, cols], preferred_element_type=jnp.float32))
    o_ref[...] = jnp.concatenate(outs, axis=1).astype(o_ref.dtype)


def attn_bwd_kernel(q_ref, k_ref, v_ref, do_ref, sc_ref, sr_ref, vr_ref, dqkv_ref):
    n = q_ref.shape[0]
    width = q_ref.shape[1]
    hp = pl.program_id(1)
    model_width = dqkv_ref.shape[1] // 3
    allowed = seg_mask(sc_ref[...], sr_ref[...], vr_ref[...], n)
    dqs, dks, dvs = [], [], []
    for j in range(width // HD):
        cols = slice(j * HD, (j + 1) * HD)
        qh, kh, vh, doh = q_ref[:, cols], k_ref[:, cols], v_ref[:, cols], do_ref[:, cols]
        probs = soft_rows(qh, kh, allowed)
        dvs.append(
            lax.dot_general(probs.astype(jnp.bfloat16), doh, (((0,), (0,)), ((), ())),
                            preferred_element_type=jnp.float32)
        )
        dprobs = lax.dot_general(doh, vh, (((1,), (1,)), ((), ())), preferred_element_type=jnp.float32)
        row_term = jnp.sum(probs * dprobs, axis=-1, keepdims=True)
        dscore = jnp.where(allowed, probs * (dprobs - row_term), 0.0).astype(jnp.bfloat16)
        dqs.append(jnp.dot(dscore, kh, preferred_element_type=jnp.float32) * (1.0 / HD**0.5))
        dks.append(
            lax.dot_general(dscore, qh, (((0,), (0,)), ((), ())), preferred_element_type=jnp.float32)
            * (1.0 / HD**0.5)
        )
    at = pl.multiple_of(hp * width, width)
    dqkv_ref[:, pl.ds(at, width)] = jnp.concatenate(dqs, axis=1).astype(dqkv_ref.dtype)
    dqkv_ref[:, pl.ds(at + model_width, width)] = jnp.concatenate(dks, axis=1).astype(dqkv_ref.dtype)
    dqkv_ref[:, pl.ds(at + 2 * model_width, width)] = jnp.concatenate(dvs, axis=1).astype(dqkv_ref.dtype)


def mask_operands(segment_ids, valid):
    return (segment_ids[:, :, None], segment_ids[:, None, :], valid[:, None, :])


def attention_fwd(qkv, segment_ids, valid):
    rows, width3 = qkv.shape
    model_width = width3 // 3
    n_seq, seq_len = segment_ids.shape
    blk = 2 * HD
    n_hp = model_width // blk
    off = model_width // blk
    seg_spec = [
        pl.BlockSpec((None, seq_len, 1), lambda s, h: (s, 0, 0)),
        pl.BlockSpec((None, 1, seq_len), lambda s, h: (s, 0, 0)),
        pl.BlockSpec((None, 1, seq_len), lambda s, h: (s, 0, 0)),
    ]
    flops = 4 * n_seq * seq_len * seq_len * model_width
    return pl.pallas_call(
        attn_fwd_kernel,
        out_shape=jax.ShapeDtypeStruct((rows, model_width), jnp.bfloat16),
        grid=(n_seq, n_hp),
        in_specs=[
            pl.BlockSpec((seq_len, blk), lambda s, h: (s, h)),
            pl.BlockSpec((seq_len, blk), lambda s, h: (s, off + h)),
            pl.BlockSpec((seq_len, blk), lambda s, h: (s, 2 * off + h)),
        ]
        + seg_spec,
        out_specs=pl.BlockSpec((seq_len, blk), lambda s, h: (s, h)),
        cost_estimate=pl.CostEstimate(
            flops=flops,
            transcendentals=n_seq * seq_len * seq_len * (model_width // HD),
            bytes_accessed=qkv.size * 2 + rows * model_width * 2,
        ),
    )(qkv, qkv, qkv, *mask_operands(segment_ids, valid))


def attention_bwd(qkv, grad_o, segment_ids, valid):
    rows, width3 = qkv.shape
    model_width = width3 // 3
    n_seq, seq_len = segment_ids.shape
    blk = 2 * HD
    n_hp = model_width // blk
    off = model_width // blk
    seg_spec = [
        pl.BlockSpec((None, seq_len, 1), lambda s, h: (s, 0, 0)),
        pl.BlockSpec((None, 1, seq_len), lambda s, h: (s, 0, 0)),
        pl.BlockSpec((None, 1, seq_len), lambda s, h: (s, 0, 0)),
    ]
    flops = 10 * n_seq * seq_len * seq_len * model_width
    return pl.pallas_call(
        attn_bwd_kernel,
        out_shape=jax.ShapeDtypeStruct((rows, width3), jnp.bfloat16),
        grid=(n_seq, n_hp),
        in_specs=[
            pl.BlockSpec((seq_len, blk), lambda s, h: (s, h)),
            pl.BlockSpec((seq_len, blk), lambda s, h: (s, off + h)),
            pl.BlockSpec((seq_len, blk), lambda s, h: (s, 2 * off + h)),
            pl.BlockSpec((seq_len, blk), lambda s, h: (s, h)),
        ]
        + seg_spec,
        out_specs=pl.BlockSpec((seq_len, width3), lambda s, h: (s, 0)),
        cost_estimate=pl.CostEstimate(
            flops=flops,
            transcendentals=n_seq * seq_len * seq_len * (model_width // HD),
            bytes_accessed=qkv.size * 4 + rows * model_width * 2,
        ),
    )(qkv, qkv, qkv, grad_o, *mask_operands(segment_ids, valid))


MESH_ID = pl.DeviceIdType.MESH


def ring_maps(n_wide, n_narrow):
    n_dev = n_wide * n_narrow
    if (n_wide, n_narrow) == (8, 4):
        def pos_of(w, n):
            z, y, x, c = w // 2, w % 2, n // 2, n % 2
            q = 2 * x + (x + y) % 2
            k = 4 * q + z + (q % 2) * (3 - 2 * z)
            return 2 * k + c

        def coords_of(p):
            k, c = p // 2, p % 2
            q, r = k // 4, k % 4
            z = r + (q % 2) * (3 - 2 * r)
            x = q // 2
            y = (q % 2 + x) % 2
            return z * 2 + y, x * 2 + c

    else:
        def pos_of(w, n):
            return w * n_narrow + n

        def coords_of(p):
            return p // n_narrow, p % n_narrow

    return n_dev, pos_of, coords_of


def ring_reduce_scatter(parts, mesh_shape, after=(), collective_id=0):
    n_wide, n_narrow = mesh_shape
    n_dev, pos_of, coords_of = ring_maps(n_wide, n_narrow)
    specs = []
    for i, (a, rb, split) in enumerate(parts):
        cols = a.shape[1]
        if split:
            specs.append((i, 0, 0, cols // 2))
        else:
            specs.append((i, 0, 0, cols))
    for i, (a, rb, split) in enumerate(parts):
        if split:
            specs.append((i, 1, a.shape[1] // 2, a.shape[1] // 2))
    n_in = len(parts)
    n_after = len(after)
    n_sp = len(specs)
    last_step = n_dev - 2

    def kernel(*refs):
        ins = refs[:n_in]
        outs = refs[n_in + n_after : 2 * n_in + n_after]
        at = 2 * n_in + n_after
        bufs = refs[at : at + n_sp]
        locs = refs[at + n_sp : at + 2 * n_sp]
        send_sem, recv_sem, loc_sem, credit = refs[at + 2 * n_sp :]
        p = pos_of(lax.axis_index("wide"), lax.axis_index("narrow"))
        right = coords_of((p + 1) % n_dev)
        left = coords_of((p + n_dev - 1) % n_dev)
        nbr_send = (right, left)
        nbr_recv = (left, right)

        def rows_of(q, rb):
            cw, cn = coords_of(q % n_dev)
            start = (cw * n_narrow + cn) * rb
            if rb % 8 == 0:
                start = pl.multiple_of(start, 8)
            return pl.ds(start, rb)

        def remote(j, s):
            return pltpu.make_async_remote_copy(
                src_ref=bufs[j].at[s % 3],
                dst_ref=bufs[j].at[(s + 1) % 3],
                send_sem=send_sem.at[j, s % 3],
                recv_sem=recv_sem.at[j, (s + 1) % 3],
                device_id=nbr_send[specs[j][1]],
                device_id_type=MESH_ID,
            )

        def local(j, s):
            i, dirn, c0, cw = specs[j]
            q = (p + 2 * n_dev - s - 2) if dirn == 0 else (p + s + 2)
            return pltpu.make_async_copy(
                ins[i].at[rows_of(q, parts[i][1]), pl.ds(c0, cw)], locs[j].at[s % 2], loc_sem.at[j, s % 2]
            )

        barrier = pltpu.get_barrier_semaphore()
        for nb in (left, right):
            pl.semaphore_signal(barrier, 1, device_id=nb, device_id_type=MESH_ID)
        pl.semaphore_wait(barrier, 2)

        for j, (i, dirn, c0, cw) in enumerate(specs):
            q = p + n_dev - 1 if dirn == 0 else p + 1
            cp = pltpu.make_async_copy(
                ins[i].at[rows_of(q, parts[i][1]), pl.ds(c0, cw)], bufs[j].at[0], loc_sem.at[j, 1]
            )
            cp.start()
            cp.wait()
        for j in range(n_sp):
            remote(j, 0).start()
            local(j, 0).start()

        def step(s, carry):
            for j in range(n_sp):
                dirn = specs[j][1]
                local(j, s).wait()
                remote(j, s).wait_recv()
                nxt = (s + 1) % 3
                bufs[j][nxt] = bufs[j][nxt] + locs[j][s % 2]
                if j == 0 or specs[j - 1][1] != dirn:

                    @pl.when((s >= 1) & (s + 1 <= last_step))
                    def _():
                        pl.semaphore_wait(credit.at[dirn], 1)

                @pl.when(s + 1 <= last_step)
                def _():
                    remote(j, s + 1).start()
                    local(j, s + 1).start()

            for j in range(n_sp):
                remote(j, s).wait_send()
            for dirn in (0, 1):

                @pl.when(s <= last_step - 2)
                def _():
                    pl.semaphore_signal(
                        credit.at[dirn], 1, device_id=nbr_recv[dirn], device_id_type=MESH_ID
                    )

            return carry

        lax.fori_loop(0, last_step + 1, step, 0)
        fin = (last_step + 1) % 3
        for j, (i, dirn, c0, cw) in enumerate(specs):
            outs[i][:, pl.ds(c0, cw)] = bufs[j][fin]

    out_shape = [jax.ShapeDtypeStruct((rb, a.shape[1]), a.dtype) for (a, rb, _) in parts]
    scratch = [pltpu.VMEM((3, parts[i][1], cw), jnp.float32) for (i, _, _, cw) in specs]
    scratch += [pltpu.VMEM((2, parts[i][1], cw), jnp.float32) for (i, _, _, cw) in specs]
    scratch += [
        pltpu.SemaphoreType.DMA((n_sp, 3)),
        pltpu.SemaphoreType.DMA((n_sp, 3)),
        pltpu.SemaphoreType.DMA((n_sp, 2)),
        pltpu.SemaphoreType.REGULAR((2,)),
    ]
    total = sum(a.size * 4 for (a, _, _) in parts)
    return pl.pallas_call(
        kernel,
        out_shape=out_shape,
        in_specs=[pl.BlockSpec(memory_space=pl.ANY)] * (n_in + n_after),
        out_specs=[pl.BlockSpec(memory_space=pltpu.VMEM)] * n_in,
        scratch_shapes=scratch,
        compiler_params=pltpu.CompilerParams(
            collective_id=collective_id, has_side_effects=True, vmem_limit_bytes=48 * 1024 * 1024
        ),
        cost_estimate=pl.CostEstimate(flops=total // 4, transcendentals=0, bytes_accessed=2 * total),
    )(*[a for (a, _, _) in parts], *after)


def ring_all_gather(parts, mesh_shape, collective_id=1):
    n_wide, n_narrow = mesh_shape
    n_dev, pos_of, coords_of = ring_maps(n_wide, n_narrow)
    n_in = len(parts)
    steps = (n_dev // 2, n_dev - 1 - n_dev // 2)

    def kernel(*refs):
        ins = refs[:n_in]
        outs = refs[n_in : 2 * n_in]
        send_sem, recv_sem, loc_sem = refs[2 * n_in :]
        p = pos_of(lax.axis_index("wide"), lax.axis_index("narrow"))
        right = coords_of((p + 1) % n_dev)
        left = coords_of((p + n_dev - 1) % n_dev)
        nbr_send = (right, left)

        def rows_of(q, rb):
            cw, cn = coords_of(q % n_dev)
            return pl.ds(pl.multiple_of((cw * n_narrow + cn) * rb, rb), rb)

        def copy(i, dirn, s, q):
            view = outs[i].at[rows_of(q, parts[i].shape[0])]
            return pltpu.make_async_remote_copy(
                src_ref=view,
                dst_ref=view,
                send_sem=send_sem.at[dirn, i, s],
                recv_sem=recv_sem.at[dirn, i, s],
                device_id=nbr_send[dirn],
                device_id_type=MESH_ID,
            )

        def sent(i, dirn, s):
            return copy(i, dirn, s, (p + n_dev - s) if dirn == 0 else (p + s))

        def arriving(i, dirn, s):
            return copy(i, dirn, s, (p + n_dev - 1 - s) if dirn == 0 else (p + 1 + s))

        barrier = pltpu.get_barrier_semaphore()
        for nb in (left, right):
            pl.semaphore_signal(barrier, 1, device_id=nb, device_id_type=MESH_ID)
        pl.semaphore_wait(barrier, 2)

        for i in range(n_in):
            cp = pltpu.make_async_copy(ins[i], outs[i].at[rows_of(p, parts[i].shape[0])], loc_sem.at[i])
            cp.start()
            cp.wait()

        def step(s, carry):
            for dirn in (0, 1):

                @pl.when(s < steps[dirn])
                def _():
                    for i in range(n_in):

                        @pl.when(s >= 1)
                        def _():
                            arriving(i, dirn, s - 1).wait_recv()

                        sent(i, dirn, s).start()

            return carry

        lax.fori_loop(0, steps[0], step, 0)
        for dirn in (0, 1):
            for i in range(n_in):
                arriving(i, dirn, steps[dirn] - 1).wait_recv()

        def drain(s, carry):
            for dirn in (0, 1):

                @pl.when(s < steps[dirn])
                def _():
                    for i in range(n_in):
                        sent(i, dirn, s).wait_send()

            return carry

        lax.fori_loop(0, steps[0], drain, 0)

    out_shape = [jax.ShapeDtypeStruct((n_dev * a.shape[0], a.shape[1]), a.dtype) for a in parts]
    total = sum(n_dev * a.size * a.dtype.itemsize for a in parts)
    return pl.pallas_call(
        kernel,
        out_shape=out_shape,
        in_specs=[pl.BlockSpec(memory_space=pl.ANY)] * n_in,
        out_specs=[pl.BlockSpec(memory_space=pltpu.VMEM)] * n_in,
        scratch_shapes=[
            pltpu.SemaphoreType.DMA((2, n_in, steps[0])),
            pltpu.SemaphoreType.DMA((2, n_in, steps[0])),
            pltpu.SemaphoreType.DMA((n_in,)),
        ],
        compiler_params=pltpu.CompilerParams(collective_id=collective_id, has_side_effects=True),
        cost_estimate=pl.CostEstimate(flops=0, transcendentals=0, bytes_accessed=2 * total),
    )(*parts)


def pack_rows(pieces, width):
    flat = jnp.concatenate(pieces)
    return jnp.pad(flat, (0, width - flat.shape[0]))[None, :]


def split_owned(packed, sizes):
    out = []
    at = 0
    for size in sizes:
        out.append(packed[:, at : at + size].reshape(-1))
        at += size
    return out


def on_device(
    inputs,
    w_qkv,
    qv_bias,
    w_out,
    out_bias,
    ln1_gain,
    ln1_shift,
    ln2_gain,
    ln2_shift,
    w_up,
    up_bias,
    w_down,
    down_bias,
    segment_ids,
    valid,
    cotangent,
    mesh_shape=None,
):
    row_count = inputs.shape[0]
    model_width = inputs.shape[1]
    seq_count = segment_ids.shape[0]
    seq_len = segment_ids.shape[1]
    head_count = model_width // HD
    n_dev = mesh_shape[0] * mesh_shape[1]
    small = (qv_bias, out_bias, ln1_gain, ln1_shift, ln2_gain, ln2_shift, up_bias, down_bias)
    small_sizes = [a.shape[0] for a in small]
    n_small = sum(small_sizes)
    width_q = w_qkv.shape[1]
    rows_q = w_qkv.shape[0]
    rows_o = w_out.size // width_q
    rows_u = w_up.size // width_q
    up_view = 16
    ring_up = mesh_shape == (8, 4) and w_up.size % (2 * up_view * 128) == 0
    pieces = [w_qkv, w_out.reshape(rows_o, width_q)]
    if not ring_up:
        pieces.append(w_up.reshape(rows_u, width_q))
    attn_buf = jnp.concatenate(pieces + [pack_rows(small, width_q)], axis=0)
    attn_all = lax.all_gather(attn_buf, ALL, axis=0, tiled=False)
    qkv_full = attn_all[:, :rows_q].reshape(-1, width_q)
    out_full = attn_all[:, rows_q : rows_q + rows_o].reshape(-1, model_width)
    at = rows_q + rows_o
    if ring_up:
        up_v = w_up.reshape(up_view, -1)
        half_v = up_v.shape[1] // 2
        up_a, up_b = ring_all_gather([up_v[:, :half_v], up_v[:, half_v:]], mesh_shape)
        up_full = jnp.concatenate([up_a, up_b], axis=1).reshape(-1, w_up.shape[1])
    else:
        up_full = attn_all[:, at : at + rows_u].reshape(-1, w_up.shape[1])
        at = at + rows_u
    small_full = split_owned(attn_all[:, at, :n_small], small_sizes)
    qv_full, outb_full, gain_one, shift_one, gain_two, shift_two, upb_full, downb_full = small_full
    down_full = lax.all_gather(w_down, ALL, axis=0, tiled=True)

    gain_one = gain_one.astype(jnp.float32)
    shift_one = shift_one.astype(jnp.float32)
    qv_full = qv_full.astype(jnp.float32)
    rows = inputs.astype(jnp.float32)
    normed_one, recip_one = norm_parts(rows)
    h_one = (normed_one * gain_one + shift_one).astype(jnp.bfloat16)
    qkv_rows = jnp.dot(h_one, qkv_full, preferred_element_type=jnp.float32)
    zero_bias = jnp.zeros((model_width,), jnp.float32)
    qkv_bias = jnp.concatenate([qv_full[:model_width], zero_bias, qv_full[model_width:]])
    qkv_b = (qkv_rows + qkv_bias).astype(jnp.bfloat16)
    attended = attention_fwd(qkv_b, segment_ids, valid)
    mid_rows = (
        rows
        + jnp.dot(attended, out_full, preferred_element_type=jnp.float32)
        + outb_full.astype(jnp.float32)
    )
    gain_two = gain_two.astype(jnp.float32)
    shift_two = shift_two.astype(jnp.float32)
    normed_two, recip_two = norm_parts(mid_rows)
    h_two = (normed_two * gain_two + shift_two).astype(jnp.bfloat16)
    upper = jnp.dot(h_two, up_full, preferred_element_type=jnp.float32) + upb_full.astype(
        jnp.float32
    )
    gelu_rows = jax.nn.gelu(upper, approximate=False).astype(jnp.bfloat16)
    out_rows = (
        mid_rows
        + jnp.dot(gelu_rows, down_full, preferred_element_type=jnp.float32)
        + downb_full.astype(jnp.float32)
    )
    block_out = out_rows.astype(jnp.bfloat16)
    dy_rows = cotangent.astype(jnp.float32)
    grad_wdown = jnp.einsum("tf,td->fd", gelu_rows, cotangent, preferred_element_type=jnp.float32)
    grad_bdown = col_sum(cotangent)
    grad_g = jnp.einsum("td,fd->tf", cotangent, down_full, preferred_element_type=jnp.float32)
    cdf_part = 0.5 * (1.0 + jax.scipy.special.erf(upper * 0.7071067811865476))
    pdf_part = jnp.exp(-0.5 * upper * upper) * 0.3989422804014327
    grad_u = (grad_g * (cdf_part + upper * pdf_part)).astype(jnp.bfloat16)
    grad_bup = col_sum(grad_u)
    grad_wup = jnp.einsum("td,tf->df", h_two, grad_u, preferred_element_type=jnp.float32)
    grad_h2 = jnp.einsum("tf,df->td", grad_u, up_full, preferred_element_type=jnp.float32)
    grad_g2 = jnp.sum(grad_h2 * normed_two, axis=0)
    grad_c2 = jnp.sum(grad_h2, axis=0)
    grad_mid = dy_rows + norm_back(grad_h2, gain_two, normed_two, recip_two)
    grad_a = grad_mid.astype(jnp.bfloat16)
    grad_wout = jnp.einsum("tc,td->cd", attended, grad_a, preferred_element_type=jnp.float32)
    grad_bout = col_sum(grad_a)
    grad_o = jnp.einsum("td,cd->tc", grad_a, out_full, preferred_element_type=jnp.float32).astype(
        jnp.bfloat16
    )
    grad_qkv = attention_bwd(qkv_b, grad_o, segment_ids, valid)
    grad_cols = col_sum(grad_qkv)
    grad_bqv = jnp.concatenate([grad_cols[:model_width], grad_cols[2 * model_width :]])
    grad_wqkv = jnp.einsum("td,te->de", h_one, grad_qkv, preferred_element_type=jnp.float32)
    grad_h1 = jnp.einsum("te,de->td", grad_qkv, qkv_full, preferred_element_type=jnp.float32)
    grad_g1 = jnp.sum(grad_h1 * normed_one, axis=0)
    grad_c1 = jnp.sum(grad_h1, axis=0)
    grad_inputs = grad_mid + norm_back(grad_h1, gain_one, normed_one, recip_one)

    small_grads = (grad_bqv, grad_bout, grad_g1, grad_c1, grad_g2, grad_c2, grad_bup, grad_bdown)
    owned = jnp.concatenate([g.reshape(n_dev, -1) for g in small_grads], axis=1)
    lanes = 128
    small_rows = 8 * pl.cdiv(pl.cdiv(n_small, lanes), 8)
    owned = jnp.pad(owned, ((0, 0), (0, small_rows * lanes - n_small))).reshape(-1, lanes)
    parts = [
        (grad_wqkv, w_qkv.shape[0], True),
        (grad_wout, w_out.shape[0], True),
        (grad_wup, w_up.shape[0], True),
        (owned, small_rows, False),
    ]
    down_sum = lax.psum_scatter(grad_wdown, ALL, scatter_dimension=0, tiled=True)
    if all(rb % 8 == 0 and a.shape[1] % 256 == 0 for (a, rb, _) in parts[:3]):
        sums = ring_reduce_scatter(parts, mesh_shape, after=(grad_inputs, block_out))
    else:
        sums = [lax.psum_scatter(a, ALL, scatter_dimension=0, tiled=True) for (a, _, _) in parts]
    sums = list(sums[:3]) + [down_sum] + list(sums[3:])
    small_sums = split_owned(sums[4].reshape(1, -1), small_sizes)
    bqv, bout, g1, c1, g2, c2, bup, bdown = small_sums
    return (
        block_out,
        grad_inputs,
        sums[0],
        bqv,
        sums[1],
        bout,
        g1,
        c1,
        g2,
        c2,
        sums[2],
        bup,
        sums[3],
        bdown,
    )


def solution(mesh):
    in_specs = (
        P(("wide", "narrow"), None),
        P(("wide", "narrow"), None),
        P(("wide", "narrow")),
        P(("wide", "narrow"), None),
        P(("wide", "narrow")),
        P(("wide", "narrow")),
        P(("wide", "narrow")),
        P(("wide", "narrow")),
        P(("wide", "narrow")),
        P(("wide", "narrow"), None),
        P(("wide", "narrow")),
        P(("wide", "narrow"), None),
        P(("wide", "narrow")),
        P(("wide", "narrow"), None),
        P(("wide", "narrow"), None),
        P(("wide", "narrow"), None),
    )
    out_specs = (
        P(("wide", "narrow"), None),
        P(("wide", "narrow"), None),
        P(("wide", "narrow"), None),
        P(("wide", "narrow")),
        P(("wide", "narrow"), None),
        P(("wide", "narrow")),
        P(("wide", "narrow")),
        P(("wide", "narrow")),
        P(("wide", "narrow")),
        P(("wide", "narrow")),
        P(("wide", "narrow"), None),
        P(("wide", "narrow")),
        P(("wide", "narrow"), None),
        P(("wide", "narrow")),
    )
    body = functools.partial(on_device, mesh_shape=(mesh.shape["wide"], mesh.shape["narrow"]))
    return jax.shard_map(
        body, mesh=mesh, in_specs=in_specs, out_specs=out_specs, check_vma=False
    )
```

```python
import functools
import jax
import jax.numpy as jnp
from jax import lax
from jax.experimental import pallas as pl
from jax.experimental.pallas import tpu as pltpu
from jax.sharding import PartitionSpec as P

HD = 64
ALL = ("wide", "narrow")

EPSILON = 1e-06


def norm_parts(rows):
    center = rows - jnp.mean(rows, axis=-1, keepdims=True)
    recip = lax.rsqrt(jnp.mean(center * center, axis=-1, keepdims=True) + EPSILON)
    return (center * recip, recip)


def norm_back(grad_h, gain, normed, recip):
    scaled = grad_h * gain
    return recip * (
        scaled
        - jnp.mean(scaled, axis=-1, keepdims=True)
        - normed * jnp.mean(scaled * normed, axis=-1, keepdims=True)
    )


def col_sum(rows):
    return jnp.sum(rows.astype(jnp.float32), axis=0)


def seg_mask(seg_col, seg_row, val_row, n):
    rows = lax.broadcasted_iota(jnp.int32, (n, n), 0)
    cols = lax.broadcasted_iota(jnp.int32, (n, n), 1)
    return (seg_col == seg_row) & ((val_row == 1) | (rows == cols))


def soft_rows(qh, kh, allowed):
    scores = lax.dot_general(qh, kh, (((1,), (1,)), ((), ())), preferred_element_type=jnp.float32)
    scores = jnp.where(allowed, scores * (1.0 / HD**0.5), -1e30)
    top = jnp.max(scores, axis=-1, keepdims=True)
    expo = jnp.exp(scores - top)
    return expo * (1.0 / jnp.sum(expo, axis=-1, keepdims=True))


def attn_fwd_kernel(q_ref, k_ref, v_ref, sc_ref, sr_ref, vr_ref, o_ref):
    n = q_ref.shape[0]
    allowed = seg_mask(sc_ref[...], sr_ref[...], vr_ref[...], n)
    outs = []
    for j in range(q_ref.shape[1] // HD):
        cols = slice(j * HD, (j + 1) * HD)
        probs = soft_rows(q_ref[:, cols], k_ref[:, cols], allowed).astype(jnp.bfloat16)
        outs.append(jnp.dot(probs, v_ref[:, cols], preferred_element_type=jnp.float32))
    o_ref[...] = jnp.concatenate(outs, axis=1).astype(o_ref.dtype)


def attn_bwd_kernel(q_ref, k_ref, v_ref, do_ref, sc_ref, sr_ref, vr_ref, dqkv_ref):
    n = q_ref.shape[0]
    width = q_ref.shape[1]
    hp = pl.program_id(1)
    model_width = dqkv_ref.shape[1] // 3
    allowed = seg_mask(sc_ref[...], sr_ref[...], vr_ref[...], n)
    dqs, dks, dvs = [], [], []
    for j in range(width // HD):
        cols = slice(j * HD, (j + 1) * HD)
        qh, kh, vh, doh = q_ref[:, cols], k_ref[:, cols], v_ref[:, cols], do_ref[:, cols]
        probs = soft_rows(qh, kh, allowed)
        dvs.append(
            lax.dot_general(probs.astype(jnp.bfloat16), doh, (((0,), (0,)), ((), ())),
                            preferred_element_type=jnp.float32)
        )
        dprobs = lax.dot_general(doh, vh, (((1,), (1,)), ((), ())), preferred_element_type=jnp.float32)
        row_term = jnp.sum(probs * dprobs, axis=-1, keepdims=True)
        dscore = jnp.where(allowed, probs * (dprobs - row_term), 0.0).astype(jnp.bfloat16)
        dqs.append(jnp.dot(dscore, kh, preferred_element_type=jnp.float32) * (1.0 / HD**0.5))
        dks.append(
            lax.dot_general(dscore, qh, (((0,), (0,)), ((), ())), preferred_element_type=jnp.float32)
            * (1.0 / HD**0.5)
        )
    at = pl.multiple_of(hp * width, width)
    dqkv_ref[:, pl.ds(at, width)] = jnp.concatenate(dqs, axis=1).astype(dqkv_ref.dtype)
    dqkv_ref[:, pl.ds(at + model_width, width)] = jnp.concatenate(dks, axis=1).astype(dqkv_ref.dtype)
    dqkv_ref[:, pl.ds(at + 2 * model_width, width)] = jnp.concatenate(dvs, axis=1).astype(dqkv_ref.dtype)


def mask_operands(segment_ids, valid):
    return (segment_ids[:, :, None], segment_ids[:, None, :], valid[:, None, :])


def attention_fwd(qkv, segment_ids, valid):
    rows, width3 = qkv.shape
    model_width = width3 // 3
    n_seq, seq_len = segment_ids.shape
    blk = 2 * HD
    n_hp = model_width // blk
    off = model_width // blk
    seg_spec = [
        pl.BlockSpec((None, seq_len, 1), lambda s, h: (s, 0, 0)),
        pl.BlockSpec((None, 1, seq_len), lambda s, h: (s, 0, 0)),
        pl.BlockSpec((None, 1, seq_len), lambda s, h: (s, 0, 0)),
    ]
    flops = 4 * n_seq * seq_len * seq_len * model_width
    return pl.pallas_call(
        attn_fwd_kernel,
        out_shape=jax.ShapeDtypeStruct((rows, model_width), jnp.bfloat16),
        grid=(n_seq, n_hp),
        in_specs=[
            pl.BlockSpec((seq_len, blk), lambda s, h: (s, h)),
            pl.BlockSpec((seq_len, blk), lambda s, h: (s, off + h)),
            pl.BlockSpec((seq_len, blk), lambda s, h: (s, 2 * off + h)),
        ]
        + seg_spec,
        out_specs=pl.BlockSpec((seq_len, blk), lambda s, h: (s, h)),
        cost_estimate=pl.CostEstimate(
            flops=flops,
            transcendentals=n_seq * seq_len * seq_len * (model_width // HD),
            bytes_accessed=qkv.size * 2 + rows * model_width * 2,
        ),
    )(qkv, qkv, qkv, *mask_operands(segment_ids, valid))


def attention_bwd(qkv, grad_o, segment_ids, valid):
    rows, width3 = qkv.shape
    model_width = width3 // 3
    n_seq, seq_len = segment_ids.shape
    blk = 2 * HD
    n_hp = model_width // blk
    off = model_width // blk
    seg_spec = [
        pl.BlockSpec((None, seq_len, 1), lambda s, h: (s, 0, 0)),
        pl.BlockSpec((None, 1, seq_len), lambda s, h: (s, 0, 0)),
        pl.BlockSpec((None, 1, seq_len), lambda s, h: (s, 0, 0)),
    ]
    flops = 10 * n_seq * seq_len * seq_len * model_width
    return pl.pallas_call(
        attn_bwd_kernel,
        out_shape=jax.ShapeDtypeStruct((rows, width3), jnp.bfloat16),
        grid=(n_seq, n_hp),
        in_specs=[
            pl.BlockSpec((seq_len, blk), lambda s, h: (s, h)),
            pl.BlockSpec((seq_len, blk), lambda s, h: (s, off + h)),
            pl.BlockSpec((seq_len, blk), lambda s, h: (s, 2 * off + h)),
            pl.BlockSpec((seq_len, blk), lambda s, h: (s, h)),
        ]
        + seg_spec,
        out_specs=pl.BlockSpec((seq_len, width3), lambda s, h: (s, 0)),
        cost_estimate=pl.CostEstimate(
            flops=flops,
            transcendentals=n_seq * seq_len * seq_len * (model_width // HD),
            bytes_accessed=qkv.size * 4 + rows * model_width * 2,
        ),
    )(qkv, qkv, qkv, grad_o, *mask_operands(segment_ids, valid))


MESH_ID = pl.DeviceIdType.MESH


def ring_maps(n_wide, n_narrow):
    n_dev = n_wide * n_narrow
    if (n_wide, n_narrow) == (8, 4):
        def pos_of(w, n):
            z, y, x, c = w // 2, w % 2, n // 2, n % 2
            q = 2 * x + (x + y) % 2
            k = 4 * q + z + (q % 2) * (3 - 2 * z)
            return 2 * k + c

        def coords_of(p):
            k, c = p // 2, p % 2
            q, r = k // 4, k % 4
            z = r + (q % 2) * (3 - 2 * r)
            x = q // 2
            y = (q % 2 + x) % 2
            return z * 2 + y, x * 2 + c

    else:
        def pos_of(w, n):
            return w * n_narrow + n

        def coords_of(p):
            return p // n_narrow, p % n_narrow

    return n_dev, pos_of, coords_of


def ring_reduce_scatter(parts, mesh_shape, after=(), collective_id=0):
    n_wide, n_narrow = mesh_shape
    n_dev, pos_of, coords_of = ring_maps(n_wide, n_narrow)
    specs = []
    for i, (a, rb, split) in enumerate(parts):
        cols = a.shape[1]
        if split:
            specs.append((i, 0, 0, cols // 2))
        else:
            specs.append((i, 0, 0, cols))
    for i, (a, rb, split) in enumerate(parts):
        if split:
            specs.append((i, 1, a.shape[1] // 2, a.shape[1] // 2))
    n_in = len(parts)
    n_after = len(after)
    n_sp = len(specs)
    last_step = n_dev - 2

    def kernel(*refs):
        ins = refs[:n_in]
        outs = refs[n_in + n_after : 2 * n_in + n_after]
        at = 2 * n_in + n_after
        bufs = refs[at : at + n_sp]
        locs = refs[at + n_sp : at + 2 * n_sp]
        send_sem, recv_sem, loc_sem, credit = refs[at + 2 * n_sp :]
        p = pos_of(lax.axis_index("wide"), lax.axis_index("narrow"))
        right = coords_of((p + 1) % n_dev)
        left = coords_of((p + n_dev - 1) % n_dev)
        nbr_send = (right, left)
        nbr_recv = (left, right)

        def rows_of(q, rb):
            cw, cn = coords_of(q % n_dev)
            start = (cw * n_narrow + cn) * rb
            if rb % 8 == 0:
                start = pl.multiple_of(start, 8)
            return pl.ds(start, rb)

        def remote(j, s):
            return pltpu.make_async_remote_copy(
                src_ref=bufs[j].at[s % 3],
                dst_ref=bufs[j].at[(s + 1) % 3],
                send_sem=send_sem.at[j, s % 3],
                recv_sem=recv_sem.at[j, (s + 1) % 3],
                device_id=nbr_send[specs[j][1]],
                device_id_type=MESH_ID,
            )

        def local(j, s):
            i, dirn, c0, cw = specs[j]
            q = (p + 2 * n_dev - s - 2) if dirn == 0 else (p + s + 2)
            return pltpu.make_async_copy(
                ins[i].at[rows_of(q, parts[i][1]), pl.ds(c0, cw)], locs[j].at[s % 2], loc_sem.at[j, s % 2]
            )

        barrier = pltpu.get_barrier_semaphore()
        for nb in (left, right):
            pl.semaphore_signal(barrier, 1, device_id=nb, device_id_type=MESH_ID)
        pl.semaphore_wait(barrier, 2)

        for j, (i, dirn, c0, cw) in enumerate(specs):
            q = p + n_dev - 1 if dirn == 0 else p + 1
            cp = pltpu.make_async_copy(
                ins[i].at[rows_of(q, parts[i][1]), pl.ds(c0, cw)], bufs[j].at[0], loc_sem.at[j, 1]
            )
            cp.start()
            cp.wait()
        for j in range(n_sp):
            remote(j, 0).start()
            local(j, 0).start()

        def step(s, carry):
            for j in range(n_sp):
                dirn = specs[j][1]
                local(j, s).wait()
                remote(j, s).wait_recv()
                nxt = (s + 1) % 3
                bufs[j][nxt] = bufs[j][nxt] + locs[j][s % 2]
                if j == 0 or specs[j - 1][1] != dirn:

                    @pl.when((s >= 1) & (s + 1 <= last_step))
                    def _():
                        pl.semaphore_wait(credit.at[dirn], 1)

                @pl.when(s + 1 <= last_step)
                def _():
                    remote(j, s + 1).start()
                    local(j, s + 1).start()

            for j in range(n_sp):
                remote(j, s).wait_send()
            for dirn in (0, 1):

                @pl.when(s <= last_step - 2)
                def _():
                    pl.semaphore_signal(
                        credit.at[dirn], 1, device_id=nbr_recv[dirn], device_id_type=MESH_ID
                    )

            return carry

        lax.fori_loop(0, last_step + 1, step, 0)
        fin = (last_step + 1) % 3
        for j, (i, dirn, c0, cw) in enumerate(specs):
            outs[i][:, pl.ds(c0, cw)] = bufs[j][fin]

    out_shape = [jax.ShapeDtypeStruct((rb, a.shape[1]), a.dtype) for (a, rb, _) in parts]
    scratch = [pltpu.VMEM((3, parts[i][1], cw), jnp.float32) for (i, _, _, cw) in specs]
    scratch += [pltpu.VMEM((2, parts[i][1], cw), jnp.float32) for (i, _, _, cw) in specs]
    scratch += [
        pltpu.SemaphoreType.DMA((n_sp, 3)),
        pltpu.SemaphoreType.DMA((n_sp, 3)),
        pltpu.SemaphoreType.DMA((n_sp, 2)),
        pltpu.SemaphoreType.REGULAR((2,)),
    ]
    total = sum(a.size * 4 for (a, _, _) in parts)
    return pl.pallas_call(
        kernel,
        out_shape=out_shape,
        in_specs=[pl.BlockSpec(memory_space=pl.ANY)] * (n_in + n_after),
        out_specs=[pl.BlockSpec(memory_space=pltpu.VMEM)] * n_in,
        scratch_shapes=scratch,
        compiler_params=pltpu.CompilerParams(
            collective_id=collective_id, has_side_effects=True, vmem_limit_bytes=48 * 1024 * 1024
        ),
        cost_estimate=pl.CostEstimate(flops=total // 4, transcendentals=0, bytes_accessed=2 * total),
    )(*[a for (a, _, _) in parts], *after)


def ring_all_gather(parts, mesh_shape, collective_id=1):
    n_wide, n_narrow = mesh_shape
    n_dev, pos_of, coords_of = ring_maps(n_wide, n_narrow)
    n_in = len(parts)
    steps = (n_dev // 2, n_dev - 1 - n_dev // 2)

    def kernel(*refs):
        ins = refs[:n_in]
        outs = refs[n_in : 2 * n_in]
        send_sem, recv_sem, loc_sem = refs[2 * n_in :]
        p = pos_of(lax.axis_index("wide"), lax.axis_index("narrow"))
        right = coords_of((p + 1) % n_dev)
        left = coords_of((p + n_dev - 1) % n_dev)
        nbr_send = (right, left)

        def rows_of(q, rb):
            cw, cn = coords_of(q % n_dev)
            return pl.ds(pl.multiple_of((cw * n_narrow + cn) * rb, rb), rb)

        def copy(i, dirn, s, q):
            view = outs[i].at[rows_of(q, parts[i].shape[0])]
            return pltpu.make_async_remote_copy(
                src_ref=view,
                dst_ref=view,
                send_sem=send_sem.at[dirn, i, s],
                recv_sem=recv_sem.at[dirn, i, s],
                device_id=nbr_send[dirn],
                device_id_type=MESH_ID,
            )

        def sent(i, dirn, s):
            return copy(i, dirn, s, (p + n_dev - s) if dirn == 0 else (p + s))

        def arriving(i, dirn, s):
            return copy(i, dirn, s, (p + n_dev - 1 - s) if dirn == 0 else (p + 1 + s))

        barrier = pltpu.get_barrier_semaphore()
        for nb in (left, right):
            pl.semaphore_signal(barrier, 1, device_id=nb, device_id_type=MESH_ID)
        pl.semaphore_wait(barrier, 2)

        for i in range(n_in):
            cp = pltpu.make_async_copy(ins[i], outs[i].at[rows_of(p, parts[i].shape[0])], loc_sem.at[i])
            cp.start()
            cp.wait()

        def step(s, carry):
            for dirn in (0, 1):

                @pl.when(s < steps[dirn])
                def _():
                    for i in range(n_in):

                        @pl.when(s >= 1)
                        def _():
                            arriving(i, dirn, s - 1).wait_recv()

                        sent(i, dirn, s).start()

            return carry

        lax.fori_loop(0, steps[0], step, 0)
        for dirn in (0, 1):
            for i in range(n_in):
                arriving(i, dirn, steps[dirn] - 1).wait_recv()

        def drain(s, carry):
            for dirn in (0, 1):

                @pl.when(s < steps[dirn])
                def _():
                    for i in range(n_in):
                        sent(i, dirn, s).wait_send()

            return carry

        lax.fori_loop(0, steps[0], drain, 0)

    out_shape = [jax.ShapeDtypeStruct((n_dev * a.shape[0], a.shape[1]), a.dtype) for a in parts]
    total = sum(n_dev * a.size * a.dtype.itemsize for a in parts)
    return pl.pallas_call(
        kernel,
        out_shape=out_shape,
        in_specs=[pl.BlockSpec(memory_space=pl.ANY)] * n_in,
        out_specs=[pl.BlockSpec(memory_space=pltpu.VMEM)] * n_in,
        scratch_shapes=[
            pltpu.SemaphoreType.DMA((2, n_in, steps[0])),
            pltpu.SemaphoreType.DMA((2, n_in, steps[0])),
            pltpu.SemaphoreType.DMA((n_in,)),
        ],
        compiler_params=pltpu.CompilerParams(collective_id=collective_id, has_side_effects=True),
        cost_estimate=pl.CostEstimate(flops=0, transcendentals=0, bytes_accessed=2 * total),
    )(*parts)


def pack_rows(pieces, width):
    flat = jnp.concatenate(pieces)
    return jnp.pad(flat, (0, width - flat.shape[0]))[None, :]


def split_owned(packed, sizes):
    out = []
    at = 0
    for size in sizes:
        out.append(packed[:, at : at + size].reshape(-1))
        at += size
    return out


def on_device(
    inputs,
    w_qkv,
    qv_bias,
    w_out,
    out_bias,
    ln1_gain,
    ln1_shift,
    ln2_gain,
    ln2_shift,
    w_up,
    up_bias,
    w_down,
    down_bias,
    segment_ids,
    valid,
    cotangent,
    mesh_shape=None,
):
    row_count = inputs.shape[0]
    model_width = inputs.shape[1]
    seq_count = segment_ids.shape[0]
    seq_len = segment_ids.shape[1]
    head_count = model_width // HD
    n_dev = mesh_shape[0] * mesh_shape[1]
    small = (qv_bias, out_bias, ln1_gain, ln1_shift, ln2_gain, ln2_shift, up_bias, down_bias)
    small_sizes = [a.shape[0] for a in small]
    n_small = sum(small_sizes)
    width_q = w_qkv.shape[1]
    rows_q = w_qkv.shape[0]
    rows_o = w_out.size // width_q
    rows_u = w_up.size // width_q
    up_view = 16
    ring_up = mesh_shape == (8, 4) and w_up.size % (2 * up_view * 128) == 0
    pieces = [w_qkv, w_out.reshape(rows_o, width_q)]
    if not ring_up:
        pieces.append(w_up.reshape(rows_u, width_q))
    attn_buf = jnp.concatenate(pieces + [pack_rows(small, width_q)], axis=0)
    attn_all = lax.all_gather(attn_buf, ALL, axis=0, tiled=False)
    qkv_full = attn_all[:, :rows_q].reshape(-1, width_q)
    out_full = attn_all[:, rows_q : rows_q + rows_o].reshape(-1, model_width)
    at = rows_q + rows_o
    if ring_up:
        up_v = w_up.reshape(up_view, -1)
        half_v = up_v.shape[1] // 2
        up_a, up_b = ring_all_gather([up_v[:, :half_v], up_v[:, half_v:]], mesh_shape)
        up_full = jnp.concatenate([up_a, up_b], axis=1).reshape(-1, w_up.shape[1])
    else:
        up_full = attn_all[:, at : at + rows_u].reshape(-1, w_up.shape[1])
        at = at + rows_u
    small_full = split_owned(attn_all[:, at, :n_small], small_sizes)
    qv_full, outb_full, gain_one, shift_one, gain_two, shift_two, upb_full, downb_full = small_full
    down_full = lax.all_gather(w_down, ALL, axis=0, tiled=True)

    gain_one = gain_one.astype(jnp.float32)
    shift_one = shift_one.astype(jnp.float32)
    qv_full = qv_full.astype(jnp.float32)
    rows = inputs.astype(jnp.float32)
    normed_one, recip_one = norm_parts(rows)
    h_one = (normed_one * gain_one + shift_one).astype(jnp.bfloat16)
    qkv_rows = jnp.dot(h_one, qkv_full, preferred_element_type=jnp.float32)
    zero_bias = jnp.zeros((model_width,), jnp.float32)
    qkv_bias = jnp.concatenate([qv_full[:model_width], zero_bias, qv_full[model_width:]])
    qkv_b = (qkv_rows + qkv_bias).astype(jnp.bfloat16)
    attended = attention_fwd(qkv_b, segment_ids, valid)
    mid_rows = (
        rows
        + jnp.dot(attended, out_full, preferred_element_type=jnp.float32)
        + outb_full.astype(jnp.float32)
    )
    gain_two = gain_two.astype(jnp.float32)
    shift_two = shift_two.astype(jnp.float32)
    normed_two, recip_two = norm_parts(mid_rows)
    h_two = (normed_two * gain_two + shift_two).astype(jnp.bfloat16)
    upper = jnp.dot(h_two, up_full, preferred_element_type=jnp.float32) + upb_full.astype(
        jnp.float32
    )
    upper = lax.optimization_barrier(upper)
    gelu_rows = jax.nn.gelu(upper, approximate=False).astype(jnp.bfloat16)
    out_rows = (
        mid_rows
        + jnp.dot(gelu_rows, down_full, preferred_element_type=jnp.float32)
        + downb_full.astype(jnp.float32)
    )
    block_out = out_rows.astype(jnp.bfloat16)
    dy_rows = cotangent.astype(jnp.float32)
    grad_wdown = jnp.einsum("tf,td->fd", gelu_rows, cotangent, preferred_element_type=jnp.float32)
    grad_bdown = col_sum(cotangent)
    grad_g = jnp.einsum("td,fd->tf", cotangent, down_full, preferred_element_type=jnp.float32)
    cdf_part = 0.5 * (1.0 + jax.scipy.special.erf(upper * 0.7071067811865476))
    pdf_part = jnp.exp(-0.5 * upper * upper) * 0.3989422804014327
    grad_u = (grad_g * (cdf_part + upper * pdf_part)).astype(jnp.bfloat16)
    grad_bup = col_sum(grad_u)
    grad_wup = jnp.einsum("td,tf->df", h_two, grad_u, preferred_element_type=jnp.float32)
    grad_h2 = jnp.einsum("tf,df->td", grad_u, up_full, preferred_element_type=jnp.float32)
    grad_g2 = jnp.sum(grad_h2 * normed_two, axis=0)
    grad_c2 = jnp.sum(grad_h2, axis=0)
    grad_mid = dy_rows + norm_back(grad_h2, gain_two, normed_two, recip_two)
    grad_a = grad_mid.astype(jnp.bfloat16)
    grad_wout = jnp.einsum("tc,td->cd", attended, grad_a, preferred_element_type=jnp.float32)
    grad_bout = col_sum(grad_a)
    grad_o = jnp.einsum("td,cd->tc", grad_a, out_full, preferred_element_type=jnp.float32).astype(
        jnp.bfloat16
    )
    grad_qkv = attention_bwd(qkv_b, grad_o, segment_ids, valid)
    grad_cols = col_sum(grad_qkv)
    grad_bqv = jnp.concatenate([grad_cols[:model_width], grad_cols[2 * model_width :]])
    grad_wqkv = jnp.einsum("td,te->de", h_one, grad_qkv, preferred_element_type=jnp.float32)
    grad_h1 = jnp.einsum("te,de->td", grad_qkv, qkv_full, preferred_element_type=jnp.float32)
    grad_g1 = jnp.sum(grad_h1 * normed_one, axis=0)
    grad_c1 = jnp.sum(grad_h1, axis=0)
    grad_inputs = grad_mid + norm_back(grad_h1, gain_one, normed_one, recip_one)

    small_grads = (grad_bqv, grad_bout, grad_g1, grad_c1, grad_g2, grad_c2, grad_bup, grad_bdown)
    owned = jnp.concatenate([g.reshape(n_dev, -1) for g in small_grads], axis=1)
    lanes = 128
    small_rows = 8 * pl.cdiv(pl.cdiv(n_small, lanes), 8)
    owned = jnp.pad(owned, ((0, 0), (0, small_rows * lanes - n_small))).reshape(-1, lanes)
    parts = [
        (grad_wqkv, w_qkv.shape[0], True),
        (grad_wout, w_out.shape[0], True),
        (grad_wup, w_up.shape[0], True),
        (owned, small_rows, False),
    ]
    down_sum = lax.psum_scatter(grad_wdown, ALL, scatter_dimension=0, tiled=True)
    if all(rb % 8 == 0 and a.shape[1] % 256 == 0 for (a, rb, _) in parts[:3]):
        sums = ring_reduce_scatter(parts, mesh_shape, after=(grad_inputs, block_out))
    else:
        sums = [lax.psum_scatter(a, ALL, scatter_dimension=0, tiled=True) for (a, _, _) in parts]
    sums = list(sums[:3]) + [down_sum] + list(sums[3:])
    small_sums = split_owned(sums[4].reshape(1, -1), small_sizes)
    bqv, bout, g1, c1, g2, c2, bup, bdown = small_sums
    return (
        block_out,
        grad_inputs,
        sums[0],
        bqv,
        sums[1],
        bout,
        g1,
        c1,
        g2,
        c2,
        sums[2],
        bup,
        sums[3],
        bdown,
    )


def solution(mesh):
    in_specs = (
        P(("wide", "narrow"), None),
        P(("wide", "narrow"), None),
        P(("wide", "narrow")),
        P(("wide", "narrow"), None),
        P(("wide", "narrow")),
        P(("wide", "narrow")),
        P(("wide", "narrow")),
        P(("wide", "narrow")),
        P(("wide", "narrow")),
        P(("wide", "narrow"), None),
        P(("wide", "narrow")),
        P(("wide", "narrow"), None),
        P(("wide", "narrow")),
        P(("wide", "narrow"), None),
        P(("wide", "narrow"), None),
        P(("wide", "narrow"), None),
    )
    out_specs = (
        P(("wide", "narrow"), None),
        P(("wide", "narrow"), None),
        P(("wide", "narrow"), None),
        P(("wide", "narrow")),
        P(("wide", "narrow"), None),
        P(("wide", "narrow")),
        P(("wide", "narrow")),
        P(("wide", "narrow")),
        P(("wide", "narrow")),
        P(("wide", "narrow")),
        P(("wide", "narrow"), None),
        P(("wide", "narrow")),
        P(("wide", "narrow"), None),
        P(("wide", "narrow")),
    )
    body = functools.partial(on_device, mesh_shape=(mesh.shape["wide"], mesh.shape["narrow"]))
    return jax.shard_map(
        body, mesh=mesh, in_specs=in_specs, out_specs=out_specs, check_vma=False
    )
```

```python
import functools
import jax
import jax.numpy as jnp
from jax import lax
from jax.experimental import pallas as pl
from jax.experimental.pallas import tpu as pltpu
from jax.sharding import PartitionSpec as P

HD = 64
ALL = ("wide", "narrow")

EPSILON = 1e-06


def norm_parts(rows):
    center = rows - jnp.mean(rows, axis=-1, keepdims=True)
    recip = lax.rsqrt(jnp.mean(center * center, axis=-1, keepdims=True) + EPSILON)
    return (center * recip, recip)


def norm_back(grad_h, gain, normed, recip):
    scaled = grad_h * gain
    return recip * (
        scaled
        - jnp.mean(scaled, axis=-1, keepdims=True)
        - normed * jnp.mean(scaled * normed, axis=-1, keepdims=True)
    )


def col_sum(rows):
    return jnp.sum(rows.astype(jnp.float32), axis=0)


def seg_mask(seg_col, seg_row, val_row, n):
    rows = lax.broadcasted_iota(jnp.int32, (n, n), 0)
    cols = lax.broadcasted_iota(jnp.int32, (n, n), 1)
    return (seg_col == seg_row) & ((val_row == 1) | (rows == cols))


def soft_rows(qh, kh, allowed):
    scores = lax.dot_general(qh, kh, (((1,), (1,)), ((), ())), preferred_element_type=jnp.float32)
    scores = jnp.where(allowed, scores * (1.0 / HD**0.5), -1e30)
    top = jnp.max(scores, axis=-1, keepdims=True)
    expo = jnp.exp(scores - top)
    return expo * (1.0 / jnp.sum(expo, axis=-1, keepdims=True))


def attn_fwd_kernel(q_ref, k_ref, v_ref, sc_ref, sr_ref, vr_ref, o_ref):
    n = q_ref.shape[0]
    allowed = seg_mask(sc_ref[...], sr_ref[...], vr_ref[...], n)
    outs = []
    for j in range(q_ref.shape[1] // HD):
        cols = slice(j * HD, (j + 1) * HD)
        probs = soft_rows(q_ref[:, cols], k_ref[:, cols], allowed).astype(jnp.bfloat16)
        outs.append(jnp.dot(probs, v_ref[:, cols], preferred_element_type=jnp.float32))
    o_ref[...] = jnp.concatenate(outs, axis=1).astype(o_ref.dtype)


def attn_bwd_kernel(q_ref, k_ref, v_ref, do_ref, sc_ref, sr_ref, vr_ref, dqkv_ref):
    n = q_ref.shape[0]
    width = q_ref.shape[1]
    hp = pl.program_id(1)
    model_width = dqkv_ref.shape[1] // 3
    allowed = seg_mask(sc_ref[...], sr_ref[...], vr_ref[...], n)
    dqs, dks, dvs = [], [], []
    for j in range(width // HD):
        cols = slice(j * HD, (j + 1) * HD)
        qh, kh, vh, doh = q_ref[:, cols], k_ref[:, cols], v_ref[:, cols], do_ref[:, cols]
        probs = soft_rows(qh, kh, allowed)
        dvs.append(
            lax.dot_general(probs.astype(jnp.bfloat16), doh, (((0,), (0,)), ((), ())),
                            preferred_element_type=jnp.float32)
        )
        dprobs = lax.dot_general(doh, vh, (((1,), (1,)), ((), ())), preferred_element_type=jnp.float32)
        row_term = jnp.sum(probs * dprobs, axis=-1, keepdims=True)
        dscore = jnp.where(allowed, probs * (dprobs - row_term), 0.0).astype(jnp.bfloat16)
        dqs.append(jnp.dot(dscore, kh, preferred_element_type=jnp.float32) * (1.0 / HD**0.5))
        dks.append(
            lax.dot_general(dscore, qh, (((0,), (0,)), ((), ())), preferred_element_type=jnp.float32)
            * (1.0 / HD**0.5)
        )
    at = pl.multiple_of(hp * width, width)
    dqkv_ref[:, pl.ds(at, width)] = jnp.concatenate(dqs, axis=1).astype(dqkv_ref.dtype)
    dqkv_ref[:, pl.ds(at + model_width, width)] = jnp.concatenate(dks, axis=1).astype(dqkv_ref.dtype)
    dqkv_ref[:, pl.ds(at + 2 * model_width, width)] = jnp.concatenate(dvs, axis=1).astype(dqkv_ref.dtype)


def mask_operands(segment_ids, valid):
    return (segment_ids[:, :, None], segment_ids[:, None, :], valid[:, None, :])


def attention_fwd(qkv, segment_ids, valid):
    rows, width3 = qkv.shape
    model_width = width3 // 3
    n_seq, seq_len = segment_ids.shape
    blk = 4 * HD
    n_hp = model_width // blk
    off = model_width // blk
    seg_spec = [
        pl.BlockSpec((None, seq_len, 1), lambda s, h: (s, 0, 0)),
        pl.BlockSpec((None, 1, seq_len), lambda s, h: (s, 0, 0)),
        pl.BlockSpec((None, 1, seq_len), lambda s, h: (s, 0, 0)),
    ]
    flops = 4 * n_seq * seq_len * seq_len * model_width
    return pl.pallas_call(
        attn_fwd_kernel,
        out_shape=jax.ShapeDtypeStruct((rows, model_width), jnp.bfloat16),
        grid=(n_seq, n_hp),
        in_specs=[
            pl.BlockSpec((seq_len, blk), lambda s, h: (s, h)),
            pl.BlockSpec((seq_len, blk), lambda s, h: (s, off + h)),
            pl.BlockSpec((seq_len, blk), lambda s, h: (s, 2 * off + h)),
        ]
        + seg_spec,
        out_specs=pl.BlockSpec((seq_len, blk), lambda s, h: (s, h)),
        cost_estimate=pl.CostEstimate(
            flops=flops,
            transcendentals=n_seq * seq_len * seq_len * (model_width // HD),
            bytes_accessed=qkv.size * 2 + rows * model_width * 2,
        ),
    )(qkv, qkv, qkv, *mask_operands(segment_ids, valid))


def attention_bwd(qkv, grad_o, segment_ids, valid):
    rows, width3 = qkv.shape
    model_width = width3 // 3
    n_seq, seq_len = segment_ids.shape
    blk = 4 * HD
    n_hp = model_width // blk
    off = model_width // blk
    seg_spec = [
        pl.BlockSpec((None, seq_len, 1), lambda s, h: (s, 0, 0)),
        pl.BlockSpec((None, 1, seq_len), lambda s, h: (s, 0, 0)),
        pl.BlockSpec((None, 1, seq_len), lambda s, h: (s, 0, 0)),
    ]
    flops = 10 * n_seq * seq_len * seq_len * model_width
    return pl.pallas_call(
        attn_bwd_kernel,
        out_shape=jax.ShapeDtypeStruct((rows, width3), jnp.bfloat16),
        grid=(n_seq, n_hp),
        in_specs=[
            pl.BlockSpec((seq_len, blk), lambda s, h: (s, h)),
            pl.BlockSpec((seq_len, blk), lambda s, h: (s, off + h)),
            pl.BlockSpec((seq_len, blk), lambda s, h: (s, 2 * off + h)),
            pl.BlockSpec((seq_len, blk), lambda s, h: (s, h)),
        ]
        + seg_spec,
        out_specs=pl.BlockSpec((seq_len, width3), lambda s, h: (s, 0)),
        cost_estimate=pl.CostEstimate(
            flops=flops,
            transcendentals=n_seq * seq_len * seq_len * (model_width // HD),
            bytes_accessed=qkv.size * 4 + rows * model_width * 2,
        ),
    )(qkv, qkv, qkv, grad_o, *mask_operands(segment_ids, valid))


MESH_ID = pl.DeviceIdType.MESH


def ring_maps(n_wide, n_narrow):
    n_dev = n_wide * n_narrow
    if (n_wide, n_narrow) == (8, 4):
        def pos_of(w, n):
            z, y, x, c = w // 2, w % 2, n // 2, n % 2
            q = 2 * x + (x + y) % 2
            k = 4 * q + z + (q % 2) * (3 - 2 * z)
            return 2 * k + c

        def coords_of(p):
            k, c = p // 2, p % 2
            q, r = k // 4, k % 4
            z = r + (q % 2) * (3 - 2 * r)
            x = q // 2
            y = (q % 2 + x) % 2
            return z * 2 + y, x * 2 + c

    else:
        def pos_of(w, n):
            return w * n_narrow + n

        def coords_of(p):
            return p // n_narrow, p % n_narrow

    return n_dev, pos_of, coords_of


def ring_reduce_scatter(parts, mesh_shape, after=(), collective_id=0):
    n_wide, n_narrow = mesh_shape
    n_dev, pos_of, coords_of = ring_maps(n_wide, n_narrow)
    specs = []
    for i, (a, rb, split) in enumerate(parts):
        cols = a.shape[1]
        if split:
            specs.append((i, 0, 0, cols // 2))
        else:
            specs.append((i, 0, 0, cols))
    for i, (a, rb, split) in enumerate(parts):
        if split:
            specs.append((i, 1, a.shape[1] // 2, a.shape[1] // 2))
    n_in = len(parts)
    n_after = len(after)
    n_sp = len(specs)
    last_step = n_dev - 2

    def kernel(*refs):
        ins = refs[:n_in]
        outs = refs[n_in + n_after : 2 * n_in + n_after]
        at = 2 * n_in + n_after
        bufs = refs[at : at + n_sp]
        locs = refs[at + n_sp : at + 2 * n_sp]
        send_sem, recv_sem, loc_sem, credit = refs[at + 2 * n_sp :]
        p = pos_of(lax.axis_index("wide"), lax.axis_index("narrow"))
        right = coords_of((p + 1) % n_dev)
        left = coords_of((p + n_dev - 1) % n_dev)
        nbr_send = (right, left)
        nbr_recv = (left, right)

        def rows_of(q, rb):
            cw, cn = coords_of(q % n_dev)
            start = (cw * n_narrow + cn) * rb
            if rb % 8 == 0:
                start = pl.multiple_of(start, 8)
            return pl.ds(start, rb)

        def remote(j, s):
            return pltpu.make_async_remote_copy(
                src_ref=bufs[j].at[s % 3],
                dst_ref=bufs[j].at[(s + 1) % 3],
                send_sem=send_sem.at[j, s % 3],
                recv_sem=recv_sem.at[j, (s + 1) % 3],
                device_id=nbr_send[specs[j][1]],
                device_id_type=MESH_ID,
            )

        def local(j, s):
            i, dirn, c0, cw = specs[j]
            q = (p + 2 * n_dev - s - 2) if dirn == 0 else (p + s + 2)
            return pltpu.make_async_copy(
                ins[i].at[rows_of(q, parts[i][1]), pl.ds(c0, cw)], locs[j].at[s % 2], loc_sem.at[j, s % 2]
            )

        barrier = pltpu.get_barrier_semaphore()
        for nb in (left, right):
            pl.semaphore_signal(barrier, 1, device_id=nb, device_id_type=MESH_ID)
        pl.semaphore_wait(barrier, 2)

        for j, (i, dirn, c0, cw) in enumerate(specs):
            q = p + n_dev - 1 if dirn == 0 else p + 1
            cp = pltpu.make_async_copy(
                ins[i].at[rows_of(q, parts[i][1]), pl.ds(c0, cw)], bufs[j].at[0], loc_sem.at[j, 1]
            )
            cp.start()
            cp.wait()
        for j in range(n_sp):
            remote(j, 0).start()
            local(j, 0).start()

        def step(s, carry):
            for j in range(n_sp):
                dirn = specs[j][1]
                local(j, s).wait()
                remote(j, s).wait_recv()
                nxt = (s + 1) % 3
                bufs[j][nxt] = bufs[j][nxt] + locs[j][s % 2]
                if j == 0 or specs[j - 1][1] != dirn:

                    @pl.when((s >= 1) & (s + 1 <= last_step))
                    def _():
                        pl.semaphore_wait(credit.at[dirn], 1)

                @pl.when(s + 1 <= last_step)
                def _():
                    remote(j, s + 1).start()
                    local(j, s + 1).start()

            for j in range(n_sp):
                remote(j, s).wait_send()
            for dirn in (0, 1):

                @pl.when(s <= last_step - 2)
                def _():
                    pl.semaphore_signal(
                        credit.at[dirn], 1, device_id=nbr_recv[dirn], device_id_type=MESH_ID
                    )

            return carry

        lax.fori_loop(0, last_step + 1, step, 0)
        fin = (last_step + 1) % 3
        for j, (i, dirn, c0, cw) in enumerate(specs):
            outs[i][:, pl.ds(c0, cw)] = bufs[j][fin]

    out_shape = [jax.ShapeDtypeStruct((rb, a.shape[1]), a.dtype) for (a, rb, _) in parts]
    scratch = [pltpu.VMEM((3, parts[i][1], cw), jnp.float32) for (i, _, _, cw) in specs]
    scratch += [pltpu.VMEM((2, parts[i][1], cw), jnp.float32) for (i, _, _, cw) in specs]
    scratch += [
        pltpu.SemaphoreType.DMA((n_sp, 3)),
        pltpu.SemaphoreType.DMA((n_sp, 3)),
        pltpu.SemaphoreType.DMA((n_sp, 2)),
        pltpu.SemaphoreType.REGULAR((2,)),
    ]
    total = sum(a.size * 4 for (a, _, _) in parts)
    return pl.pallas_call(
        kernel,
        out_shape=out_shape,
        in_specs=[pl.BlockSpec(memory_space=pl.ANY)] * (n_in + n_after),
        out_specs=[pl.BlockSpec(memory_space=pltpu.VMEM)] * n_in,
        scratch_shapes=scratch,
        compiler_params=pltpu.CompilerParams(
            collective_id=collective_id, has_side_effects=True, vmem_limit_bytes=48 * 1024 * 1024
        ),
        cost_estimate=pl.CostEstimate(flops=total // 4, transcendentals=0, bytes_accessed=2 * total),
    )(*[a for (a, _, _) in parts], *after)


def ring_all_gather(parts, mesh_shape, collective_id=1):
    n_wide, n_narrow = mesh_shape
    n_dev, pos_of, coords_of = ring_maps(n_wide, n_narrow)
    n_in = len(parts)
    steps = (n_dev // 2, n_dev - 1 - n_dev // 2)

    def kernel(*refs):
        ins = refs[:n_in]
        outs = refs[n_in : 2 * n_in]
        send_sem, recv_sem, loc_sem = refs[2 * n_in :]
        p = pos_of(lax.axis_index("wide"), lax.axis_index("narrow"))
        right = coords_of((p + 1) % n_dev)
        left = coords_of((p + n_dev - 1) % n_dev)
        nbr_send = (right, left)

        def rows_of(q, rb):
            cw, cn = coords_of(q % n_dev)
            return pl.ds(pl.multiple_of((cw * n_narrow + cn) * rb, rb), rb)

        def copy(i, dirn, s, q):
            view = outs[i].at[rows_of(q, parts[i].shape[0])]
            return pltpu.make_async_remote_copy(
                src_ref=view,
                dst_ref=view,
                send_sem=send_sem.at[dirn, i, s],
                recv_sem=recv_sem.at[dirn, i, s],
                device_id=nbr_send[dirn],
                device_id_type=MESH_ID,
            )

        def sent(i, dirn, s):
            return copy(i, dirn, s, (p + n_dev - s) if dirn == 0 else (p + s))

        def arriving(i, dirn, s):
            return copy(i, dirn, s, (p + n_dev - 1 - s) if dirn == 0 else (p + 1 + s))

        barrier = pltpu.get_barrier_semaphore()
        for nb in (left, right):
            pl.semaphore_signal(barrier, 1, device_id=nb, device_id_type=MESH_ID)
        pl.semaphore_wait(barrier, 2)

        for i in range(n_in):
            cp = pltpu.make_async_copy(ins[i], outs[i].at[rows_of(p, parts[i].shape[0])], loc_sem.at[i])
            cp.start()
            cp.wait()

        def step(s, carry):
            for dirn in (0, 1):

                @pl.when(s < steps[dirn])
                def _():
                    for i in range(n_in):

                        @pl.when(s >= 1)
                        def _():
                            arriving(i, dirn, s - 1).wait_recv()

                        sent(i, dirn, s).start()

            return carry

        lax.fori_loop(0, steps[0], step, 0)
        for dirn in (0, 1):
            for i in range(n_in):
                arriving(i, dirn, steps[dirn] - 1).wait_recv()

        def drain(s, carry):
            for dirn in (0, 1):

                @pl.when(s < steps[dirn])
                def _():
                    for i in range(n_in):
                        sent(i, dirn, s).wait_send()

            return carry

        lax.fori_loop(0, steps[0], drain, 0)

    out_shape = [jax.ShapeDtypeStruct((n_dev * a.shape[0], a.shape[1]), a.dtype) for a in parts]
    total = sum(n_dev * a.size * a.dtype.itemsize for a in parts)
    return pl.pallas_call(
        kernel,
        out_shape=out_shape,
        in_specs=[pl.BlockSpec(memory_space=pl.ANY)] * n_in,
        out_specs=[pl.BlockSpec(memory_space=pltpu.VMEM)] * n_in,
        scratch_shapes=[
            pltpu.SemaphoreType.DMA((2, n_in, steps[0])),
            pltpu.SemaphoreType.DMA((2, n_in, steps[0])),
            pltpu.SemaphoreType.DMA((n_in,)),
        ],
        compiler_params=pltpu.CompilerParams(collective_id=collective_id, has_side_effects=True),
        cost_estimate=pl.CostEstimate(flops=0, transcendentals=0, bytes_accessed=2 * total),
    )(*parts)


def pack_rows(pieces, width):
    flat = jnp.concatenate(pieces)
    return jnp.pad(flat, (0, width - flat.shape[0]))[None, :]


def split_owned(packed, sizes):
    out = []
    at = 0
    for size in sizes:
        out.append(packed[:, at : at + size].reshape(-1))
        at += size
    return out


def on_device(
    inputs,
    w_qkv,
    qv_bias,
    w_out,
    out_bias,
    ln1_gain,
    ln1_shift,
    ln2_gain,
    ln2_shift,
    w_up,
    up_bias,
    w_down,
    down_bias,
    segment_ids,
    valid,
    cotangent,
    mesh_shape=None,
):
    row_count = inputs.shape[0]
    model_width = inputs.shape[1]
    seq_count = segment_ids.shape[0]
    seq_len = segment_ids.shape[1]
    head_count = model_width // HD
    n_dev = mesh_shape[0] * mesh_shape[1]
    small = (qv_bias, out_bias, ln1_gain, ln1_shift, ln2_gain, ln2_shift, up_bias, down_bias)
    small_sizes = [a.shape[0] for a in small]
    n_small = sum(small_sizes)
    width_q = w_qkv.shape[1]
    rows_q = w_qkv.shape[0]
    rows_o = w_out.size // width_q
    rows_u = w_up.size // width_q
    up_view = 16
    ring_up = mesh_shape == (8, 4) and w_up.size % (2 * up_view * 128) == 0
    pieces = [w_qkv, w_out.reshape(rows_o, width_q)]
    if not ring_up:
        pieces.append(w_up.reshape(rows_u, width_q))
    attn_buf = jnp.concatenate(pieces + [pack_rows(small, width_q)], axis=0)
    attn_all = lax.all_gather(attn_buf, ALL, axis=0, tiled=False)
    qkv_full = attn_all[:, :rows_q].reshape(-1, width_q)
    out_full = attn_all[:, rows_q : rows_q + rows_o].reshape(-1, model_width)
    at = rows_q + rows_o
    if ring_up:
        up_v = w_up.reshape(up_view, -1)
        half_v = up_v.shape[1] // 2
        up_a, up_b = ring_all_gather([up_v[:, :half_v], up_v[:, half_v:]], mesh_shape)
        up_full = jnp.concatenate([up_a, up_b], axis=1).reshape(-1, w_up.shape[1])
    else:
        up_full = attn_all[:, at : at + rows_u].reshape(-1, w_up.shape[1])
        at = at + rows_u
    small_full = split_owned(attn_all[:, at, :n_small], small_sizes)
    qv_full, outb_full, gain_one, shift_one, gain_two, shift_two, upb_full, downb_full = small_full
    down_full = lax.all_gather(w_down, ALL, axis=0, tiled=True)

    gain_one = gain_one.astype(jnp.float32)
    shift_one = shift_one.astype(jnp.float32)
    qv_full = qv_full.astype(jnp.float32)
    rows = inputs.astype(jnp.float32)
    normed_one, recip_one = norm_parts(rows)
    h_one = (normed_one * gain_one + shift_one).astype(jnp.bfloat16)
    qkv_rows = jnp.dot(h_one, qkv_full, preferred_element_type=jnp.float32)
    zero_bias = jnp.zeros((model_width,), jnp.float32)
    qkv_bias = jnp.concatenate([qv_full[:model_width], zero_bias, qv_full[model_width:]])
    qkv_b = (qkv_rows + qkv_bias).astype(jnp.bfloat16)
    attended = attention_fwd(qkv_b, segment_ids, valid)
    mid_rows = (
        rows
        + jnp.dot(attended, out_full, preferred_element_type=jnp.float32)
        + outb_full.astype(jnp.float32)
    )
    gain_two = gain_two.astype(jnp.float32)
    shift_two = shift_two.astype(jnp.float32)
    normed_two, recip_two = norm_parts(mid_rows)
    h_two = (normed_two * gain_two + shift_two).astype(jnp.bfloat16)
    upper = jnp.dot(h_two, up_full, preferred_element_type=jnp.float32) + upb_full.astype(
        jnp.float32
    )
    upper = lax.optimization_barrier(upper)
    gelu_rows = jax.nn.gelu(upper, approximate=False).astype(jnp.bfloat16)
    out_rows = (
        mid_rows
        + jnp.dot(gelu_rows, down_full, preferred_element_type=jnp.float32)
        + downb_full.astype(jnp.float32)
    )
    block_out = out_rows.astype(jnp.bfloat16)
    dy_rows = cotangent.astype(jnp.float32)
    grad_wdown = jnp.einsum("tf,td->fd", gelu_rows, cotangent, preferred_element_type=jnp.float32)
    grad_bdown = col_sum(cotangent)
    grad_g = jnp.einsum("td,fd->tf", cotangent, down_full, preferred_element_type=jnp.float32)
    cdf_part = 0.5 * (1.0 + jax.scipy.special.erf(upper * 0.7071067811865476))
    pdf_part = jnp.exp(-0.5 * upper * upper) * 0.3989422804014327
    grad_u = (grad_g * (cdf_part + upper * pdf_part)).astype(jnp.bfloat16)
    grad_bup = col_sum(grad_u)
    grad_wup = jnp.einsum("td,tf->df", h_two, grad_u, preferred_element_type=jnp.float32)
    grad_h2 = jnp.einsum("tf,df->td", grad_u, up_full, preferred_element_type=jnp.float32)
    grad_g2 = jnp.sum(grad_h2 * normed_two, axis=0)
    grad_c2 = jnp.sum(grad_h2, axis=0)
    grad_mid = dy_rows + norm_back(grad_h2, gain_two, normed_two, recip_two)
    grad_a = grad_mid.astype(jnp.bfloat16)
    grad_wout = jnp.einsum("tc,td->cd", attended, grad_a, preferred_element_type=jnp.float32)
    grad_bout = col_sum(grad_a)
    grad_o = jnp.einsum("td,cd->tc", grad_a, out_full, preferred_element_type=jnp.float32).astype(
        jnp.bfloat16
    )
    grad_qkv = attention_bwd(qkv_b, grad_o, segment_ids, valid)
    grad_cols = col_sum(grad_qkv)
    grad_bqv = jnp.concatenate([grad_cols[:model_width], grad_cols[2 * model_width :]])
    grad_wqkv = jnp.einsum("td,te->de", h_one, grad_qkv, preferred_element_type=jnp.float32)
    grad_h1 = jnp.einsum("te,de->td", grad_qkv, qkv_full, preferred_element_type=jnp.float32)
    grad_g1 = jnp.sum(grad_h1 * normed_one, axis=0)
    grad_c1 = jnp.sum(grad_h1, axis=0)
    grad_inputs = grad_mid + norm_back(grad_h1, gain_one, normed_one, recip_one)

    small_grads = (grad_bqv, grad_bout, grad_g1, grad_c1, grad_g2, grad_c2, grad_bup, grad_bdown)
    owned = jnp.concatenate([g.reshape(n_dev, -1) for g in small_grads], axis=1)
    lanes = 128
    small_rows = 8 * pl.cdiv(pl.cdiv(n_small, lanes), 8)
    owned = jnp.pad(owned, ((0, 0), (0, small_rows * lanes - n_small))).reshape(-1, lanes)
    parts = [
        (grad_wqkv, w_qkv.shape[0], True),
        (grad_wout, w_out.shape[0], True),
        (grad_wup, w_up.shape[0], True),
        (owned, small_rows, False),
    ]
    down_sum = lax.psum_scatter(grad_wdown, ALL, scatter_dimension=0, tiled=True)
    if all(rb % 8 == 0 and a.shape[1] % 256 == 0 for (a, rb, _) in parts[:3]):
        sums = ring_reduce_scatter(parts, mesh_shape, after=(grad_inputs, block_out))
    else:
        sums = [lax.psum_scatter(a, ALL, scatter_dimension=0, tiled=True) for (a, _, _) in parts]
    sums = list(sums[:3]) + [down_sum] + list(sums[3:])
    small_sums = split_owned(sums[4].reshape(1, -1), small_sizes)
    bqv, bout, g1, c1, g2, c2, bup, bdown = small_sums
    return (
        block_out,
        grad_inputs,
        sums[0],
        bqv,
        sums[1],
        bout,
        g1,
        c1,
        g2,
        c2,
        sums[2],
        bup,
        sums[3],
        bdown,
    )


def solution(mesh):
    in_specs = (
        P(("wide", "narrow"), None),
        P(("wide", "narrow"), None),
        P(("wide", "narrow")),
        P(("wide", "narrow"), None),
        P(("wide", "narrow")),
        P(("wide", "narrow")),
        P(("wide", "narrow")),
        P(("wide", "narrow")),
        P(("wide", "narrow")),
        P(("wide", "narrow"), None),
        P(("wide", "narrow")),
        P(("wide", "narrow"), None),
        P(("wide", "narrow")),
        P(("wide", "narrow"), None),
        P(("wide", "narrow"), None),
        P(("wide", "narrow"), None),
    )
    out_specs = (
        P(("wide", "narrow"), None),
        P(("wide", "narrow"), None),
        P(("wide", "narrow"), None),
        P(("wide", "narrow")),
        P(("wide", "narrow"), None),
        P(("wide", "narrow")),
        P(("wide", "narrow")),
        P(("wide", "narrow")),
        P(("wide", "narrow")),
        P(("wide", "narrow")),
        P(("wide", "narrow"), None),
        P(("wide", "narrow")),
        P(("wide", "narrow"), None),
        P(("wide", "narrow")),
    )
    body = functools.partial(on_device, mesh_shape=(mesh.shape["wide"], mesh.shape["narrow"]))
    return jax.shard_map(
        body, mesh=mesh, in_specs=in_specs, out_specs=out_specs, check_vma=False
    )
```

```python
import functools
import jax
import jax.numpy as jnp
from jax import lax
from jax.experimental import pallas as pl
from jax.experimental.pallas import tpu as pltpu
from jax.sharding import PartitionSpec as P

HD = 64
ALL = ("wide", "narrow")

EPSILON = 1e-06


def norm_parts(rows):
    center = rows - jnp.mean(rows, axis=-1, keepdims=True)
    recip = lax.rsqrt(jnp.mean(center * center, axis=-1, keepdims=True) + EPSILON)
    return (center * recip, recip)


def norm_back(grad_h, gain, normed, recip):
    scaled = grad_h * gain
    return recip * (
        scaled
        - jnp.mean(scaled, axis=-1, keepdims=True)
        - normed * jnp.mean(scaled * normed, axis=-1, keepdims=True)
    )


def col_sum(rows):
    return jnp.sum(rows.astype(jnp.float32), axis=0)


def seg_mask(seg_col, seg_row, val_row, n):
    rows = lax.broadcasted_iota(jnp.int32, (n, n), 0)
    cols = lax.broadcasted_iota(jnp.int32, (n, n), 1)
    return (seg_col == seg_row) & ((val_row == 1) | (rows == cols))


def soft_rows(qh, kh, allowed):
    scores = lax.dot_general(qh, kh, (((1,), (1,)), ((), ())), preferred_element_type=jnp.float32)
    scores = jnp.where(allowed, scores * (1.0 / HD**0.5), -1e30)
    top = jnp.max(scores, axis=-1, keepdims=True)
    expo = jnp.exp(scores - top)
    return expo * (1.0 / jnp.sum(expo, axis=-1, keepdims=True))


def attn_fwd_kernel(q_ref, k_ref, v_ref, sc_ref, sr_ref, vr_ref, o_ref):
    n = q_ref.shape[0]
    allowed = seg_mask(sc_ref[...], sr_ref[...], vr_ref[...], n)
    outs = []
    for j in range(q_ref.shape[1] // HD):
        cols = slice(j * HD, (j + 1) * HD)
        probs = soft_rows(q_ref[:, cols], k_ref[:, cols], allowed).astype(jnp.bfloat16)
        outs.append(jnp.dot(probs, v_ref[:, cols], preferred_element_type=jnp.float32))
    o_ref[...] = jnp.concatenate(outs, axis=1).astype(o_ref.dtype)


def attn_bwd_kernel(q_ref, k_ref, v_ref, do_ref, sc_ref, sr_ref, vr_ref, dqkv_ref):
    n = q_ref.shape[0]
    width = q_ref.shape[1]
    hp = pl.program_id(1)
    model_width = dqkv_ref.shape[1] // 3
    allowed = seg_mask(sc_ref[...], sr_ref[...], vr_ref[...], n)
    dqs, dks, dvs = [], [], []
    for j in range(width // HD):
        cols = slice(j * HD, (j + 1) * HD)
        qh, kh, vh, doh = q_ref[:, cols], k_ref[:, cols], v_ref[:, cols], do_ref[:, cols]
        probs = soft_rows(qh, kh, allowed)
        dvs.append(
            lax.dot_general(probs.astype(jnp.bfloat16), doh, (((0,), (0,)), ((), ())),
                            preferred_element_type=jnp.float32)
        )
        dprobs = lax.dot_general(doh, vh, (((1,), (1,)), ((), ())), preferred_element_type=jnp.float32)
        row_term = jnp.sum(probs * dprobs, axis=-1, keepdims=True)
        dscore = jnp.where(allowed, probs * (dprobs - row_term), 0.0).astype(jnp.bfloat16)
        dqs.append(jnp.dot(dscore, kh, preferred_element_type=jnp.float32) * (1.0 / HD**0.5))
        dks.append(
            lax.dot_general(dscore, qh, (((0,), (0,)), ((), ())), preferred_element_type=jnp.float32)
            * (1.0 / HD**0.5)
        )
    at = pl.multiple_of(hp * width, width)
    dqkv_ref[:, pl.ds(at, width)] = jnp.concatenate(dqs, axis=1).astype(dqkv_ref.dtype)
    dqkv_ref[:, pl.ds(at + model_width, width)] = jnp.concatenate(dks, axis=1).astype(dqkv_ref.dtype)
    dqkv_ref[:, pl.ds(at + 2 * model_width, width)] = jnp.concatenate(dvs, axis=1).astype(dqkv_ref.dtype)


def mask_operands(segment_ids, valid):
    return (segment_ids[:, :, None], segment_ids[:, None, :], valid[:, None, :])


def attention_fwd(qkv, segment_ids, valid):
    rows, width3 = qkv.shape
    model_width = width3 // 3
    n_seq, seq_len = segment_ids.shape
    blk = 6 * HD
    n_hp = model_width // blk
    off = model_width // blk
    seg_spec = [
        pl.BlockSpec((None, seq_len, 1), lambda s, h: (s, 0, 0)),
        pl.BlockSpec((None, 1, seq_len), lambda s, h: (s, 0, 0)),
        pl.BlockSpec((None, 1, seq_len), lambda s, h: (s, 0, 0)),
    ]
    flops = 4 * n_seq * seq_len * seq_len * model_width
    return pl.pallas_call(
        attn_fwd_kernel,
        out_shape=jax.ShapeDtypeStruct((rows, model_width), jnp.bfloat16),
        grid=(n_seq, n_hp),
        in_specs=[
            pl.BlockSpec((seq_len, blk), lambda s, h: (s, h)),
            pl.BlockSpec((seq_len, blk), lambda s, h: (s, off + h)),
            pl.BlockSpec((seq_len, blk), lambda s, h: (s, 2 * off + h)),
        ]
        + seg_spec,
        out_specs=pl.BlockSpec((seq_len, blk), lambda s, h: (s, h)),
        cost_estimate=pl.CostEstimate(
            flops=flops,
            transcendentals=n_seq * seq_len * seq_len * (model_width // HD),
            bytes_accessed=qkv.size * 2 + rows * model_width * 2,
        ),
    )(qkv, qkv, qkv, *mask_operands(segment_ids, valid))


def attention_bwd(qkv, grad_o, segment_ids, valid):
    rows, width3 = qkv.shape
    model_width = width3 // 3
    n_seq, seq_len = segment_ids.shape
    blk = 6 * HD
    n_hp = model_width // blk
    off = model_width // blk
    seg_spec = [
        pl.BlockSpec((None, seq_len, 1), lambda s, h: (s, 0, 0)),
        pl.BlockSpec((None, 1, seq_len), lambda s, h: (s, 0, 0)),
        pl.BlockSpec((None, 1, seq_len), lambda s, h: (s, 0, 0)),
    ]
    flops = 10 * n_seq * seq_len * seq_len * model_width
    return pl.pallas_call(
        attn_bwd_kernel,
        out_shape=jax.ShapeDtypeStruct((rows, width3), jnp.bfloat16),
        grid=(n_seq, n_hp),
        in_specs=[
            pl.BlockSpec((seq_len, blk), lambda s, h: (s, h)),
            pl.BlockSpec((seq_len, blk), lambda s, h: (s, off + h)),
            pl.BlockSpec((seq_len, blk), lambda s, h: (s, 2 * off + h)),
            pl.BlockSpec((seq_len, blk), lambda s, h: (s, h)),
        ]
        + seg_spec,
        out_specs=pl.BlockSpec((seq_len, width3), lambda s, h: (s, 0)),
        cost_estimate=pl.CostEstimate(
            flops=flops,
            transcendentals=n_seq * seq_len * seq_len * (model_width // HD),
            bytes_accessed=qkv.size * 4 + rows * model_width * 2,
        ),
    )(qkv, qkv, qkv, grad_o, *mask_operands(segment_ids, valid))


MESH_ID = pl.DeviceIdType.MESH


def ring_maps(n_wide, n_narrow):
    n_dev = n_wide * n_narrow
    if (n_wide, n_narrow) == (8, 4):
        def pos_of(w, n):
            z, y, x, c = w // 2, w % 2, n // 2, n % 2
            q = 2 * x + (x + y) % 2
            k = 4 * q + z + (q % 2) * (3 - 2 * z)
            return 2 * k + c

        def coords_of(p):
            k, c = p // 2, p % 2
            q, r = k // 4, k % 4
            z = r + (q % 2) * (3 - 2 * r)
            x = q // 2
            y = (q % 2 + x) % 2
            return z * 2 + y, x * 2 + c

    else:
        def pos_of(w, n):
            return w * n_narrow + n

        def coords_of(p):
            return p // n_narrow, p % n_narrow

    return n_dev, pos_of, coords_of


def ring_reduce_scatter(parts, mesh_shape, after=(), collective_id=0):
    n_wide, n_narrow = mesh_shape
    n_dev, pos_of, coords_of = ring_maps(n_wide, n_narrow)
    specs = []
    for i, (a, rb, split) in enumerate(parts):
        cols = a.shape[1]
        if split:
            specs.append((i, 0, 0, cols // 2))
        else:
            specs.append((i, 0, 0, cols))
    for i, (a, rb, split) in enumerate(parts):
        if split:
            specs.append((i, 1, a.shape[1] // 2, a.shape[1] // 2))
    n_in = len(parts)
    n_after = len(after)
    n_sp = len(specs)
    last_step = n_dev - 2

    def kernel(*refs):
        ins = refs[:n_in]
        outs = refs[n_in + n_after : 2 * n_in + n_after]
        at = 2 * n_in + n_after
        bufs = refs[at : at + n_sp]
        locs = refs[at + n_sp : at + 2 * n_sp]
        send_sem, recv_sem, loc_sem, credit = refs[at + 2 * n_sp :]
        p = pos_of(lax.axis_index("wide"), lax.axis_index("narrow"))
        right = coords_of((p + 1) % n_dev)
        left = coords_of((p + n_dev - 1) % n_dev)
        nbr_send = (right, left)
        nbr_recv = (left, right)

        def rows_of(q, rb):
            cw, cn = coords_of(q % n_dev)
            start = (cw * n_narrow + cn) * rb
            if rb % 8 == 0:
                start = pl.multiple_of(start, 8)
            return pl.ds(start, rb)

        def remote(j, s):
            return pltpu.make_async_remote_copy(
                src_ref=bufs[j].at[s % 3],
                dst_ref=bufs[j].at[(s + 1) % 3],
                send_sem=send_sem.at[j, s % 3],
                recv_sem=recv_sem.at[j, (s + 1) % 3],
                device_id=nbr_send[specs[j][1]],
                device_id_type=MESH_ID,
            )

        def local(j, s):
            i, dirn, c0, cw = specs[j]
            q = (p + 2 * n_dev - s - 2) if dirn == 0 else (p + s + 2)
            return pltpu.make_async_copy(
                ins[i].at[rows_of(q, parts[i][1]), pl.ds(c0, cw)], locs[j].at[s % 2], loc_sem.at[j, s % 2]
            )

        barrier = pltpu.get_barrier_semaphore()
        for nb in (left, right):
            pl.semaphore_signal(barrier, 1, device_id=nb, device_id_type=MESH_ID)
        pl.semaphore_wait(barrier, 2)

        for j, (i, dirn, c0, cw) in enumerate(specs):
            q = p + n_dev - 1 if dirn == 0 else p + 1
            cp = pltpu.make_async_copy(
                ins[i].at[rows_of(q, parts[i][1]), pl.ds(c0, cw)], bufs[j].at[0], loc_sem.at[j, 1]
            )
            cp.start()
            cp.wait()
        for j in range(n_sp):
            remote(j, 0).start()
            local(j, 0).start()

        def step(s, carry):
            for j in range(n_sp):
                dirn = specs[j][1]
                local(j, s).wait()
                remote(j, s).wait_recv()
                nxt = (s + 1) % 3
                bufs[j][nxt] = bufs[j][nxt] + locs[j][s % 2]
                if j == 0 or specs[j - 1][1] != dirn:

                    @pl.when((s >= 1) & (s + 1 <= last_step))
                    def _():
                        pl.semaphore_wait(credit.at[dirn], 1)

                @pl.when(s + 1 <= last_step)
                def _():
                    remote(j, s + 1).start()
                    local(j, s + 1).start()

            for j in range(n_sp):
                remote(j, s).wait_send()
            for dirn in (0, 1):

                @pl.when(s <= last_step - 2)
                def _():
                    pl.semaphore_signal(
                        credit.at[dirn], 1, device_id=nbr_recv[dirn], device_id_type=MESH_ID
                    )

            return carry

        lax.fori_loop(0, last_step + 1, step, 0)
        fin = (last_step + 1) % 3
        for j, (i, dirn, c0, cw) in enumerate(specs):
            outs[i][:, pl.ds(c0, cw)] = bufs[j][fin]

    out_shape = [jax.ShapeDtypeStruct((rb, a.shape[1]), a.dtype) for (a, rb, _) in parts]
    scratch = [pltpu.VMEM((3, parts[i][1], cw), jnp.float32) for (i, _, _, cw) in specs]
    scratch += [pltpu.VMEM((2, parts[i][1], cw), jnp.float32) for (i, _, _, cw) in specs]
    scratch += [
        pltpu.SemaphoreType.DMA((n_sp, 3)),
        pltpu.SemaphoreType.DMA((n_sp, 3)),
        pltpu.SemaphoreType.DMA((n_sp, 2)),
        pltpu.SemaphoreType.REGULAR((2,)),
    ]
    total = sum(a.size * 4 for (a, _, _) in parts)
    return pl.pallas_call(
        kernel,
        out_shape=out_shape,
        in_specs=[pl.BlockSpec(memory_space=pl.ANY)] * (n_in + n_after),
        out_specs=[pl.BlockSpec(memory_space=pltpu.VMEM)] * n_in,
        scratch_shapes=scratch,
        compiler_params=pltpu.CompilerParams(
            collective_id=collective_id, has_side_effects=True, vmem_limit_bytes=48 * 1024 * 1024
        ),
        cost_estimate=pl.CostEstimate(flops=total // 4, transcendentals=0, bytes_accessed=2 * total),
    )(*[a for (a, _, _) in parts], *after)


def ring_all_gather(parts, mesh_shape, collective_id=1):
    n_wide, n_narrow = mesh_shape
    n_dev, pos_of, coords_of = ring_maps(n_wide, n_narrow)
    n_in = len(parts)
    steps = (n_dev // 2, n_dev - 1 - n_dev // 2)

    def kernel(*refs):
        ins = refs[:n_in]
        outs = refs[n_in : 2 * n_in]
        send_sem, recv_sem, loc_sem = refs[2 * n_in :]
        p = pos_of(lax.axis_index("wide"), lax.axis_index("narrow"))
        right = coords_of((p + 1) % n_dev)
        left = coords_of((p + n_dev - 1) % n_dev)
        nbr_send = (right, left)

        def rows_of(q, rb):
            cw, cn = coords_of(q % n_dev)
            return pl.ds(pl.multiple_of((cw * n_narrow + cn) * rb, rb), rb)

        def copy(i, dirn, s, q):
            view = outs[i].at[rows_of(q, parts[i].shape[0])]
            return pltpu.make_async_remote_copy(
                src_ref=view,
                dst_ref=view,
                send_sem=send_sem.at[dirn, i, s],
                recv_sem=recv_sem.at[dirn, i, s],
                device_id=nbr_send[dirn],
                device_id_type=MESH_ID,
            )

        def sent(i, dirn, s):
            return copy(i, dirn, s, (p + n_dev - s) if dirn == 0 else (p + s))

        def arriving(i, dirn, s):
            return copy(i, dirn, s, (p + n_dev - 1 - s) if dirn == 0 else (p + 1 + s))

        barrier = pltpu.get_barrier_semaphore()
        for nb in (left, right):
            pl.semaphore_signal(barrier, 1, device_id=nb, device_id_type=MESH_ID)
        pl.semaphore_wait(barrier, 2)

        for i in range(n_in):
            cp = pltpu.make_async_copy(ins[i], outs[i].at[rows_of(p, parts[i].shape[0])], loc_sem.at[i])
            cp.start()
            cp.wait()

        def step(s, carry):
            for dirn in (0, 1):

                @pl.when(s < steps[dirn])
                def _():
                    for i in range(n_in):

                        @pl.when(s >= 1)
                        def _():
                            arriving(i, dirn, s - 1).wait_recv()

                        sent(i, dirn, s).start()

            return carry

        lax.fori_loop(0, steps[0], step, 0)
        for dirn in (0, 1):
            for i in range(n_in):
                arriving(i, dirn, steps[dirn] - 1).wait_recv()

        def drain(s, carry):
            for dirn in (0, 1):

                @pl.when(s < steps[dirn])
                def _():
                    for i in range(n_in):
                        sent(i, dirn, s).wait_send()

            return carry

        lax.fori_loop(0, steps[0], drain, 0)

    out_shape = [jax.ShapeDtypeStruct((n_dev * a.shape[0], a.shape[1]), a.dtype) for a in parts]
    total = sum(n_dev * a.size * a.dtype.itemsize for a in parts)
    return pl.pallas_call(
        kernel,
        out_shape=out_shape,
        in_specs=[pl.BlockSpec(memory_space=pl.ANY)] * n_in,
        out_specs=[pl.BlockSpec(memory_space=pltpu.VMEM)] * n_in,
        scratch_shapes=[
            pltpu.SemaphoreType.DMA((2, n_in, steps[0])),
            pltpu.SemaphoreType.DMA((2, n_in, steps[0])),
            pltpu.SemaphoreType.DMA((n_in,)),
        ],
        compiler_params=pltpu.CompilerParams(collective_id=collective_id, has_side_effects=True),
        cost_estimate=pl.CostEstimate(flops=0, transcendentals=0, bytes_accessed=2 * total),
    )(*parts)


def pack_rows(pieces, width):
    flat = jnp.concatenate(pieces)
    return jnp.pad(flat, (0, width - flat.shape[0]))[None, :]


def split_owned(packed, sizes):
    out = []
    at = 0
    for size in sizes:
        out.append(packed[:, at : at + size].reshape(-1))
        at += size
    return out


def on_device(
    inputs,
    w_qkv,
    qv_bias,
    w_out,
    out_bias,
    ln1_gain,
    ln1_shift,
    ln2_gain,
    ln2_shift,
    w_up,
    up_bias,
    w_down,
    down_bias,
    segment_ids,
    valid,
    cotangent,
    mesh_shape=None,
):
    row_count = inputs.shape[0]
    model_width = inputs.shape[1]
    seq_count = segment_ids.shape[0]
    seq_len = segment_ids.shape[1]
    head_count = model_width // HD
    n_dev = mesh_shape[0] * mesh_shape[1]
    small = (qv_bias, out_bias, ln1_gain, ln1_shift, ln2_gain, ln2_shift, up_bias, down_bias)
    small_sizes = [a.shape[0] for a in small]
    n_small = sum(small_sizes)
    width_q = w_qkv.shape[1]
    rows_q = w_qkv.shape[0]
    rows_o = w_out.size // width_q
    rows_u = w_up.size // width_q
    up_view = 16
    ring_up = mesh_shape == (8, 4) and w_up.size % (2 * up_view * 128) == 0
    pieces = [w_qkv, w_out.reshape(rows_o, width_q)]
    if not ring_up:
        pieces.append(w_up.reshape(rows_u, width_q))
    attn_buf = jnp.concatenate(pieces + [pack_rows(small, width_q)], axis=0)
    attn_all = lax.all_gather(attn_buf, ALL, axis=0, tiled=False)
    qkv_full = attn_all[:, :rows_q].reshape(-1, width_q)
    out_full = attn_all[:, rows_q : rows_q + rows_o].reshape(-1, model_width)
    at = rows_q + rows_o
    if ring_up:
        up_v = w_up.reshape(up_view, -1)
        half_v = up_v.shape[1] // 2
        up_a, up_b = ring_all_gather([up_v[:, :half_v], up_v[:, half_v:]], mesh_shape)
        up_full = jnp.concatenate([up_a, up_b], axis=1).reshape(-1, w_up.shape[1])
    else:
        up_full = attn_all[:, at : at + rows_u].reshape(-1, w_up.shape[1])
        at = at + rows_u
    small_full = split_owned(attn_all[:, at, :n_small], small_sizes)
    qv_full, outb_full, gain_one, shift_one, gain_two, shift_two, upb_full, downb_full = small_full
    down_full = lax.all_gather(w_down, ALL, axis=0, tiled=True)

    gain_one = gain_one.astype(jnp.float32)
    shift_one = shift_one.astype(jnp.float32)
    qv_full = qv_full.astype(jnp.float32)
    rows = inputs.astype(jnp.float32)
    normed_one, recip_one = norm_parts(rows)
    h_one = (normed_one * gain_one + shift_one).astype(jnp.bfloat16)
    qkv_rows = jnp.dot(h_one, qkv_full, preferred_element_type=jnp.float32)
    zero_bias = jnp.zeros((model_width,), jnp.float32)
    qkv_bias = jnp.concatenate([qv_full[:model_width], zero_bias, qv_full[model_width:]])
    qkv_b = (qkv_rows + qkv_bias).astype(jnp.bfloat16)
    attended = attention_fwd(qkv_b, segment_ids, valid)
    mid_rows = (
        rows
        + jnp.dot(attended, out_full, preferred_element_type=jnp.float32)
        + outb_full.astype(jnp.float32)
    )
    gain_two = gain_two.astype(jnp.float32)
    shift_two = shift_two.astype(jnp.float32)
    normed_two, recip_two = norm_parts(mid_rows)
    h_two = (normed_two * gain_two + shift_two).astype(jnp.bfloat16)
    upper = jnp.dot(h_two, up_full, preferred_element_type=jnp.float32) + upb_full.astype(
        jnp.float32
    )
    upper = lax.optimization_barrier(upper)
    gelu_rows = jax.nn.gelu(upper, approximate=False).astype(jnp.bfloat16)
    out_rows = (
        mid_rows
        + jnp.dot(gelu_rows, down_full, preferred_element_type=jnp.float32)
        + downb_full.astype(jnp.float32)
    )
    block_out = out_rows.astype(jnp.bfloat16)
    dy_rows = cotangent.astype(jnp.float32)
    grad_wdown = jnp.einsum("tf,td->fd", gelu_rows, cotangent, preferred_element_type=jnp.float32)
    grad_bdown = col_sum(cotangent)
    grad_g = jnp.einsum("td,fd->tf", cotangent, down_full, preferred_element_type=jnp.float32)
    cdf_part = 0.5 * (1.0 + jax.scipy.special.erf(upper * 0.7071067811865476))
    pdf_part = jnp.exp(-0.5 * upper * upper) * 0.3989422804014327
    grad_u = (grad_g * (cdf_part + upper * pdf_part)).astype(jnp.bfloat16)
    grad_bup = col_sum(grad_u)
    grad_wup = jnp.einsum("td,tf->df", h_two, grad_u, preferred_element_type=jnp.float32)
    grad_h2 = jnp.einsum("tf,df->td", grad_u, up_full, preferred_element_type=jnp.float32)
    grad_g2 = jnp.sum(grad_h2 * normed_two, axis=0)
    grad_c2 = jnp.sum(grad_h2, axis=0)
    grad_mid = dy_rows + norm_back(grad_h2, gain_two, normed_two, recip_two)
    grad_a = grad_mid.astype(jnp.bfloat16)
    grad_wout = jnp.einsum("tc,td->cd", attended, grad_a, preferred_element_type=jnp.float32)
    grad_bout = col_sum(grad_a)
    grad_o = jnp.einsum("td,cd->tc", grad_a, out_full, preferred_element_type=jnp.float32).astype(
        jnp.bfloat16
    )
    grad_qkv = attention_bwd(qkv_b, grad_o, segment_ids, valid)
    grad_cols = col_sum(grad_qkv)
    grad_bqv = jnp.concatenate([grad_cols[:model_width], grad_cols[2 * model_width :]])
    grad_wqkv = jnp.einsum("td,te->de", h_one, grad_qkv, preferred_element_type=jnp.float32)
    grad_h1 = jnp.einsum("te,de->td", grad_qkv, qkv_full, preferred_element_type=jnp.float32)
    grad_g1 = jnp.sum(grad_h1 * normed_one, axis=0)
    grad_c1 = jnp.sum(grad_h1, axis=0)
    grad_inputs = grad_mid + norm_back(grad_h1, gain_one, normed_one, recip_one)

    small_grads = (grad_bqv, grad_bout, grad_g1, grad_c1, grad_g2, grad_c2, grad_bup, grad_bdown)
    owned = jnp.concatenate([g.reshape(n_dev, -1) for g in small_grads], axis=1)
    lanes = 128
    small_rows = 8 * pl.cdiv(pl.cdiv(n_small, lanes), 8)
    owned = jnp.pad(owned, ((0, 0), (0, small_rows * lanes - n_small))).reshape(-1, lanes)
    parts = [
        (grad_wqkv, w_qkv.shape[0], True),
        (grad_wout, w_out.shape[0], True),
        (grad_wup, w_up.shape[0], True),
        (owned, small_rows, False),
    ]
    down_sum = lax.psum_scatter(grad_wdown, ALL, scatter_dimension=0, tiled=True)
    if all(rb % 8 == 0 and a.shape[1] % 256 == 0 for (a, rb, _) in parts[:3]):
        sums = ring_reduce_scatter(parts, mesh_shape, after=(grad_inputs, block_out))
    else:
        sums = [lax.psum_scatter(a, ALL, scatter_dimension=0, tiled=True) for (a, _, _) in parts]
    sums = list(sums[:3]) + [down_sum] + list(sums[3:])
    small_sums = split_owned(sums[4].reshape(1, -1), small_sizes)
    bqv, bout, g1, c1, g2, c2, bup, bdown = small_sums
    return (
        block_out,
        grad_inputs,
        sums[0],
        bqv,
        sums[1],
        bout,
        g1,
        c1,
        g2,
        c2,
        sums[2],
        bup,
        sums[3],
        bdown,
    )


def solution(mesh):
    in_specs = (
        P(("wide", "narrow"), None),
        P(("wide", "narrow"), None),
        P(("wide", "narrow")),
        P(("wide", "narrow"), None),
        P(("wide", "narrow")),
        P(("wide", "narrow")),
        P(("wide", "narrow")),
        P(("wide", "narrow")),
        P(("wide", "narrow")),
        P(("wide", "narrow"), None),
        P(("wide", "narrow")),
        P(("wide", "narrow"), None),
        P(("wide", "narrow")),
        P(("wide", "narrow"), None),
        P(("wide", "narrow"), None),
        P(("wide", "narrow"), None),
    )
    out_specs = (
        P(("wide", "narrow"), None),
        P(("wide", "narrow"), None),
        P(("wide", "narrow"), None),
        P(("wide", "narrow")),
        P(("wide", "narrow"), None),
        P(("wide", "narrow")),
        P(("wide", "narrow")),
        P(("wide", "narrow")),
        P(("wide", "narrow")),
        P(("wide", "narrow")),
        P(("wide", "narrow"), None),
        P(("wide", "narrow")),
        P(("wide", "narrow"), None),
        P(("wide", "narrow")),
    )
    body = functools.partial(on_device, mesh_shape=(mesh.shape["wide"], mesh.shape["narrow"]))
    return jax.shard_map(
        body, mesh=mesh, in_specs=in_specs, out_specs=out_specs, check_vma=False
    )
```

```python
import functools
import jax
import jax.numpy as jnp
from jax import lax
from jax.experimental import pallas as pl
from jax.experimental.pallas import tpu as pltpu
from jax.sharding import PartitionSpec as P

HD = 64
ALL = ("wide", "narrow")

EPSILON = 1e-06


def norm_parts(rows):
    center = rows - jnp.mean(rows, axis=-1, keepdims=True)
    recip = lax.rsqrt(jnp.mean(center * center, axis=-1, keepdims=True) + EPSILON)
    return (center * recip, recip)


def norm_back(grad_h, gain, normed, recip):
    scaled = grad_h * gain
    return recip * (
        scaled
        - jnp.mean(scaled, axis=-1, keepdims=True)
        - normed * jnp.mean(scaled * normed, axis=-1, keepdims=True)
    )


def col_sum(rows):
    return jnp.sum(rows.astype(jnp.float32), axis=0)


def seg_mask(seg_col, seg_row, val_row, n):
    rows = lax.broadcasted_iota(jnp.int32, (n, n), 0)
    cols = lax.broadcasted_iota(jnp.int32, (n, n), 1)
    return (seg_col == seg_row) & ((val_row == 1) | (rows == cols))


def soft_rows(qh, kh, allowed):
    scores = lax.dot_general(qh, kh, (((1,), (1,)), ((), ())), preferred_element_type=jnp.float32)
    scores = jnp.where(allowed, scores * (1.0 / HD**0.5), -1e30)
    top = jnp.max(scores, axis=-1, keepdims=True)
    expo = jnp.exp(scores - top)
    return expo * (1.0 / jnp.sum(expo, axis=-1, keepdims=True))


def attn_fwd_kernel(q_ref, k_ref, v_ref, sc_ref, sr_ref, vr_ref, o_ref):
    n = q_ref.shape[0]
    allowed = seg_mask(sc_ref[...], sr_ref[...], vr_ref[...], n)
    outs = []
    for j in range(q_ref.shape[1] // HD):
        cols = slice(j * HD, (j + 1) * HD)
        probs = soft_rows(q_ref[:, cols], k_ref[:, cols], allowed).astype(jnp.bfloat16)
        outs.append(jnp.dot(probs, v_ref[:, cols], preferred_element_type=jnp.float32))
    o_ref[...] = jnp.concatenate(outs, axis=1).astype(o_ref.dtype)


def attn_bwd_kernel(q_ref, k_ref, v_ref, do_ref, sc_ref, sr_ref, vr_ref, dqkv_ref):
    n = q_ref.shape[0]
    width = q_ref.shape[1]
    hp = pl.program_id(1)
    model_width = dqkv_ref.shape[1] // 3
    allowed = seg_mask(sc_ref[...], sr_ref[...], vr_ref[...], n)
    dqs, dks, dvs = [], [], []
    for j in range(width // HD):
        cols = slice(j * HD, (j + 1) * HD)
        qh, kh, vh, doh = q_ref[:, cols], k_ref[:, cols], v_ref[:, cols], do_ref[:, cols]
        probs = soft_rows(qh, kh, allowed)
        dvs.append(
            lax.dot_general(probs.astype(jnp.bfloat16), doh, (((0,), (0,)), ((), ())),
                            preferred_element_type=jnp.float32)
        )
        dprobs = lax.dot_general(doh, vh, (((1,), (1,)), ((), ())), preferred_element_type=jnp.float32)
        row_term = jnp.sum(probs * dprobs, axis=-1, keepdims=True)
        dscore = jnp.where(allowed, probs * (dprobs - row_term), 0.0).astype(jnp.bfloat16)
        dqs.append(jnp.dot(dscore, kh, preferred_element_type=jnp.float32) * (1.0 / HD**0.5))
        dks.append(
            lax.dot_general(dscore, qh, (((0,), (0,)), ((), ())), preferred_element_type=jnp.float32)
            * (1.0 / HD**0.5)
        )
    at = pl.multiple_of(hp * width, width)
    dqkv_ref[:, pl.ds(at, width)] = jnp.concatenate(dqs, axis=1).astype(dqkv_ref.dtype)
    dqkv_ref[:, pl.ds(at + model_width, width)] = jnp.concatenate(dks, axis=1).astype(dqkv_ref.dtype)
    dqkv_ref[:, pl.ds(at + 2 * model_width, width)] = jnp.concatenate(dvs, axis=1).astype(dqkv_ref.dtype)


def mask_operands(segment_ids, valid):
    return (segment_ids[:, :, None], segment_ids[:, None, :], valid[:, None, :])


def attention_fwd(qkv, segment_ids, valid):
    rows, width3 = qkv.shape
    model_width = width3 // 3
    n_seq, seq_len = segment_ids.shape
    blk = 12 * HD
    n_hp = model_width // blk
    off = model_width // blk
    seg_spec = [
        pl.BlockSpec((None, seq_len, 1), lambda s, h: (s, 0, 0)),
        pl.BlockSpec((None, 1, seq_len), lambda s, h: (s, 0, 0)),
        pl.BlockSpec((None, 1, seq_len), lambda s, h: (s, 0, 0)),
    ]
    flops = 4 * n_seq * seq_len * seq_len * model_width
    return pl.pallas_call(
        attn_fwd_kernel,
        out_shape=jax.ShapeDtypeStruct((rows, model_width), jnp.bfloat16),
        grid=(n_seq, n_hp),
        in_specs=[
            pl.BlockSpec((seq_len, blk), lambda s, h: (s, h)),
            pl.BlockSpec((seq_len, blk), lambda s, h: (s, off + h)),
            pl.BlockSpec((seq_len, blk), lambda s, h: (s, 2 * off + h)),
        ]
        + seg_spec,
        out_specs=pl.BlockSpec((seq_len, blk), lambda s, h: (s, h)),
        cost_estimate=pl.CostEstimate(
            flops=flops,
            transcendentals=n_seq * seq_len * seq_len * (model_width // HD),
            bytes_accessed=qkv.size * 2 + rows * model_width * 2,
        ),
    )(qkv, qkv, qkv, *mask_operands(segment_ids, valid))


def attention_bwd(qkv, grad_o, segment_ids, valid):
    rows, width3 = qkv.shape
    model_width = width3 // 3
    n_seq, seq_len = segment_ids.shape
    blk = 6 * HD
    n_hp = model_width // blk
    off = model_width // blk
    seg_spec = [
        pl.BlockSpec((None, seq_len, 1), lambda s, h: (s, 0, 0)),
        pl.BlockSpec((None, 1, seq_len), lambda s, h: (s, 0, 0)),
        pl.BlockSpec((None, 1, seq_len), lambda s, h: (s, 0, 0)),
    ]
    flops = 10 * n_seq * seq_len * seq_len * model_width
    return pl.pallas_call(
        attn_bwd_kernel,
        out_shape=jax.ShapeDtypeStruct((rows, width3), jnp.bfloat16),
        grid=(n_seq, n_hp),
        in_specs=[
            pl.BlockSpec((seq_len, blk), lambda s, h: (s, h)),
            pl.BlockSpec((seq_len, blk), lambda s, h: (s, off + h)),
            pl.BlockSpec((seq_len, blk), lambda s, h: (s, 2 * off + h)),
            pl.BlockSpec((seq_len, blk), lambda s, h: (s, h)),
        ]
        + seg_spec,
        out_specs=pl.BlockSpec((seq_len, width3), lambda s, h: (s, 0)),
        cost_estimate=pl.CostEstimate(
            flops=flops,
            transcendentals=n_seq * seq_len * seq_len * (model_width // HD),
            bytes_accessed=qkv.size * 4 + rows * model_width * 2,
        ),
    )(qkv, qkv, qkv, grad_o, *mask_operands(segment_ids, valid))


MESH_ID = pl.DeviceIdType.MESH


def ring_maps(n_wide, n_narrow):
    n_dev = n_wide * n_narrow
    if (n_wide, n_narrow) == (8, 4):
        def pos_of(w, n):
            z, y, x, c = w // 2, w % 2, n // 2, n % 2
            q = 2 * x + (x + y) % 2
            k = 4 * q + z + (q % 2) * (3 - 2 * z)
            return 2 * k + c

        def coords_of(p):
            k, c = p // 2, p % 2
            q, r = k // 4, k % 4
            z = r + (q % 2) * (3 - 2 * r)
            x = q // 2
            y = (q % 2 + x) % 2
            return z * 2 + y, x * 2 + c

    else:
        def pos_of(w, n):
            return w * n_narrow + n

        def coords_of(p):
            return p // n_narrow, p % n_narrow

    return n_dev, pos_of, coords_of


def ring_reduce_scatter(parts, mesh_shape, after=(), collective_id=0):
    n_wide, n_narrow = mesh_shape
    n_dev, pos_of, coords_of = ring_maps(n_wide, n_narrow)
    specs = []
    for i, (a, rb, split) in enumerate(parts):
        cols = a.shape[1]
        if split:
            specs.append((i, 0, 0, cols // 2))
        else:
            specs.append((i, 0, 0, cols))
    for i, (a, rb, split) in enumerate(parts):
        if split:
            specs.append((i, 1, a.shape[1] // 2, a.shape[1] // 2))
    n_in = len(parts)
    n_after = len(after)
    n_sp = len(specs)
    last_step = n_dev - 2

    def kernel(*refs):
        ins = refs[:n_in]
        outs = refs[n_in + n_after : 2 * n_in + n_after]
        at = 2 * n_in + n_after
        bufs = refs[at : at + n_sp]
        locs = refs[at + n_sp : at + 2 * n_sp]
        send_sem, recv_sem, loc_sem, credit = refs[at + 2 * n_sp :]
        p = pos_of(lax.axis_index("wide"), lax.axis_index("narrow"))
        right = coords_of((p + 1) % n_dev)
        left = coords_of((p + n_dev - 1) % n_dev)
        nbr_send = (right, left)
        nbr_recv = (left, right)

        def rows_of(q, rb):
            cw, cn = coords_of(q % n_dev)
            start = (cw * n_narrow + cn) * rb
            if rb % 8 == 0:
                start = pl.multiple_of(start, 8)
            return pl.ds(start, rb)

        def remote(j, s):
            return pltpu.make_async_remote_copy(
                src_ref=bufs[j].at[s % 3],
                dst_ref=bufs[j].at[(s + 1) % 3],
                send_sem=send_sem.at[j, s % 3],
                recv_sem=recv_sem.at[j, (s + 1) % 3],
                device_id=nbr_send[specs[j][1]],
                device_id_type=MESH_ID,
            )

        def local(j, s):
            i, dirn, c0, cw = specs[j]
            q = (p + 2 * n_dev - s - 2) if dirn == 0 else (p + s + 2)
            return pltpu.make_async_copy(
                ins[i].at[rows_of(q, parts[i][1]), pl.ds(c0, cw)], locs[j].at[s % 2], loc_sem.at[j, s % 2]
            )

        barrier = pltpu.get_barrier_semaphore()
        for nb in (left, right):
            pl.semaphore_signal(barrier, 1, device_id=nb, device_id_type=MESH_ID)
        pl.semaphore_wait(barrier, 2)

        for j, (i, dirn, c0, cw) in enumerate(specs):
            q = p + n_dev - 1 if dirn == 0 else p + 1
            cp = pltpu.make_async_copy(
                ins[i].at[rows_of(q, parts[i][1]), pl.ds(c0, cw)], bufs[j].at[0], loc_sem.at[j, 1]
            )
            cp.start()
            cp.wait()
        for j in range(n_sp):
            remote(j, 0).start()
            local(j, 0).start()

        def step(s, carry):
            for j in range(n_sp):
                dirn = specs[j][1]
                local(j, s).wait()
                remote(j, s).wait_recv()
                nxt = (s + 1) % 3
                bufs[j][nxt] = bufs[j][nxt] + locs[j][s % 2]
                if j == 0 or specs[j - 1][1] != dirn:

                    @pl.when((s >= 1) & (s + 1 <= last_step))
                    def _():
                        pl.semaphore_wait(credit.at[dirn], 1)

                @pl.when(s + 1 <= last_step)
                def _():
                    remote(j, s + 1).start()
                    local(j, s + 1).start()

            for j in range(n_sp):
                remote(j, s).wait_send()
            for dirn in (0, 1):

                @pl.when(s <= last_step - 2)
                def _():
                    pl.semaphore_signal(
                        credit.at[dirn], 1, device_id=nbr_recv[dirn], device_id_type=MESH_ID
                    )

            return carry

        lax.fori_loop(0, last_step + 1, step, 0)
        fin = (last_step + 1) % 3
        for j, (i, dirn, c0, cw) in enumerate(specs):
            outs[i][:, pl.ds(c0, cw)] = bufs[j][fin]

    out_shape = [jax.ShapeDtypeStruct((rb, a.shape[1]), a.dtype) for (a, rb, _) in parts]
    scratch = [pltpu.VMEM((3, parts[i][1], cw), jnp.float32) for (i, _, _, cw) in specs]
    scratch += [pltpu.VMEM((2, parts[i][1], cw), jnp.float32) for (i, _, _, cw) in specs]
    scratch += [
        pltpu.SemaphoreType.DMA((n_sp, 3)),
        pltpu.SemaphoreType.DMA((n_sp, 3)),
        pltpu.SemaphoreType.DMA((n_sp, 2)),
        pltpu.SemaphoreType.REGULAR((2,)),
    ]
    total = sum(a.size * 4 for (a, _, _) in parts)
    return pl.pallas_call(
        kernel,
        out_shape=out_shape,
        in_specs=[pl.BlockSpec(memory_space=pl.ANY)] * (n_in + n_after),
        out_specs=[pl.BlockSpec(memory_space=pltpu.VMEM)] * n_in,
        scratch_shapes=scratch,
        compiler_params=pltpu.CompilerParams(
            collective_id=collective_id, has_side_effects=True, vmem_limit_bytes=48 * 1024 * 1024
        ),
        cost_estimate=pl.CostEstimate(flops=total // 4, transcendentals=0, bytes_accessed=2 * total),
    )(*[a for (a, _, _) in parts], *after)


def ring_all_gather(parts, mesh_shape, collective_id=1):
    n_wide, n_narrow = mesh_shape
    n_dev, pos_of, coords_of = ring_maps(n_wide, n_narrow)
    n_in = len(parts)
    steps = (n_dev // 2, n_dev - 1 - n_dev // 2)

    def kernel(*refs):
        ins = refs[:n_in]
        outs = refs[n_in : 2 * n_in]
        send_sem, recv_sem, loc_sem = refs[2 * n_in :]
        p = pos_of(lax.axis_index("wide"), lax.axis_index("narrow"))
        right = coords_of((p + 1) % n_dev)
        left = coords_of((p + n_dev - 1) % n_dev)
        nbr_send = (right, left)

        def rows_of(q, rb):
            cw, cn = coords_of(q % n_dev)
            return pl.ds(pl.multiple_of((cw * n_narrow + cn) * rb, rb), rb)

        def copy(i, dirn, s, q):
            view = outs[i].at[rows_of(q, parts[i].shape[0])]
            return pltpu.make_async_remote_copy(
                src_ref=view,
                dst_ref=view,
                send_sem=send_sem.at[dirn, i, s],
                recv_sem=recv_sem.at[dirn, i, s],
                device_id=nbr_send[dirn],
                device_id_type=MESH_ID,
            )

        def sent(i, dirn, s):
            return copy(i, dirn, s, (p + n_dev - s) if dirn == 0 else (p + s))

        def arriving(i, dirn, s):
            return copy(i, dirn, s, (p + n_dev - 1 - s) if dirn == 0 else (p + 1 + s))

        barrier = pltpu.get_barrier_semaphore()
        for nb in (left, right):
            pl.semaphore_signal(barrier, 1, device_id=nb, device_id_type=MESH_ID)
        pl.semaphore_wait(barrier, 2)

        for i in range(n_in):
            cp = pltpu.make_async_copy(ins[i], outs[i].at[rows_of(p, parts[i].shape[0])], loc_sem.at[i])
            cp.start()
            cp.wait()

        def step(s, carry):
            for dirn in (0, 1):

                @pl.when(s < steps[dirn])
                def _():
                    for i in range(n_in):

                        @pl.when(s >= 1)
                        def _():
                            arriving(i, dirn, s - 1).wait_recv()

                        sent(i, dirn, s).start()

            return carry

        lax.fori_loop(0, steps[0], step, 0)
        for dirn in (0, 1):
            for i in range(n_in):
                arriving(i, dirn, steps[dirn] - 1).wait_recv()

        def drain(s, carry):
            for dirn in (0, 1):

                @pl.when(s < steps[dirn])
                def _():
                    for i in range(n_in):
                        sent(i, dirn, s).wait_send()

            return carry

        lax.fori_loop(0, steps[0], drain, 0)

    out_shape = [jax.ShapeDtypeStruct((n_dev * a.shape[0], a.shape[1]), a.dtype) for a in parts]
    total = sum(n_dev * a.size * a.dtype.itemsize for a in parts)
    return pl.pallas_call(
        kernel,
        out_shape=out_shape,
        in_specs=[pl.BlockSpec(memory_space=pl.ANY)] * n_in,
        out_specs=[pl.BlockSpec(memory_space=pltpu.VMEM)] * n_in,
        scratch_shapes=[
            pltpu.SemaphoreType.DMA((2, n_in, steps[0])),
            pltpu.SemaphoreType.DMA((2, n_in, steps[0])),
            pltpu.SemaphoreType.DMA((n_in,)),
        ],
        compiler_params=pltpu.CompilerParams(collective_id=collective_id, has_side_effects=True),
        cost_estimate=pl.CostEstimate(flops=0, transcendentals=0, bytes_accessed=2 * total),
    )(*parts)


def pack_rows(pieces, width):
    flat = jnp.concatenate(pieces)
    return jnp.pad(flat, (0, width - flat.shape[0]))[None, :]


def split_owned(packed, sizes):
    out = []
    at = 0
    for size in sizes:
        out.append(packed[:, at : at + size].reshape(-1))
        at += size
    return out


def on_device(
    inputs,
    w_qkv,
    qv_bias,
    w_out,
    out_bias,
    ln1_gain,
    ln1_shift,
    ln2_gain,
    ln2_shift,
    w_up,
    up_bias,
    w_down,
    down_bias,
    segment_ids,
    valid,
    cotangent,
    mesh_shape=None,
):
    row_count = inputs.shape[0]
    model_width = inputs.shape[1]
    seq_count = segment_ids.shape[0]
    seq_len = segment_ids.shape[1]
    head_count = model_width // HD
    n_dev = mesh_shape[0] * mesh_shape[1]
    small = (qv_bias, out_bias, ln1_gain, ln1_shift, ln2_gain, ln2_shift, up_bias, down_bias)
    small_sizes = [a.shape[0] for a in small]
    n_small = sum(small_sizes)
    width_q = w_qkv.shape[1]
    rows_q = w_qkv.shape[0]
    rows_o = w_out.size // width_q
    rows_u = w_up.size // width_q
    up_view = 16
    ring_up = mesh_shape == (8, 4) and w_up.size % (2 * up_view * 128) == 0
    pieces = [w_qkv, w_out.reshape(rows_o, width_q)]
    if not ring_up:
        pieces.append(w_up.reshape(rows_u, width_q))
    attn_buf = jnp.concatenate(pieces + [pack_rows(small, width_q)], axis=0)
    attn_all = lax.all_gather(attn_buf, ALL, axis=0, tiled=False)
    qkv_full = attn_all[:, :rows_q].reshape(-1, width_q)
    out_full = attn_all[:, rows_q : rows_q + rows_o].reshape(-1, model_width)
    at = rows_q + rows_o
    if ring_up:
        up_v = w_up.reshape(up_view, -1)
        half_v = up_v.shape[1] // 2
        up_a, up_b = ring_all_gather([up_v[:, :half_v], up_v[:, half_v:]], mesh_shape)
        up_full = jnp.concatenate([up_a, up_b], axis=1).reshape(-1, w_up.shape[1])
    else:
        up_full = attn_all[:, at : at + rows_u].reshape(-1, w_up.shape[1])
        at = at + rows_u
    small_full = split_owned(attn_all[:, at, :n_small], small_sizes)
    qv_full, outb_full, gain_one, shift_one, gain_two, shift_two, upb_full, downb_full = small_full
    down_full = lax.all_gather(w_down, ALL, axis=0, tiled=True)

    gain_one = gain_one.astype(jnp.float32)
    shift_one = shift_one.astype(jnp.float32)
    qv_full = qv_full.astype(jnp.float32)
    rows = inputs.astype(jnp.float32)
    normed_one, recip_one = norm_parts(rows)
    h_one = (normed_one * gain_one + shift_one).astype(jnp.bfloat16)
    qkv_rows = jnp.dot(h_one, qkv_full, preferred_element_type=jnp.float32)
    zero_bias = jnp.zeros((model_width,), jnp.float32)
    qkv_bias = jnp.concatenate([qv_full[:model_width], zero_bias, qv_full[model_width:]])
    qkv_b = (qkv_rows + qkv_bias).astype(jnp.bfloat16)
    attended = attention_fwd(qkv_b, segment_ids, valid)
    mid_rows = (
        rows
        + jnp.dot(attended, out_full, preferred_element_type=jnp.float32)
        + outb_full.astype(jnp.float32)
    )
    gain_two = gain_two.astype(jnp.float32)
    shift_two = shift_two.astype(jnp.float32)
    normed_two, recip_two = norm_parts(mid_rows)
    h_two = (normed_two * gain_two + shift_two).astype(jnp.bfloat16)
    upper = jnp.dot(h_two, up_full, preferred_element_type=jnp.float32) + upb_full.astype(
        jnp.float32
    )
    upper = lax.optimization_barrier(upper)
    gelu_rows = jax.nn.gelu(upper, approximate=False).astype(jnp.bfloat16)
    out_rows = (
        mid_rows
        + jnp.dot(gelu_rows, down_full, preferred_element_type=jnp.float32)
        + downb_full.astype(jnp.float32)
    )
    block_out = out_rows.astype(jnp.bfloat16)
    dy_rows = cotangent.astype(jnp.float32)
    grad_wdown = jnp.einsum("tf,td->fd", gelu_rows, cotangent, preferred_element_type=jnp.float32)
    grad_bdown = col_sum(cotangent)
    grad_g = jnp.einsum("td,fd->tf", cotangent, down_full, preferred_element_type=jnp.float32)
    cdf_part = 0.5 * (1.0 + jax.scipy.special.erf(upper * 0.7071067811865476))
    pdf_part = jnp.exp(-0.5 * upper * upper) * 0.3989422804014327
    grad_u = (grad_g * (cdf_part + upper * pdf_part)).astype(jnp.bfloat16)
    grad_bup = col_sum(grad_u)
    grad_wup = jnp.einsum("td,tf->df", h_two, grad_u, preferred_element_type=jnp.float32)
    grad_h2 = jnp.einsum("tf,df->td", grad_u, up_full, preferred_element_type=jnp.float32)
    grad_g2 = jnp.sum(grad_h2 * normed_two, axis=0)
    grad_c2 = jnp.sum(grad_h2, axis=0)
    grad_mid = dy_rows + norm_back(grad_h2, gain_two, normed_two, recip_two)
    grad_a = grad_mid.astype(jnp.bfloat16)
    grad_wout = jnp.einsum("tc,td->cd", attended, grad_a, preferred_element_type=jnp.float32)
    grad_bout = col_sum(grad_a)
    grad_o = jnp.einsum("td,cd->tc", grad_a, out_full, preferred_element_type=jnp.float32).astype(
        jnp.bfloat16
    )
    grad_qkv = attention_bwd(qkv_b, grad_o, segment_ids, valid)
    grad_cols = col_sum(grad_qkv)
    grad_bqv = jnp.concatenate([grad_cols[:model_width], grad_cols[2 * model_width :]])
    grad_wqkv = jnp.einsum("td,te->de", h_one, grad_qkv, preferred_element_type=jnp.float32)
    grad_h1 = jnp.einsum("te,de->td", grad_qkv, qkv_full, preferred_element_type=jnp.float32)
    grad_g1 = jnp.sum(grad_h1 * normed_one, axis=0)
    grad_c1 = jnp.sum(grad_h1, axis=0)
    grad_inputs = grad_mid + norm_back(grad_h1, gain_one, normed_one, recip_one)

    small_grads = (grad_bqv, grad_bout, grad_g1, grad_c1, grad_g2, grad_c2, grad_bup, grad_bdown)
    owned = jnp.concatenate([g.reshape(n_dev, -1) for g in small_grads], axis=1)
    lanes = 128
    small_rows = 8 * pl.cdiv(pl.cdiv(n_small, lanes), 8)
    owned = jnp.pad(owned, ((0, 0), (0, small_rows * lanes - n_small))).reshape(-1, lanes)
    parts = [
        (grad_wqkv, w_qkv.shape[0], True),
        (grad_wout, w_out.shape[0], True),
        (grad_wup, w_up.shape[0], True),
        (owned, small_rows, False),
    ]
    down_sum = lax.psum_scatter(grad_wdown, ALL, scatter_dimension=0, tiled=True)
    if all(rb % 8 == 0 and a.shape[1] % 256 == 0 for (a, rb, _) in parts[:3]):
        sums = ring_reduce_scatter(parts, mesh_shape, after=(grad_inputs, block_out))
    else:
        sums = [lax.psum_scatter(a, ALL, scatter_dimension=0, tiled=True) for (a, _, _) in parts]
    sums = list(sums[:3]) + [down_sum] + list(sums[3:])
    small_sums = split_owned(sums[4].reshape(1, -1), small_sizes)
    bqv, bout, g1, c1, g2, c2, bup, bdown = small_sums
    return (
        block_out,
        grad_inputs,
        sums[0],
        bqv,
        sums[1],
        bout,
        g1,
        c1,
        g2,
        c2,
        sums[2],
        bup,
        sums[3],
        bdown,
    )


def solution(mesh):
    in_specs = (
        P(("wide", "narrow"), None),
        P(("wide", "narrow"), None),
        P(("wide", "narrow")),
        P(("wide", "narrow"), None),
        P(("wide", "narrow")),
        P(("wide", "narrow")),
        P(("wide", "narrow")),
        P(("wide", "narrow")),
        P(("wide", "narrow")),
        P(("wide", "narrow"), None),
        P(("wide", "narrow")),
        P(("wide", "narrow"), None),
        P(("wide", "narrow")),
        P(("wide", "narrow"), None),
        P(("wide", "narrow"), None),
        P(("wide", "narrow"), None),
    )
    out_specs = (
        P(("wide", "narrow"), None),
        P(("wide", "narrow"), None),
        P(("wide", "narrow"), None),
        P(("wide", "narrow")),
        P(("wide", "narrow"), None),
        P(("wide", "narrow")),
        P(("wide", "narrow")),
        P(("wide", "narrow")),
        P(("wide", "narrow")),
        P(("wide", "narrow")),
        P(("wide", "narrow"), None),
        P(("wide", "narrow")),
        P(("wide", "narrow"), None),
        P(("wide", "narrow")),
    )
    body = functools.partial(on_device, mesh_shape=(mesh.shape["wide"], mesh.shape["narrow"]))
    return jax.shard_map(
        body, mesh=mesh, in_specs=in_specs, out_specs=out_specs, check_vma=False
    )
```

```python
import functools
import jax
import jax.numpy as jnp
from jax import lax
from jax.experimental import pallas as pl
from jax.experimental.pallas import tpu as pltpu
from jax.sharding import PartitionSpec as P

HD = 64
ALL = ("wide", "narrow")

EPSILON = 1e-06


def norm_parts(rows):
    center = rows - jnp.mean(rows, axis=-1, keepdims=True)
    recip = lax.rsqrt(jnp.mean(center * center, axis=-1, keepdims=True) + EPSILON)
    return (center * recip, recip)


def norm_back(grad_h, gain, normed, recip):
    scaled = grad_h * gain
    return recip * (
        scaled
        - jnp.mean(scaled, axis=-1, keepdims=True)
        - normed * jnp.mean(scaled * normed, axis=-1, keepdims=True)
    )


def col_sum(rows):
    return jnp.sum(rows.astype(jnp.float32), axis=0)


def seg_mask(seg_col, seg_row, val_row, n):
    rows = lax.broadcasted_iota(jnp.int32, (n, n), 0)
    cols = lax.broadcasted_iota(jnp.int32, (n, n), 1)
    return (seg_col == seg_row) & ((val_row == 1) | (rows == cols))


def soft_rows(qh, kh, allowed):
    scores = lax.dot_general(qh, kh, (((1,), (1,)), ((), ())), preferred_element_type=jnp.float32)
    scores = jnp.where(allowed, scores * (1.0 / HD**0.5), -1e30)
    top = jnp.max(scores, axis=-1, keepdims=True)
    expo = jnp.exp(scores - top)
    return expo * (1.0 / jnp.sum(expo, axis=-1, keepdims=True))


def attn_fwd_kernel(q_ref, k_ref, v_ref, sc_ref, sr_ref, vr_ref, o_ref):
    n = q_ref.shape[0]
    allowed = seg_mask(sc_ref[...], sr_ref[...], vr_ref[...], n)
    outs = []
    for j in range(q_ref.shape[1] // HD):
        cols = slice(j * HD, (j + 1) * HD)
        probs = soft_rows(q_ref[:, cols], k_ref[:, cols], allowed).astype(jnp.bfloat16)
        outs.append(jnp.dot(probs, v_ref[:, cols], preferred_element_type=jnp.float32))
    o_ref[...] = jnp.concatenate(outs, axis=1).astype(o_ref.dtype)


def attn_bwd_kernel(q_ref, k_ref, v_ref, do_ref, sc_ref, sr_ref, vr_ref, dqkv_ref):
    n = q_ref.shape[0]
    width = q_ref.shape[1]
    hp = pl.program_id(1)
    model_width = dqkv_ref.shape[1] // 3
    allowed = seg_mask(sc_ref[...], sr_ref[...], vr_ref[...], n)
    dqs, dks, dvs = [], [], []
    for j in range(width // HD):
        cols = slice(j * HD, (j + 1) * HD)
        qh, kh, vh, doh = q_ref[:, cols], k_ref[:, cols], v_ref[:, cols], do_ref[:, cols]
        probs = soft_rows(qh, kh, allowed)
        dvs.append(
            lax.dot_general(probs.astype(jnp.bfloat16), doh, (((0,), (0,)), ((), ())),
                            preferred_element_type=jnp.float32)
        )
        dprobs = lax.dot_general(doh, vh, (((1,), (1,)), ((), ())), preferred_element_type=jnp.float32)
        row_term = jnp.sum(probs * dprobs, axis=-1, keepdims=True)
        dscore = jnp.where(allowed, probs * (dprobs - row_term), 0.0).astype(jnp.bfloat16)
        dqs.append(jnp.dot(dscore, kh, preferred_element_type=jnp.float32) * (1.0 / HD**0.5))
        dks.append(
            lax.dot_general(dscore, qh, (((0,), (0,)), ((), ())), preferred_element_type=jnp.float32)
            * (1.0 / HD**0.5)
        )
    at = pl.multiple_of(hp * width, width)
    dqkv_ref[:, pl.ds(at, width)] = jnp.concatenate(dqs, axis=1).astype(dqkv_ref.dtype)
    dqkv_ref[:, pl.ds(at + model_width, width)] = jnp.concatenate(dks, axis=1).astype(dqkv_ref.dtype)
    dqkv_ref[:, pl.ds(at + 2 * model_width, width)] = jnp.concatenate(dvs, axis=1).astype(dqkv_ref.dtype)


def mask_operands(segment_ids, valid):
    return (segment_ids[:, :, None], segment_ids[:, None, :], valid[:, None, :])


def attention_fwd(qkv, segment_ids, valid):
    rows, width3 = qkv.shape
    model_width = width3 // 3
    n_seq, seq_len = segment_ids.shape
    blk = 12 * HD
    n_hp = model_width // blk
    off = model_width // blk
    seg_spec = [
        pl.BlockSpec((None, seq_len, 1), lambda s, h: (s, 0, 0)),
        pl.BlockSpec((None, 1, seq_len), lambda s, h: (s, 0, 0)),
        pl.BlockSpec((None, 1, seq_len), lambda s, h: (s, 0, 0)),
    ]
    flops = 4 * n_seq * seq_len * seq_len * model_width
    return pl.pallas_call(
        attn_fwd_kernel,
        out_shape=jax.ShapeDtypeStruct((rows, model_width), jnp.bfloat16),
        grid=(n_seq, n_hp),
        in_specs=[
            pl.BlockSpec((seq_len, blk), lambda s, h: (s, h)),
            pl.BlockSpec((seq_len, blk), lambda s, h: (s, off + h)),
            pl.BlockSpec((seq_len, blk), lambda s, h: (s, 2 * off + h)),
        ]
        + seg_spec,
        out_specs=pl.BlockSpec((seq_len, blk), lambda s, h: (s, h)),
        cost_estimate=pl.CostEstimate(
            flops=flops,
            transcendentals=n_seq * seq_len * seq_len * (model_width // HD),
            bytes_accessed=qkv.size * 2 + rows * model_width * 2,
        ),
    )(qkv, qkv, qkv, *mask_operands(segment_ids, valid))


def attention_bwd(qkv, grad_o, segment_ids, valid):
    rows, width3 = qkv.shape
    model_width = width3 // 3
    n_seq, seq_len = segment_ids.shape
    blk = 12 * HD
    n_hp = model_width // blk
    off = model_width // blk
    seg_spec = [
        pl.BlockSpec((None, seq_len, 1), lambda s, h: (s, 0, 0)),
        pl.BlockSpec((None, 1, seq_len), lambda s, h: (s, 0, 0)),
        pl.BlockSpec((None, 1, seq_len), lambda s, h: (s, 0, 0)),
    ]
    flops = 10 * n_seq * seq_len * seq_len * model_width
    return pl.pallas_call(
        attn_bwd_kernel,
        out_shape=jax.ShapeDtypeStruct((rows, width3), jnp.bfloat16),
        grid=(n_seq, n_hp),
        in_specs=[
            pl.BlockSpec((seq_len, blk), lambda s, h: (s, h)),
            pl.BlockSpec((seq_len, blk), lambda s, h: (s, off + h)),
            pl.BlockSpec((seq_len, blk), lambda s, h: (s, 2 * off + h)),
            pl.BlockSpec((seq_len, blk), lambda s, h: (s, h)),
        ]
        + seg_spec,
        out_specs=pl.BlockSpec((seq_len, width3), lambda s, h: (s, 0)),
        cost_estimate=pl.CostEstimate(
            flops=flops,
            transcendentals=n_seq * seq_len * seq_len * (model_width // HD),
            bytes_accessed=qkv.size * 4 + rows * model_width * 2,
        ),
    )(qkv, qkv, qkv, grad_o, *mask_operands(segment_ids, valid))


MESH_ID = pl.DeviceIdType.MESH


def ring_maps(n_wide, n_narrow):
    n_dev = n_wide * n_narrow
    if (n_wide, n_narrow) == (8, 4):
        def pos_of(w, n):
            z, y, x, c = w // 2, w % 2, n // 2, n % 2
            q = 2 * x + (x + y) % 2
            k = 4 * q + z + (q % 2) * (3 - 2 * z)
            return 2 * k + c

        def coords_of(p):
            k, c = p // 2, p % 2
            q, r = k // 4, k % 4
            z = r + (q % 2) * (3 - 2 * r)
            x = q // 2
            y = (q % 2 + x) % 2
            return z * 2 + y, x * 2 + c

    else:
        def pos_of(w, n):
            return w * n_narrow + n

        def coords_of(p):
            return p // n_narrow, p % n_narrow

    return n_dev, pos_of, coords_of


def ring_reduce_scatter(parts, mesh_shape, after=(), collective_id=0):
    n_wide, n_narrow = mesh_shape
    n_dev, pos_of, coords_of = ring_maps(n_wide, n_narrow)
    specs = []
    for i, (a, rb, split) in enumerate(parts):
        cols = a.shape[1]
        if split:
            specs.append((i, 0, 0, cols // 2))
        else:
            specs.append((i, 0, 0, cols))
    for i, (a, rb, split) in enumerate(parts):
        if split:
            specs.append((i, 1, a.shape[1] // 2, a.shape[1] // 2))
    n_in = len(parts)
    n_after = len(after)
    n_sp = len(specs)
    last_step = n_dev - 2

    def kernel(*refs):
        ins = refs[:n_in]
        outs = refs[n_in + n_after : 2 * n_in + n_after]
        at = 2 * n_in + n_after
        bufs = refs[at : at + n_sp]
        locs = refs[at + n_sp : at + 2 * n_sp]
        send_sem, recv_sem, loc_sem, credit = refs[at + 2 * n_sp :]
        p = pos_of(lax.axis_index("wide"), lax.axis_index("narrow"))
        right = coords_of((p + 1) % n_dev)
        left = coords_of((p + n_dev - 1) % n_dev)
        nbr_send = (right, left)
        nbr_recv = (left, right)

        def rows_of(q, rb):
            cw, cn = coords_of(q % n_dev)
            start = (cw * n_narrow + cn) * rb
            if rb % 8 == 0:
                start = pl.multiple_of(start, 8)
            return pl.ds(start, rb)

        def remote(j, s):
            return pltpu.make_async_remote_copy(
                src_ref=bufs[j].at[s % 3],
                dst_ref=bufs[j].at[(s + 1) % 3],
                send_sem=send_sem.at[j, s % 3],
                recv_sem=recv_sem.at[j, (s + 1) % 3],
                device_id=nbr_send[specs[j][1]],
                device_id_type=MESH_ID,
            )

        def local(j, s):
            i, dirn, c0, cw = specs[j]
            q = (p + 2 * n_dev - s - 2) if dirn == 0 else (p + s + 2)
            return pltpu.make_async_copy(
                ins[i].at[rows_of(q, parts[i][1]), pl.ds(c0, cw)], locs[j].at[s % 2], loc_sem.at[j, s % 2]
            )

        barrier = pltpu.get_barrier_semaphore()
        for nb in (left, right):
            pl.semaphore_signal(barrier, 1, device_id=nb, device_id_type=MESH_ID)
        pl.semaphore_wait(barrier, 2)

        for j, (i, dirn, c0, cw) in enumerate(specs):
            q = p + n_dev - 1 if dirn == 0 else p + 1
            cp = pltpu.make_async_copy(
                ins[i].at[rows_of(q, parts[i][1]), pl.ds(c0, cw)], bufs[j].at[0], loc_sem.at[j, 1]
            )
            cp.start()
            cp.wait()
        for j in range(n_sp):
            remote(j, 0).start()
            local(j, 0).start()

        def step(s, carry):
            for j in range(n_sp):
                dirn = specs[j][1]
                local(j, s).wait()
                remote(j, s).wait_recv()
                nxt = (s + 1) % 3
                bufs[j][nxt] = bufs[j][nxt] + locs[j][s % 2]
                if j == 0 or specs[j - 1][1] != dirn:

                    @pl.when((s >= 1) & (s + 1 <= last_step))
                    def _():
                        pl.semaphore_wait(credit.at[dirn], 1)

                @pl.when(s + 1 <= last_step)
                def _():
                    remote(j, s + 1).start()
                    local(j, s + 1).start()

            for j in range(n_sp):
                remote(j, s).wait_send()
            for dirn in (0, 1):

                @pl.when(s <= last_step - 2)
                def _():
                    pl.semaphore_signal(
                        credit.at[dirn], 1, device_id=nbr_recv[dirn], device_id_type=MESH_ID
                    )

            return carry

        lax.fori_loop(0, last_step + 1, step, 0)
        fin = (last_step + 1) % 3
        for j, (i, dirn, c0, cw) in enumerate(specs):
            outs[i][:, pl.ds(c0, cw)] = bufs[j][fin]

    out_shape = [jax.ShapeDtypeStruct((rb, a.shape[1]), a.dtype) for (a, rb, _) in parts]
    scratch = [pltpu.VMEM((3, parts[i][1], cw), jnp.float32) for (i, _, _, cw) in specs]
    scratch += [pltpu.VMEM((2, parts[i][1], cw), jnp.float32) for (i, _, _, cw) in specs]
    scratch += [
        pltpu.SemaphoreType.DMA((n_sp, 3)),
        pltpu.SemaphoreType.DMA((n_sp, 3)),
        pltpu.SemaphoreType.DMA((n_sp, 2)),
        pltpu.SemaphoreType.REGULAR((2,)),
    ]
    total = sum(a.size * 4 for (a, _, _) in parts)
    return pl.pallas_call(
        kernel,
        out_shape=out_shape,
        in_specs=[pl.BlockSpec(memory_space=pl.ANY)] * (n_in + n_after),
        out_specs=[pl.BlockSpec(memory_space=pltpu.VMEM)] * n_in,
        scratch_shapes=scratch,
        compiler_params=pltpu.CompilerParams(
            collective_id=collective_id, has_side_effects=True, vmem_limit_bytes=48 * 1024 * 1024
        ),
        cost_estimate=pl.CostEstimate(flops=total // 4, transcendentals=0, bytes_accessed=2 * total),
    )(*[a for (a, _, _) in parts], *after)


def ring_all_gather(parts, mesh_shape, collective_id=1):
    n_wide, n_narrow = mesh_shape
    n_dev, pos_of, coords_of = ring_maps(n_wide, n_narrow)
    n_in = len(parts)
    steps = (n_dev // 2, n_dev - 1 - n_dev // 2)

    def kernel(*refs):
        ins = refs[:n_in]
        outs = refs[n_in : 2 * n_in]
        send_sem, recv_sem, loc_sem = refs[2 * n_in :]
        p = pos_of(lax.axis_index("wide"), lax.axis_index("narrow"))
        right = coords_of((p + 1) % n_dev)
        left = coords_of((p + n_dev - 1) % n_dev)
        nbr_send = (right, left)

        def rows_of(q, rb):
            cw, cn = coords_of(q % n_dev)
            return pl.ds(pl.multiple_of((cw * n_narrow + cn) * rb, rb), rb)

        def copy(i, dirn, s, q):
            view = outs[i].at[rows_of(q, parts[i].shape[0])]
            return pltpu.make_async_remote_copy(
                src_ref=view,
                dst_ref=view,
                send_sem=send_sem.at[dirn, i, s],
                recv_sem=recv_sem.at[dirn, i, s],
                device_id=nbr_send[dirn],
                device_id_type=MESH_ID,
            )

        def sent(i, dirn, s):
            return copy(i, dirn, s, (p + n_dev - s) if dirn == 0 else (p + s))

        def arriving(i, dirn, s):
            return copy(i, dirn, s, (p + n_dev - 1 - s) if dirn == 0 else (p + 1 + s))

        barrier = pltpu.get_barrier_semaphore()
        for nb in (left, right):
            pl.semaphore_signal(barrier, 1, device_id=nb, device_id_type=MESH_ID)
        pl.semaphore_wait(barrier, 2)

        for i in range(n_in):
            cp = pltpu.make_async_copy(ins[i], outs[i].at[rows_of(p, parts[i].shape[0])], loc_sem.at[i])
            cp.start()
            cp.wait()

        def step(s, carry):
            for dirn in (0, 1):

                @pl.when(s < steps[dirn])
                def _():
                    for i in range(n_in):

                        @pl.when(s >= 1)
                        def _():
                            arriving(i, dirn, s - 1).wait_recv()

                        sent(i, dirn, s).start()

            return carry

        lax.fori_loop(0, steps[0], step, 0)
        for dirn in (0, 1):
            for i in range(n_in):
                arriving(i, dirn, steps[dirn] - 1).wait_recv()

        def drain(s, carry):
            for dirn in (0, 1):

                @pl.when(s < steps[dirn])
                def _():
                    for i in range(n_in):
                        sent(i, dirn, s).wait_send()

            return carry

        lax.fori_loop(0, steps[0], drain, 0)

    out_shape = [jax.ShapeDtypeStruct((n_dev * a.shape[0], a.shape[1]), a.dtype) for a in parts]
    total = sum(n_dev * a.size * a.dtype.itemsize for a in parts)
    return pl.pallas_call(
        kernel,
        out_shape=out_shape,
        in_specs=[pl.BlockSpec(memory_space=pl.ANY)] * n_in,
        out_specs=[pl.BlockSpec(memory_space=pltpu.VMEM)] * n_in,
        scratch_shapes=[
            pltpu.SemaphoreType.DMA((2, n_in, steps[0])),
            pltpu.SemaphoreType.DMA((2, n_in, steps[0])),
            pltpu.SemaphoreType.DMA((n_in,)),
        ],
        compiler_params=pltpu.CompilerParams(collective_id=collective_id, has_side_effects=True),
        cost_estimate=pl.CostEstimate(flops=0, transcendentals=0, bytes_accessed=2 * total),
    )(*parts)


def pack_rows(pieces, width):
    flat = jnp.concatenate(pieces)
    return jnp.pad(flat, (0, width - flat.shape[0]))[None, :]


def split_owned(packed, sizes):
    out = []
    at = 0
    for size in sizes:
        out.append(packed[:, at : at + size].reshape(-1))
        at += size
    return out


def on_device(
    inputs,
    w_qkv,
    qv_bias,
    w_out,
    out_bias,
    ln1_gain,
    ln1_shift,
    ln2_gain,
    ln2_shift,
    w_up,
    up_bias,
    w_down,
    down_bias,
    segment_ids,
    valid,
    cotangent,
    mesh_shape=None,
):
    row_count = inputs.shape[0]
    model_width = inputs.shape[1]
    seq_count = segment_ids.shape[0]
    seq_len = segment_ids.shape[1]
    head_count = model_width // HD
    n_dev = mesh_shape[0] * mesh_shape[1]
    small = (qv_bias, out_bias, ln1_gain, ln1_shift, ln2_gain, ln2_shift, up_bias, down_bias)
    small_sizes = [a.shape[0] for a in small]
    n_small = sum(small_sizes)
    width_q = w_qkv.shape[1]
    rows_q = w_qkv.shape[0]
    rows_o = w_out.size // width_q
    rows_u = w_up.size // width_q
    up_view = 16
    ring_up = mesh_shape == (8, 4) and w_up.size % (2 * up_view * 128) == 0
    pieces = [w_qkv, w_out.reshape(rows_o, width_q)]
    if not ring_up:
        pieces.append(w_up.reshape(rows_u, width_q))
    attn_buf = jnp.concatenate(pieces + [pack_rows(small, width_q)], axis=0)
    attn_all = lax.all_gather(attn_buf, ALL, axis=0, tiled=False)
    qkv_full = attn_all[:, :rows_q].reshape(-1, width_q)
    out_full = attn_all[:, rows_q : rows_q + rows_o].reshape(-1, model_width)
    at = rows_q + rows_o
    if ring_up:
        up_v = w_up.reshape(up_view, -1)
        half_v = up_v.shape[1] // 2
        up_a, up_b = ring_all_gather([up_v[:, :half_v], up_v[:, half_v:]], mesh_shape)
        up_full = jnp.concatenate([up_a, up_b], axis=1).reshape(-1, w_up.shape[1])
    else:
        up_full = attn_all[:, at : at + rows_u].reshape(-1, w_up.shape[1])
        at = at + rows_u
    small_full = split_owned(attn_all[:, at, :n_small], small_sizes)
    qv_full, outb_full, gain_one, shift_one, gain_two, shift_two, upb_full, downb_full = small_full
    down_full = lax.all_gather(w_down, ALL, axis=0, tiled=True)

    gain_one = gain_one.astype(jnp.float32)
    shift_one = shift_one.astype(jnp.float32)
    qv_full = qv_full.astype(jnp.float32)
    rows = inputs.astype(jnp.float32)
    normed_one, recip_one = norm_parts(rows)
    h_one = (normed_one * gain_one + shift_one).astype(jnp.bfloat16)
    qkv_rows = jnp.dot(h_one, qkv_full, preferred_element_type=jnp.float32)
    zero_bias = jnp.zeros((model_width,), jnp.float32)
    qkv_bias = jnp.concatenate([qv_full[:model_width], zero_bias, qv_full[model_width:]])
    qkv_b = (qkv_rows + qkv_bias).astype(jnp.bfloat16)
    attended = attention_fwd(qkv_b, segment_ids, valid)
    mid_rows = (
        rows
        + jnp.dot(attended, out_full, preferred_element_type=jnp.float32)
        + outb_full.astype(jnp.float32)
    )
    gain_two = gain_two.astype(jnp.float32)
    shift_two = shift_two.astype(jnp.float32)
    normed_two, recip_two = norm_parts(mid_rows)
    h_two = (normed_two * gain_two + shift_two).astype(jnp.bfloat16)
    upper = jnp.dot(h_two, up_full, preferred_element_type=jnp.float32) + upb_full.astype(
        jnp.float32
    )
    upper = lax.optimization_barrier(upper)
    gelu_rows = jax.nn.gelu(upper, approximate=False).astype(jnp.bfloat16)
    out_rows = (
        mid_rows
        + jnp.dot(gelu_rows, down_full, preferred_element_type=jnp.float32)
        + downb_full.astype(jnp.float32)
    )
    block_out = out_rows.astype(jnp.bfloat16)
    dy_rows = cotangent.astype(jnp.float32)
    grad_wdown = jnp.einsum("tf,td->fd", gelu_rows, cotangent, preferred_element_type=jnp.float32)
    grad_bdown = col_sum(cotangent)
    grad_g = jnp.einsum("td,fd->tf", cotangent, down_full, preferred_element_type=jnp.float32)
    cdf_part = 0.5 * (1.0 + jax.scipy.special.erf(upper * 0.7071067811865476))
    pdf_part = jnp.exp(-0.5 * upper * upper) * 0.3989422804014327
    grad_u = (grad_g * (cdf_part + upper * pdf_part)).astype(jnp.bfloat16)
    grad_bup = col_sum(grad_u)
    grad_wup = jnp.einsum("td,tf->df", h_two, grad_u, preferred_element_type=jnp.float32)
    grad_h2 = jnp.einsum("tf,df->td", grad_u, up_full, preferred_element_type=jnp.float32)
    grad_g2 = jnp.sum(grad_h2 * normed_two, axis=0)
    grad_c2 = jnp.sum(grad_h2, axis=0)
    grad_mid = dy_rows + norm_back(grad_h2, gain_two, normed_two, recip_two)
    grad_a = grad_mid.astype(jnp.bfloat16)
    grad_wout = jnp.einsum("tc,td->cd", attended, grad_a, preferred_element_type=jnp.float32)
    grad_bout = col_sum(grad_a)
    grad_o = jnp.einsum("td,cd->tc", grad_a, out_full, preferred_element_type=jnp.float32).astype(
        jnp.bfloat16
    )
    grad_qkv = attention_bwd(qkv_b, grad_o, segment_ids, valid)
    grad_cols = col_sum(grad_qkv)
    grad_bqv = jnp.concatenate([grad_cols[:model_width], grad_cols[2 * model_width :]])
    grad_wqkv = jnp.einsum("td,te->de", h_one, grad_qkv, preferred_element_type=jnp.float32)
    grad_h1 = jnp.einsum("te,de->td", grad_qkv, qkv_full, preferred_element_type=jnp.float32)
    grad_g1 = jnp.sum(grad_h1 * normed_one, axis=0)
    grad_c1 = jnp.sum(grad_h1, axis=0)
    grad_inputs = grad_mid + norm_back(grad_h1, gain_one, normed_one, recip_one)

    small_grads = (grad_bqv, grad_bout, grad_g1, grad_c1, grad_g2, grad_c2, grad_bup, grad_bdown)
    owned = jnp.concatenate([g.reshape(n_dev, -1) for g in small_grads], axis=1)
    lanes = 128
    small_rows = 8 * pl.cdiv(pl.cdiv(n_small, lanes), 8)
    owned = jnp.pad(owned, ((0, 0), (0, small_rows * lanes - n_small))).reshape(-1, lanes)
    parts = [
        (grad_wqkv, w_qkv.shape[0], True),
        (grad_wout, w_out.shape[0], True),
        (grad_wup, w_up.shape[0], True),
        (owned, small_rows, False),
    ]
    down_sum = lax.psum_scatter(grad_wdown, ALL, scatter_dimension=0, tiled=True)
    if all(rb % 8 == 0 and a.shape[1] % 256 == 0 for (a, rb, _) in parts[:3]):
        sums = ring_reduce_scatter(parts, mesh_shape, after=(grad_inputs, block_out))
    else:
        sums = [lax.psum_scatter(a, ALL, scatter_dimension=0, tiled=True) for (a, _, _) in parts]
    sums = list(sums[:3]) + [down_sum] + list(sums[3:])
    small_sums = split_owned(sums[4].reshape(1, -1), small_sizes)
    bqv, bout, g1, c1, g2, c2, bup, bdown = small_sums
    return (
        block_out,
        grad_inputs,
        sums[0],
        bqv,
        sums[1],
        bout,
        g1,
        c1,
        g2,
        c2,
        sums[2],
        bup,
        sums[3],
        bdown,
    )


def solution(mesh):
    in_specs = (
        P(("wide", "narrow"), None),
        P(("wide", "narrow"), None),
        P(("wide", "narrow")),
        P(("wide", "narrow"), None),
        P(("wide", "narrow")),
        P(("wide", "narrow")),
        P(("wide", "narrow")),
        P(("wide", "narrow")),
        P(("wide", "narrow")),
        P(("wide", "narrow"), None),
        P(("wide", "narrow")),
        P(("wide", "narrow"), None),
        P(("wide", "narrow")),
        P(("wide", "narrow"), None),
        P(("wide", "narrow"), None),
        P(("wide", "narrow"), None),
    )
    out_specs = (
        P(("wide", "narrow"), None),
        P(("wide", "narrow"), None),
        P(("wide", "narrow"), None),
        P(("wide", "narrow")),
        P(("wide", "narrow"), None),
        P(("wide", "narrow")),
        P(("wide", "narrow")),
        P(("wide", "narrow")),
        P(("wide", "narrow")),
        P(("wide", "narrow")),
        P(("wide", "narrow"), None),
        P(("wide", "narrow")),
        P(("wide", "narrow"), None),
        P(("wide", "narrow")),
    )
    body = functools.partial(on_device, mesh_shape=(mesh.shape["wide"], mesh.shape["narrow"]))
    return jax.shard_map(
        body, mesh=mesh, in_specs=in_specs, out_specs=out_specs, check_vma=False
    )
```

```python
import functools
import jax
import jax.numpy as jnp
from jax import lax
from jax.experimental import pallas as pl
from jax.experimental.pallas import tpu as pltpu
from jax.sharding import PartitionSpec as P

HD = 64
ALL = ("wide", "narrow")

EPSILON = 1e-06


def norm_parts(rows):
    center = rows - jnp.mean(rows, axis=-1, keepdims=True)
    recip = lax.rsqrt(jnp.mean(center * center, axis=-1, keepdims=True) + EPSILON)
    return (center * recip, recip)


def norm_back(grad_h, gain, normed, recip):
    scaled = grad_h * gain
    return recip * (
        scaled
        - jnp.mean(scaled, axis=-1, keepdims=True)
        - normed * jnp.mean(scaled * normed, axis=-1, keepdims=True)
    )


def col_sum(rows):
    return jnp.sum(rows.astype(jnp.float32), axis=0)


def seg_mask(seg_col, seg_row, val_row, n):
    rows = lax.broadcasted_iota(jnp.int32, (n, n), 0)
    cols = lax.broadcasted_iota(jnp.int32, (n, n), 1)
    return (seg_col == seg_row) & ((val_row == 1) | (rows == cols))


def soft_rows(qh, kh, allowed):
    scores = lax.dot_general(qh, kh, (((1,), (1,)), ((), ())), preferred_element_type=jnp.float32)
    scores = jnp.where(allowed, scores * (1.0 / HD**0.5), -1e30)
    top = jnp.max(scores, axis=-1, keepdims=True)
    expo = jnp.exp(scores - top)
    return expo * (1.0 / jnp.sum(expo, axis=-1, keepdims=True))


def attn_fwd_kernel(q_ref, k_ref, v_ref, sc_ref, sr_ref, vr_ref, o_ref):
    n = q_ref.shape[0]
    allowed = seg_mask(sc_ref[...], sr_ref[...], vr_ref[...], n)
    outs = []
    for j in range(q_ref.shape[1] // HD):
        cols = slice(j * HD, (j + 1) * HD)
        probs = soft_rows(q_ref[:, cols], k_ref[:, cols], allowed).astype(jnp.bfloat16)
        outs.append(jnp.dot(probs, v_ref[:, cols], preferred_element_type=jnp.float32))
    o_ref[...] = jnp.concatenate(outs, axis=1).astype(o_ref.dtype)


def attn_bwd_kernel(q_ref, k_ref, v_ref, do_ref, sc_ref, sr_ref, vr_ref, dqkv_ref):
    n = q_ref.shape[0]
    width = q_ref.shape[1]
    hp = pl.program_id(1)
    model_width = dqkv_ref.shape[1] // 3
    allowed = seg_mask(sc_ref[...], sr_ref[...], vr_ref[...], n)
    dqs, dks, dvs = [], [], []
    for j in range(width // HD):
        cols = slice(j * HD, (j + 1) * HD)
        qh, kh, vh, doh = q_ref[:, cols], k_ref[:, cols], v_ref[:, cols], do_ref[:, cols]
        probs = soft_rows(qh, kh, allowed)
        dvs.append(
            lax.dot_general(probs.astype(jnp.bfloat16), doh, (((0,), (0,)), ((), ())),
                            preferred_element_type=jnp.float32)
        )
        dprobs = lax.dot_general(doh, vh, (((1,), (1,)), ((), ())), preferred_element_type=jnp.float32)
        row_term = jnp.sum(probs * dprobs, axis=-1, keepdims=True)
        dscore = jnp.where(allowed, probs * (dprobs - row_term), 0.0).astype(jnp.bfloat16)
        dqs.append(jnp.dot(dscore, kh, preferred_element_type=jnp.float32) * (1.0 / HD**0.5))
        dks.append(
            lax.dot_general(dscore, qh, (((0,), (0,)), ((), ())), preferred_element_type=jnp.float32)
            * (1.0 / HD**0.5)
        )
    at = pl.multiple_of(hp * width, width)
    dqkv_ref[:, pl.ds(at, width)] = jnp.concatenate(dqs, axis=1).astype(dqkv_ref.dtype)
    dqkv_ref[:, pl.ds(at + model_width, width)] = jnp.concatenate(dks, axis=1).astype(dqkv_ref.dtype)
    dqkv_ref[:, pl.ds(at + 2 * model_width, width)] = jnp.concatenate(dvs, axis=1).astype(dqkv_ref.dtype)


def mask_operands(segment_ids, valid):
    return (segment_ids[:, :, None], segment_ids[:, None, :], valid[:, None, :])


def attention_fwd(qkv, segment_ids, valid):
    rows, width3 = qkv.shape
    model_width = width3 // 3
    n_seq, seq_len = segment_ids.shape
    blk = 12 * HD
    n_hp = model_width // blk
    off = model_width // blk
    seg_spec = [
        pl.BlockSpec((None, seq_len, 1), lambda s, h: (s, 0, 0)),
        pl.BlockSpec((None, 1, seq_len), lambda s, h: (s, 0, 0)),
        pl.BlockSpec((None, 1, seq_len), lambda s, h: (s, 0, 0)),
    ]
    flops = 4 * n_seq * seq_len * seq_len * model_width
    return pl.pallas_call(
        attn_fwd_kernel,
        out_shape=jax.ShapeDtypeStruct((rows, model_width), jnp.bfloat16),
        grid=(n_seq, n_hp),
        in_specs=[
            pl.BlockSpec((seq_len, blk), lambda s, h: (s, h)),
            pl.BlockSpec((seq_len, blk), lambda s, h: (s, off + h)),
            pl.BlockSpec((seq_len, blk), lambda s, h: (s, 2 * off + h)),
        ]
        + seg_spec,
        out_specs=pl.BlockSpec((seq_len, blk), lambda s, h: (s, h)),
        cost_estimate=pl.CostEstimate(
            flops=flops,
            transcendentals=n_seq * seq_len * seq_len * (model_width // HD),
            bytes_accessed=qkv.size * 2 + rows * model_width * 2,
        ),
    )(qkv, qkv, qkv, *mask_operands(segment_ids, valid))


def attention_bwd(qkv, grad_o, segment_ids, valid):
    rows, width3 = qkv.shape
    model_width = width3 // 3
    n_seq, seq_len = segment_ids.shape
    blk = 12 * HD
    n_hp = model_width // blk
    off = model_width // blk
    seg_spec = [
        pl.BlockSpec((None, seq_len, 1), lambda s, h: (s, 0, 0)),
        pl.BlockSpec((None, 1, seq_len), lambda s, h: (s, 0, 0)),
        pl.BlockSpec((None, 1, seq_len), lambda s, h: (s, 0, 0)),
    ]
    flops = 10 * n_seq * seq_len * seq_len * model_width
    return pl.pallas_call(
        attn_bwd_kernel,
        out_shape=jax.ShapeDtypeStruct((rows, width3), jnp.bfloat16),
        grid=(n_seq, n_hp),
        in_specs=[
            pl.BlockSpec((seq_len, blk), lambda s, h: (s, h)),
            pl.BlockSpec((seq_len, blk), lambda s, h: (s, off + h)),
            pl.BlockSpec((seq_len, blk), lambda s, h: (s, 2 * off + h)),
            pl.BlockSpec((seq_len, blk), lambda s, h: (s, h)),
        ]
        + seg_spec,
        out_specs=pl.BlockSpec((seq_len, width3), lambda s, h: (s, 0)),
        cost_estimate=pl.CostEstimate(
            flops=flops,
            transcendentals=n_seq * seq_len * seq_len * (model_width // HD),
            bytes_accessed=qkv.size * 4 + rows * model_width * 2,
        ),
    )(qkv, qkv, qkv, grad_o, *mask_operands(segment_ids, valid))


MESH_ID = pl.DeviceIdType.MESH


def ring_maps(n_wide, n_narrow):
    n_dev = n_wide * n_narrow
    if (n_wide, n_narrow) == (8, 4):
        def pos_of(w, n):
            z, y, x, c = w // 2, w % 2, n // 2, n % 2
            q = 2 * x + (x + y) % 2
            k = 4 * q + z + (q % 2) * (3 - 2 * z)
            return 2 * k + c

        def coords_of(p):
            k, c = p // 2, p % 2
            q, r = k // 4, k % 4
            z = r + (q % 2) * (3 - 2 * r)
            x = q // 2
            y = (q % 2 + x) % 2
            return z * 2 + y, x * 2 + c

    else:
        def pos_of(w, n):
            return w * n_narrow + n

        def coords_of(p):
            return p // n_narrow, p % n_narrow

    return n_dev, pos_of, coords_of


def ring_reduce_scatter(parts, mesh_shape, after=(), collective_id=0):
    n_wide, n_narrow = mesh_shape
    n_dev, pos_of, coords_of = ring_maps(n_wide, n_narrow)
    specs = []
    for i, (a, rb, split) in enumerate(parts):
        cols = a.shape[1]
        if split:
            specs.append((i, 0, 0, cols // 2))
        else:
            specs.append((i, 0, 0, cols))
    for i, (a, rb, split) in enumerate(parts):
        if split:
            specs.append((i, 1, a.shape[1] // 2, a.shape[1] // 2))
    n_in = len(parts)
    n_after = len(after)
    n_sp = len(specs)
    last_step = n_dev - 2

    def kernel(*refs):
        ins = refs[:n_in]
        outs = refs[n_in + n_after : 2 * n_in + n_after]
        at = 2 * n_in + n_after
        bufs = refs[at : at + n_sp]
        locs = refs[at + n_sp : at + 2 * n_sp]
        send_sem, recv_sem, loc_sem, credit = refs[at + 2 * n_sp :]
        p = pos_of(lax.axis_index("wide"), lax.axis_index("narrow"))
        right = coords_of((p + 1) % n_dev)
        left = coords_of((p + n_dev - 1) % n_dev)
        nbr_send = (right, left)
        nbr_recv = (left, right)

        def rows_of(q, rb):
            cw, cn = coords_of(q % n_dev)
            start = (cw * n_narrow + cn) * rb
            if rb % 8 == 0:
                start = pl.multiple_of(start, 8)
            return pl.ds(start, rb)

        def remote(j, s):
            return pltpu.make_async_remote_copy(
                src_ref=bufs[j].at[s % 3],
                dst_ref=bufs[j].at[(s + 1) % 3],
                send_sem=send_sem.at[j, s % 3],
                recv_sem=recv_sem.at[j, (s + 1) % 3],
                device_id=nbr_send[specs[j][1]],
                device_id_type=MESH_ID,
            )

        def local(j, s):
            i, dirn, c0, cw = specs[j]
            q = (p + 2 * n_dev - s - 2) if dirn == 0 else (p + s + 2)
            return pltpu.make_async_copy(
                ins[i].at[rows_of(q, parts[i][1]), pl.ds(c0, cw)], locs[j].at[s % 2], loc_sem.at[j, s % 2]
            )

        barrier = pltpu.get_barrier_semaphore()
        for nb in (left, right):
            pl.semaphore_signal(barrier, 1, device_id=nb, device_id_type=MESH_ID)
        pl.semaphore_wait(barrier, 2)

        for j, (i, dirn, c0, cw) in enumerate(specs):
            q = p + n_dev - 1 if dirn == 0 else p + 1
            cp = pltpu.make_async_copy(
                ins[i].at[rows_of(q, parts[i][1]), pl.ds(c0, cw)], bufs[j].at[0], loc_sem.at[j, 1]
            )
            cp.start()
            cp.wait()
        for j in range(n_sp):
            remote(j, 0).start()
            local(j, 0).start()

        def step(s, carry):
            for j in range(n_sp):
                dirn = specs[j][1]
                local(j, s).wait()
                remote(j, s).wait_recv()
                nxt = (s + 1) % 3
                bufs[j][nxt] = bufs[j][nxt] + locs[j][s % 2]
                if j == 0 or specs[j - 1][1] != dirn:

                    @pl.when((s >= 1) & (s + 1 <= last_step))
                    def _():
                        pl.semaphore_wait(credit.at[dirn], 1)

                @pl.when(s + 1 <= last_step)
                def _():
                    remote(j, s + 1).start()
                    local(j, s + 1).start()

            for j in range(n_sp):
                remote(j, s).wait_send()
            for dirn in (0, 1):

                @pl.when(s <= last_step - 2)
                def _():
                    pl.semaphore_signal(
                        credit.at[dirn], 1, device_id=nbr_recv[dirn], device_id_type=MESH_ID
                    )

            return carry

        lax.fori_loop(0, last_step + 1, step, 0)
        fin = (last_step + 1) % 3
        for j, (i, dirn, c0, cw) in enumerate(specs):
            outs[i][:, pl.ds(c0, cw)] = bufs[j][fin]

    out_shape = [jax.ShapeDtypeStruct((rb, a.shape[1]), a.dtype) for (a, rb, _) in parts]
    scratch = [pltpu.VMEM((3, parts[i][1], cw), jnp.float32) for (i, _, _, cw) in specs]
    scratch += [pltpu.VMEM((2, parts[i][1], cw), jnp.float32) for (i, _, _, cw) in specs]
    scratch += [
        pltpu.SemaphoreType.DMA((n_sp, 3)),
        pltpu.SemaphoreType.DMA((n_sp, 3)),
        pltpu.SemaphoreType.DMA((n_sp, 2)),
        pltpu.SemaphoreType.REGULAR((2,)),
    ]
    total = sum(a.size * 4 for (a, _, _) in parts)
    return pl.pallas_call(
        kernel,
        out_shape=out_shape,
        in_specs=[pl.BlockSpec(memory_space=pl.ANY)] * (n_in + n_after),
        out_specs=[pl.BlockSpec(memory_space=pltpu.VMEM)] * n_in,
        scratch_shapes=scratch,
        compiler_params=pltpu.CompilerParams(
            collective_id=collective_id, has_side_effects=True, vmem_limit_bytes=48 * 1024 * 1024
        ),
        cost_estimate=pl.CostEstimate(flops=total // 4, transcendentals=0, bytes_accessed=2 * total),
    )(*[a for (a, _, _) in parts], *after)


def ring_all_gather(parts, mesh_shape, collective_id=1):
    n_wide, n_narrow = mesh_shape
    n_dev, pos_of, coords_of = ring_maps(n_wide, n_narrow)
    n_in = len(parts)
    steps = (n_dev // 2, n_dev - 1 - n_dev // 2)

    def kernel(*refs):
        ins = refs[:n_in]
        outs = refs[n_in : 2 * n_in]
        send_sem, recv_sem, loc_sem = refs[2 * n_in :]
        p = pos_of(lax.axis_index("wide"), lax.axis_index("narrow"))
        right = coords_of((p + 1) % n_dev)
        left = coords_of((p + n_dev - 1) % n_dev)
        nbr_send = (right, left)

        def rows_of(q, rb):
            cw, cn = coords_of(q % n_dev)
            return pl.ds(pl.multiple_of((cw * n_narrow + cn) * rb, rb), rb)

        def copy(i, dirn, s, q):
            view = outs[i].at[rows_of(q, parts[i].shape[0])]
            return pltpu.make_async_remote_copy(
                src_ref=view,
                dst_ref=view,
                send_sem=send_sem.at[dirn, i, s],
                recv_sem=recv_sem.at[dirn, i, s],
                device_id=nbr_send[dirn],
                device_id_type=MESH_ID,
            )

        def sent(i, dirn, s):
            return copy(i, dirn, s, (p + n_dev - s) if dirn == 0 else (p + s))

        def arriving(i, dirn, s):
            return copy(i, dirn, s, (p + n_dev - 1 - s) if dirn == 0 else (p + 1 + s))

        barrier = pltpu.get_barrier_semaphore()
        for nb in (left, right):
            pl.semaphore_signal(barrier, 1, device_id=nb, device_id_type=MESH_ID)
        pl.semaphore_wait(barrier, 2)

        for i in range(n_in):
            cp = pltpu.make_async_copy(ins[i], outs[i].at[rows_of(p, parts[i].shape[0])], loc_sem.at[i])
            cp.start()
            cp.wait()

        def step(s, carry):
            for dirn in (0, 1):

                @pl.when(s < steps[dirn])
                def _():
                    for i in range(n_in):

                        @pl.when(s >= 1)
                        def _():
                            arriving(i, dirn, s - 1).wait_recv()

                        sent(i, dirn, s).start()

            return carry

        lax.fori_loop(0, steps[0], step, 0)
        for dirn in (0, 1):
            for i in range(n_in):
                arriving(i, dirn, steps[dirn] - 1).wait_recv()

        def drain(s, carry):
            for dirn in (0, 1):

                @pl.when(s < steps[dirn])
                def _():
                    for i in range(n_in):
                        sent(i, dirn, s).wait_send()

            return carry

        lax.fori_loop(0, steps[0], drain, 0)

    out_shape = [jax.ShapeDtypeStruct((n_dev * a.shape[0], a.shape[1]), a.dtype) for a in parts]
    total = sum(n_dev * a.size * a.dtype.itemsize for a in parts)
    return pl.pallas_call(
        kernel,
        out_shape=out_shape,
        in_specs=[pl.BlockSpec(memory_space=pl.ANY)] * n_in,
        out_specs=[pl.BlockSpec(memory_space=pltpu.VMEM)] * n_in,
        scratch_shapes=[
            pltpu.SemaphoreType.DMA((2, n_in, steps[0])),
            pltpu.SemaphoreType.DMA((2, n_in, steps[0])),
            pltpu.SemaphoreType.DMA((n_in,)),
        ],
        compiler_params=pltpu.CompilerParams(collective_id=collective_id, has_side_effects=True),
        cost_estimate=pl.CostEstimate(flops=0, transcendentals=0, bytes_accessed=2 * total),
    )(*parts)


def pack_rows(pieces, width):
    flat = jnp.concatenate(pieces)
    return jnp.pad(flat, (0, width - flat.shape[0]))[None, :]


def split_owned(packed, sizes):
    out = []
    at = 0
    for size in sizes:
        out.append(packed[:, at : at + size].reshape(-1))
        at += size
    return out


def on_device(
    inputs,
    w_qkv,
    qv_bias,
    w_out,
    out_bias,
    ln1_gain,
    ln1_shift,
    ln2_gain,
    ln2_shift,
    w_up,
    up_bias,
    w_down,
    down_bias,
    segment_ids,
    valid,
    cotangent,
    mesh_shape=None,
):
    row_count = inputs.shape[0]
    model_width = inputs.shape[1]
    seq_count = segment_ids.shape[0]
    seq_len = segment_ids.shape[1]
    head_count = model_width // HD
    n_dev = mesh_shape[0] * mesh_shape[1]
    small = (qv_bias, out_bias, ln1_gain, ln1_shift, ln2_gain, ln2_shift, up_bias, down_bias)
    small_sizes = [a.shape[0] for a in small]
    n_small = sum(small_sizes)
    width_q = w_qkv.shape[1]
    rows_q = w_qkv.shape[0]
    rows_o = w_out.size // width_q
    rows_u = w_up.size // width_q
    up_view = 16
    ring_up = mesh_shape == (8, 4) and w_up.size % (2 * up_view * 128) == 0
    ring_up = ring_up and w_out.size % (up_view * 128) == 0 and w_up.size % (4 * up_view * 128) == 0
    pieces = [w_qkv]
    if not ring_up:
        pieces += [w_out.reshape(rows_o, width_q), w_up.reshape(rows_u, width_q)]
    attn_buf = jnp.concatenate(pieces + [pack_rows(small, width_q)], axis=0)
    attn_all = lax.all_gather(attn_buf, ALL, axis=0, tiled=False)
    qkv_full = attn_all[:, :rows_q].reshape(-1, width_q)
    at = rows_q
    if ring_up:
        up_v = w_up.reshape(up_view, -1)
        quarter = up_v.shape[1] // 4
        got = ring_all_gather(
            [w_out.reshape(up_view, -1)] + [up_v[:, k * quarter : (k + 1) * quarter] for k in range(4)],
            mesh_shape,
        )
        out_full = got[0].reshape(-1, model_width)
        up_full = jnp.concatenate(got[1:], axis=1).reshape(-1, w_up.shape[1])
    else:
        out_full = attn_all[:, at : at + rows_o].reshape(-1, model_width)
        at = at + rows_o
        up_full = attn_all[:, at : at + rows_u].reshape(-1, w_up.shape[1])
        at = at + rows_u
    small_full = split_owned(attn_all[:, at, :n_small], small_sizes)
    qv_full, outb_full, gain_one, shift_one, gain_two, shift_two, upb_full, downb_full = small_full
    down_full = lax.all_gather(w_down, ALL, axis=0, tiled=True)

    gain_one = gain_one.astype(jnp.float32)
    shift_one = shift_one.astype(jnp.float32)
    qv_full = qv_full.astype(jnp.float32)
    rows = inputs.astype(jnp.float32)
    normed_one, recip_one = norm_parts(rows)
    h_one = (normed_one * gain_one + shift_one).astype(jnp.bfloat16)
    qkv_rows = jnp.dot(h_one, qkv_full, preferred_element_type=jnp.float32)
    zero_bias = jnp.zeros((model_width,), jnp.float32)
    qkv_bias = jnp.concatenate([qv_full[:model_width], zero_bias, qv_full[model_width:]])
    qkv_b = (qkv_rows + qkv_bias).astype(jnp.bfloat16)
    attended = attention_fwd(qkv_b, segment_ids, valid)
    mid_rows = (
        rows
        + jnp.dot(attended, out_full, preferred_element_type=jnp.float32)
        + outb_full.astype(jnp.float32)
    )
    gain_two = gain_two.astype(jnp.float32)
    shift_two = shift_two.astype(jnp.float32)
    normed_two, recip_two = norm_parts(mid_rows)
    h_two = (normed_two * gain_two + shift_two).astype(jnp.bfloat16)
    upper = jnp.dot(h_two, up_full, preferred_element_type=jnp.float32) + upb_full.astype(
        jnp.float32
    )
    upper = lax.optimization_barrier(upper)
    gelu_rows = jax.nn.gelu(upper, approximate=False).astype(jnp.bfloat16)
    out_rows = (
        mid_rows
        + jnp.dot(gelu_rows, down_full, preferred_element_type=jnp.float32)
        + downb_full.astype(jnp.float32)
    )
    block_out = out_rows.astype(jnp.bfloat16)
    dy_rows = cotangent.astype(jnp.float32)
    grad_wdown = jnp.einsum("tf,td->fd", gelu_rows, cotangent, preferred_element_type=jnp.float32)
    grad_bdown = col_sum(cotangent)
    grad_g = jnp.einsum("td,fd->tf", cotangent, down_full, preferred_element_type=jnp.float32)
    cdf_part = 0.5 * (1.0 + jax.scipy.special.erf(upper * 0.7071067811865476))
    pdf_part = jnp.exp(-0.5 * upper * upper) * 0.3989422804014327
    grad_u = (grad_g * (cdf_part + upper * pdf_part)).astype(jnp.bfloat16)
    grad_bup = col_sum(grad_u)
    grad_wup = jnp.einsum("td,tf->df", h_two, grad_u, preferred_element_type=jnp.float32)
    grad_h2 = jnp.einsum("tf,df->td", grad_u, up_full, preferred_element_type=jnp.float32)
    grad_g2 = jnp.sum(grad_h2 * normed_two, axis=0)
    grad_c2 = jnp.sum(grad_h2, axis=0)
    grad_mid = dy_rows + norm_back(grad_h2, gain_two, normed_two, recip_two)
    grad_a = grad_mid.astype(jnp.bfloat16)
    grad_wout = jnp.einsum("tc,td->cd", attended, grad_a, preferred_element_type=jnp.float32)
    grad_bout = col_sum(grad_a)
    grad_o = jnp.einsum("td,cd->tc", grad_a, out_full, preferred_element_type=jnp.float32).astype(
        jnp.bfloat16
    )
    grad_qkv = attention_bwd(qkv_b, grad_o, segment_ids, valid)
    grad_cols = col_sum(grad_qkv)
    grad_bqv = jnp.concatenate([grad_cols[:model_width], grad_cols[2 * model_width :]])
    grad_wqkv = jnp.einsum("td,te->de", h_one, grad_qkv, preferred_element_type=jnp.float32)
    grad_h1 = jnp.einsum("te,de->td", grad_qkv, qkv_full, preferred_element_type=jnp.float32)
    grad_g1 = jnp.sum(grad_h1 * normed_one, axis=0)
    grad_c1 = jnp.sum(grad_h1, axis=0)
    grad_inputs = grad_mid + norm_back(grad_h1, gain_one, normed_one, recip_one)

    small_grads = (grad_bqv, grad_bout, grad_g1, grad_c1, grad_g2, grad_c2, grad_bup, grad_bdown)
    owned = jnp.concatenate([g.reshape(n_dev, -1) for g in small_grads], axis=1)
    lanes = 128
    small_rows = 8 * pl.cdiv(pl.cdiv(n_small, lanes), 8)
    owned = jnp.pad(owned, ((0, 0), (0, small_rows * lanes - n_small))).reshape(-1, lanes)
    parts = [
        (grad_wqkv, w_qkv.shape[0], True),
        (grad_wout, w_out.shape[0], True),
        (grad_wup, w_up.shape[0], True),
        (owned, small_rows, False),
    ]
    down_sum = lax.psum_scatter(grad_wdown, ALL, scatter_dimension=0, tiled=True)
    if all(rb % 8 == 0 and a.shape[1] % 256 == 0 for (a, rb, _) in parts[:3]):
        sums = ring_reduce_scatter(parts, mesh_shape, after=(grad_inputs, block_out))
    else:
        sums = [lax.psum_scatter(a, ALL, scatter_dimension=0, tiled=True) for (a, _, _) in parts]
    sums = list(sums[:3]) + [down_sum] + list(sums[3:])
    small_sums = split_owned(sums[4].reshape(1, -1), small_sizes)
    bqv, bout, g1, c1, g2, c2, bup, bdown = small_sums
    return (
        block_out,
        grad_inputs,
        sums[0],
        bqv,
        sums[1],
        bout,
        g1,
        c1,
        g2,
        c2,
        sums[2],
        bup,
        sums[3],
        bdown,
    )


def solution(mesh):
    in_specs = (
        P(("wide", "narrow"), None),
        P(("wide", "narrow"), None),
        P(("wide", "narrow")),
        P(("wide", "narrow"), None),
        P(("wide", "narrow")),
        P(("wide", "narrow")),
        P(("wide", "narrow")),
        P(("wide", "narrow")),
        P(("wide", "narrow")),
        P(("wide", "narrow"), None),
        P(("wide", "narrow")),
        P(("wide", "narrow"), None),
        P(("wide", "narrow")),
        P(("wide", "narrow"), None),
        P(("wide", "narrow"), None),
        P(("wide", "narrow"), None),
    )
    out_specs = (
        P(("wide", "narrow"), None),
        P(("wide", "narrow"), None),
        P(("wide", "narrow"), None),
        P(("wide", "narrow")),
        P(("wide", "narrow"), None),
        P(("wide", "narrow")),
        P(("wide", "narrow")),
        P(("wide", "narrow")),
        P(("wide", "narrow")),
        P(("wide", "narrow")),
        P(("wide", "narrow"), None),
        P(("wide", "narrow")),
        P(("wide", "narrow"), None),
        P(("wide", "narrow")),
    )
    body = functools.partial(on_device, mesh_shape=(mesh.shape["wide"], mesh.shape["narrow"]))
    return jax.shard_map(
        body, mesh=mesh, in_specs=in_specs, out_specs=out_specs, check_vma=False
    )
```
